32 devices in a mesh: fsdp: 4 (over x, core), ctx: 4 (over z), tp: 2 (over y).
Axes of the slice: x: 2, y: 2, z: 4, core: 2. Of those that a mesh axis runs over, the one named last changes fastest.
Arguments:
- inputs: bfloat16 [4, 4096, 1024], P('fsdp', 'ctx'), may hold values from -6 to 6
- lengths: int32 [4], P('fsdp'), may hold values from 1024 to 4096, as said below
- first_gain: bfloat16 [1024], P('fsdp'), may hold values from 0.099609375 to 1.8984375
- query_weight: bfloat16 [1024, 1024], P('fsdp', 'tp'), may hold values from -0.25 to 0.25
- key_weight: bfloat16 [1024, 1024], P('fsdp', 'tp'), may hold values from -0.25 to 0.25
- value_weight: bfloat16 [1024, 1024], P('fsdp', 'tp'), may hold values from -0.1875 to 0.1875
- out_weight: bfloat16 [1024, 1024], P('tp', 'fsdp'), may hold values from -1 to 1
- second_gain: bfloat16 [1024], P('fsdp'), may hold values from 0.099609375 to 1.8984375
- gate_weight: bfloat16 [1024, 2816], P('fsdp', 'tp'), may hold values from -0.1875 to 0.1875
- up_weight: bfloat16 [1024, 2816], P('fsdp', 'tp'), may hold values from -0.1875 to 0.1875
- down_weight: bfloat16 [2816, 1024], P('tp', 'fsdp'), may hold values from -0.21875 to 0.21875
- cotangent: bfloat16 [4, 4096, 1024], P('fsdp', 'ctx'), may hold values from -6 to 6
Outputs:
- output: bfloat16 [4, 4096, 1024], P('fsdp', 'ctx')
- input_gradient: bfloat16 [4, 4096, 1024], P('fsdp', 'ctx')
- first_gain_gradient: float32 [1024], P('fsdp')
- query_weight_gradient: float32 [1024, 1024], P('fsdp', 'tp')
- key_weight_gradient: float32 [1024, 1024], P('fsdp', 'tp')
- value_weight_gradient: float32 [1024, 1024], P('fsdp', 'tp')
- out_weight_gradient: float32 [1024, 1024], P('tp', 'fsdp')
- second_gain_gradient: float32 [1024], P('fsdp')
- gate_weight_gradient: float32 [1024, 2816], P('fsdp', 'tp')
- up_weight_gradient: float32 [1024, 2816], P('fsdp', 'tp')
- down_weight_gradient: float32 [2816, 1024], P('tp', 'fsdp')
The draws below stay inside these ranges and needn't reach their ends.
Inputs may be any that keep to these rules, and one draw needn't show every extreme that they name: Positions at lengths[s] and beyond are padding. Some slot has length 4096 and some slot 1024.
All inputs are finite; a program needn't handle non-finite values.
Results may differ from the reference program's by a relative error of at most 0.015.
The reference program's roundings to bfloat16 on the way count: a program that leaves them out, or rounds other values in their place, can miss the bound.
Values may be sent and summed in bfloat16 or wider, within the bound.
A program may use at most 192 MiB of HBM per device.

```python
import jax
import jax.numpy as jnp
from jax import lax

D = 1024
HEADS = 16
HD = 64
FF = 2816
SLOT = 4096
SEQS = 4


def draw_lengths(key, part):
    base = jax.random.randint(jax.random.fold_in(key, 11), (SEQS,), SLOT // 4, SLOT + 1)
    order = jax.random.permutation(jax.random.fold_in(key, 12), SEQS)
    base = base.at[order[0]].set(SLOT)
    base = base.at[order[1]].set(SLOT // 4)
    return base.astype(jnp.int32)


def levels(own_key, dims, shards, least, high):
    loudness = 1.0
    for axis_at, blocks in shards:
        steps = jax.random.uniform(jax.random.fold_in(jax.random.fold_in(own_key, 6), axis_at), (blocks,), jnp.float32, least / len(shards), high / len(shards))
        loudness = loudness * jnp.repeat(jnp.exp(steps), dims[axis_at] // blocks).reshape((-1,) + (1,) * (len(dims) - 1 - axis_at))
    return loudness


def scatter_about(own_key, extent, spread, bound, pieces=(), kind=jnp.bfloat16):
    array = spread * jax.random.normal(own_key, extent, jnp.float32)
    if pieces:
        array = array * levels(own_key, extent, pieces, -0.22, 0.18)
    return jnp.clip(array, -bound, bound).astype(kind)


def setup_inputs(seed: int = 0) -> dict:
    arg_keys = jax.random.split(jax.random.key(seed), 13)
    return {
        "inputs": scatter_about(arg_keys[0], (SEQS, SLOT, D), 1.0, 6.0, ((0, 4), (1, 4))),
        "lengths": draw_lengths(jax.random.fold_in(arg_keys[12], 71), 0),
        "first_gain": jnp.clip(1.0 + 0.18 * jax.random.normal(arg_keys[2], (D,), jnp.float32), 0.099609375, 1.8984375).astype(jnp.bfloat16),
        "query_weight": scatter_about(arg_keys[3], (D, D), (D // 2) ** -0.5, 0.25, ((0, 4), (1, 2))),
        "key_weight": scatter_about(arg_keys[4], (D, D), (D // 2) ** -0.5, 0.25, ((0, 4), (1, 2))),
        "value_weight": scatter_about(arg_keys[5], (D, D), D ** -0.5, 0.1875, ((0, 4), (1, 2))),
        "out_weight": scatter_about(arg_keys[6], (D, D), 32 ** -0.5, 1.0, ((0, 2), (1, 4))),
        "second_gain": jnp.clip(1.0 + 0.18 * jax.random.normal(arg_keys[7], (D,), jnp.float32), 0.099609375, 1.8984375).astype(jnp.bfloat16),
        "gate_weight": scatter_about(arg_keys[8], (D, FF), D ** -0.5, 0.1875, ((0, 4), (1, 2))),
        "up_weight": scatter_about(arg_keys[9], (D, FF), D ** -0.5, 0.1875, ((0, 4), (1, 2))),
        "down_weight": scatter_about(arg_keys[10], (FF, D), (FF // 4) ** -0.5, 0.21875, ((0, 2), (1, 4))),
        "cotangent": scatter_about(arg_keys[11], (SEQS, SLOT, D), 1.0, 6.0, ((0, 4), (1, 4))),
    }


@jax.custom_vjp
def low(v):
    return lax.optimization_barrier(v.astype(jnp.bfloat16)).astype(jnp.float32)

@jax.custom_vjp
def low_back(v):
    return v

def low_keep(v):
    return (low(v), None)

def low_pass(kept, grad):
    return (grad,)

def back_keep(v):
    return (v, None)

def back_low(kept, grad):
    return (low(grad),)
low.defvjp(low_keep, low_pass)
low_back.defvjp(back_keep, back_low)
EPSILON = 1e-05
HIGHEST = lax.Precision.HIGHEST

def normalize(values, gain):
    inverse = lax.rsqrt(lax.optimization_barrier(jnp.mean(values * values, axis=-1, keepdims=True)) + EPSILON)
    return values * inverse * gain

def product(left, right):
    return jnp.dot(left, right, precision=HIGHEST)

def attend_block(queries, start, keys, values, length):
    block_rows = queries.shape[0]
    factor = HD ** (-0.5)
    query_pos = start + jnp.arange(block_rows, dtype=jnp.int32)
    key_pos = jnp.arange(keys.shape[0], dtype=jnp.int32)
    scores = low_back(jnp.einsum('qhd,khd->hqk', queries, keys, precision=HIGHEST) * factor)
    allowed = (key_pos[None, :] <= query_pos[:, None]) & (key_pos[None, :] < length)
    scores = jnp.where(allowed[None], scores, -1000000000.0)
    highest = lax.optimization_barrier(jnp.max(scores, axis=-1, keepdims=True))
    exponent = jnp.exp(scores - highest)
    weights = low(exponent / lax.optimization_barrier(jnp.sum(exponent, axis=-1, keepdims=True)))
    return jnp.einsum('hqk,khd->qhd', weights, values, precision=HIGHEST)

def layer(sequence, length, params):
    first_gain, query_weight, key_weight, value_weight, out_weight, second_gain, gate_weight, up_weight, down_weight = params
    slot_count = sequence.shape[0]
    block_rows = min(512, slot_count)
    normed_one = low(normalize(sequence, first_gain))
    queries = low(low_back(product(normed_one, query_weight))).reshape(slot_count, HEADS, HD)
    keys = low(low_back(product(normed_one, key_weight))).reshape(slot_count, HEADS, HD)
    values = low(low_back(product(normed_one, value_weight))).reshape(slot_count, HEADS, HD)
    starts = (jnp.arange(slot_count // block_rows) * block_rows).astype(jnp.int32)
    blocked = queries.reshape(slot_count // block_rows, block_rows, HEADS, HD)
    checked = jax.checkpoint(attend_block)

    def one_block(operand):
        return checked(operand[0], operand[1], keys, values, length)
    mixture = lax.map(one_block, (blocked, starts))
    attended = low(low_back(mixture.reshape(slot_count, HEADS * HD)))
    middle = sequence + low_back(product(attended, out_weight))
    normed_two = low(normalize(middle, second_gain))
    gate = low_back(product(normed_two, gate_weight))
    upward = low_back(product(normed_two, up_weight))
    hidden = low(jax.nn.silu(gate) * upward)
    result = middle + low_back(product(hidden, down_weight))
    valid = (jnp.arange(slot_count, dtype=jnp.int32) < length).astype(result.dtype)
    return result * valid[:, None]

def reference(inputs, lengths, first_gain, query_weight, key_weight, value_weight, out_weight, second_gain, gate_weight, up_weight, down_weight, cotangent):
    params = (first_gain.astype(jnp.float32), query_weight.astype(jnp.float32), key_weight.astype(jnp.float32), value_weight.astype(jnp.float32), out_weight.astype(jnp.float32), second_gain.astype(jnp.float32), gate_weight.astype(jnp.float32), up_weight.astype(jnp.float32), down_weight.astype(jnp.float32))
    checked_layer = jax.checkpoint(layer)

    def forward(sequences, weights_all):

        def one_slot(operand):
            return checked_layer(operand[0], operand[1], weights_all)
        return lax.map(one_slot, (sequences, lengths))
    output, pullback = jax.vjp(forward, inputs.astype(jnp.float32), params)
    d_inputs, d_params = pullback(cotangent.astype(jnp.float32))
    return (output.astype(jnp.bfloat16), d_inputs.astype(jnp.bfloat16), d_params[0], d_params[1], d_params[2], d_params[3], d_params[4], d_params[5], d_params[6], d_params[7], d_params[8])
```

```python
import functools

import jax
import jax.numpy as jnp
from jax import lax
from jax.experimental import pallas as pl
from jax.experimental.pallas import tpu as pltpu
from jax.sharding import PartitionSpec as P

HD = 64
EPSILON = 1e-05
MASKED = -1000000000.0
NN = (((1,), (0,)), ((), ()))
NT = (((1,), (1,)), ((), ()))
TN = (((0,), (0,)), ((), ()))
BF = jnp.bfloat16
F32 = jnp.float32


def mm(left, right, dims):
    return lax.dot_general(left, right, dims, preferred_element_type=F32)


def spread_keys(keys, start, length):
    rows = keys.shape[0]
    pos = start + lax.broadcasted_iota(jnp.int32, (rows, HD), 0)
    lane = lax.broadcasted_iota(jnp.int32, (rows, HD), 1)
    bias = jnp.where((lane == 0) & (pos >= length), MASKED, 0.0)
    return jnp.concatenate([keys, bias], axis=1).astype(BF)


def spread_queries(queries):
    row = lax.broadcasted_iota(jnp.int32, queries.shape, 0)
    ones = jnp.where(row == 0, 1.0, 0.0)
    return jnp.concatenate([queries * HD**-0.5, ones], axis=0).astype(BF)


def attend_kernel(tile, len_ref, qkv, o_ref, of_ref, lse_ref, kx, qx, vx):
    slabs, _, rows = qkv.shape
    halves = o_ref.shape[1]
    half = rows // halves
    length = len_ref[0]
    per = rows // tile
    blocks = slabs * per
    for z in range(slabs):
        keys = qkv[z, HD : 2 * HD, :].astype(F32).T
        kx[z * rows : (z + 1) * rows, :] = spread_keys(keys, z * rows, length)
        queries = spread_queries(qkv[z, 0:HD, :].astype(F32))
        for b in range(per):
            cut = slice(b * tile, (b + 1) * tile)
            qx[z * per + b] = queries[:, cut]
            vx[z * per + b] = qkv[z, 2 * HD : 3 * HD, cut]
    later = lax.broadcasted_iota(jnp.int32, (tile, tile), 0) > lax.broadcasted_iota(
        jnp.int32, (tile, tile), 1
    )

    def query_block(i, _):
        queries = qx[i]

        def step(j, carry, masked):
            highest, total, mix = carry
            keys = kx[pl.ds(pl.multiple_of(j * tile, tile), tile), :]
            scores = mm(keys, queries, NN)
            if masked:
                scores = jnp.where(later, MASKED, scores)
            new = jnp.maximum(highest, jnp.max(scores, axis=0, keepdims=True))
            scale = jnp.exp(highest - new)
            probs = jnp.exp(scores - new)
            total = total * scale + jnp.sum(probs, axis=0, keepdims=True)
            mix = mix * scale + mm(vx[j], probs.astype(BF), NN)
            return new, total, mix

        first = (
            jnp.full((1, tile), -jnp.inf, F32),
            jnp.zeros((1, tile), F32),
            jnp.zeros((HD, tile), F32),
        )
        carry = lax.fori_loop(0, i, lambda j, c: step(j, c, False), first)
        highest, total, mix = step(i, carry, True)
        mix = mix / total
        z = i // per
        base = lax.rem(i, per) * tile
        of_ref[z, :, pl.ds(pl.multiple_of(base, tile), tile)] = mix
        lse_ref[z, :, pl.ds(pl.multiple_of(base, tile), tile)] = highest + jnp.log(total)
        low = mix.astype(BF)
        if tile >= half:
            for t in range(tile // half):
                o_ref[z, base // half + t] = low[:, t * half : (t + 1) * half]
        else:
            o_ref[z, base // half, :, pl.ds(pl.multiple_of(lax.rem(base, half), tile), tile)] = low
        return 0

    lax.fori_loop(0, blocks, query_block, 0)


def attend(length, qkv, halves, tile):
    slabs, _, rows = qkv.shape
    total = slabs * rows
    tile = min(tile, rows)
    work = total * (total + tile) // 2
    vmem = pl.BlockSpec(memory_space=pltpu.VMEM)
    return pl.pallas_call(
        functools.partial(attend_kernel, tile),
        out_shape=(
            jax.ShapeDtypeStruct((slabs, halves, HD, rows // halves), BF),
            jax.ShapeDtypeStruct((slabs, HD, rows), F32),
            jax.ShapeDtypeStruct((slabs, 1, rows), F32),
        ),
        in_specs=[pl.BlockSpec(memory_space=pltpu.SMEM), vmem],
        out_specs=(vmem, vmem, vmem),
        scratch_shapes=[
            pltpu.VMEM((total, 2 * HD), BF),
            pltpu.VMEM((total // tile, 2 * HD, tile), BF),
            pltpu.VMEM((total // tile, HD, tile), BF),
        ],
        compiler_params=pltpu.CompilerParams(vmem_limit_bytes=40 << 20),
        cost_estimate=pl.CostEstimate(
            flops=work * 256 * 4, bytes_accessed=qkv.size * 4, transcendentals=work
        ),
    )(length, qkv)


def attend_back_kernel(tile, len_ref, qkv, do_ref, of_ref, lse_ref, out, kx, qx, vx, kt, dox, dq, st):
    slabs, _, rows = qkv.shape
    halves, half = do_ref.shape[1], do_ref.shape[3]
    length = len_ref[0]
    per = rows // tile
    blocks = slabs * per
    for z in range(slabs):
        keys = qkv[z, HD : 2 * HD, :]
        kx[z * rows : (z + 1) * rows, :] = spread_keys(keys.astype(F32).T, z * rows, length)
        queries = spread_queries(qkv[z, 0:HD, :].astype(F32))
        values = qkv[z, 2 * HD : 3 * HD, :].astype(F32).T
        vx[z * rows : (z + 1) * rows, :] = jnp.concatenate(
            [values, jnp.zeros((rows, HD), F32)], axis=1
        ).astype(BF)
        d_mix = jnp.concatenate([do_ref[z, t] for t in range(halves)], axis=1)
        delta = jnp.sum(d_mix.astype(F32) * of_ref[z], axis=0, keepdims=True)
        for b in range(per):
            cut = slice(b * tile, (b + 1) * tile)
            n = z * per + b
            qx[n] = queries[:, cut]
            kt[n] = keys[:, cut]
            dox[n, 0:HD] = d_mix[:, cut]
            dox[n, HD : 2 * HD] = jnp.zeros((HD, tile), BF)
            st[n, 0:1] = lse_ref[z, :, cut]
            st[n, 1:2] = delta[:, cut]
    dq[...] = jnp.zeros_like(dq)
    later = lax.broadcasted_iota(jnp.int32, (tile, tile), 0) > lax.broadcasted_iota(
        jnp.int32, (tile, tile), 1
    )

    def key_block(j, _):
        here = pl.ds(pl.multiple_of(j * tile, tile), tile)
        keys = kx[here, :]
        values = vx[here, :]

        def step(i, carry, masked):
            dk, dv = carry
            scores = mm(keys, qx[i], NN)
            if masked:
                scores = jnp.where(later, MASKED, scores)
            probs = jnp.exp(scores - st[i, 0:1])
            d_probs = mm(values, dox[i], NN)
            d_scores = (probs * (d_probs - st[i, 1:2])).astype(BF)
            dv = dv + mm(dox[i, 0:HD], probs.astype(BF), NT)
            dk = dk + mm(qx[i, 0:HD], d_scores, NT)
            dq[i] += mm(kt[j], d_scores, NN)
            return dk, dv

        zero = jnp.zeros((HD, tile), F32)
        carry = step(j, (zero, zero), True)
        dk, dv = lax.fori_loop(j + 1, blocks, lambda i, c: step(i, c, False), carry)
        z = j // per
        cut = pl.ds(pl.multiple_of(lax.rem(j, per) * tile, tile), tile)
        out[z, 0:HD, cut] = (dq[j] * HD**-0.5).astype(BF)
        out[z, HD : 2 * HD, cut] = dk.astype(BF)
        out[z, 2 * HD : 3 * HD, cut] = dv.astype(BF)
        return 0

    lax.fori_loop(0, blocks, key_block, 0)


def attend_back(length, qkv, d_mix, mix, lse, tile):
    slabs, _, rows = qkv.shape
    total = slabs * rows
    tile = min(tile, rows)
    blocks = total // tile
    work = total * (total + tile) // 2
    vmem = pl.BlockSpec(memory_space=pltpu.VMEM)
    return pl.pallas_call(
        functools.partial(attend_back_kernel, tile),
        out_shape=jax.ShapeDtypeStruct((slabs, 3 * HD, rows), BF),
        in_specs=[pl.BlockSpec(memory_space=pltpu.SMEM), vmem, vmem, vmem, vmem],
        out_specs=vmem,
        scratch_shapes=[
            pltpu.VMEM((total, 2 * HD), BF),
            pltpu.VMEM((blocks, 2 * HD, tile), BF),
            pltpu.VMEM((total, 2 * HD), BF),
            pltpu.VMEM((blocks, HD, tile), BF),
            pltpu.VMEM((blocks, 2 * HD, tile), BF),
            pltpu.VMEM((blocks, HD, tile), F32),
            pltpu.VMEM((blocks, 8, tile), F32),
        ],
        compiler_params=pltpu.CompilerParams(vmem_limit_bytes=40 << 20),
        cost_estimate=pl.CostEstimate(
            flops=work * 256 * 10, bytes_accessed=qkv.size * 8, transcendentals=work
        ),
    )(length, qkv, d_mix, mix, lse)


def normalize(values, gain):
    inverse = lax.rsqrt(jnp.mean(values * values, axis=-1, keepdims=True) + EPSILON)
    scaled = values * inverse
    return scaled, inverse, (scaled * gain).astype(BF)


def norm_back(d_normed, scaled, inverse, gain):
    d_scaled = d_normed * gain
    d_gain = jnp.sum(d_normed * scaled, axis=0)
    d_values = inverse * (d_scaled - scaled * jnp.mean(d_scaled * scaled, axis=-1, keepdims=True))
    return d_values, d_gain


def shards(
    inputs,
    lengths,
    first_gain,
    query_weight,
    key_weight,
    value_weight,
    out_weight,
    second_gain,
    gate_weight,
    up_weight,
    down_weight,
    cotangent,
):
    slabs, halves, parts = lax.axis_size("ctx"), lax.axis_size("tp"), lax.axis_size("fsdp")
    rows, width = inputs.shape[1], inputs.shape[2]
    depth = query_weight.shape[0]
    group = query_weight.shape[1] // HD // slabs
    half = rows // halves
    ff = gate_weight.shape[1]
    everywhere = ("tp", "fsdp")
    side = lax.axis_index("tp") * half

    gains = lax.all_gather(jnp.stack([first_gain, second_gain]), "fsdp", axis=1, tiled=True)
    gain_one, gain_two = gains[0].astype(F32), gains[1].astype(F32)
    stacked = jnp.stack(
        [w.reshape(depth, slabs, group, HD) for w in (query_weight, key_weight, value_weight)]
    ).transpose(1, 3, 2, 0, 4)
    qkv_width = slabs * 3 * HD
    w_qkv = lax.all_gather(
        stacked.reshape(depth, group * qkv_width), "fsdp", axis=0, tiled=True
    )
    w_heads = [w_qkv[:, h * qkv_width : (h + 1) * qkv_width] for h in range(group)]
    w_out = lax.all_gather(out_weight, everywhere, axis=0, tiled=False)
    w_out = w_out.reshape(halves, parts, -1, depth).transpose(0, 2, 1, 3).reshape(width, width)
    w_gate = lax.all_gather(gate_weight, everywhere, axis=0, tiled=True).reshape(halves, width, ff)
    w_up = lax.all_gather(up_weight, everywhere, axis=0, tiled=True).reshape(halves, width, ff)
    w_down = lax.all_gather(down_weight.T, everywhere, axis=0, tiled=True).reshape(halves, width, ff)

    residual = inputs[0].astype(F32)
    _, _, normed_one = normalize(residual, gain_one)
    qkv = []
    for h in range(group):
        part = mm(w_heads[h], normed_one, (((0,), (1,)), ((), ()))).astype(BF)
        part = part.reshape(slabs, 3 * HD, rows)
        qkv.append(lax.all_to_all(part, "ctx", 0, 0, tiled=True))
    arrived, saved = [], []
    for h in range(group):
        mix, mix_full, lse = attend(lengths, qkv[h], halves, 1024)
        saved.append((mix_full, lse))
        mix = mix.reshape(slabs * halves, HD, half)
        mix = lax.all_to_all(mix, ("ctx", "tp"), 0, 0, tiled=True)
        arrived.append(mix.reshape(slabs, halves, HD, half))
    attended = jnp.stack(arrived).transpose(2, 1, 0, 3, 4).reshape(width, half)

    position = lax.axis_index("ctx") * rows + side + jnp.arange(half, dtype=jnp.int32)
    valid = (position < lengths[0]).astype(F32)[:, None]
    own = lax.dynamic_slice_in_dim(inputs[0], side, half, 0).astype(F32)
    middle = own + mm(attended, w_out, TN)
    scaled_two, inverse_two, normed_two = normalize(middle, gain_two)
    d_result = lax.dynamic_slice_in_dim(cotangent[0], side, half, 0).astype(F32) * valid
    d_branch = d_result.astype(BF)
    ffn = jnp.zeros((half, width), F32)
    d_normed_two = jnp.zeros((half, width), F32)
    g_ffn = []
    for t in range(halves):
        gate = mm(normed_two, w_gate[t], NN)
        upward = mm(normed_two, w_up[t], NN)
        sigmoid_gate = jax.nn.sigmoid(gate)
        activated = gate * sigmoid_gate
        hidden = (activated * upward).astype(BF)
        ffn = ffn + mm(hidden, w_down[t], NT)
        d_hidden = mm(d_branch, w_down[t], NN)
        d_gate = (d_hidden * upward * sigmoid_gate * (1.0 + gate * (1.0 - sigmoid_gate))).astype(BF)
        d_up = (d_hidden * activated).astype(BF)
        d_normed_two = d_normed_two + mm(d_gate, w_gate[t], NT) + mm(d_up, w_up[t], NT)
        g_ffn.append(
            [
                mm(normed_two, d_gate, TN).astype(BF),
                mm(normed_two, d_up, TN).astype(BF),
                mm(d_branch, hidden, TN).astype(BF),
            ]
        )
    output = ((middle + ffn) * valid).astype(BF)
    output = lax.all_gather(output, "tp", axis=0, tiled=True)
    d_from_two, d_gain_two = norm_back(d_normed_two, scaled_two, inverse_two, gain_two)
    d_middle = d_result + d_from_two
    d_attn = d_middle.astype(BF)
    d_attended = mm(w_out, d_attn, NT).astype(BF)
    d_attended = d_attended.reshape(halves, slabs, group, HD, half).transpose(2, 1, 0, 3, 4)
    d_mix = [
        lax.all_to_all(
            d_attended[h].reshape(slabs * halves, HD, half), ("ctx", "tp"), 0, 0, tiled=True
        ).reshape(slabs, halves, HD, half)
        for h in range(group)
    ]

    d_qkv = [
        lax.all_to_all(
            attend_back(lengths, qkv[h], d_mix[h], *saved[h], 1024), "ctx", 0, 0, tiled=True
        ).reshape(qkv_width, rows)
        for h in range(group)
    ]
    d_normed_one = jnp.zeros((rows, width), F32)
    g_qkv = []
    for h in range(group):
        d_normed_one = d_normed_one + mm(d_qkv[h], w_heads[h], (((0,), (1,)), ((), ())))
        g_qkv.append(mm(normed_one, d_qkv[h], (((0,), (1,)), ((), ()))).astype(BF))
    d_normed_one = lax.psum_scatter(
        d_normed_one.astype(BF), "tp", scatter_dimension=0, tiled=True
    ).astype(F32)
    scaled_one, inverse_one, _ = normalize(own, gain_one)
    d_from_one, d_gain_one = norm_back(d_normed_one, scaled_one, inverse_one, gain_one)
    input_gradient = (d_middle + d_from_one).astype(BF)
    input_gradient = lax.all_gather(input_gradient, "tp", axis=0, tiled=True)

    stack_ffn = jnp.stack(
        [jnp.stack([g.reshape(parts, depth, ff) for g in gs], axis=1) for gs in g_ffn]
    )
    s_ffn = lax.psum_scatter(
        stack_ffn.reshape(halves * parts * 3 * depth, ff), everywhere, scatter_dimension=0, tiled=True
    )
    s_ffn = lax.psum(s_ffn, "ctx").reshape(3, depth, ff).astype(F32)
    g_out = mm(attended, d_attn, NN).astype(BF)
    g_out = g_out.reshape(halves, width // halves, parts, depth).transpose(0, 2, 1, 3)
    s_out = lax.psum_scatter(
        g_out.reshape(width * parts, depth), everywhere, scatter_dimension=0, tiled=True
    )
    s_out = lax.psum(s_out, "ctx").astype(F32)
    s_qkv = lax.psum_scatter(
        jnp.concatenate(g_qkv, axis=1), "fsdp", scatter_dimension=0, tiled=True
    )
    s_qkv = lax.psum(s_qkv, "ctx").reshape(depth, group, slabs, 3, HD).transpose(3, 0, 2, 1, 4)
    s_qkv = s_qkv.reshape(3, depth, slabs * group * HD).astype(F32)
    d_gains = lax.psum(jnp.stack([d_gain_one, d_gain_two]), ("ctx", "tp"))
    d_gains = lax.psum_scatter(d_gains, "fsdp", scatter_dimension=1, tiled=True)
    return (
        output[None],
        input_gradient[None],
        d_gains[0],
        s_qkv[0],
        s_qkv[1],
        s_qkv[2],
        s_out,
        d_gains[1],
        s_ffn[0],
        s_ffn[1],
        s_ffn[2].T,
    )


def solution(mesh):
    rows = P("fsdp", "ctx", None)
    gain = P("fsdp")
    inward = P("fsdp", "tp")
    outward = P("tp", "fsdp")
    return jax.shard_map(
        shards,
        mesh=mesh,
        in_specs=(
            rows, gain, gain, inward, inward, inward, outward, gain, inward, inward, outward, rows,
        ),
        out_specs=(
            rows, rows, gain, inward, inward, inward, outward, gain, inward, inward, outward,
        ),
        check_vma=False,
    )
```

```python
import functools

import jax
import jax.numpy as jnp
from jax import lax
from jax.experimental import pallas as pl
from jax.experimental.pallas import tpu as pltpu
from jax.sharding import PartitionSpec as P

HD = 64
EPSILON = 1e-05
MASKED = -1000000000.0
NN = (((1,), (0,)), ((), ()))
NT = (((1,), (1,)), ((), ()))
TN = (((0,), (0,)), ((), ()))
BF = jnp.bfloat16
F32 = jnp.float32


def mm(left, right, dims):
    return lax.dot_general(left, right, dims, preferred_element_type=F32)


def spread_keys(keys, start, length):
    rows = keys.shape[0]
    pos = start + lax.broadcasted_iota(jnp.int32, (rows, HD), 0)
    lane = lax.broadcasted_iota(jnp.int32, (rows, HD), 1)
    bias = jnp.where((lane == 0) & (pos >= length), MASKED, 0.0)
    return jnp.concatenate([keys, bias], axis=1).astype(BF)


def spread_queries(queries):
    row = lax.broadcasted_iota(jnp.int32, queries.shape, 0)
    ones = jnp.where(row == 0, 1.0, 0.0)
    return jnp.concatenate([queries * HD**-0.5, ones], axis=0).astype(BF)


def attend_kernel(tile, len_ref, qkv, o_ref, of_ref, lse_ref, kx, qx, vx):
    slabs, _, rows = qkv.shape
    halves = o_ref.shape[1]
    half = rows // halves
    length = len_ref[0]
    per = rows // tile
    blocks = slabs * per
    for z in range(slabs):
        keys = qkv[z, HD : 2 * HD, :].astype(F32).T
        kx[z * rows : (z + 1) * rows, :] = spread_keys(keys, z * rows, length)
        queries = spread_queries(qkv[z, 0:HD, :].astype(F32))
        for b in range(per):
            cut = slice(b * tile, (b + 1) * tile)
            qx[z * per + b] = queries[:, cut]
            vx[z * per + b] = qkv[z, 2 * HD : 3 * HD, cut]
    later = lax.broadcasted_iota(jnp.int32, (tile, tile), 0) > lax.broadcasted_iota(
        jnp.int32, (tile, tile), 1
    )

    def query_block(i, _):
        queries = qx[i]

        def step(j, carry, masked):
            highest, total, mix = carry
            keys = kx[pl.ds(pl.multiple_of(j * tile, tile), tile), :]
            scores = mm(keys, queries, NN)
            if masked:
                scores = jnp.where(later, MASKED, scores)
            new = jnp.maximum(highest, jnp.max(scores, axis=0, keepdims=True))
            scale = jnp.exp(highest - new)
            probs = jnp.exp(scores - new)
            total = total * scale + jnp.sum(probs, axis=0, keepdims=True)
            mix = mix * scale + mm(vx[j], probs.astype(BF), NN)
            return new, total, mix

        first = (
            jnp.full((1, tile), -jnp.inf, F32),
            jnp.zeros((1, tile), F32),
            jnp.zeros((HD, tile), F32),
        )
        carry = lax.fori_loop(0, i, lambda j, c: step(j, c, False), first)
        highest, total, mix = step(i, carry, True)
        mix = mix / total
        z = i // per
        base = lax.rem(i, per) * tile
        of_ref[z, :, pl.ds(pl.multiple_of(base, tile), tile)] = mix
        lse_ref[z, :, pl.ds(pl.multiple_of(base, tile), tile)] = highest + jnp.log(total)
        low = mix.astype(BF)
        if tile >= half:
            for t in range(tile // half):
                o_ref[z, base // half + t] = low[:, t * half : (t + 1) * half]
        else:
            o_ref[z, base // half, :, pl.ds(pl.multiple_of(lax.rem(base, half), tile), tile)] = low
        return 0

    lax.fori_loop(0, blocks, query_block, 0)


def attend(length, qkv, halves, tile):
    slabs, _, rows = qkv.shape
    total = slabs * rows
    tile = min(tile, rows)
    work = total * (total + tile) // 2
    vmem = pl.BlockSpec(memory_space=pltpu.VMEM)
    return pl.pallas_call(
        functools.partial(attend_kernel, tile),
        out_shape=(
            jax.ShapeDtypeStruct((slabs, halves, HD, rows // halves), BF),
            jax.ShapeDtypeStruct((slabs, HD, rows), F32),
            jax.ShapeDtypeStruct((slabs, 1, rows), F32),
        ),
        in_specs=[pl.BlockSpec(memory_space=pltpu.SMEM), vmem],
        out_specs=(vmem, vmem, vmem),
        scratch_shapes=[
            pltpu.VMEM((total, 2 * HD), BF),
            pltpu.VMEM((total // tile, 2 * HD, tile), BF),
            pltpu.VMEM((total // tile, HD, tile), BF),
        ],
        compiler_params=pltpu.CompilerParams(vmem_limit_bytes=40 << 20),
        cost_estimate=pl.CostEstimate(
            flops=work * 256 * 4, bytes_accessed=qkv.size * 4, transcendentals=work
        ),
    )(length, qkv)


def attend_back_kernel(tile, len_ref, qkv, do_ref, of_ref, lse_ref, out, kx, qx, vx, kt, dox, dq, st):
    slabs, _, rows = qkv.shape
    halves, half = do_ref.shape[1], do_ref.shape[3]
    length = len_ref[0]
    per = rows // tile
    blocks = slabs * per
    for z in range(slabs):
        keys = qkv[z, HD : 2 * HD, :]
        kx[z * rows : (z + 1) * rows, :] = spread_keys(keys.astype(F32).T, z * rows, length)
        queries = spread_queries(qkv[z, 0:HD, :].astype(F32))
        values = qkv[z, 2 * HD : 3 * HD, :].astype(F32).T
        vx[z * rows : (z + 1) * rows, :] = jnp.concatenate(
            [values, jnp.zeros((rows, HD), F32)], axis=1
        ).astype(BF)
        d_mix = jnp.concatenate([do_ref[z, t] for t in range(halves)], axis=1)
        delta = jnp.sum(d_mix.astype(F32) * of_ref[z], axis=0, keepdims=True)
        for b in range(per):
            cut = slice(b * tile, (b + 1) * tile)
            n = z * per + b
            qx[n] = queries[:, cut]
            kt[n] = keys[:, cut]
            dox[n, 0:HD] = d_mix[:, cut]
            dox[n, HD : 2 * HD] = jnp.zeros((HD, tile), BF)
            st[n, 0:1] = lse_ref[z, :, cut]
            st[n, 1:2] = delta[:, cut]
    dq[...] = jnp.zeros_like(dq)
    later = lax.broadcasted_iota(jnp.int32, (tile, tile), 0) > lax.broadcasted_iota(
        jnp.int32, (tile, tile), 1
    )

    def key_block(j, _):
        here = pl.ds(pl.multiple_of(j * tile, tile), tile)
        keys = kx[here, :]
        values = vx[here, :]

        def step(i, carry, masked):
            dk, dv = carry
            scores = mm(keys, qx[i], NN)
            if masked:
                scores = jnp.where(later, MASKED, scores)
            probs = jnp.exp(scores - st[i, 0:1])
            d_probs = mm(values, dox[i], NN)
            d_scores = (probs * (d_probs - st[i, 1:2])).astype(BF)
            dv = dv + mm(dox[i, 0:HD], probs.astype(BF), NT)
            dk = dk + mm(qx[i, 0:HD], d_scores, NT)
            dq[i] += mm(kt[j], d_scores, NN)
            return dk, dv

        zero = jnp.zeros((HD, tile), F32)
        carry = step(j, (zero, zero), True)
        dk, dv = lax.fori_loop(j + 1, blocks, lambda i, c: step(i, c, False), carry)
        z = j // per
        cut = pl.ds(pl.multiple_of(lax.rem(j, per) * tile, tile), tile)
        out[z, 0:HD, cut] = (dq[j] * HD**-0.5).astype(BF)
        out[z, HD : 2 * HD, cut] = dk.astype(BF)
        out[z, 2 * HD : 3 * HD, cut] = dv.astype(BF)
        return 0

    lax.fori_loop(0, blocks, key_block, 0)


def attend_back(length, qkv, d_mix, mix, lse, tile):
    slabs, _, rows = qkv.shape
    total = slabs * rows
    tile = min(tile, rows)
    blocks = total // tile
    work = total * (total + tile) // 2
    vmem = pl.BlockSpec(memory_space=pltpu.VMEM)
    return pl.pallas_call(
        functools.partial(attend_back_kernel, tile),
        out_shape=jax.ShapeDtypeStruct((slabs, 3 * HD, rows), BF),
        in_specs=[pl.BlockSpec(memory_space=pltpu.SMEM), vmem, vmem, vmem, vmem],
        out_specs=vmem,
        scratch_shapes=[
            pltpu.VMEM((total, 2 * HD), BF),
            pltpu.VMEM((blocks, 2 * HD, tile), BF),
            pltpu.VMEM((total, 2 * HD), BF),
            pltpu.VMEM((blocks, HD, tile), BF),
            pltpu.VMEM((blocks, 2 * HD, tile), BF),
            pltpu.VMEM((blocks, HD, tile), F32),
            pltpu.VMEM((blocks, 8, tile), F32),
        ],
        compiler_params=pltpu.CompilerParams(vmem_limit_bytes=40 << 20),
        cost_estimate=pl.CostEstimate(
            flops=work * 256 * 10, bytes_accessed=qkv.size * 8, transcendentals=work
        ),
    )(length, qkv, d_mix, mix, lse)


def widths(total, step):
    return [(at, min(step, total - at)) for at in range(0, total, step)]


def middle_kernel(
    ff, scal, mix_a, mix_b, own, cot, gain, w_hbm,
    out_ref, dmid_ref, do_a, do_b, acts, normed_ref, branch_ref, dattn_ref, dgain_ref,
    w, att_t, mid, scale, dn, sems,
):
    slabs, halves, _, half = mix_a.shape
    width = own.shape[1]
    inner = width // halves
    base = 3 * ff
    cuts = [(t, base, inner) for t in range(halves)]
    cuts += [(t, k * ff, ff) for t in range(halves) for k in range(3)]
    loads = [
        pltpu.make_async_copy(
            w_hbm.at[t, :, at : at + n], w.at[t, :, at : at + n], sems.at[k]
        )
        for k, (t, at, n) in enumerate(cuts)
    ]
    for load in loads:
        load.start()
    length, first = scal[0], scal[1]
    step = 256
    rows = 64

    for t in range(halves):
        for z in range(slabs):
            at = z * 2 * HD
            att_t[at : at + HD, :] = mix_a[z, t]
            att_t[at + HD : at + 2 * HD, :] = mix_b[z, t]
        acts[t, :, base : base + inner] = att_t[...].astype(F32).T.astype(BF)
    for k in range(halves):
        loads[k].wait()

    def project(n, _):
        cut = pl.ds(pl.multiple_of(n * step, step), step)
        total = own[:, cut].astype(F32)
        for t in range(halves):
            total = total + mm(acts[t, :, base : base + inner], w[t, cut, base : base + inner], NT)
        mid[:, cut] = total
        return 0

    lax.fori_loop(0, width // step, project, 0)

    def row_mask(r):
        pos = first + r * rows + lax.broadcasted_iota(jnp.int32, (rows, 1), 0)
        return jnp.where(pos < length, 1.0, 0.0)

    def norm(r, _):
        cut = pl.ds(pl.multiple_of(r * rows, rows), rows)
        values = mid[cut, :]
        inverse = lax.rsqrt(jnp.mean(values * values, axis=1, keepdims=True) + EPSILON)
        scale[cut, :] = jnp.broadcast_to(inverse, (rows, 128))
        normed_ref[cut, :] = (values * inverse * gain[...]).astype(BF)
        branch_ref[cut, :] = (cot[cut, :].astype(F32) * row_mask(r)).astype(BF)
        return 0

    lax.fori_loop(0, half // rows, norm, 0)

    for t in range(halves):
        for k in range(3):
            loads[halves + 3 * t + k].wait()

        def columns(at, n):
            def cut(k):
                return pl.ds(pl.multiple_of(k * ff + at, 128), n)

            gate = mm(normed_ref[...], w[t, :, cut(0)], NN)
            upward = mm(normed_ref[...], w[t, :, cut(1)], NN)
            d_hidden = mm(branch_ref[...], w[t, :, cut(2)], NN)
            sig = 1.0 / (1.0 + jnp.exp(-gate))
            active = gate * sig
            acts[t, :, cut(2)] = (active * upward).astype(BF)
            acts[t, :, cut(0)] = (
                d_hidden * upward * sig * (1.0 + gate * (1.0 - sig))
            ).astype(BF)
            acts[t, :, cut(1)] = (d_hidden * active).astype(BF)

        def chunk(c, _):
            columns(c * step, step)
            return 0

        lax.fori_loop(0, ff // step, chunk, 0)
        if ff % step:
            columns(ff - ff % step, ff % step)

    def back(n, _):
        cut = pl.ds(pl.multiple_of(n * step, step), step)
        total = mid[:, cut]
        grad = jnp.zeros((half, step), F32)
        for t in range(halves):
            total = total + mm(acts[t, :, 2 * ff : base], w[t, cut, 2 * ff : base], NT)
            grad = grad + mm(acts[t, :, 0:ff], w[t, cut, 0:ff], NT)
            grad = grad + mm(acts[t, :, ff : 2 * ff], w[t, cut, ff : 2 * ff], NT)
        dmid_ref[:, cut] = total
        dn[:, cut] = grad
        return 0

    lax.fori_loop(0, width // step, back, 0)
    dgain_ref[...] = jnp.zeros_like(dgain_ref)

    def finish(r, _):
        cut = pl.ds(pl.multiple_of(r * rows, rows), rows)
        mask = row_mask(r)
        out_ref[cut, :] = (dmid_ref[cut, :] * mask).astype(BF)
        inverse = scale[cut, 0:1]
        scaled = mid[cut, :] * inverse
        grad = dn[cut, :]
        part = grad * scaled
        dgain_ref[...] += jnp.sum(part.reshape(rows // 8, 8, width), axis=0)
        d_scaled = grad * gain[...]
        mean = jnp.mean(d_scaled * scaled, axis=1, keepdims=True)
        total = cot[cut, :].astype(F32) * mask + inverse * (d_scaled - scaled * mean)
        dmid_ref[cut, :] = total
        dattn_ref[cut, :] = total.astype(BF)
        return 0

    lax.fori_loop(0, half // rows, finish, 0)
    for t in range(halves):
        for z in range(0, slabs, 2):
            at = base + z * 2 * HD
            grad = mm(dattn_ref[...], w[t, :, at : at + 4 * HD], NN).T.astype(BF)
            for k in range(2):
                do_a[z + k, t] = grad[2 * k * HD : (2 * k + 1) * HD]
                do_b[z + k, t] = grad[(2 * k + 1) * HD : (2 * k + 2) * HD]


def middle_stage(scalars, mix_a, mix_b, own, cot, gain, w):
    halves, width, lanes = w.shape
    slabs, _, _, half = mix_a.shape
    ff = (lanes - width // halves) // 3
    vmem = pl.BlockSpec(memory_space=pltpu.VMEM)
    flops = 2 * half * width * (6 * ff * halves + 2 * width)
    return pl.pallas_call(
        functools.partial(middle_kernel, ff),
        out_shape=(
            jax.ShapeDtypeStruct((half, width), BF),
            jax.ShapeDtypeStruct((half, width), F32),
            jax.ShapeDtypeStruct(mix_a.shape, BF),
            jax.ShapeDtypeStruct(mix_a.shape, BF),
            jax.ShapeDtypeStruct((halves, half, lanes), BF),
            jax.ShapeDtypeStruct((half, width), BF),
            jax.ShapeDtypeStruct((half, width), BF),
            jax.ShapeDtypeStruct((half, width), BF),
            jax.ShapeDtypeStruct((8, width), F32),
        ),
        in_specs=[pl.BlockSpec(memory_space=pltpu.SMEM)] + [vmem] * 5 + [pl.BlockSpec(memory_space=pl.ANY)],
        out_specs=(vmem,) * 9,
        scratch_shapes=[
            pltpu.VMEM((halves, width, lanes), BF),
            pltpu.VMEM((width // halves, half), BF),
            pltpu.VMEM((half, width), F32),
            pltpu.VMEM((half, 128), F32),
            pltpu.VMEM((half, width), F32),
            pltpu.SemaphoreType.DMA((4 * halves,)),
        ],
        compiler_params=pltpu.CompilerParams(vmem_limit_bytes=58 << 20),
        cost_estimate=pl.CostEstimate(
            flops=flops, bytes_accessed=2 * w.size + 16 * half * width, transcendentals=half * lanes
        ),
    )(scalars, mix_a, mix_b, own, cot, gain, w)


def gradient_kernel(ff, normed, branch, dattn, acts, out_ref, turned):
    base = 3 * ff

    @pl.when(pl.program_id(1) == 0)
    def _():
        for k, ref in enumerate((normed, branch, dattn)):
            turned[k] = ref[...].astype(F32).T.astype(BF)

    lanes = out_ref.shape[2]
    for k, (at, end) in enumerate(((0, 2 * ff), (2 * ff, base), (base, lanes))):
        for b, n in widths(end - at, 1024):
            cut = slice(at + b, at + b + n)
            out_ref[0, :, cut] = mm(turned[k], acts[0, :, cut], NN).astype(BF)


def gradient_stage(normed, branch, dattn, acts, ff):
    halves, half, lanes = acts.shape
    width = normed.shape[1]
    step = 256
    left = pl.BlockSpec((half, step), lambda n, t: (0, n))
    return pl.pallas_call(
        functools.partial(gradient_kernel, ff),
        out_shape=jax.ShapeDtypeStruct((halves, width, lanes), BF),
        grid=(width // step, halves),
        in_specs=[left, left, left, pl.BlockSpec((1, half, lanes), lambda n, t: (t, 0, 0))],
        out_specs=pl.BlockSpec((1, step, lanes), lambda n, t: (t, n, 0)),
        scratch_shapes=[pltpu.VMEM((3, step, half), BF)],
        compiler_params=pltpu.CompilerParams(
            vmem_limit_bytes=40 << 20, dimension_semantics=("arbitrary", "arbitrary")
        ),
        cost_estimate=pl.CostEstimate(
            flops=2 * acts.size * width, bytes_accessed=2 * (acts.size + halves * width * lanes), transcendentals=0
        ),
    )(normed, branch, dattn, acts)


def normalize(values, gain):
    inverse = lax.rsqrt(jnp.mean(values * values, axis=-1, keepdims=True) + EPSILON)
    scaled = values * inverse
    return scaled, inverse, (scaled * gain).astype(BF)


def norm_back(d_normed, scaled, inverse, gain):
    d_scaled = d_normed * gain
    d_gain = jnp.sum(d_normed * scaled, axis=0)
    d_values = inverse * (d_scaled - scaled * jnp.mean(d_scaled * scaled, axis=-1, keepdims=True))
    return d_values, d_gain


def swap_halves(values):
    return lax.ppermute(values, "tp", [(0, 1), (1, 0)])


def both_halves(values):
    half = values.shape[0]
    side = lax.axis_index("tp") * half
    whole = jnp.zeros((2 * half,) + values.shape[1:], values.dtype)
    whole = lax.dynamic_update_slice_in_dim(whole, values, side, 0)
    return lax.dynamic_update_slice_in_dim(whole, swap_halves(values), half - side, 0)


def shards(
    inputs,
    lengths,
    first_gain,
    query_weight,
    key_weight,
    value_weight,
    out_weight,
    second_gain,
    gate_weight,
    up_weight,
    down_weight,
    cotangent,
):
    slabs, halves, parts = lax.axis_size("ctx"), lax.axis_size("tp"), lax.axis_size("fsdp")
    rows, width = inputs.shape[1], inputs.shape[2]
    depth = query_weight.shape[0]
    group = query_weight.shape[1] // HD // slabs
    half = rows // halves
    ff = gate_weight.shape[1]
    everywhere = ("tp", "fsdp")
    side = lax.axis_index("tp") * half

    gains = lax.all_gather(jnp.stack([first_gain, second_gain]), "fsdp", axis=1, tiled=True)
    gain_one, gain_two = gains[0].astype(F32), gains[1].astype(F32)
    stacked = jnp.stack(
        [w.reshape(depth, slabs, group, HD) for w in (query_weight, key_weight, value_weight)]
    ).transpose(1, 3, 2, 0, 4)
    qkv_width = slabs * 3 * HD
    w_qkv = lax.all_gather(
        stacked.reshape(depth, group * qkv_width), "fsdp", axis=0, tiled=True
    )
    w_heads = [w_qkv[:, h * qkv_width : (h + 1) * qkv_width] for h in range(group)]
    w_rest = jnp.concatenate([gate_weight, up_weight, down_weight.T, out_weight.T], axis=1)
    w_rest = lax.all_gather(w_rest, everywhere, axis=0, tiled=True).reshape(halves, width, -1)

    residual = inputs[0].astype(F32)
    _, _, normed_one = normalize(residual, gain_one)
    qkv = []
    for h in range(group):
        part = mm(w_heads[h], normed_one, (((0,), (1,)), ((), ()))).astype(BF)
        part = part.reshape(slabs, 3 * HD, rows)
        qkv.append(lax.all_to_all(part, "ctx", 0, 0, tiled=True))
    arrived, saved = [], []
    for h in range(group):
        mix, mix_full, lse = attend(lengths, qkv[h], halves, 1024)
        saved.append((mix_full, lse))
        mix = mix.reshape(slabs * halves, HD, half)
        mix = lax.all_to_all(mix, ("ctx", "tp"), 0, 0, tiled=True)
        arrived.append(mix.reshape(slabs, halves, HD, half))

    own = lax.dynamic_slice_in_dim(inputs[0], side, half, 0)
    cot = lax.dynamic_slice_in_dim(cotangent[0], side, half, 0)
    scalars = jnp.stack([lengths[0], lax.axis_index("ctx") * rows + side])
    output, d_middle, do_a, do_b, acts, normed_two, d_branch, d_attn, d_gain_two = middle_stage(
        scalars, *arrived, own, cot, gain_two[None], w_rest
    )
    output = both_halves(output)
    d_mix = [
        lax.all_to_all(
            d.reshape(slabs * halves, HD, half), ("ctx", "tp"), 0, 0, tiled=True
        ).reshape(slabs, halves, HD, half)
        for d in (do_a, do_b)
    ]
    g_rest = gradient_stage(normed_two, d_branch, d_attn, acts, ff)
    d_mix[0], g_rest = lax.optimization_barrier((d_mix[0], g_rest))
    s_rest = lax.psum_scatter(
        g_rest.reshape(halves * width, -1), everywhere, scatter_dimension=0, tiled=True
    )
    s_rest = lax.psum(s_rest, "ctx").astype(F32)

    d_qkv = [
        lax.all_to_all(
            attend_back(lengths, qkv[h], d_mix[h], *saved[h], 1024), "ctx", 0, 0, tiled=True
        ).reshape(qkv_width, rows)
        for h in range(group)
    ]
    d_normed_one = jnp.zeros((rows, width), F32)
    g_qkv = []
    for h in range(group):
        d_normed_one = d_normed_one + mm(d_qkv[h], w_heads[h], (((0,), (1,)), ((), ())))
        g_qkv.append(mm(normed_one, d_qkv[h], (((0,), (1,)), ((), ()))).astype(BF))
    theirs = lax.dynamic_slice_in_dim(d_normed_one, half - side, half, 0).astype(BF)
    d_normed_one = lax.dynamic_slice_in_dim(d_normed_one, side, half, 0)
    d_normed_one = d_normed_one + swap_halves(theirs).astype(F32)
    scaled_one, inverse_one, _ = normalize(own.astype(F32), gain_one)
    d_from_one, d_gain_one = norm_back(d_normed_one, scaled_one, inverse_one, gain_one)
    input_gradient = both_halves((d_middle + d_from_one).astype(BF))

    s_qkv = lax.psum_scatter(
        jnp.concatenate(g_qkv, axis=1), "fsdp", scatter_dimension=0, tiled=True
    )
    s_qkv = lax.psum(s_qkv, "ctx").reshape(depth, group, slabs, 3, HD).transpose(3, 0, 2, 1, 4)
    s_qkv = s_qkv.reshape(3, depth, slabs * group * HD).astype(F32)
    d_gains = lax.psum(jnp.stack([d_gain_one, jnp.sum(d_gain_two, axis=0)]), ("fsdp", "ctx", "tp"))
    d_gains = lax.dynamic_slice_in_dim(d_gains, lax.axis_index("fsdp") * depth, depth, 1)
    return (
        output[None],
        input_gradient[None],
        d_gains[0],
        s_qkv[0],
        s_qkv[1],
        s_qkv[2],
        s_rest[:, 3 * ff :].T,
        d_gains[1],
        s_rest[:, :ff],
        s_rest[:, ff : 2 * ff],
        s_rest[:, 2 * ff : 3 * ff].T,
    )


def solution(mesh):
    rows = P("fsdp", "ctx", None)
    gain = P("fsdp")
    inward = P("fsdp", "tp")
    outward = P("tp", "fsdp")
    return jax.shard_map(
        shards,
        mesh=mesh,
        in_specs=(
            rows, gain, gain, inward, inward, inward, outward, gain, inward, inward, outward, rows,
        ),
        out_specs=(
            rows, rows, gain, inward, inward, inward, outward, gain, inward, inward, outward,
        ),
        check_vma=False,
    )
```

```python
import functools

import jax
import jax.numpy as jnp
from jax import lax
from jax.experimental import pallas as pl
from jax.experimental.pallas import tpu as pltpu
from jax.experimental.layout import Layout, with_layout_constraint
from jax.sharding import PartitionSpec as P

HD = 64
EPSILON = 1e-05
MASKED = -1000000000.0
NN = (((1,), (0,)), ((), ()))
NT = (((1,), (1,)), ((), ()))
TN = (((0,), (0,)), ((), ()))
BF = jnp.bfloat16
F32 = jnp.float32


def mm(left, right, dims):
    return lax.dot_general(left, right, dims, preferred_element_type=F32)


def spread_keys(keys, start, length):
    rows = keys.shape[0]
    pos = start + lax.broadcasted_iota(jnp.int32, (rows, HD), 0)
    lane = lax.broadcasted_iota(jnp.int32, (rows, HD), 1)
    bias = jnp.where((lane == 0) & (pos >= length), MASKED, 0.0)
    return jnp.concatenate([keys, bias], axis=1).astype(BF)


def spread_queries(queries):
    row = lax.broadcasted_iota(jnp.int32, queries.shape, 0)
    ones = jnp.where(row == 0, 1.0, 0.0)
    return jnp.concatenate([queries * HD**-0.5, ones], axis=0).astype(BF)


def attend_kernel(tile, len_ref, qkv, o_ref, of_ref, lse_ref, kx, qx, vx):
    slabs, _, rows = qkv.shape
    halves = o_ref.shape[1]
    half = rows // halves
    length = len_ref[0]
    per = rows // tile
    blocks = slabs * per
    for z in range(slabs):
        keys = qkv[z, HD : 2 * HD, :].astype(F32).T
        kx[z * rows : (z + 1) * rows, :] = spread_keys(keys, z * rows, length)
        queries = spread_queries(qkv[z, 0:HD, :].astype(F32))
        for b in range(per):
            cut = slice(b * tile, (b + 1) * tile)
            qx[z * per + b] = queries[:, cut]
            vx[z * per + b] = qkv[z, 2 * HD : 3 * HD, cut]
    later = lax.broadcasted_iota(jnp.int32, (tile, tile), 0) > lax.broadcasted_iota(
        jnp.int32, (tile, tile), 1
    )

    def query_block(i, _):
        queries = qx[i]

        def step(j, carry, masked):
            highest, total, mix = carry
            keys = kx[pl.ds(pl.multiple_of(j * tile, tile), tile), :]
            scores = mm(keys, queries, NN)
            if masked:
                scores = jnp.where(later, MASKED, scores)
            new = jnp.maximum(highest, jnp.max(scores, axis=0, keepdims=True))
            scale = jnp.exp(highest - new)
            probs = jnp.exp(scores - new)
            total = total * scale + jnp.sum(probs, axis=0, keepdims=True)
            mix = mix * scale + mm(vx[j], probs.astype(BF), NN)
            return new, total, mix

        first = (
            jnp.full((1, tile), -jnp.inf, F32),
            jnp.zeros((1, tile), F32),
            jnp.zeros((HD, tile), F32),
        )
        carry = lax.fori_loop(0, i, lambda j, c: step(j, c, False), first)
        highest, total, mix = step(i, carry, True)
        mix = mix / total
        z = i // per
        base = lax.rem(i, per) * tile
        of_ref[z, :, pl.ds(pl.multiple_of(base, tile), tile)] = mix
        lse_ref[z, :, pl.ds(pl.multiple_of(base, tile), tile)] = highest + jnp.log(total)
        low = mix.astype(BF)
        if tile >= half:
            for t in range(tile // half):
                o_ref[z, base // half + t] = low[:, t * half : (t + 1) * half]
        else:
            o_ref[z, base // half, :, pl.ds(pl.multiple_of(lax.rem(base, half), tile), tile)] = low
        return 0

    lax.fori_loop(0, blocks, query_block, 0)


def attend(length, qkv, halves, tile):
    slabs, _, rows = qkv.shape
    total = slabs * rows
    tile = min(tile, rows)
    work = total * (total + tile) // 2
    vmem = pl.BlockSpec(memory_space=pltpu.VMEM)
    return pl.pallas_call(
        functools.partial(attend_kernel, tile),
        out_shape=(
            jax.ShapeDtypeStruct((slabs, halves, HD, rows // halves), BF),
            jax.ShapeDtypeStruct((slabs, HD, rows), F32),
            jax.ShapeDtypeStruct((slabs, 1, rows), F32),
        ),
        in_specs=[pl.BlockSpec(memory_space=pltpu.SMEM), vmem],
        out_specs=(vmem, vmem, vmem),
        scratch_shapes=[
            pltpu.VMEM((total, 2 * HD), BF),
            pltpu.VMEM((total // tile, 2 * HD, tile), BF),
            pltpu.VMEM((total // tile, HD, tile), BF),
        ],
        compiler_params=pltpu.CompilerParams(vmem_limit_bytes=40 << 20),
        cost_estimate=pl.CostEstimate(
            flops=work * 256 * 4, bytes_accessed=qkv.size * 4, transcendentals=work
        ),
    )(length, qkv)


def attend_back_kernel(tile, len_ref, qkv, do_ref, of_ref, lse_ref, out, kx, qx, vx, kt, dox, dq, st):
    slabs, _, rows = qkv.shape
    halves, half = do_ref.shape[1], do_ref.shape[3]
    length = len_ref[0]
    per = rows // tile
    blocks = slabs * per
    for z in range(slabs):
        keys = qkv[z, HD : 2 * HD, :]
        kx[z * rows : (z + 1) * rows, :] = spread_keys(keys.astype(F32).T, z * rows, length)
        queries = spread_queries(qkv[z, 0:HD, :].astype(F32))
        values = qkv[z, 2 * HD : 3 * HD, :].astype(F32).T
        vx[z * rows : (z + 1) * rows, :] = jnp.concatenate(
            [values, jnp.zeros((rows, HD), F32)], axis=1
        ).astype(BF)
        d_mix = jnp.concatenate([do_ref[z, t] for t in range(halves)], axis=1)
        delta = jnp.sum(d_mix.astype(F32) * of_ref[z], axis=0, keepdims=True)
        for b in range(per):
            cut = slice(b * tile, (b + 1) * tile)
            n = z * per + b
            qx[n] = queries[:, cut]
            kt[n] = keys[:, cut]
            dox[n, 0:HD] = d_mix[:, cut]
            dox[n, HD : 2 * HD] = jnp.zeros((HD, tile), BF)
            st[n, 0:1] = lse_ref[z, :, cut]
            st[n, 1:2] = delta[:, cut]
    dq[...] = jnp.zeros_like(dq)
    later = lax.broadcasted_iota(jnp.int32, (tile, tile), 0) > lax.broadcasted_iota(
        jnp.int32, (tile, tile), 1
    )

    def key_block(j, _):
        here = pl.ds(pl.multiple_of(j * tile, tile), tile)
        keys = kx[here, :]
        values = vx[here, :]

        def step(i, carry, masked):
            dk, dv = carry
            scores = mm(keys, qx[i], NN)
            if masked:
                scores = jnp.where(later, MASKED, scores)
            probs = jnp.exp(scores - st[i, 0:1])
            d_probs = mm(values, dox[i], NN)
            d_scores = (probs * (d_probs - st[i, 1:2])).astype(BF)
            dv = dv + mm(dox[i, 0:HD], probs.astype(BF), NT)
            dk = dk + mm(qx[i, 0:HD], d_scores, NT)
            dq[i] += mm(kt[j], d_scores, NN)
            return dk, dv

        zero = jnp.zeros((HD, tile), F32)
        carry = step(j, (zero, zero), True)
        dk, dv = lax.fori_loop(j + 1, blocks, lambda i, c: step(i, c, False), carry)
        z = j // per
        cut = pl.ds(pl.multiple_of(lax.rem(j, per) * tile, tile), tile)
        out[z, 0:HD, cut] = (dq[j] * HD**-0.5).astype(BF)
        out[z, HD : 2 * HD, cut] = dk.astype(BF)
        out[z, 2 * HD : 3 * HD, cut] = dv.astype(BF)
        return 0

    lax.fori_loop(0, blocks, key_block, 0)


def attend_back(length, qkv, d_mix, mix, lse, tile):
    slabs, _, rows = qkv.shape
    total = slabs * rows
    tile = min(tile, rows)
    blocks = total // tile
    work = total * (total + tile) // 2
    vmem = pl.BlockSpec(memory_space=pltpu.VMEM)
    return pl.pallas_call(
        functools.partial(attend_back_kernel, tile),
        out_shape=jax.ShapeDtypeStruct((slabs, 3 * HD, rows), BF),
        in_specs=[pl.BlockSpec(memory_space=pltpu.SMEM), vmem, vmem, vmem, vmem],
        out_specs=vmem,
        scratch_shapes=[
            pltpu.VMEM((total, 2 * HD), BF),
            pltpu.VMEM((blocks, 2 * HD, tile), BF),
            pltpu.VMEM((total, 2 * HD), BF),
            pltpu.VMEM((blocks, HD, tile), BF),
            pltpu.VMEM((blocks, 2 * HD, tile), BF),
            pltpu.VMEM((blocks, HD, tile), F32),
            pltpu.VMEM((blocks, 8, tile), F32),
        ],
        compiler_params=pltpu.CompilerParams(vmem_limit_bytes=40 << 20),
        cost_estimate=pl.CostEstimate(
            flops=work * 256 * 10, bytes_accessed=qkv.size * 8, transcendentals=work
        ),
    )(length, qkv, d_mix, mix, lse)


def widths(total, step):
    return [(at, min(step, total - at)) for at in range(0, total, step)]


def middle_kernel(
    ff, scal, mix_a, mix_b, own, cot, gain, w_hbm,
    out_ref, dmid_ref, do_a, do_b, acts, normed_ref, branch_ref, dattn_ref,
    w, att_t, mid, scale, dn, sems,
):
    slabs, halves, _, half = mix_a.shape
    width = own.shape[1]
    inner = width // halves
    base = 3 * ff
    cuts = [(t, base, inner) for t in range(halves)]
    cuts += [(t, k * ff, ff) for t in range(halves) for k in range(3)]
    loads = [
        pltpu.make_async_copy(
            w_hbm.at[t, :, at : at + n], w.at[t, :, at : at + n], sems.at[k]
        )
        for k, (t, at, n) in enumerate(cuts)
    ]
    for load in loads:
        load.start()
    length, first = scal[0], scal[1]
    step = 256
    rows = 64

    for t in range(halves):
        for z in range(slabs):
            at = z * 2 * HD
            att_t[at : at + HD, :] = mix_a[z, t]
            att_t[at + HD : at + 2 * HD, :] = mix_b[z, t]
        acts[t, :, base : base + inner] = att_t[...].astype(F32).T.astype(BF)
    for k in range(halves):
        loads[k].wait()

    def project(n, _):
        cut = pl.ds(pl.multiple_of(n * step, step), step)
        total = own[:, cut].astype(F32)
        for t in range(halves):
            total = total + mm(acts[t, :, base : base + inner], w[t, cut, base : base + inner], NT)
        mid[:, cut] = total
        return 0

    lax.fori_loop(0, width // step, project, 0)

    def row_mask(r):
        pos = first + r * rows + lax.broadcasted_iota(jnp.int32, (rows, 1), 0)
        return jnp.where(pos < length, 1.0, 0.0)

    def norm(r, _):
        cut = pl.ds(pl.multiple_of(r * rows, rows), rows)
        values = mid[cut, :]
        inverse = lax.rsqrt(jnp.mean(values * values, axis=1, keepdims=True) + EPSILON)
        scale[cut, :] = jnp.broadcast_to(inverse, (rows, 128))
        normed_ref[cut, :] = (values * inverse * gain[...]).astype(BF)
        branch_ref[cut, :] = (cot[cut, :].astype(F32) * row_mask(r)).astype(BF)
        return 0

    lax.fori_loop(0, half // rows, norm, 0)

    for t in range(halves):
        for k in range(3):
            loads[halves + 3 * t + k].wait()

        def columns(at, n):
            def cut(k):
                return pl.ds(pl.multiple_of(k * ff + at, 128), n)

            gate = mm(normed_ref[...], w[t, :, cut(0)], NN)
            upward = mm(normed_ref[...], w[t, :, cut(1)], NN)
            d_hidden = mm(branch_ref[...], w[t, :, cut(2)], NN)
            sig = 1.0 / (1.0 + jnp.exp(-gate))
            active = gate * sig
            acts[t, :, cut(2)] = (active * upward).astype(BF)
            acts[t, :, cut(0)] = (
                d_hidden * upward * sig * (1.0 + gate * (1.0 - sig))
            ).astype(BF)
            acts[t, :, cut(1)] = (d_hidden * active).astype(BF)

        def chunk(c, _):
            columns(c * step, step)
            return 0

        lax.fori_loop(0, ff // step, chunk, 0)
        if ff % step:
            columns(ff - ff % step, ff % step)

    def back(n, _):
        cut = pl.ds(pl.multiple_of(n * step, step), step)
        total = mid[:, cut]
        grad = jnp.zeros((half, step), F32)
        for t in range(halves):
            total = total + mm(acts[t, :, 2 * ff : base], w[t, cut, 2 * ff : base], NT)
            grad = grad + mm(acts[t, :, 0:ff], w[t, cut, 0:ff], NT)
            grad = grad + mm(acts[t, :, ff : 2 * ff], w[t, cut, ff : 2 * ff], NT)
        dmid_ref[:, cut] = total
        dn[:, cut] = grad
        return 0

    lax.fori_loop(0, width // step, back, 0)

    def finish(r, _):
        cut = pl.ds(pl.multiple_of(r * rows, rows), rows)
        mask = row_mask(r)
        out_ref[cut, :] = (dmid_ref[cut, :] * mask).astype(BF)
        inverse = scale[cut, 0:1]
        scaled = mid[cut, :] * inverse
        grad = dn[cut, :]
        d_scaled = grad * gain[...]
        mean = jnp.mean(d_scaled * scaled, axis=1, keepdims=True)
        total = cot[cut, :].astype(F32) * mask + inverse * (d_scaled - scaled * mean)
        dmid_ref[cut, :] = total
        dattn_ref[cut, :] = total.astype(BF)
        return 0

    lax.fori_loop(0, half // rows, finish, 0)
    for t in range(halves):
        for z in range(0, slabs, 2):
            at = base + z * 2 * HD
            grad = mm(dattn_ref[...], w[t, :, at : at + 4 * HD], NN).T.astype(BF)
            for k in range(2):
                do_a[z + k, t] = grad[2 * k * HD : (2 * k + 1) * HD]
                do_b[z + k, t] = grad[(2 * k + 1) * HD : (2 * k + 2) * HD]


def middle_stage(scalars, mix_a, mix_b, own, cot, gain, w):
    halves, width, lanes = w.shape
    slabs, _, _, half = mix_a.shape
    ff = (lanes - width // halves) // 3
    vmem = pl.BlockSpec(memory_space=pltpu.VMEM)
    flops = 2 * half * width * (6 * ff * halves + 2 * width)
    return pl.pallas_call(
        functools.partial(middle_kernel, ff),
        out_shape=(
            jax.ShapeDtypeStruct((half, width), BF),
            jax.ShapeDtypeStruct((half, width), F32),
            jax.ShapeDtypeStruct(mix_a.shape, BF),
            jax.ShapeDtypeStruct(mix_a.shape, BF),
            jax.ShapeDtypeStruct((halves, half, lanes), BF),
            jax.ShapeDtypeStruct((half, width), BF),
            jax.ShapeDtypeStruct((half, width), BF),
            jax.ShapeDtypeStruct((half, width), BF),
        ),
        in_specs=[pl.BlockSpec(memory_space=pltpu.SMEM)] + [vmem] * 5 + [pl.BlockSpec(memory_space=pl.ANY)],
        out_specs=(vmem,) * 8,
        scratch_shapes=[
            pltpu.VMEM((halves, width, lanes), BF),
            pltpu.VMEM((width // halves, half), BF),
            pltpu.VMEM((half, width), F32),
            pltpu.VMEM((half, 128), F32),
            pltpu.VMEM((half, width), F32),
            pltpu.SemaphoreType.DMA((4 * halves,)),
        ],
        compiler_params=pltpu.CompilerParams(vmem_limit_bytes=58 << 20),
        cost_estimate=pl.CostEstimate(
            flops=flops, bytes_accessed=2 * w.size + 16 * half * width, transcendentals=half * lanes
        ),
    )(scalars, mix_a, mix_b, own, cot, gain, w)


def gradient_kernel(cuts, scal, normed, branch, dattn, acts, *refs):
    *outs, turned = refs
    roles = len(outs) == 3

    place = pl.program_id(1) * pl.num_programs(2) + pl.program_id(2)

    @pl.when(pl.program_id(0) == 0)
    def _():
        for k, ref in enumerate((normed, branch, dattn)):
            turned[place, k] = ref[...].astype(F32).T.astype(BF)

    def fill(ref, start, stop, shift):
        for k, (at, end) in enumerate(cuts):
            at, end = max(at, start), min(end, stop)
            for b, n in widths(end - at, 1024):
                value = mm(turned[place, k], acts[0, :, at + b : at + b + n], NN).astype(BF)
                ref[..., at + b - shift : at + b + n - shift] = value.reshape(
                    ref.shape[:-1] + (n,)
                )

    split = outs[0].shape[-1]
    fill(outs[0], 0, split, 0)
    if roles:
        lanes = split + outs[1].shape[-1]

        @pl.when(pl.program_id(1) == 0)
        def _():
            fill(outs[1], split, lanes, split)

        @pl.when(pl.program_id(1) == 1)
        def _():
            fill(outs[2], split, lanes, split)


def gradient_stage(normed, branch, dattn, acts, ff, parts, split):
    halves, half, lanes = acts.shape
    width = normed.shape[1]
    roles = 2 if split < lanes else 1
    step = 256
    blocks = width // step // roles
    cuts = ((0, 2 * ff), (2 * ff, 3 * ff), (3 * ff, lanes))

    def row(r, n, core):
        return n * 2 + lax.rem(1 - r + core[0], 2) if roles == 2 else n

    def left_at(t, r, n, core):
        first = 1 - jnp.minimum(t, 1)
        return (0, first * row(r, n, core) + (1 - first) * row(roles - 1, blocks - 1, core))

    def sent_at(t, r, n, core):
        return (t, n * (1 - r) + (blocks - 1) * r, 0, 0)

    def kept_at(t, r, n, core):
        back = (1 - r) * jnp.minimum(t, 1)
        return (t - back, n * r + (blocks - 1) * back, 0, 0)

    left = pl.BlockSpec((half, step), left_at)
    out_shape = [jax.ShapeDtypeStruct((halves, width, split), BF)]
    out_specs = [pl.BlockSpec((1, step, split), lambda t, r, n, core: (t, row(r, n, core), 0))]
    if roles == 2:
        out_shape += [jax.ShapeDtypeStruct((halves, blocks, step, lanes - split), BF)] * 2
        out_specs += [
            pl.BlockSpec((1, 1, step, lanes - split), sent_at),
            pl.BlockSpec((1, 1, step, lanes - split), kept_at),
        ]
    return pl.pallas_call(
        functools.partial(gradient_kernel, cuts),
        out_shape=out_shape,
        grid_spec=pltpu.PrefetchScalarGridSpec(
            num_scalar_prefetch=1,
            grid=(halves, roles, blocks),
            in_specs=[left, left, left, pl.BlockSpec((1, half, lanes), lambda t, r, n, core: (t, 0, 0))],
            out_specs=out_specs,
            scratch_shapes=[pltpu.VMEM((width // step, 3, step, half), BF)],
        ),
        compiler_params=pltpu.CompilerParams(
            vmem_limit_bytes=40 << 20, dimension_semantics=("arbitrary",) * 3
        ),
        cost_estimate=pl.CostEstimate(
            flops=2 * acts.size * width, bytes_accessed=2 * (acts.size + halves * width * lanes), transcendentals=0
        ),
    )(jnp.reshape(lax.rem(lax.axis_index("fsdp"), 2), (1,)), normed, branch, dattn, acts)


def normalize(values, gain):
    inverse = lax.rsqrt(jnp.mean(values * values, axis=-1, keepdims=True) + EPSILON)
    scaled = values * inverse
    return scaled, inverse, (scaled * gain).astype(BF)


def norm_back(d_normed, scaled, inverse, gain):
    d_scaled = d_normed * gain
    d_values = inverse * (d_scaled - scaled * jnp.mean(d_scaled * scaled, axis=-1, keepdims=True))
    return d_values


def rows_first(values):
    return with_layout_constraint(values, Layout(major_to_minor=tuple(range(values.ndim))))


def swap(values, axis, bit):
    count = lax.axis_size(axis)
    return lax.ppermute(values, axis, [(k, k ^ bit) for k in range(count)])


def plus(left, right):
    return (left.astype(F32) + right.astype(F32)).astype(BF)


def pick(values, index, axis):
    return lax.dynamic_index_in_dim(values, index, axis, keepdims=False)


def both_halves(values):
    half = values.shape[0]
    side = lax.axis_index("tp") * half
    whole = jnp.zeros((2 * half,) + values.shape[1:], values.dtype)
    whole = lax.dynamic_update_slice_in_dim(whole, values, side, 0)
    return lax.dynamic_update_slice_in_dim(whole, swap(values, "tp", 1), half - side, 0)


def sum_blocks(values):
    slabs = lax.axis_size("ctx")
    cut = values.reshape((slabs, values.shape[0] // slabs) + values.shape[1:])
    cut = lax.all_to_all(cut, "ctx", 0, 0, tiled=True)
    total = jnp.sum(cut.astype(F32), axis=0).astype(BF)
    total = lax.all_to_all(
        jnp.broadcast_to(total[None], (slabs,) + total.shape), "ctx", 0, 0, tiled=True
    )
    return total.reshape(values.shape)


def shards(
    inputs,
    lengths,
    first_gain,
    query_weight,
    key_weight,
    value_weight,
    out_weight,
    second_gain,
    gate_weight,
    up_weight,
    down_weight,
    cotangent,
):
    slabs, halves, parts = lax.axis_size("ctx"), lax.axis_size("tp"), lax.axis_size("fsdp")
    rows, width = inputs.shape[1], inputs.shape[2]
    depth = query_weight.shape[0]
    group = query_weight.shape[1] // HD // slabs
    half = rows // halves
    ff = gate_weight.shape[1]
    everywhere = ("tp", "fsdp")
    side = lax.axis_index("tp") * half

    gains = lax.all_gather(jnp.stack([first_gain, second_gain]), "fsdp", axis=1, tiled=True)
    gain_one, gain_two = gains[0].astype(F32), gains[1].astype(F32)
    stacked = jnp.stack(
        [w.reshape(depth, slabs, group, HD) for w in (query_weight, key_weight, value_weight)]
    ).transpose(1, 3, 2, 0, 4)
    qkv_width = slabs * 3 * HD
    w_qkv = lax.all_gather(
        stacked.reshape(depth, group * qkv_width), "fsdp", axis=0, tiled=True
    )
    w_heads = [w_qkv[:, h * qkv_width : (h + 1) * qkv_width] for h in range(group)]
    w_rest = jnp.concatenate([gate_weight, up_weight, down_weight.T, out_weight.T], axis=1)
    w_rest = rows_first(lax.all_gather(rows_first(w_rest), everywhere, axis=0, tiled=True))
    w_rest = w_rest.reshape(halves, width, -1)

    residual = inputs[0].astype(F32)
    _, _, normed_one = normalize(residual, gain_one)
    qkv = []
    for h in range(group):
        part = mm(w_heads[h], normed_one, (((0,), (1,)), ((), ()))).astype(BF)
        part = part.reshape(slabs, 3 * HD, rows)
        qkv.append(lax.all_to_all(part, "ctx", 0, 0, tiled=True))
    arrived, saved = [], []
    for h in range(group):
        mix, mix_full, lse = attend(lengths, qkv[h], halves, 1024)
        saved.append((mix_full, lse))
        mix = mix.reshape(slabs * halves, HD, half)
        mix = lax.all_to_all(mix, ("ctx", "tp"), 0, 0, tiled=True)
        arrived.append(mix.reshape(slabs, halves, HD, half))

    own = lax.dynamic_slice_in_dim(inputs[0], side, half, 0)
    cot = lax.dynamic_slice_in_dim(cotangent[0], side, half, 0)
    scalars = jnp.stack([lengths[0], lax.axis_index("ctx") * rows + side])
    output, d_middle, do_a, do_b, acts, normed_two, d_branch, d_attn = middle_stage(
        scalars, *arrived, own, cot, gain_two[None], w_rest
    )
    output = both_halves(output)
    d_mix = [
        lax.all_to_all(
            d.reshape(slabs * halves, HD, half), ("ctx", "tp"), 0, 0, tiled=True
        ).reshape(slabs, halves, HD, half)
        for d in (do_a, do_b)
    ]
    paired = parts == 4 and halves == 2
    lanes = acts.shape[2]
    split = 2 * ff if paired else lanes
    g_some, *g_rest = gradient_stage(normed_two, d_branch, d_attn, acts, ff, parts, split)
    d_mix[0], g_some, g_rest = lax.optimization_barrier((d_mix[0], g_some, g_rest))
    s_some = lax.psum_scatter(
        rows_first(g_some.reshape(halves * width, -1)), everywhere, scatter_dimension=0, tiled=True
    )
    s_some = rows_first(s_some)

    core, column, line = (
        lax.rem(lax.axis_index("fsdp"), 2),
        lax.axis_index("fsdp") // 2,
        lax.axis_index("tp"),
    )
    d_local = [None] * group
    d_qkv = [None] * group
    d_local[0] = attend_back(lengths, qkv[0], d_mix[0], *saved[0], 1024)
    if paired:
        got = swap(g_rest[0], "fsdp", 1)
        got, d_local[0] = lax.optimization_barrier((got, d_local[0]))
        total = plus(g_rest[1], got)
        cut = total.shape[2] // 2
        low, high = total[:, :, :cut], total[:, :, cut:]
        low_out, high_out = pick(low, 1 - line, 0), pick(high, 1 - column, 1)
        low, high = pick(low, line, 0), pick(high, column, 1)
        d_mix[1], low_out, high_out, low, high = lax.optimization_barrier(
            (d_mix[1], low_out, high_out, low, high)
        )
    for h in range(group):
        if h:
            d_local[h] = attend_back(lengths, qkv[h], d_mix[h], *saved[h], 1024)
        if h == 1 and paired:
            got_low, got_high = swap(low_out, "tp", 1), swap(high_out, "fsdp", 2)
            got_low, got_high, d_local[1] = lax.optimization_barrier(
                (got_low, got_high, d_local[1])
            )
            low, high = plus(low, got_low), plus(high, got_high)
            got_low = swap(pick(low, 1 - column, 0), "fsdp", 2)
            got_high = swap(pick(high, 1 - line, 0), "tp", 1)
            low = plus(pick(low, column, 0), got_low)
            high = plus(pick(high, line, 0), got_high)
            s_rest = jnp.concatenate([low, high], axis=0)
        d_qkv[h] = lax.all_to_all(d_local[h], "ctx", 0, 0, tiled=True).reshape(qkv_width, rows)
        if h:
            d_qkv[h - 1], d_local[h] = lax.optimization_barrier((d_qkv[h - 1], d_local[h]))
    if paired:
        s_some = jnp.concatenate([s_some, s_rest], axis=1)
        d_qkv[0], s_some = lax.optimization_barrier((d_qkv[0], s_some))
    s_all = lax.psum(s_some, "ctx")
    d_normed_one = jnp.zeros((rows, width), F32)
    s_qkv = []
    for h in range(group):
        d_normed_one = d_normed_one + mm(d_qkv[h], w_heads[h], (((0,), (1,)), ((), ())))
        if h == group - 1:
            d_normed_one, d_qkv[h] = lax.optimization_barrier((d_normed_one, d_qkv[h]))
        grad = mm(normed_one, d_qkv[h], (((0,), (1,)), ((), ()))).astype(BF)
        if paired:
            grad = rows_first(grad).reshape(2, 2, depth, qkv_width)
            got = swap(pick(grad, 1 - core, 1), "fsdp", 1)
            grad = plus(pick(grad, core, 1), got)
            got = swap(pick(grad, 1 - column, 0), "fsdp", 2)
            s_qkv.append(plus(pick(grad, column, 0), got))
        else:
            grad = lax.psum_scatter(grad, "fsdp", scatter_dimension=0, tiled=True)
            s_qkv.append(lax.psum(grad, "ctx"))
    if paired:
        total = sum_blocks(jnp.concatenate(s_qkv, axis=1))
        total, s_all = lax.optimization_barrier((total, s_all))
        s_qkv = [total[:, h * qkv_width : (h + 1) * qkv_width] for h in range(group)]
    theirs = lax.dynamic_slice_in_dim(d_normed_one, half - side, half, 0).astype(BF)
    d_normed_one = lax.dynamic_slice_in_dim(d_normed_one, side, half, 0)
    d_normed_one = d_normed_one + swap(theirs, "tp", 1).astype(F32)
    scaled_one, inverse_one, _ = normalize(own.astype(F32), gain_one)
    d_from_one = norm_back(d_normed_one, scaled_one, inverse_one, gain_one)
    input_gradient = both_halves((d_middle + d_from_one).astype(BF))

    s_all = s_all.astype(F32)
    s_qkv = jnp.stack([s.reshape(depth, slabs, 3, HD) for s in s_qkv], axis=2)
    s_qkv = s_qkv.transpose(3, 0, 1, 2, 4).reshape(3, depth, slabs * group * HD).astype(F32)
    d_gain_one = sum(
        jnp.sum(w.astype(F32) * s, axis=1)
        for w, s in zip((query_weight, key_weight, value_weight), s_qkv)
    ) / first_gain.astype(F32)
    d_gain_two = (
        jnp.sum(gate_weight.astype(F32) * s_all[:, :ff], axis=1)
        + jnp.sum(up_weight.astype(F32) * s_all[:, ff : 2 * ff], axis=1)
    ) / second_gain.astype(F32)
    d_gains = jnp.stack([d_gain_one, d_gain_two])
    d_gains = d_gains + swap(d_gains, "tp", 1) if paired else lax.psum(d_gains, "tp")
    return (
        output[None],
        input_gradient[None],
        d_gains[0],
        s_qkv[0],
        s_qkv[1],
        s_qkv[2],
        s_all[:, 3 * ff :].T,
        d_gains[1],
        s_all[:, :ff],
        s_all[:, ff : 2 * ff],
        s_all[:, 2 * ff : 3 * ff].T,
    )


def solution(mesh):
    rows = P("fsdp", "ctx", None)
    gain = P("fsdp")
    inward = P("fsdp", "tp")
    outward = P("tp", "fsdp")
    return jax.shard_map(
        shards,
        mesh=mesh,
        in_specs=(
            rows, gain, gain, inward, inward, inward, outward, gain, inward, inward, outward, rows,
        ),
        out_specs=(
            rows, rows, gain, inward, inward, inward, outward, gain, inward, inward, outward,
        ),
        check_vma=False,
    )
```

```python
import functools

import jax
import jax.numpy as jnp
from jax import lax
from jax.experimental import pallas as pl
from jax.experimental.pallas import tpu as pltpu
from jax.experimental.layout import Layout, with_layout_constraint
from jax.sharding import PartitionSpec as P

HD = 64
EPSILON = 1e-05
MASKED = -1000000000.0
NN = (((1,), (0,)), ((), ()))
NT = (((1,), (1,)), ((), ()))
TN = (((0,), (0,)), ((), ()))
BF = jnp.bfloat16
F32 = jnp.float32


def mm(left, right, dims):
    return lax.dot_general(left, right, dims, preferred_element_type=F32)


def spread_keys(keys, start, length):
    rows = keys.shape[0]
    pos = start + lax.broadcasted_iota(jnp.int32, (rows, HD), 0)
    lane = lax.broadcasted_iota(jnp.int32, (rows, HD), 1)
    bias = jnp.where((lane == 0) & (pos >= length), MASKED, 0.0)
    return jnp.concatenate([keys, bias], axis=1).astype(BF)


def spread_queries(queries):
    row = lax.broadcasted_iota(jnp.int32, queries.shape, 0)
    ones = jnp.where(row == 0, 1.0, 0.0)
    return jnp.concatenate([queries * HD**-0.5, ones], axis=0).astype(BF)


def attend_kernel(tile, len_ref, qkv, o_ref, of_ref, lse_ref, kx, qx, vx):
    slabs, _, rows = qkv.shape
    halves = o_ref.shape[1]
    half = rows // halves
    length = len_ref[0]
    per = rows // tile
    blocks = slabs * per
    for z in range(slabs):
        keys = qkv[z, HD : 2 * HD, :].astype(F32).T
        kx[z * rows : (z + 1) * rows, :] = spread_keys(keys, z * rows, length)
        queries = spread_queries(qkv[z, 0:HD, :].astype(F32))
        for b in range(per):
            cut = slice(b * tile, (b + 1) * tile)
            qx[z * per + b] = queries[:, cut]
            vx[z * per + b] = qkv[z, 2 * HD : 3 * HD, cut]
    later = lax.broadcasted_iota(jnp.int32, (tile, tile), 0) > lax.broadcasted_iota(
        jnp.int32, (tile, tile), 1
    )

    def query_block(i, _):
        queries = qx[i]

        def step(j, carry, masked):
            highest, total, mix = carry
            keys = kx[pl.ds(pl.multiple_of(j * tile, tile), tile), :]
            scores = mm(keys, queries, NN)
            if masked:
                scores = jnp.where(later, MASKED, scores)
            new = jnp.maximum(highest, jnp.max(scores, axis=0, keepdims=True))
            scale = jnp.exp(highest - new)
            probs = jnp.exp(scores - new)
            total = total * scale + jnp.sum(probs, axis=0, keepdims=True)
            mix = mix * scale + mm(vx[j], probs.astype(BF), NN)
            return new, total, mix

        first = (
            jnp.full((1, tile), -jnp.inf, F32),
            jnp.zeros((1, tile), F32),
            jnp.zeros((HD, tile), F32),
        )
        carry = lax.fori_loop(0, i, lambda j, c: step(j, c, False), first)
        highest, total, mix = step(i, carry, True)
        mix = mix / total
        z = i // per
        base = lax.rem(i, per) * tile
        of_ref[z, :, pl.ds(pl.multiple_of(base, tile), tile)] = mix
        lse_ref[z, :, pl.ds(pl.multiple_of(base, tile), tile)] = highest + jnp.log(total)
        low = mix.astype(BF)
        if tile >= half:
            for t in range(tile // half):
                o_ref[z, base // half + t] = low[:, t * half : (t + 1) * half]
        else:
            o_ref[z, base // half, :, pl.ds(pl.multiple_of(lax.rem(base, half), tile), tile)] = low
        return 0

    lax.fori_loop(0, blocks, query_block, 0)


def attend(length, qkv, halves, tile):
    slabs, _, rows = qkv.shape
    total = slabs * rows
    tile = min(tile, rows)
    work = total * (total + tile) // 2
    vmem = pl.BlockSpec(memory_space=pltpu.VMEM)
    return pl.pallas_call(
        functools.partial(attend_kernel, tile),
        out_shape=(
            jax.ShapeDtypeStruct((slabs, halves, HD, rows // halves), BF),
            jax.ShapeDtypeStruct((slabs, HD, rows), F32),
            jax.ShapeDtypeStruct((slabs, 1, rows), F32),
        ),
        in_specs=[pl.BlockSpec(memory_space=pltpu.SMEM), vmem],
        out_specs=(vmem, vmem, vmem),
        scratch_shapes=[
            pltpu.VMEM((total, 2 * HD), BF),
            pltpu.VMEM((total // tile, 2 * HD, tile), BF),
            pltpu.VMEM((total // tile, HD, tile), BF),
        ],
        compiler_params=pltpu.CompilerParams(vmem_limit_bytes=40 << 20),
        cost_estimate=pl.CostEstimate(
            flops=work * 256 * 4, bytes_accessed=qkv.size * 4, transcendentals=work
        ),
    )(length, qkv)


def attend_back_kernel(tile, len_ref, qkv, do_ref, of_ref, lse_ref, out, kx, qx, vx, kt, dox, dq, st):
    slabs, _, rows = qkv.shape
    halves, half = do_ref.shape[1], do_ref.shape[3]
    length = len_ref[0]
    per = rows // tile
    blocks = slabs * per
    for z in range(slabs):
        keys = qkv[z, HD : 2 * HD, :]
        kx[z * rows : (z + 1) * rows, :] = spread_keys(keys.astype(F32).T, z * rows, length)
        queries = spread_queries(qkv[z, 0:HD, :].astype(F32))
        values = qkv[z, 2 * HD : 3 * HD, :].astype(F32).T
        vx[z * rows : (z + 1) * rows, :] = jnp.concatenate(
            [values, jnp.zeros((rows, HD), F32)], axis=1
        ).astype(BF)
        d_mix = jnp.concatenate([do_ref[z, t] for t in range(halves)], axis=1)
        delta = jnp.sum(d_mix.astype(F32) * of_ref[z], axis=0, keepdims=True)
        for b in range(per):
            cut = slice(b * tile, (b + 1) * tile)
            n = z * per + b
            qx[n] = queries[:, cut]
            kt[n] = keys[:, cut]
            dox[n, 0:HD] = d_mix[:, cut]
            dox[n, HD : 2 * HD] = jnp.zeros((HD, tile), BF)
            st[n, 0:1] = lse_ref[z, :, cut]
            st[n, 1:2] = delta[:, cut]
    dq[...] = jnp.zeros_like(dq)
    later = lax.broadcasted_iota(jnp.int32, (tile, tile), 0) > lax.broadcasted_iota(
        jnp.int32, (tile, tile), 1
    )

    def key_block(j, _):
        here = pl.ds(pl.multiple_of(j * tile, tile), tile)
        keys = kx[here, :]
        values = vx[here, :]

        def step(i, carry, masked):
            dk, dv = carry
            scores = mm(keys, qx[i], NN)
            if masked:
                scores = jnp.where(later, MASKED, scores)
            probs = jnp.exp(scores - st[i, 0:1])
            d_probs = mm(values, dox[i], NN)
            d_scores = (probs * (d_probs - st[i, 1:2])).astype(BF)
            dv = dv + mm(dox[i, 0:HD], probs.astype(BF), NT)
            dk = dk + mm(qx[i, 0:HD], d_scores, NT)
            dq[i] += mm(kt[j], d_scores, NN)
            return dk, dv

        zero = jnp.zeros((HD, tile), F32)
        carry = step(j, (zero, zero), True)
        dk, dv = lax.fori_loop(j + 1, blocks, lambda i, c: step(i, c, False), carry)
        z = j // per
        cut = pl.ds(pl.multiple_of(lax.rem(j, per) * tile, tile), tile)
        out[z, 0:HD, cut] = (dq[j] * HD**-0.5).astype(BF)
        out[z, HD : 2 * HD, cut] = dk.astype(BF)
        out[z, 2 * HD : 3 * HD, cut] = dv.astype(BF)
        return 0

    lax.fori_loop(0, blocks, key_block, 0)


def attend_back(length, qkv, d_mix, mix, lse, tile):
    slabs, _, rows = qkv.shape
    total = slabs * rows
    tile = min(tile, rows)
    blocks = total // tile
    work = total * (total + tile) // 2
    vmem = pl.BlockSpec(memory_space=pltpu.VMEM)
    return pl.pallas_call(
        functools.partial(attend_back_kernel, tile),
        out_shape=jax.ShapeDtypeStruct((slabs, 3 * HD, rows), BF),
        in_specs=[pl.BlockSpec(memory_space=pltpu.SMEM), vmem, vmem, vmem, vmem],
        out_specs=vmem,
        scratch_shapes=[
            pltpu.VMEM((total, 2 * HD), BF),
            pltpu.VMEM((blocks, 2 * HD, tile), BF),
            pltpu.VMEM((total, 2 * HD), BF),
            pltpu.VMEM((blocks, HD, tile), BF),
            pltpu.VMEM((blocks, 2 * HD, tile), BF),
            pltpu.VMEM((blocks, HD, tile), F32),
            pltpu.VMEM((blocks, 8, tile), F32),
        ],
        compiler_params=pltpu.CompilerParams(vmem_limit_bytes=40 << 20),
        cost_estimate=pl.CostEstimate(
            flops=work * 256 * 10, bytes_accessed=qkv.size * 8, transcendentals=work
        ),
    )(length, qkv, d_mix, mix, lse)


def widths(total, step):
    return [(at, min(step, total - at)) for at in range(0, total, step)]


def middle_kernel(
    ff, split, scal, mix_a, mix_b, own, cot, gain, w_hbm,
    out_ref, dmid_ref, got_a, got_b, *refs,
):
    n_out = 3 if split < w_hbm.shape[2] else 1
    grads = refs[:n_out]
    (w, acts, att_t, mid, scale, dn, normed_ref, branch_ref, dattn_ref, turned, do_a, do_b,
     sems, out_sems, send_sems, recv_sems, local_sems) = refs[n_out:]
    slabs, halves, _, half = mix_a.shape
    width = own.shape[1]
    inner = width // halves
    base = 3 * ff
    lanes = base + inner
    here, line = lax.axis_index("ctx"), lax.axis_index("tp")
    core = lax.rem(lax.axis_index("fsdp"), 2)
    barrier = pltpu.get_barrier_semaphore()
    peers = [(dz, dt) for dz in range(slabs) for dt in range(halves) if dz or dt]

    def peer(dz, dt):
        return lax.rem(here + dz, slabs), lax.rem(line + dt, halves)

    for dz, dt in peers:
        z, t = peer(dz, dt)
        pl.semaphore_signal(
            barrier, inc=1, device_id={"ctx": z, "tp": t}, device_id_type=pl.DeviceIdType.MESH
        )
    cuts = [(t, base, inner) for t in range(halves)]
    cuts += [(t, k * ff, ff) for t in range(halves) for k in range(3)]
    loads = [
        pltpu.make_async_copy(
            w_hbm.at[t, :, at : at + n], w.at[t, :, at : at + n], sems.at[k]
        )
        for k, (t, at, n) in enumerate(cuts)
    ]
    for load in loads:
        load.start()
    length, first = scal[0], scal[1]
    step = 256
    rows = 64

    for t in range(halves):
        for z in range(slabs):
            at = z * 2 * HD
            att_t[at : at + HD, :] = mix_a[z, t]
            att_t[at + HD : at + 2 * HD, :] = mix_b[z, t]
        acts[t, :, base:lanes] = att_t[...].astype(F32).T.astype(BF)
    for k in range(halves):
        loads[k].wait()

    def project(n, _):
        cut = pl.ds(pl.multiple_of(n * step, step), step)
        total = own[:, cut].astype(F32)
        for t in range(halves):
            total = total + mm(acts[t, :, base:lanes], w[t, cut, base:lanes], NT)
        mid[:, cut] = total
        return 0

    lax.fori_loop(0, width // step, project, 0)

    def row_mask(r):
        pos = first + r * rows + lax.broadcasted_iota(jnp.int32, (rows, 1), 0)
        return jnp.where(pos < length, 1.0, 0.0)

    def norm(r, _):
        cut = pl.ds(pl.multiple_of(r * rows, rows), rows)
        values = mid[cut, :]
        inverse = lax.rsqrt(jnp.mean(values * values, axis=1, keepdims=True) + EPSILON)
        scale[cut, :] = jnp.broadcast_to(inverse, (rows, 128))
        normed_ref[cut, :] = (values * inverse * gain[...]).astype(BF)
        branch_ref[cut, :] = (cot[cut, :].astype(F32) * row_mask(r)).astype(BF)
        return 0

    lax.fori_loop(0, half // rows, norm, 0)

    for t in range(halves):
        for k in range(3):
            loads[halves + 3 * t + k].wait()

        def columns(at, n):
            def cut(k):
                return pl.ds(pl.multiple_of(k * ff + at, 128), n)

            gate = mm(normed_ref[...], w[t, :, cut(0)], NN)
            upward = mm(normed_ref[...], w[t, :, cut(1)], NN)
            d_hidden = mm(branch_ref[...], w[t, :, cut(2)], NN)
            sig = 1.0 / (1.0 + jnp.exp(-gate))
            active = gate * sig
            acts[t, :, cut(2)] = (active * upward).astype(BF)
            acts[t, :, cut(0)] = (
                d_hidden * upward * sig * (1.0 + gate * (1.0 - sig))
            ).astype(BF)
            acts[t, :, cut(1)] = (d_hidden * active).astype(BF)

        def chunk(c, _):
            columns(c * step, step)
            return 0

        lax.fori_loop(0, ff // step, chunk, 0)
        if ff % step:
            columns(ff - ff % step, ff % step)

    def back(n, _):
        cut = pl.ds(pl.multiple_of(n * step, step), step)
        total = mid[:, cut]
        grad = jnp.zeros((half, step), F32)
        for t in range(halves):
            total = total + mm(acts[t, :, 2 * ff : base], w[t, cut, 2 * ff : base], NT)
            grad = grad + mm(acts[t, :, 0:ff], w[t, cut, 0:ff], NT)
            grad = grad + mm(acts[t, :, ff : 2 * ff], w[t, cut, ff : 2 * ff], NT)
        dmid_ref[:, cut] = total
        dn[:, cut] = grad
        return 0

    lax.fori_loop(0, width // step, back, 0)

    def finish(r, _):
        cut = pl.ds(pl.multiple_of(r * rows, rows), rows)
        mask = row_mask(r)
        out_ref[cut, :] = (dmid_ref[cut, :] * mask).astype(BF)
        inverse = scale[cut, 0:1]
        scaled = mid[cut, :] * inverse
        d_scaled = dn[cut, :] * gain[...]
        mean = jnp.mean(d_scaled * scaled, axis=1, keepdims=True)
        total = cot[cut, :].astype(F32) * mask + inverse * (d_scaled - scaled * mean)
        dmid_ref[cut, :] = total
        dattn_ref[cut, :] = total.astype(BF)
        return 0

    lax.fori_loop(0, half // rows, finish, 0)
    for t in range(halves):
        for z in range(0, slabs, 2):
            at = base + z * 2 * HD
            grad = mm(dattn_ref[...], w[t, :, at : at + 4 * HD], NN).T.astype(BF)
            for k in range(2):
                do_a[z + k, t] = grad[2 * k * HD : (2 * k + 1) * HD]
                do_b[z + k, t] = grad[(2 * k + 1) * HD : (2 * k + 2) * HD]

    pl.semaphore_wait(barrier, len(peers))
    moves = []
    for k, (dz, dt) in enumerate(peers):
        z, t = peer(dz, dt)
        for h, (source, target) in enumerate(((do_a, got_a), (do_b, got_b))):
            move = pltpu.make_async_remote_copy(
                src_ref=source.at[z, t],
                dst_ref=target.at[here, line],
                send_sem=send_sems.at[2 * k + h],
                recv_sem=recv_sems.at[2 * k + h],
                device_id={"ctx": z, "tp": t},
                device_id_type=pl.DeviceIdType.MESH,
            )
            move.start()
            moves.append(move)
    for h, (source, target) in enumerate(((do_a, got_a), (do_b, got_b))):
        move = pltpu.make_async_copy(
            source.at[here, line], target.at[here, line], local_sems.at[h]
        )
        move.start()
        moves.append(move)

    regions = ((0, 2 * ff), (2 * ff, base), (base, lanes))

    def store(n, t):
        cut = pl.ds(pl.multiple_of(n * step, step), step)
        pltpu.make_async_copy(
            w.at[t, cut, 0:split], grads[0].at[t, cut, :], out_sems.at[n, t, 0]
        ).start()
        if n_out == 3:
            for side in range(2):

                @pl.when(lax.rem(n + core, 2) == 1 - side)
                def _():
                    pltpu.make_async_copy(
                        w.at[t, cut, split:lanes], grads[1 + side].at[t, n // 2], out_sems.at[n, t, 1]
                    ).start()

    def gradient(n, _):
        cut = pl.ds(pl.multiple_of(n * step, step), step)
        for k, ref in enumerate((normed_ref, branch_ref, dattn_ref)):
            turned[k] = ref[:, cut].astype(F32).T.astype(BF)
        for t in range(halves):
            for k, (at, end) in enumerate(regions):
                for b, m in widths(end - at, 1024):
                    value = mm(turned[k], acts[t, :, at + b : at + b + m], NN)
                    w[t, cut, at + b : at + b + m] = value.astype(BF)
            store(n, t)
        return 0

    lax.fori_loop(0, width // step, gradient, 0)

    def settle(n, _):
        cut = pl.ds(pl.multiple_of(n * step, step), step)
        for t in range(halves):
            pltpu.make_async_copy(
                w.at[t, cut, 0:split], grads[0].at[t, cut, :], out_sems.at[n, t, 0]
            ).wait()
            if n_out == 3:
                pltpu.make_async_copy(
                    w.at[t, cut, split:lanes], grads[1].at[t, n // 2], out_sems.at[n, t, 1]
                ).wait()
        return 0

    lax.fori_loop(0, width // step, settle, 0)
    for move in moves:
        move.wait()


def middle_stage(scalars, mix_a, mix_b, own, cot, gain, w, split):
    halves, width, lanes = w.shape
    slabs, _, _, half = mix_a.shape
    ff = (lanes - width // halves) // 3
    blocks = width // 256
    peers = slabs * halves - 1
    vmem = pl.BlockSpec(memory_space=pltpu.VMEM)
    outside = pl.BlockSpec(memory_space=pl.ANY)
    out_shape = [
        jax.ShapeDtypeStruct((half, width), BF),
        jax.ShapeDtypeStruct((half, width), F32),
        jax.ShapeDtypeStruct(mix_a.shape, BF),
        jax.ShapeDtypeStruct(mix_a.shape, BF),
        jax.ShapeDtypeStruct((halves, width, split), BF),
    ]
    out_specs = [vmem] * 4 + [outside]
    if split < lanes:
        out_shape += [jax.ShapeDtypeStruct((halves, blocks // 2, 256, lanes - split), BF)] * 2
        out_specs += [outside] * 2
    flops = 2 * half * width * (9 * ff * halves + 3 * width)
    return pl.pallas_call(
        functools.partial(middle_kernel, ff, split),
        out_shape=out_shape,
        in_specs=[pl.BlockSpec(memory_space=pltpu.SMEM)] + [vmem] * 5 + [outside],
        out_specs=out_specs,
        scratch_shapes=[
            pltpu.VMEM((halves, width, lanes), BF),
            pltpu.VMEM((halves, half, lanes), BF),
            pltpu.VMEM((width // halves, half), BF),
            pltpu.VMEM((half, width), F32),
            pltpu.VMEM((half, 128), F32),
            pltpu.VMEM((half, width), F32),
            pltpu.VMEM((half, width), BF),
            pltpu.VMEM((half, width), BF),
            pltpu.VMEM((half, width), BF),
            pltpu.VMEM((3, 256, half), BF),
            pltpu.VMEM(mix_a.shape, BF),
            pltpu.VMEM(mix_a.shape, BF),
            pltpu.SemaphoreType.DMA((4 * halves,)),
            pltpu.SemaphoreType.DMA((blocks, halves, 2)),
            pltpu.SemaphoreType.DMA((2 * peers,)),
            pltpu.SemaphoreType.DMA((2 * peers,)),
            pltpu.SemaphoreType.DMA((2,)),
        ],
        compiler_params=pltpu.CompilerParams(
            vmem_limit_bytes=58 << 20, collective_id=1, has_side_effects=True
        ),
        cost_estimate=pl.CostEstimate(
            flops=flops, bytes_accessed=4 * w.size + 16 * half * width, transcendentals=half * lanes
        ),
    )(scalars, mix_a, mix_b, own, cot, gain, w)


def normalize(values, gain):
    inverse = lax.rsqrt(jnp.mean(values * values, axis=-1, keepdims=True) + EPSILON)
    scaled = values * inverse
    return scaled, inverse, (scaled * gain).astype(BF)


def norm_back(d_normed, scaled, inverse, gain):
    d_scaled = d_normed * gain
    d_values = inverse * (d_scaled - scaled * jnp.mean(d_scaled * scaled, axis=-1, keepdims=True))
    return d_values


def rows_first(values):
    return with_layout_constraint(values, Layout(major_to_minor=tuple(range(values.ndim))))


def swap(values, axis, bit):
    count = lax.axis_size(axis)
    return lax.ppermute(values, axis, [(k, k ^ bit) for k in range(count)])


def plus(left, right):
    return (left.astype(F32) + right.astype(F32)).astype(BF)


def pick(values, index, axis):
    return lax.dynamic_index_in_dim(values, index, axis, keepdims=False)


def both_halves(values):
    half = values.shape[0]
    side = lax.axis_index("tp") * half
    whole = jnp.zeros((2 * half,) + values.shape[1:], values.dtype)
    whole = lax.dynamic_update_slice_in_dim(whole, values, side, 0)
    return lax.dynamic_update_slice_in_dim(whole, swap(values, "tp", 1), half - side, 0)


def sum_blocks(values):
    slabs = lax.axis_size("ctx")
    cut = values.reshape((slabs, values.shape[0] // slabs) + values.shape[1:])
    cut = lax.all_to_all(cut, "ctx", 0, 0, tiled=True)
    total = jnp.sum(cut.astype(F32), axis=0).astype(BF)
    total = lax.all_to_all(
        jnp.broadcast_to(total[None], (slabs,) + total.shape), "ctx", 0, 0, tiled=True
    )
    return total.reshape(values.shape)


def shards(
    inputs,
    lengths,
    first_gain,
    query_weight,
    key_weight,
    value_weight,
    out_weight,
    second_gain,
    gate_weight,
    up_weight,
    down_weight,
    cotangent,
):
    slabs, halves, parts = lax.axis_size("ctx"), lax.axis_size("tp"), lax.axis_size("fsdp")
    rows, width = inputs.shape[1], inputs.shape[2]
    depth = query_weight.shape[0]
    group = query_weight.shape[1] // HD // slabs
    half = rows // halves
    ff = gate_weight.shape[1]
    everywhere = ("tp", "fsdp")
    side = lax.axis_index("tp") * half

    gains = lax.all_gather(jnp.stack([first_gain, second_gain]), "fsdp", axis=1, tiled=True)
    gain_one, gain_two = gains[0].astype(F32), gains[1].astype(F32)
    stacked = jnp.stack(
        [w.reshape(depth, slabs, group, HD) for w in (query_weight, key_weight, value_weight)]
    ).transpose(1, 3, 2, 0, 4)
    qkv_width = slabs * 3 * HD
    w_qkv = lax.all_gather(
        stacked.reshape(depth, group * qkv_width), "fsdp", axis=0, tiled=True
    )
    w_heads = [w_qkv[:, h * qkv_width : (h + 1) * qkv_width] for h in range(group)]
    w_rest = jnp.concatenate([gate_weight, up_weight, down_weight.T, out_weight.T], axis=1)
    w_rest = rows_first(lax.all_gather(rows_first(w_rest), everywhere, axis=0, tiled=True))
    w_rest = w_rest.reshape(halves, width, -1)

    residual = inputs[0].astype(F32)
    _, _, normed_one = normalize(residual, gain_one)
    qkv = []
    for h in range(group):
        part = mm(w_heads[h], normed_one, (((0,), (1,)), ((), ()))).astype(BF)
        part = part.reshape(slabs, 3 * HD, rows)
        qkv.append(lax.all_to_all(part, "ctx", 0, 0, tiled=True))
    arrived, saved = [], []
    for h in range(group):
        mix, mix_full, lse = attend(lengths, qkv[h], halves, 1024)
        saved.append((mix_full, lse))
        mix = mix.reshape(slabs * halves, HD, half)
        mix = lax.all_to_all(mix, ("ctx", "tp"), 0, 0, tiled=True)
        arrived.append(mix.reshape(slabs, halves, HD, half))

    own = lax.dynamic_slice_in_dim(inputs[0], side, half, 0)
    cot = lax.dynamic_slice_in_dim(cotangent[0], side, half, 0)
    scalars = jnp.stack([lengths[0], lax.axis_index("ctx") * rows + side])
    paired = parts == 4 and halves == 2
    split = 2 * ff if paired else w_rest.shape[2]
    output, d_middle, *d_mix, = middle_stage(
        scalars, *arrived, own, cot, gain_two[None], w_rest, split
    )
    d_mix, (g_some, *g_rest) = d_mix[:2], d_mix[2:]
    output = both_halves(output)
    s_some = lax.psum_scatter(
        rows_first(g_some.reshape(halves * width, -1)), everywhere, scatter_dimension=0, tiled=True
    )
    s_some = rows_first(s_some)

    core, column, line = (
        lax.rem(lax.axis_index("fsdp"), 2),
        lax.axis_index("fsdp") // 2,
        lax.axis_index("tp"),
    )
    d_local = [None] * group
    d_qkv = [None] * group
    d_local[0] = attend_back(lengths, qkv[0], d_mix[0], *saved[0], 1024)
    if paired:
        got = swap(g_rest[0], "fsdp", 1)
        got, d_local[0] = lax.optimization_barrier((got, d_local[0]))
        total = plus(g_rest[1], got)
        cut = total.shape[2] // 2
        low, high = total[:, :, :cut], total[:, :, cut:]
        low_out, high_out = pick(low, 1 - line, 0), pick(high, 1 - column, 1)
        low, high = pick(low, line, 0), pick(high, column, 1)
        d_mix[1], low_out, high_out, low, high = lax.optimization_barrier(
            (d_mix[1], low_out, high_out, low, high)
        )
    for h in range(group):
        if h:
            d_local[h] = attend_back(lengths, qkv[h], d_mix[h], *saved[h], 1024)
        if h == 1 and paired:
            got_low, got_high = swap(low_out, "tp", 1), swap(high_out, "fsdp", 2)
            got_low, got_high, d_local[1] = lax.optimization_barrier(
                (got_low, got_high, d_local[1])
            )
            low, high = plus(low, got_low), plus(high, got_high)
            got_low = swap(pick(low, 1 - column, 0), "fsdp", 2)
            got_high = swap(pick(high, 1 - line, 0), "tp", 1)
            low = plus(pick(low, column, 0), got_low)
            high = plus(pick(high, line, 0), got_high)
            s_rest = jnp.concatenate([low, high], axis=0)
        d_qkv[h] = lax.all_to_all(d_local[h], "ctx", 0, 0, tiled=True).reshape(qkv_width, rows)
        if h:
            d_qkv[h - 1], d_local[h] = lax.optimization_barrier((d_qkv[h - 1], d_local[h]))
    if paired:
        s_some = jnp.concatenate([s_some, s_rest], axis=1)
        d_qkv[0], s_some = lax.optimization_barrier((d_qkv[0], s_some))
    s_all = lax.psum(s_some, "ctx")
    d_normed_one = jnp.zeros((rows, width), F32)
    s_qkv = []
    for h in range(group):
        d_normed_one = d_normed_one + mm(d_qkv[h], w_heads[h], (((0,), (1,)), ((), ())))
        if h == group - 1:
            d_normed_one, d_qkv[h] = lax.optimization_barrier((d_normed_one, d_qkv[h]))
        grad = mm(normed_one, d_qkv[h], (((0,), (1,)), ((), ()))).astype(BF)
        if paired:
            grad = rows_first(grad).reshape(2, 2, depth, qkv_width)
            got = swap(pick(grad, 1 - core, 1), "fsdp", 1)
            grad = plus(pick(grad, core, 1), got)
            got = swap(pick(grad, 1 - column, 0), "fsdp", 2)
            s_qkv.append(plus(pick(grad, column, 0), got))
        else:
            grad = lax.psum_scatter(grad, "fsdp", scatter_dimension=0, tiled=True)
            s_qkv.append(lax.psum(grad, "ctx"))
    if paired:
        total = sum_blocks(jnp.concatenate(s_qkv, axis=1))
        total, s_all = lax.optimization_barrier((total, s_all))
        s_qkv = [total[:, h * qkv_width : (h + 1) * qkv_width] for h in range(group)]
    theirs = lax.dynamic_slice_in_dim(d_normed_one, half - side, half, 0).astype(BF)
    d_normed_one = lax.dynamic_slice_in_dim(d_normed_one, side, half, 0)
    d_normed_one = d_normed_one + swap(theirs, "tp", 1).astype(F32)
    scaled_one, inverse_one, _ = normalize(own.astype(F32), gain_one)
    d_from_one = norm_back(d_normed_one, scaled_one, inverse_one, gain_one)
    input_gradient = both_halves((d_middle + d_from_one).astype(BF))

    s_all = s_all.astype(F32)
    s_qkv = jnp.stack([s.reshape(depth, slabs, 3, HD) for s in s_qkv], axis=2)
    s_qkv = s_qkv.transpose(3, 0, 1, 2, 4).reshape(3, depth, slabs * group * HD).astype(F32)
    d_gain_one = sum(
        jnp.sum(w.astype(F32) * s, axis=1)
        for w, s in zip((query_weight, key_weight, value_weight), s_qkv)
    ) / first_gain.astype(F32)
    d_gain_two = (
        jnp.sum(gate_weight.astype(F32) * s_all[:, :ff], axis=1)
        + jnp.sum(up_weight.astype(F32) * s_all[:, ff : 2 * ff], axis=1)
    ) / second_gain.astype(F32)
    d_gains = jnp.stack([d_gain_one, d_gain_two])
    d_gains = d_gains + swap(d_gains, "tp", 1) if paired else lax.psum(d_gains, "tp")
    return (
        output[None],
        input_gradient[None],
        d_gains[0],
        s_qkv[0],
        s_qkv[1],
        s_qkv[2],
        s_all[:, 3 * ff :].T,
        d_gains[1],
        s_all[:, :ff],
        s_all[:, ff : 2 * ff],
        s_all[:, 2 * ff : 3 * ff].T,
    )


def solution(mesh):
    rows = P("fsdp", "ctx", None)
    gain = P("fsdp")
    inward = P("fsdp", "tp")
    outward = P("tp", "fsdp")
    return jax.shard_map(
        shards,
        mesh=mesh,
        in_specs=(
            rows, gain, gain, inward, inward, inward, outward, gain, inward, inward, outward, rows,
        ),
        out_specs=(
            rows, rows, gain, inward, inward, inward, outward, gain, inward, inward, outward,
        ),
        check_vma=False,
    )
```

```python
import functools

import jax
import jax.numpy as jnp
from jax import lax
from jax.experimental import pallas as pl
from jax.experimental.pallas import tpu as pltpu
from jax.experimental.layout import Layout, with_layout_constraint
from jax.sharding import PartitionSpec as P

HD = 64
EPSILON = 1e-05
MASKED = -1000000000.0
NN = (((1,), (0,)), ((), ()))
NT = (((1,), (1,)), ((), ()))
TN = (((0,), (0,)), ((), ()))
BF = jnp.bfloat16
F32 = jnp.float32


def mm(left, right, dims):
    return lax.dot_general(left, right, dims, preferred_element_type=F32)


def spread_keys(keys, start, length):
    rows = keys.shape[0]
    pos = start + lax.broadcasted_iota(jnp.int32, (rows, HD), 0)
    lane = lax.broadcasted_iota(jnp.int32, (rows, HD), 1)
    bias = jnp.where((lane == 0) & (pos >= length), MASKED, 0.0)
    return jnp.concatenate([keys, bias], axis=1).astype(BF)


def spread_queries(queries):
    row = lax.broadcasted_iota(jnp.int32, queries.shape, 0)
    ones = jnp.where(row == 0, 1.0, 0.0)
    return jnp.concatenate([queries * HD**-0.5, ones], axis=0).astype(BF)


def attend_kernel(tile, len_ref, qkv, o_ref, of_ref, lse_ref, kx, qx, vx):
    slabs, _, rows = qkv.shape
    halves = o_ref.shape[1]
    half = rows // halves
    length = len_ref[0]
    per = rows // tile
    blocks = slabs * per
    for z in range(slabs):
        keys = qkv[z, HD : 2 * HD, :].astype(F32).T
        kx[z * rows : (z + 1) * rows, :] = spread_keys(keys, z * rows, length)
        queries = spread_queries(qkv[z, 0:HD, :].astype(F32))
        for b in range(per):
            cut = slice(b * tile, (b + 1) * tile)
            qx[z * per + b] = queries[:, cut]
            vx[z * per + b] = qkv[z, 2 * HD : 3 * HD, cut]
    later = lax.broadcasted_iota(jnp.int32, (tile, tile), 0) > lax.broadcasted_iota(
        jnp.int32, (tile, tile), 1
    )

    def query_block(i, _):
        queries = qx[i]

        def step(j, carry, masked):
            highest, total, mix = carry
            keys = kx[pl.ds(pl.multiple_of(j * tile, tile), tile), :]
            scores = mm(keys, queries, NN)
            if masked:
                scores = jnp.where(later, MASKED, scores)
            new = jnp.maximum(highest, jnp.max(scores, axis=0, keepdims=True))
            scale = jnp.exp(highest - new)
            probs = jnp.exp(scores - new)
            total = total * scale + jnp.sum(probs, axis=0, keepdims=True)
            mix = mix * scale + mm(vx[j], probs.astype(BF), NN)
            return new, total, mix

        first = (
            jnp.full((1, tile), -jnp.inf, F32),
            jnp.zeros((1, tile), F32),
            jnp.zeros((HD, tile), F32),
        )
        carry = lax.fori_loop(0, i, lambda j, c: step(j, c, False), first)
        highest, total, mix = step(i, carry, True)
        mix = mix / total
        z = i // per
        base = lax.rem(i, per) * tile
        of_ref[z, :, pl.ds(pl.multiple_of(base, tile), tile)] = mix
        lse_ref[z, :, pl.ds(pl.multiple_of(base, tile), tile)] = highest + jnp.log(total)
        low = mix.astype(BF)
        if tile >= half:
            for t in range(tile // half):
                o_ref[z, base // half + t] = low[:, t * half : (t + 1) * half]
        else:
            o_ref[z, base // half, :, pl.ds(pl.multiple_of(lax.rem(base, half), tile), tile)] = low
        return 0

    lax.fori_loop(0, blocks, query_block, 0)


def attend(length, qkv, halves, tile):
    slabs, _, rows = qkv.shape
    total = slabs * rows
    tile = min(tile, rows)
    work = total * (total + tile) // 2
    vmem = pl.BlockSpec(memory_space=pltpu.VMEM)
    return pl.pallas_call(
        functools.partial(attend_kernel, tile),
        out_shape=(
            jax.ShapeDtypeStruct((slabs, halves, HD, rows // halves), BF),
            jax.ShapeDtypeStruct((slabs, HD, rows), F32),
            jax.ShapeDtypeStruct((slabs, 1, rows), F32),
        ),
        in_specs=[pl.BlockSpec(memory_space=pltpu.SMEM), vmem],
        out_specs=(vmem, vmem, vmem),
        scratch_shapes=[
            pltpu.VMEM((total, 2 * HD), BF),
            pltpu.VMEM((total // tile, 2 * HD, tile), BF),
            pltpu.VMEM((total // tile, HD, tile), BF),
        ],
        compiler_params=pltpu.CompilerParams(vmem_limit_bytes=40 << 20),
        cost_estimate=pl.CostEstimate(
            flops=work * 256 * 4, bytes_accessed=qkv.size * 4, transcendentals=work
        ),
    )(length, qkv)


def attend_back_kernel(tile, len_ref, qkv, do_ref, of_ref, lse_ref, out, kx, qx, vx, kt, dox, dq, st):
    slabs, _, rows = qkv.shape
    halves, half = do_ref.shape[1], do_ref.shape[3]
    length = len_ref[0]
    per = rows // tile
    blocks = slabs * per
    for z in range(slabs):
        keys = qkv[z, HD : 2 * HD, :]
        kx[z * rows : (z + 1) * rows, :] = spread_keys(keys.astype(F32).T, z * rows, length)
        queries = spread_queries(qkv[z, 0:HD, :].astype(F32))
        values = qkv[z, 2 * HD : 3 * HD, :].astype(F32).T
        vx[z * rows : (z + 1) * rows, :] = jnp.concatenate(
            [values, jnp.zeros((rows, HD), F32)], axis=1
        ).astype(BF)
        d_mix = jnp.concatenate([do_ref[z, t] for t in range(halves)], axis=1)
        delta = jnp.sum(d_mix.astype(F32) * of_ref[z], axis=0, keepdims=True)
        for b in range(per):
            cut = slice(b * tile, (b + 1) * tile)
            n = z * per + b
            qx[n] = queries[:, cut]
            kt[n] = keys[:, cut]
            dox[n, 0:HD] = d_mix[:, cut]
            dox[n, HD : 2 * HD] = jnp.zeros((HD, tile), BF)
            st[n, 0:1] = lse_ref[z, :, cut]
            st[n, 1:2] = delta[:, cut]
    dq[...] = jnp.zeros_like(dq)
    later = lax.broadcasted_iota(jnp.int32, (tile, tile), 0) > lax.broadcasted_iota(
        jnp.int32, (tile, tile), 1
    )

    def key_block(j, _):
        here = pl.ds(pl.multiple_of(j * tile, tile), tile)
        keys = kx[here, :]
        values = vx[here, :]

        def step(i, carry, masked):
            dk, dv = carry
            scores = mm(keys, qx[i], NN)
            if masked:
                scores = jnp.where(later, MASKED, scores)
            probs = jnp.exp(scores - st[i, 0:1])
            d_probs = mm(values, dox[i], NN)
            d_scores = (probs * (d_probs - st[i, 1:2])).astype(BF)
            dv = dv + mm(dox[i, 0:HD], probs.astype(BF), NT)
            dk = dk + mm(qx[i, 0:HD], d_scores, NT)
            dq[i] += mm(kt[j], d_scores, NN)
            return dk, dv

        zero = jnp.zeros((HD, tile), F32)
        carry = step(j, (zero, zero), True)
        dk, dv = lax.fori_loop(j + 1, blocks, lambda i, c: step(i, c, False), carry)
        z = j // per
        cut = pl.ds(pl.multiple_of(lax.rem(j, per) * tile, tile), tile)
        out[z, 0:HD, cut] = (dq[j] * HD**-0.5).astype(BF)
        out[z, HD : 2 * HD, cut] = dk.astype(BF)
        out[z, 2 * HD : 3 * HD, cut] = dv.astype(BF)
        return 0

    lax.fori_loop(0, blocks, key_block, 0)


def attend_back(length, qkv, d_mix, mix, lse, tile):
    slabs, _, rows = qkv.shape
    total = slabs * rows
    tile = min(tile, rows)
    blocks = total // tile
    work = total * (total + tile) // 2
    vmem = pl.BlockSpec(memory_space=pltpu.VMEM)
    return pl.pallas_call(
        functools.partial(attend_back_kernel, tile),
        out_shape=jax.ShapeDtypeStruct((slabs, 3 * HD, rows), BF),
        in_specs=[pl.BlockSpec(memory_space=pltpu.SMEM), vmem, vmem, vmem, vmem],
        out_specs=vmem,
        scratch_shapes=[
            pltpu.VMEM((total, 2 * HD), BF),
            pltpu.VMEM((blocks, 2 * HD, tile), BF),
            pltpu.VMEM((total, 2 * HD), BF),
            pltpu.VMEM((blocks, HD, tile), BF),
            pltpu.VMEM((blocks, 2 * HD, tile), BF),
            pltpu.VMEM((blocks, HD, tile), F32),
            pltpu.VMEM((blocks, 8, tile), F32),
        ],
        compiler_params=pltpu.CompilerParams(vmem_limit_bytes=40 << 20),
        cost_estimate=pl.CostEstimate(
            flops=work * 256 * 10, bytes_accessed=qkv.size * 8, transcendentals=work
        ),
    )(length, qkv, d_mix, mix, lse)


def widths(total, step):
    return [(at, min(step, total - at)) for at in range(0, total, step)]


def middle_kernel(
    ff, split, scal, mix_a, mix_b, own, cot, gain, w_hbm,
    out_ref, dmid_ref, got_a, got_b, *refs,
):
    n_out = 3 if split < w_hbm.shape[2] else 1
    grads = refs[:n_out]
    (w, acts, att_t, mid, scale, dn, normed_ref, branch_ref, dattn_ref, turned, do_a, do_b,
     sems, out_sems, send_sems, recv_sems, local_sems) = refs[n_out:]
    slabs, halves, _, half = mix_a.shape
    width = own.shape[1]
    inner = width // halves
    base = 3 * ff
    lanes = base + inner
    here, line = lax.axis_index("ctx"), lax.axis_index("tp")
    core = lax.rem(lax.axis_index("fsdp"), 2)
    barrier = pltpu.get_barrier_semaphore()
    peers = [(dz, dt) for dz in range(slabs) for dt in range(halves) if dz or dt]

    def peer(dz, dt):
        return lax.rem(here + dz, slabs), lax.rem(line + dt, halves)

    for dz, dt in peers:
        z, t = peer(dz, dt)
        pl.semaphore_signal(
            barrier, inc=1, device_id={"ctx": z, "tp": t}, device_id_type=pl.DeviceIdType.MESH
        )
    cuts = [(t, base, inner) for t in range(halves)]
    cuts += [(t, k * ff, ff) for t in range(halves) for k in range(3)]
    loads = [
        pltpu.make_async_copy(
            w_hbm.at[t, :, at : at + n], w.at[t, :, at : at + n], sems.at[k]
        )
        for k, (t, at, n) in enumerate(cuts)
    ]
    for load in loads:
        load.start()
    length, first = scal[0], scal[1]
    step = 256
    rows = 64

    for t in range(halves):
        for z in range(slabs):
            at = z * 2 * HD
            att_t[at : at + HD, :] = mix_a[z, t]
            att_t[at + HD : at + 2 * HD, :] = mix_b[z, t]
        acts[t, :, base:lanes] = att_t[...].astype(F32).T.astype(BF)
    for k in range(halves):
        loads[k].wait()

    def project(n, _):
        cut = pl.ds(pl.multiple_of(n * step, step), step)
        total = own[:, cut].astype(F32)
        for t in range(halves):
            total = total + mm(acts[t, :, base:lanes], w[t, cut, base:lanes], NT)
        mid[:, cut] = total
        return 0

    lax.fori_loop(0, width // step, project, 0)

    def row_mask(r):
        pos = first + r * rows + lax.broadcasted_iota(jnp.int32, (rows, 1), 0)
        return jnp.where(pos < length, 1.0, 0.0)

    def norm(r, _):
        cut = pl.ds(pl.multiple_of(r * rows, rows), rows)
        values = mid[cut, :]
        inverse = lax.rsqrt(jnp.mean(values * values, axis=1, keepdims=True) + EPSILON)
        scale[cut, :] = jnp.broadcast_to(inverse, (rows, 128))
        normed_ref[cut, :] = (values * inverse * gain[...]).astype(BF)
        branch_ref[cut, :] = (cot[cut, :].astype(F32) * row_mask(r)).astype(BF)
        return 0

    lax.fori_loop(0, half // rows, norm, 0)

    for t in range(halves):
        for k in range(3):
            loads[halves + 3 * t + k].wait()

        def columns(at, n):
            def cut(k):
                return pl.ds(pl.multiple_of(k * ff + at, 128), n)

            gate = mm(normed_ref[...], w[t, :, cut(0)], NN)
            upward = mm(normed_ref[...], w[t, :, cut(1)], NN)
            d_hidden = mm(branch_ref[...], w[t, :, cut(2)], NN)
            sig = 1.0 / (1.0 + jnp.exp(-gate))
            active = gate * sig
            acts[t, :, cut(2)] = (active * upward).astype(BF)
            acts[t, :, cut(0)] = (
                d_hidden * upward * sig * (1.0 + gate * (1.0 - sig))
            ).astype(BF)
            acts[t, :, cut(1)] = (d_hidden * active).astype(BF)

        def chunk(c, _):
            columns(c * step, step)
            return 0

        lax.fori_loop(0, ff // step, chunk, 0)
        if ff % step:
            columns(ff - ff % step, ff % step)

    def back(n, _):
        cut = pl.ds(pl.multiple_of(n * step, step), step)
        total = mid[:, cut]
        grad = jnp.zeros((half, step), F32)
        for t in range(halves):
            total = total + mm(acts[t, :, 2 * ff : base], w[t, cut, 2 * ff : base], NT)
            grad = grad + mm(acts[t, :, 0:ff], w[t, cut, 0:ff], NT)
            grad = grad + mm(acts[t, :, ff : 2 * ff], w[t, cut, ff : 2 * ff], NT)
        dmid_ref[:, cut] = total
        dn[:, cut] = grad
        return 0

    lax.fori_loop(0, width // step, back, 0)

    def finish(r, _):
        cut = pl.ds(pl.multiple_of(r * rows, rows), rows)
        mask = row_mask(r)
        out_ref[cut, :] = (dmid_ref[cut, :] * mask).astype(BF)
        inverse = scale[cut, 0:1]
        scaled = mid[cut, :] * inverse
        d_scaled = dn[cut, :] * gain[...]
        mean = jnp.mean(d_scaled * scaled, axis=1, keepdims=True)
        total = cot[cut, :].astype(F32) * mask + inverse * (d_scaled - scaled * mean)
        dmid_ref[cut, :] = total
        dattn_ref[cut, :] = total.astype(BF)
        return 0

    lax.fori_loop(0, half // rows, finish, 0)
    for t in range(halves):
        for z in range(0, slabs, 2):
            at = base + z * 2 * HD
            grad = mm(dattn_ref[...], w[t, :, at : at + 4 * HD], NN).T.astype(BF)
            for k in range(2):
                do_a[z + k, t] = grad[2 * k * HD : (2 * k + 1) * HD]
                do_b[z + k, t] = grad[(2 * k + 1) * HD : (2 * k + 2) * HD]

    pl.semaphore_wait(barrier, len(peers))
    moves = []
    for k, (dz, dt) in enumerate(peers):
        z, t = peer(dz, dt)
        for h, (source, target) in enumerate(((do_a, got_a), (do_b, got_b))):
            move = pltpu.make_async_remote_copy(
                src_ref=source.at[z, t],
                dst_ref=target.at[here, line],
                send_sem=send_sems.at[2 * k + h],
                recv_sem=recv_sems.at[2 * k + h],
                device_id={"ctx": z, "tp": t},
                device_id_type=pl.DeviceIdType.MESH,
            )
            move.start()
            moves.append(move)
    for h, (source, target) in enumerate(((do_a, got_a), (do_b, got_b))):
        move = pltpu.make_async_copy(
            source.at[here, line], target.at[here, line], local_sems.at[h]
        )
        move.start()
        moves.append(move)

    regions = ((0, 2 * ff), (2 * ff, base), (base, lanes))

    def store(n, t):
        cut = pl.ds(pl.multiple_of(n * step, step), step)
        pltpu.make_async_copy(
            w.at[t, cut, 0:split], grads[0].at[t, cut, :], out_sems.at[n, t, 0]
        ).start()
        if n_out == 3:
            for side in range(2):

                @pl.when(lax.rem(n + core, 2) == 1 - side)
                def _():
                    pltpu.make_async_copy(
                        w.at[t, cut, split:lanes], grads[1 + side].at[t, n // 2], out_sems.at[n, t, 1]
                    ).start()

    def gradient(n, _):
        cut = pl.ds(pl.multiple_of(n * step, step), step)
        for k, ref in enumerate((normed_ref, branch_ref, dattn_ref)):
            turned[k] = ref[:, cut].astype(F32).T.astype(BF)
        for t in range(halves):
            for k, (at, end) in enumerate(regions):
                for b, m in widths(end - at, 1024):
                    value = mm(turned[k], acts[t, :, at + b : at + b + m], NN)
                    w[t, cut, at + b : at + b + m] = value.astype(BF)
            store(n, t)
        return 0

    lax.fori_loop(0, width // step, gradient, 0)

    def settle(n, _):
        cut = pl.ds(pl.multiple_of(n * step, step), step)
        for t in range(halves):
            pltpu.make_async_copy(
                w.at[t, cut, 0:split], grads[0].at[t, cut, :], out_sems.at[n, t, 0]
            ).wait()
            if n_out == 3:
                pltpu.make_async_copy(
                    w.at[t, cut, split:lanes], grads[1].at[t, n // 2], out_sems.at[n, t, 1]
                ).wait()
        return 0

    lax.fori_loop(0, width // step, settle, 0)
    for move in moves:
        move.wait()


def middle_stage(scalars, mix_a, mix_b, own, cot, gain, w, split):
    halves, width, lanes = w.shape
    slabs, _, _, half = mix_a.shape
    ff = (lanes - width // halves) // 3
    blocks = width // 256
    peers = slabs * halves - 1
    vmem = pl.BlockSpec(memory_space=pltpu.VMEM)
    outside = pl.BlockSpec(memory_space=pl.ANY)
    out_shape = [
        jax.ShapeDtypeStruct((half, width), BF),
        jax.ShapeDtypeStruct((half, width), F32),
        jax.ShapeDtypeStruct(mix_a.shape, BF),
        jax.ShapeDtypeStruct(mix_a.shape, BF),
        jax.ShapeDtypeStruct((halves, width, split), BF),
    ]
    out_specs = [vmem] * 4 + [outside]
    if split < lanes:
        out_shape += [jax.ShapeDtypeStruct((halves, blocks // 2, 256, lanes - split), BF)] * 2
        out_specs += [outside] * 2
    flops = 2 * half * width * (9 * ff * halves + 3 * width)
    return pl.pallas_call(
        functools.partial(middle_kernel, ff, split),
        out_shape=out_shape,
        in_specs=[pl.BlockSpec(memory_space=pltpu.SMEM)] + [vmem] * 5 + [outside],
        out_specs=out_specs,
        scratch_shapes=[
            pltpu.VMEM((halves, width, lanes), BF),
            pltpu.VMEM((halves, half, lanes), BF),
            pltpu.VMEM((width // halves, half), BF),
            pltpu.VMEM((half, width), F32),
            pltpu.VMEM((half, 128), F32),
            pltpu.VMEM((half, width), F32),
            pltpu.VMEM((half, width), BF),
            pltpu.VMEM((half, width), BF),
            pltpu.VMEM((half, width), BF),
            pltpu.VMEM((3, 256, half), BF),
            pltpu.VMEM(mix_a.shape, BF),
            pltpu.VMEM(mix_a.shape, BF),
            pltpu.SemaphoreType.DMA((4 * halves,)),
            pltpu.SemaphoreType.DMA((blocks, halves, 2)),
            pltpu.SemaphoreType.DMA((2 * peers,)),
            pltpu.SemaphoreType.DMA((2 * peers,)),
            pltpu.SemaphoreType.DMA((2,)),
        ],
        compiler_params=pltpu.CompilerParams(
            vmem_limit_bytes=58 << 20, collective_id=1, has_side_effects=True
        ),
        cost_estimate=pl.CostEstimate(
            flops=flops, bytes_accessed=4 * w.size + 16 * half * width, transcendentals=half * lanes
        ),
    )(scalars, mix_a, mix_b, own, cot, gain, w)


class LineSum:
    def __init__(self, source, held, slots, out, sems):
        self.source, self.held, self.slots, self.out = source, held, slots, out
        self.sum_send, self.sum_recv, self.out_send, self.out_recv = sems
        here = lax.axis_index("ctx")
        self.low = here < 2
        self.place = jnp.where(self.low, here, 3 - here)
        self.inward = jnp.where(self.low, here + 1, here - 1)
        self.outward = jnp.where(self.low, here - 1, here + 1)
        self.size = out.shape[0] // 4

    def number(self, part):
        return jnp.where(self.low, part, 3 - part)

    def part(self, ref, part):
        at = pl.multiple_of(self.number(part) * self.size, self.size)
        return ref.at[pl.ds(at, self.size), :]

    def read(self, ref, part):
        at = pl.multiple_of(self.number(part) * self.size, self.size)
        return ref[pl.ds(at, self.size), :].astype(F32)

    def write(self, ref, part, value):
        at = pl.multiple_of(self.number(part) * self.size, self.size)
        ref[pl.ds(at, self.size), :] = value.astype(BF)

    def copy(self, source, target, send, recv, place):
        return pltpu.make_async_remote_copy(
            src_ref=source, dst_ref=target, send_sem=send, recv_sem=recv,
            device_id={"ctx": place}, device_id_type=pl.DeviceIdType.MESH,
        )

    def took(self, slot):
        ref = self.slots.at[slot]
        self.copy(ref, ref, self.sum_send.at[0], self.sum_recv.at[slot], self.inward).wait_recv()
        return self.slots[slot].astype(F32)

    def begin(self):
        @pl.when(self.place == 0)
        def _():
            for k in range(3):
                self.copy(
                    self.part(self.source, 3 - k), self.slots.at[k],
                    self.sum_send.at[k], self.sum_recv.at[k], self.inward,
                ).start()

    def first(self, k):
        @pl.when(self.place == 1)
        def _():
            self.write(self.held, 3 - k, self.read(self.source, 3 - k) + self.took(k))
            self.copy(
                self.part(self.held, 3 - k), self.slots.at[3 + k],
                self.sum_send.at[k], self.sum_recv.at[3 + k], self.inward,
            ).start()

    def second(self):
        @pl.when(self.place == 1)
        def _():
            self.write(self.held, 0, self.read(self.source, 0) + self.took(3))
            self.copy(
                self.part(self.held, 0), self.slots.at[3],
                self.sum_send.at[2], self.sum_recv.at[3], self.outward,
            ).start()

    def give(self, part, send, place):
        ref = self.part(self.out, part)
        return self.copy(
            ref, ref, self.out_send.at[send], self.out_recv.at[self.number(part)], place
        )

    def final(self):
        @pl.when(self.place == 1)
        def _():
            self.write(self.out, 1, self.read(self.source, 1) + self.took(2) + self.took(4))
            self.give(1, 0, self.inward).start()
            self.give(1, 1, self.outward).start()

        @pl.when(self.place == 0)
        def _():
            self.write(self.out, 0, self.read(self.source, 0) + self.took(3))
            self.give(0, 0, self.inward).start()

    def forward(self):
        @pl.when(self.place == 1)
        def _():
            for k, (part, place) in enumerate(((0, self.inward), (2, self.outward), (3, self.outward))):
                self.give(part, 2 + k, place).wait_recv()
                self.give(part, 2 + k, place).start()

    def end(self):
        for k in range(3):
            self.copy(
                self.slots.at[0], self.slots.at[0],
                self.sum_send.at[k], self.sum_recv.at[0], self.inward,
            ).wait_send()

        @pl.when(self.place == 0)
        def _():
            self.give(0, 0, self.inward).wait_send()
            for part in (1, 2, 3):
                self.give(part, 0, self.inward).wait_recv()

        @pl.when(self.place == 1)
        def _():
            for k in range(5):
                self.give(1, k, self.inward).wait_send()


def tail_kernel(
    back_a, back_b, some, low, high, normed, weights, own, gain, dmid,
    grad_out, some_out, rest_out, qa_out, qb_out,
    got_b, turned, swapped, rest, some_held, some_slots, rest_held, rest_slots,
    local, crossed, column_sum, columned, q_src, q_held, q_slots, theirs, got_theirs, mine,
    in_send, in_recv, in_local, swap_send, swap_recv, core_send, core_recv, col_send, col_recv,
    row_send, row_recv, out_send, out_recv, *line_sems,
):
    here, line, place = lax.axis_index("ctx"), lax.axis_index("tp"), lax.axis_index("fsdp")
    core, column = lax.rem(place, 2), place // 2
    sibling = {"fsdp": place + 1 - 2 * core}
    beside = {"fsdp": lax.rem(place + 2, 4)}
    across = {"tp": 1 - line}
    others = [{"ctx": lax.rem(here + k, 4)} for k in range(1, 4)]
    mesh_id = pl.DeviceIdType.MESH
    barrier = pltpu.get_barrier_semaphore()
    for device in (*others, sibling, beside, across):
        pl.semaphore_signal(barrier, inc=1, device_id=device, device_id_type=mesh_id)
    pl.semaphore_wait(barrier, 6)

    def remote(source, target, send, recv, device):
        return pltpu.make_async_remote_copy(
            src_ref=source, dst_ref=target, send_sem=send, recv_sem=recv,
            device_id=device, device_id_type=mesh_id,
        )

    block = back_a.shape[0] // 4
    rows = normed.shape[0]
    half = rows // 2
    depth = 256

    def window(ref, at):
        return ref.at[pl.ds(pl.multiple_of(at * block, block), block), :]

    sent_in = [
        remote(
            window(back_b, device["ctx"]), window(got_b, here), in_send.at[k], in_recv.at[k], device
        )
        for k, device in enumerate(others)
    ]
    for move in sent_in:
        move.start()
    stays = pltpu.make_async_copy(window(back_b, here), window(got_b, here), in_local)
    stays.start()
    swaps = [
        remote(low.at[1 - column], swapped.at[0], swap_send.at[0], swap_recv.at[0], beside),
        remote(high.at[1 - line], swapped.at[1], swap_send.at[1], swap_recv.at[1], across),
    ]
    for move in swaps:
        move.start()
    a, b, qa, qb = (
        LineSum(src, held, slots, out, line_sems[4 * k : 4 * k + 4])
        for k, (src, held, slots, out) in enumerate(
            (
                (some, some_held, some_slots, some_out),
                (rest, rest_held, rest_slots, rest_out),
                (q_src.at[0], q_held.at[0], q_slots.at[0], qa_out),
                (q_src.at[1], q_held.at[1], q_slots.at[1], qb_out),
            )
        )
    )
    a.begin()

    def weight_gradient(h, grads):
        def step(n, _):
            cut = pl.ds(pl.multiple_of(n * depth, depth), depth)
            value = mm(grads[...], normed[:, cut], NN).astype(BF)
            local[h, lax.rem(n, 2), n // 2] = value
            return 0

        lax.fori_loop(0, 4, step, 0)
        move = remote(
            local.at[h, 1 - core], crossed.at[h], core_send.at[h], core_recv.at[h], sibling
        )
        move.start()
        return move

    def column_step(h, move):
        move.wait_recv()
        for x in range(2):
            column_sum[h, x] = (
                local[h, core, x].astype(F32) + crossed[h, x].astype(F32)
            ).astype(BF)
        move = remote(
            column_sum.at[h, 1 - column], columned.at[h], col_send.at[h], col_recv.at[h], beside
        )
        move.start()
        return move

    def column_end(h, move):
        move.wait_recv()
        q_src[h] = (column_sum[h, column].astype(F32) + columned[h].astype(F32)).astype(BF)

    def turn(h, grads):
        for k in range(0, grads.shape[0], 128):
            at = h * grads.shape[0] + k
            turned[:, at : at + 128] = grads[k : k + 128, :].astype(F32).T.astype(BF)

    core_a = weight_gradient(0, back_a)
    a.first(0)
    turn(0, back_a)
    for move in swaps:
        move.wait_recv()
    quarter = low.shape[1]
    rest[0:quarter] = (low[column].astype(F32) + swapped[0].astype(F32)).astype(BF)
    rest[quarter : 2 * quarter] = (high[line].astype(F32) + swapped[1].astype(F32)).astype(BF)
    b.begin()
    a.first(1)
    col_a = column_step(0, core_a)
    a.second()
    stays.wait()
    for move in sent_in:
        move.wait_recv()
    turn(1, got_b)

    pieces = 2
    piece = half // pieces
    sent_rows = []
    for k in range(pieces):
        cut = slice(k * piece, (k + 1) * piece)
        start = pl.multiple_of((1 - line) * half + k * piece, piece)

        def make(n, _):
            wide = pl.ds(pl.multiple_of(n * depth, depth), depth)
            value = mm(turned[pl.ds(start, piece), :], weights[wide, :], NT)
            theirs[cut, wide] = value.astype(BF)
            return 0

        lax.fori_loop(0, 4, make, 0)
        move = remote(theirs.at[cut], got_theirs.at[cut], row_send.at[k], row_recv.at[k], across)
        move.start()
        sent_rows.append(move)
    b.first(0)
    core_b = weight_gradient(1, got_b)
    a.final()
    mine_start = pl.multiple_of(line * half, half)

    def make_mine(n, _):
        wide = pl.ds(pl.multiple_of(n * depth, depth), depth)
        mine[:, wide] = mm(turned[pl.ds(mine_start, half), :], weights[wide, :], NT)
        return 0

    lax.fori_loop(0, 4, make_mine, 0)
    b.first(1)
    column_end(0, col_a)
    qa.begin()
    col_b = column_step(1, core_b)
    sent_out = []
    small = 64
    for k in range(pieces):
        sent_rows[k].wait_recv()

        def back(r, _):
            at = pl.multiple_of(k * piece + r * small, small)
            cut = pl.ds(at, small)
            values = own[cut, :].astype(F32)
            inverse = lax.rsqrt(jnp.mean(values * values, axis=1, keepdims=True) + EPSILON)
            scaled = values * inverse
            d_scaled = (mine[cut, :] + got_theirs[cut, :].astype(F32)) * gain[...]
            mean = jnp.mean(d_scaled * scaled, axis=1, keepdims=True)
            total = dmid[cut, :] + inverse * (d_scaled - scaled * mean)
            grad_out[pl.ds(pl.multiple_of(line * half + at, small), small), :] = total.astype(BF)
            return 0

        lax.fori_loop(0, piece // small, back, 0)
        ref = grad_out.at[pl.ds(pl.multiple_of(line * half + k * piece, piece), piece), :]
        move = remote(ref, ref, out_send.at[k], out_recv.at[k], across)
        move.start()
        sent_out.append(move)
    b.second()
    column_end(1, col_b)
    qb.begin()
    a.forward()
    b.final()
    qa.first(0)
    qa.first(1)
    qb.first(0)
    qb.first(1)
    qa.second()
    qb.second()
    b.forward()
    qa.final()
    qb.final()
    qa.forward()
    qb.forward()
    for run in (a, b, qa, qb):
        run.end()
    for move in (*sent_in, *swaps, core_a, core_b, col_a, col_b, *sent_rows):
        move.wait_send()
    for k, move in enumerate(sent_out):
        move.wait_send()
        ref = grad_out.at[pl.ds(pl.multiple_of((1 - line) * half + k * piece, piece), piece), :]
        remote(ref, ref, out_send.at[k], out_recv.at[k], across).wait_recv()


def tail_stage(back_a, back_b, some, low, high, normed, weights, own, gain, dmid):
    rows, width = normed.shape
    half = rows // 2
    lanes_a, lanes_b = some.shape[1], low.shape[2]
    wide = back_a.shape[0]
    vmem = pl.BlockSpec(memory_space=pltpu.VMEM)
    dma = pltpu.SemaphoreType.DMA
    return pl.pallas_call(
        tail_kernel,
        out_shape=(
            jax.ShapeDtypeStruct((rows, width), BF),
            jax.ShapeDtypeStruct((256, lanes_a), BF),
            jax.ShapeDtypeStruct((256, lanes_b), BF),
            jax.ShapeDtypeStruct((wide, 256), BF),
            jax.ShapeDtypeStruct((wide, 256), BF),
        ),
        in_specs=[vmem] * 10,
        out_specs=(vmem,) * 5,
        scratch_shapes=[
            pltpu.VMEM((wide, rows), BF),
            pltpu.VMEM((rows, 2 * wide), BF),
            pltpu.VMEM((2, 128, lanes_b), BF),
            pltpu.VMEM((256, lanes_b), BF),
            pltpu.VMEM((256, lanes_a), BF),
            pltpu.VMEM((5, 64, lanes_a), BF),
            pltpu.VMEM((256, lanes_b), BF),
            pltpu.VMEM((5, 64, lanes_b), BF),
            pltpu.VMEM((2, 2, 2, wide, 256), BF),
            pltpu.VMEM((2, 2, wide, 256), BF),
            pltpu.VMEM((2, 2, wide, 256), BF),
            pltpu.VMEM((2, wide, 256), BF),
            pltpu.VMEM((2, wide, 256), BF),
            pltpu.VMEM((2, wide, 256), BF),
            pltpu.VMEM((2, 5, wide // 4, 256), BF),
            pltpu.VMEM((half, width), BF),
            pltpu.VMEM((half, width), BF),
            pltpu.VMEM((half, width), F32),
            dma((3,)), dma((3,)), dma,
            dma((2,)), dma((2,)), dma((2,)), dma((2,)), dma((2,)), dma((2,)),
            dma((2,)), dma((2,)), dma((2,)), dma((2,)),
        ]
        + [dma((3,)), dma((5,)), dma((5,)), dma((4,))] * 4,
        compiler_params=pltpu.CompilerParams(
            vmem_limit_bytes=56 << 20, collective_id=2, has_side_effects=True
        ),
        cost_estimate=pl.CostEstimate(
            flops=8 * rows * width * wide, bytes_accessed=40 << 20, transcendentals=0
        ),
    )(back_a, back_b, some, low, high, normed, weights, own, gain, dmid)


def normalize(values, gain):
    inverse = lax.rsqrt(jnp.mean(values * values, axis=-1, keepdims=True) + EPSILON)
    scaled = values * inverse
    return scaled, inverse, (scaled * gain).astype(BF)


def norm_back(d_normed, scaled, inverse, gain):
    d_scaled = d_normed * gain
    d_values = inverse * (d_scaled - scaled * jnp.mean(d_scaled * scaled, axis=-1, keepdims=True))
    return d_values


def rows_first(values):
    return with_layout_constraint(values, Layout(major_to_minor=tuple(range(values.ndim))))


def swap(values, axis, bit):
    count = lax.axis_size(axis)
    return lax.ppermute(values, axis, [(k, k ^ bit) for k in range(count)])


def plus(left, right):
    return (left.astype(F32) + right.astype(F32)).astype(BF)


def pick(values, index, axis):
    return lax.dynamic_index_in_dim(values, index, axis, keepdims=False)


def both_halves(values):
    half = values.shape[0]
    side = lax.axis_index("tp") * half
    whole = jnp.zeros((2 * half,) + values.shape[1:], values.dtype)
    whole = lax.dynamic_update_slice_in_dim(whole, values, side, 0)
    return lax.dynamic_update_slice_in_dim(whole, swap(values, "tp", 1), half - side, 0)


def sum_blocks(values):
    slabs = lax.axis_size("ctx")
    cut = values.reshape((slabs, values.shape[0] // slabs) + values.shape[1:])
    cut = lax.all_to_all(cut, "ctx", 0, 0, tiled=True)
    total = jnp.sum(cut.astype(F32), axis=0).astype(BF)
    total = lax.all_to_all(
        jnp.broadcast_to(total[None], (slabs,) + total.shape), "ctx", 0, 0, tiled=True
    )
    return total.reshape(values.shape)


def shards(
    inputs,
    lengths,
    first_gain,
    query_weight,
    key_weight,
    value_weight,
    out_weight,
    second_gain,
    gate_weight,
    up_weight,
    down_weight,
    cotangent,
):
    slabs, halves, parts = lax.axis_size("ctx"), lax.axis_size("tp"), lax.axis_size("fsdp")
    rows, width = inputs.shape[1], inputs.shape[2]
    depth = query_weight.shape[0]
    group = query_weight.shape[1] // HD // slabs
    half = rows // halves
    ff = gate_weight.shape[1]
    everywhere = ("tp", "fsdp")
    side = lax.axis_index("tp") * half

    gains = lax.all_gather(jnp.stack([first_gain, second_gain]), "fsdp", axis=1, tiled=True)
    gain_one, gain_two = gains[0].astype(F32), gains[1].astype(F32)
    stacked = jnp.stack(
        [w.reshape(depth, slabs, group, HD) for w in (query_weight, key_weight, value_weight)]
    ).transpose(1, 3, 2, 0, 4)
    qkv_width = slabs * 3 * HD
    w_qkv = lax.all_gather(
        stacked.reshape(depth, group * qkv_width), "fsdp", axis=0, tiled=True
    )
    w_heads = [w_qkv[:, h * qkv_width : (h + 1) * qkv_width] for h in range(group)]
    w_rest = jnp.concatenate([gate_weight, up_weight, down_weight.T, out_weight.T], axis=1)
    w_rest = rows_first(lax.all_gather(rows_first(w_rest), everywhere, axis=0, tiled=True))
    w_rest = w_rest.reshape(halves, width, -1)

    residual = inputs[0].astype(F32)
    _, _, normed_one = normalize(residual, gain_one)
    qkv = []
    for h in range(group):
        part = mm(w_heads[h], normed_one, (((0,), (1,)), ((), ()))).astype(BF)
        part = part.reshape(slabs, 3 * HD, rows)
        qkv.append(lax.all_to_all(part, "ctx", 0, 0, tiled=True))
    arrived, saved = [], []
    for h in range(group):
        mix, mix_full, lse = attend(lengths, qkv[h], halves, 1024)
        saved.append((mix_full, lse))
        mix = mix.reshape(slabs * halves, HD, half)
        mix = lax.all_to_all(mix, ("ctx", "tp"), 0, 0, tiled=True)
        arrived.append(mix.reshape(slabs, halves, HD, half))

    own = lax.dynamic_slice_in_dim(inputs[0], side, half, 0)
    cot = lax.dynamic_slice_in_dim(cotangent[0], side, half, 0)
    scalars = jnp.stack([lengths[0], lax.axis_index("ctx") * rows + side])
    paired = parts == 4 and halves == 2 and slabs == 4 and group == 2
    split = 2432 if paired else w_rest.shape[2]
    output, d_middle, *d_mix, = middle_stage(
        scalars, *arrived, own, cot, gain_two[None], w_rest, split
    )
    d_mix, (g_some, *g_rest) = d_mix[:2], d_mix[2:]
    output = both_halves(output)
    s_some = lax.psum_scatter(
        rows_first(g_some.reshape(halves * width, -1)), everywhere, scatter_dimension=0, tiled=True
    )
    s_some = rows_first(s_some)

    core, column, line = (
        lax.rem(lax.axis_index("fsdp"), 2),
        lax.axis_index("fsdp") // 2,
        lax.axis_index("tp"),
    )
    d_local = [None] * group
    d_local[0] = attend_back(lengths, qkv[0], d_mix[0], *saved[0], 1024)
    if paired:
        got = swap(g_rest[0], "fsdp", 1)
        got, d_local[0] = lax.optimization_barrier((got, d_local[0]))
        total = plus(g_rest[1], got)
        cut = total.shape[2] // 2
        low, high = total[:, :, :cut], total[:, :, cut:]
        low_out, high_out = pick(low, 1 - line, 0), pick(high, 1 - column, 1)
        low, high = pick(low, line, 0), pick(high, column, 1)
        d_mix[1], low_out, high_out, low, high = lax.optimization_barrier(
            (d_mix[1], low_out, high_out, low, high)
        )
    for h in range(1, group):
        d_local[h] = attend_back(lengths, qkv[h], d_mix[h], *saved[h], 1024)
    normed_rows = own.astype(F32)
    if paired:
        back_a = lax.all_to_all(d_local[0], "ctx", 0, 0, tiled=True).reshape(qkv_width, rows)
        got_low, got_high = swap(low_out, "tp", 1), swap(high_out, "fsdp", 2)
        got_low, got_high, back_a, d_local[1] = lax.optimization_barrier(
            (got_low, got_high, back_a, d_local[1])
        )
        input_gradient, s_some, s_rest, *q_grads = tail_stage(
            back_a, d_local[1].reshape(qkv_width, rows), s_some, plus(low, got_low),
            plus(high, got_high), normed_one, w_qkv, own, gain_one[None], d_middle,
        )
        s_all = jnp.concatenate([s_some, s_rest], axis=1).astype(F32)
        s_qkv = jnp.stack([q.reshape(slabs, 3, HD, depth) for q in q_grads], axis=1)
        s_qkv = s_qkv.transpose(2, 4, 0, 1, 3).reshape(3, depth, slabs * group * HD).astype(F32)
    else:
        d_qkv = [
            lax.all_to_all(d, "ctx", 0, 0, tiled=True).reshape(qkv_width, rows) for d in d_local
        ]
        d_normed_one = jnp.zeros((rows, width), F32)
        s_qkv = []
        for h in range(group):
            d_normed_one = d_normed_one + mm(d_qkv[h], w_heads[h], (((0,), (1,)), ((), ())))
            grad = mm(normed_one, d_qkv[h], (((0,), (1,)), ((), ()))).astype(BF)
            grad = lax.psum_scatter(grad, "fsdp", scatter_dimension=0, tiled=True)
            s_qkv.append(lax.psum(grad, "ctx").reshape(depth, slabs, 3, HD))
        d_normed_one = lax.psum_scatter(d_normed_one, "tp", scatter_dimension=0, tiled=True)
        scaled_one, inverse_one, _ = normalize(normed_rows, gain_one)
        d_from_one = norm_back(d_normed_one, scaled_one, inverse_one, gain_one)
        input_gradient = lax.all_gather(
            (d_middle + d_from_one).astype(BF), "tp", axis=0, tiled=True
        )
        s_qkv = jnp.stack(s_qkv, axis=2).transpose(3, 0, 1, 2, 4)
        s_qkv = s_qkv.reshape(3, depth, slabs * group * HD).astype(F32)
        s_all = lax.psum(s_some, "ctx").astype(F32)

    d_gain_one = sum(
        jnp.sum(w.astype(F32) * s, axis=1)
        for w, s in zip((query_weight, key_weight, value_weight), s_qkv)
    ) / first_gain.astype(F32)
    d_gain_two = (
        jnp.sum(gate_weight.astype(F32) * s_all[:, :ff], axis=1)
        + jnp.sum(up_weight.astype(F32) * s_all[:, ff : 2 * ff], axis=1)
    ) / second_gain.astype(F32)
    d_gains = jnp.stack([d_gain_one, d_gain_two])
    d_gains = d_gains + swap(d_gains, "tp", 1) if paired else lax.psum(d_gains, "tp")
    return (
        output[None],
        input_gradient[None],
        d_gains[0],
        s_qkv[0],
        s_qkv[1],
        s_qkv[2],
        s_all[:, 3 * ff :].T,
        d_gains[1],
        s_all[:, :ff],
        s_all[:, ff : 2 * ff],
        s_all[:, 2 * ff : 3 * ff].T,
    )


def solution(mesh):
    rows = P("fsdp", "ctx", None)
    gain = P("fsdp")
    inward = P("fsdp", "tp")
    outward = P("tp", "fsdp")
    return jax.shard_map(
        shards,
        mesh=mesh,
        in_specs=(
            rows, gain, gain, inward, inward, inward, outward, gain, inward, inward, outward, rows,
        ),
        out_specs=(
            rows, rows, gain, inward, inward, inward, outward, gain, inward, inward, outward,
        ),
        check_vma=False,
    )
```

```python
import functools

import jax
import jax.numpy as jnp
from jax import lax
from jax.experimental import pallas as pl
from jax.experimental.pallas import tpu as pltpu
from jax.experimental.layout import Layout, with_layout_constraint
from jax.sharding import PartitionSpec as P

HD = 64
EPSILON = 1e-05
MASKED = -1000000000.0
NN = (((1,), (0,)), ((), ()))
NT = (((1,), (1,)), ((), ()))
TN = (((0,), (0,)), ((), ()))
BF = jnp.bfloat16
F32 = jnp.float32


def mm(left, right, dims):
    return lax.dot_general(left, right, dims, preferred_element_type=F32)


def spread_keys(keys, start, length):
    rows = keys.shape[0]
    pos = start + lax.broadcasted_iota(jnp.int32, (rows, HD), 0)
    lane = lax.broadcasted_iota(jnp.int32, (rows, HD), 1)
    bias = jnp.where((lane == 0) & (pos >= length), MASKED, 0.0)
    return jnp.concatenate([keys, bias], axis=1).astype(BF)


def spread_queries(queries):
    row = lax.broadcasted_iota(jnp.int32, queries.shape, 0)
    ones = jnp.where(row == 0, 1.0, 0.0)
    return jnp.concatenate([queries * HD**-0.5, ones], axis=0).astype(BF)


def attend_rows(tile, length, qkv, kx, qx, vx, emit):
    slabs, _, rows = qkv.shape
    per = rows // tile
    blocks = slabs * per
    for z in range(slabs):
        keys = qkv[z, HD : 2 * HD, :].astype(F32).T
        kx[z * rows : (z + 1) * rows, :] = spread_keys(keys, z * rows, length)
        queries = spread_queries(qkv[z, 0:HD, :].astype(F32))
        for b in range(per):
            cut = slice(b * tile, (b + 1) * tile)
            qx[z * per + b] = queries[:, cut]
            vx[z * per + b] = qkv[z, 2 * HD : 3 * HD, cut]
    later = lax.broadcasted_iota(jnp.int32, (tile, tile), 0) > lax.broadcasted_iota(
        jnp.int32, (tile, tile), 1
    )

    def query_block(i, _):
        queries = qx[i]

        def step(j, carry, masked):
            highest, total, mix = carry
            keys = kx[pl.ds(pl.multiple_of(j * tile, tile), tile), :]
            scores = mm(keys, queries, NN)
            if masked:
                scores = jnp.where(later, MASKED, scores)
            new = jnp.maximum(highest, jnp.max(scores, axis=0, keepdims=True))
            scale = jnp.exp(highest - new)
            probs = jnp.exp(scores - new)
            total = total * scale + jnp.sum(probs, axis=0, keepdims=True)
            mix = mix * scale + mm(vx[j], probs.astype(BF), NN)
            return new, total, mix

        first = (
            jnp.full((1, tile), -jnp.inf, F32),
            jnp.zeros((1, tile), F32),
            jnp.zeros((HD, tile), F32),
        )
        carry = lax.fori_loop(0, i, lambda j, c: step(j, c, False), first)
        highest, total, mix = step(i, carry, True)
        emit(i, mix / total, highest + jnp.log(total))
        return 0

    lax.fori_loop(0, blocks, query_block, 0)


def attend_kernel(tile, len_ref, qkv, o_ref, of_ref, lse_ref, kx, qx, vx):
    rows = qkv.shape[2]
    halves = o_ref.shape[1]
    half = rows // halves

    def emit(i, mix, lse):
        of_ref[i] = mix
        lse_ref[i] = lse
        for t in range(halves):
            o_ref[i, t] = mix[:, t * half : (t + 1) * half].astype(BF)

    attend_rows(tile, len_ref[0], qkv, kx, qx, vx, emit)


def front_kernel(
    len_ref, x, gains_own, wq, wk, wv,
    wt, normed, gains, qkv_a, qkv_b, mix_a, mix_b, of_a, of_b, lse_a, lse_b,
    packed, parts, mixed, kx, qx, vx,
    gain_send, gain_recv, w_send, w_recv, part_send, part_recv, part_local,
    mix_send, mix_recv, mix_local,
):
    here, line, place = lax.axis_index("ctx"), lax.axis_index("tp"), lax.axis_index("fsdp")
    core, column = lax.rem(place, 2), place // 2
    pair = place + 1 - 2 * core
    other = lax.rem(place + 2, 4)
    mesh_id = pl.DeviceIdType.MESH
    slabs, halves = mix_a.shape[0], mix_a.shape[1]
    rows, width = x.shape
    half = rows // halves
    wide = slabs * 3 * HD
    depth = wq.shape[0]
    peers = [(dz, dt) for dz in range(slabs) for dt in range(halves) if dz or dt]

    def peer(dz, dt):
        return lax.rem(here + dz, slabs), lax.rem(line + dt, halves)

    barrier = pltpu.get_barrier_semaphore()
    for dz, dt in peers:
        z, t = peer(dz, dt)
        pl.semaphore_signal(barrier, inc=1, device_id={"ctx": z, "tp": t}, device_id_type=mesh_id)
    for device in (pair, other):
        pl.semaphore_signal(barrier, inc=1, device_id={"fsdp": device}, device_id_type=mesh_id)
    for q, w in enumerate((wq, wk, wv)):
        flat = w[...].astype(F32).T.astype(BF)
        for z in range(slabs):
            for h in range(2):
                at = (2 * z + h) * HD
                packed[h, (3 * z + q) * HD : (3 * z + q + 1) * HD, :] = flat[at : at + HD]

    def remote(source, target, send, recv, device):
        return pltpu.make_async_remote_copy(
            src_ref=source, dst_ref=target, send_sem=send, recv_sem=recv,
            device_id=device, device_id_type=mesh_id,
        )

    def lanes(index):
        return pl.ds(pl.multiple_of(index * depth, depth), depth)

    def weight(h, index):
        return wt.at[h * wide : (h + 1) * wide, lanes(index)]

    gains[:, lanes(place)] = gains_own[...]
    for h in range(2):
        wt[h * wide : (h + 1) * wide, lanes(place)] = packed[h]
    pl.semaphore_wait(barrier, len(peers) + 2)
    sent = []

    def launch(move):
        move.start()
        sent.append(move)
        return move

    for k, device in enumerate((pair, other)):
        launch(
            remote(
                gains_own, gains.at[:, lanes(place)], gain_send.at[k], gain_recv.at[k], {"fsdp": device}
            )
        )
    for h in range(2):
        for k, device in ((1, other), (0, pair)):
            launch(
                remote(
                    packed.at[h], weight(h, place), w_send.at[h, k], w_recv.at[h, k], {"fsdp": device}
                )
            )

    def arrived(ref, sem):
        remote(ref, ref, gain_send.at[0], sem, {"fsdp": pair}).wait_recv()

    arrived(gains.at[:, lanes(other)], gain_recv.at[1])
    launch(
        remote(
            gains.at[:, lanes(other)], gains.at[:, lanes(other)], gain_send.at[2], gain_recv.at[2],
            {"fsdp": pair},
        )
    )
    far = lax.rem(pair + 2, 4)
    arrived(gains.at[:, lanes(pair)], gain_recv.at[0])
    arrived(gains.at[:, lanes(far)], gain_recv.at[2])
    small = 64

    def norm(r, _):
        cut = pl.ds(pl.multiple_of(r * small, small), small)
        values = x[cut, :].astype(F32)
        inverse = lax.rsqrt(jnp.mean(values * values, axis=1, keepdims=True) + EPSILON)
        normed[cut, :] = (values * inverse * gains[0:1, :]).astype(BF)
        return 0

    lax.fori_loop(0, rows // small, norm, 0)
    queues = (qkv_a, qkv_b)
    waits = []
    for h in range(2):
        arrived(weight(h, other), w_recv.at[h, 1])
        launch(
            remote(
                weight(h, other), weight(h, other), w_send.at[h, 2], w_recv.at[h, 2], {"fsdp": pair}
            )
        )
    for h in range(2):
        arrived(weight(h, pair), w_recv.at[h, 0])
        arrived(weight(h, far), w_recv.at[h, 2])

        def project(n, _):
            cut = pl.ds(pl.multiple_of(n * 256, 256), 256)
            value = mm(wt[h * wide : (h + 1) * wide, :], normed[cut, :], NT).astype(BF)
            for z in range(slabs):
                parts[h, z, :, cut] = value[z * 3 * HD : (z + 1) * 3 * HD]
            return 0

        lax.fori_loop(0, rows // 256, project, 0)
        for k in range(1, slabs):
            z = lax.rem(here + k, slabs)
            waits.append(
                launch(
                    remote(
                        parts.at[h, z], queues[h].at[here], part_send.at[h, k], part_recv.at[h, k],
                        {"ctx": z},
                    )
                )
            )
        stays = pltpu.make_async_copy(parts.at[h, here], queues[h].at[here], part_local.at[h])
        stays.start()
        waits.append(stays)

    for h, (qkv, mix_ref, of_ref, lse_ref) in enumerate(
        ((qkv_a, mix_a, of_a, lse_a), (qkv_b, mix_b, of_b, lse_b))
    ):
        for move in waits[h * slabs : (h + 1) * slabs - 1]:
            move.wait_recv()
        waits[(h + 1) * slabs - 1].wait()

        def emit(i, mix, lse):
            of_ref[i] = mix
            lse_ref[i] = lse
            for t in range(halves):
                mixed[h, i, t] = mix[:, t * half : (t + 1) * half].astype(BF)
                stay = (i == here) & (line == t)

                @pl.when(stay)
                def _():
                    pltpu.make_async_copy(
                        mixed.at[h, i, t], mix_ref.at[here, line], mix_local.at[h]
                    ).start()

                @pl.when(jnp.logical_not(stay))
                def _():
                    remote(
                        mixed.at[h, i, t], mix_ref.at[here, line], mix_send.at[h, i, t],
                        mix_recv.at[h, here, line], {"ctx": i, "tp": t},
                    ).start()

        attend_rows(rows, len_ref[0], qkv, kx, qx, vx, emit)

    for move in sent:
        move.wait_send()
    for h, mix_ref in enumerate((mix_a, mix_b)):
        pltpu.make_async_copy(mixed.at[h, here, line], mix_ref.at[here, line], mix_local.at[h]).wait()
        for dz, dt in peers:
            z, t = peer(dz, dt)
            remote(
                mixed.at[h, z, t], mix_ref.at[z, t], mix_send.at[h, z, t], mix_recv.at[h, z, t],
                {"ctx": z, "tp": t},
            ).wait()


def front_stage(length, x, gains, wq, wk, wv, slabs, halves):
    rows, width = x.shape
    half = rows // halves
    wide = slabs * 3 * HD
    total = slabs * rows
    work = total * (total + rows) // 2
    vmem = pl.BlockSpec(memory_space=pltpu.VMEM)
    dma = pltpu.SemaphoreType.DMA
    shape = jax.ShapeDtypeStruct
    return pl.pallas_call(
        front_kernel,
        out_shape=(
            shape((2 * wide, width), BF),
            shape((rows, width), BF),
            shape((8, width), F32),
            *[shape((slabs, 3 * HD, rows), BF)] * 2,
            *[shape((slabs, halves, HD, half), BF)] * 2,
            *[shape((slabs, HD, rows), F32)] * 2,
            *[shape((slabs, 1, rows), F32)] * 2,
        ),
        in_specs=[pl.BlockSpec(memory_space=pltpu.SMEM)] + [vmem] * 5,
        out_specs=(vmem,) * 11,
        scratch_shapes=[
            pltpu.VMEM((2, wide, wq.shape[0]), BF),
            pltpu.VMEM((2, slabs, 3 * HD, rows), BF),
            pltpu.VMEM((2, slabs, halves, HD, half), BF),
            pltpu.VMEM((total, 2 * HD), BF),
            pltpu.VMEM((slabs, 2 * HD, rows), BF),
            pltpu.VMEM((slabs, HD, rows), BF),
            dma((3,)), dma((3,)), dma((2, 3)), dma((2, 3)),
            dma((2, slabs)), dma((2, slabs)), dma((2,)),
            dma((2, slabs, halves)), dma((2, slabs, halves)), dma((2,)),
        ],
        compiler_params=pltpu.CompilerParams(
            vmem_limit_bytes=48 << 20, collective_id=3, has_side_effects=True
        ),
        cost_estimate=pl.CostEstimate(
            flops=2 * work * 256 * 4, bytes_accessed=20 << 20, transcendentals=2 * work
        ),
    )(length, x, gains, wq, wk, wv)


def attend(length, qkv, halves, tile):
    slabs, _, rows = qkv.shape
    total = slabs * rows
    tile = min(tile, rows)
    work = total * (total + tile) // 2
    vmem = pl.BlockSpec(memory_space=pltpu.VMEM)
    return pl.pallas_call(
        functools.partial(attend_kernel, tile),
        out_shape=(
            jax.ShapeDtypeStruct((slabs, halves, HD, rows // halves), BF),
            jax.ShapeDtypeStruct((slabs, HD, rows), F32),
            jax.ShapeDtypeStruct((slabs, 1, rows), F32),
        ),
        in_specs=[pl.BlockSpec(memory_space=pltpu.SMEM), vmem],
        out_specs=(vmem, vmem, vmem),
        scratch_shapes=[
            pltpu.VMEM((total, 2 * HD), BF),
            pltpu.VMEM((total // tile, 2 * HD, tile), BF),
            pltpu.VMEM((total // tile, HD, tile), BF),
        ],
        compiler_params=pltpu.CompilerParams(vmem_limit_bytes=40 << 20),
        cost_estimate=pl.CostEstimate(
            flops=work * 256 * 4, bytes_accessed=qkv.size * 4, transcendentals=work
        ),
    )(length, qkv)


def attend_back_kernel(tile, len_ref, qkv, do_ref, of_ref, lse_ref, out, kx, qx, vx, kt, dox, dq, st):
    slabs, _, rows = qkv.shape
    halves, half = do_ref.shape[1], do_ref.shape[3]
    length = len_ref[0]
    per = rows // tile
    blocks = slabs * per
    for z in range(slabs):
        keys = qkv[z, HD : 2 * HD, :]
        kx[z * rows : (z + 1) * rows, :] = spread_keys(keys.astype(F32).T, z * rows, length)
        queries = spread_queries(qkv[z, 0:HD, :].astype(F32))
        values = qkv[z, 2 * HD : 3 * HD, :].astype(F32).T
        vx[z * rows : (z + 1) * rows, :] = jnp.concatenate(
            [values, jnp.zeros((rows, HD), F32)], axis=1
        ).astype(BF)
        d_mix = jnp.concatenate([do_ref[z, t] for t in range(halves)], axis=1)
        delta = jnp.sum(d_mix.astype(F32) * of_ref[z], axis=0, keepdims=True)
        for b in range(per):
            cut = slice(b * tile, (b + 1) * tile)
            n = z * per + b
            qx[n] = queries[:, cut]
            kt[n] = keys[:, cut]
            dox[n, 0:HD] = d_mix[:, cut]
            dox[n, HD : 2 * HD] = jnp.zeros((HD, tile), BF)
            st[n, 0:1] = lse_ref[z, :, cut]
            st[n, 1:2] = delta[:, cut]
    dq[...] = jnp.zeros_like(dq)
    later = lax.broadcasted_iota(jnp.int32, (tile, tile), 0) > lax.broadcasted_iota(
        jnp.int32, (tile, tile), 1
    )

    def key_block(j, _):
        here = pl.ds(pl.multiple_of(j * tile, tile), tile)
        keys = kx[here, :]
        values = vx[here, :]

        def step(i, carry, masked):
            dk, dv = carry
            scores = mm(keys, qx[i], NN)
            if masked:
                scores = jnp.where(later, MASKED, scores)
            probs = jnp.exp(scores - st[i, 0:1])
            d_probs = mm(values, dox[i], NN)
            d_scores = (probs * (d_probs - st[i, 1:2])).astype(BF)
            dv = dv + mm(dox[i, 0:HD], probs.astype(BF), NT)
            dk = dk + mm(qx[i, 0:HD], d_scores, NT)
            dq[i] += mm(kt[j], d_scores, NN)
            return dk, dv

        zero = jnp.zeros((HD, tile), F32)
        carry = step(j, (zero, zero), True)
        dk, dv = lax.fori_loop(j + 1, blocks, lambda i, c: step(i, c, False), carry)
        z = j // per
        cut = pl.ds(pl.multiple_of(lax.rem(j, per) * tile, tile), tile)
        out[z, 0:HD, cut] = (dq[j] * HD**-0.5).astype(BF)
        out[z, HD : 2 * HD, cut] = dk.astype(BF)
        out[z, 2 * HD : 3 * HD, cut] = dv.astype(BF)
        return 0

    lax.fori_loop(0, blocks, key_block, 0)


def attend_back(length, qkv, d_mix, mix, lse, tile):
    slabs, _, rows = qkv.shape
    total = slabs * rows
    tile = min(tile, rows)
    blocks = total // tile
    work = total * (total + tile) // 2
    vmem = pl.BlockSpec(memory_space=pltpu.VMEM)
    return pl.pallas_call(
        functools.partial(attend_back_kernel, tile),
        out_shape=jax.ShapeDtypeStruct((slabs, 3 * HD, rows), BF),
        in_specs=[pl.BlockSpec(memory_space=pltpu.SMEM), vmem, vmem, vmem, vmem],
        out_specs=vmem,
        scratch_shapes=[
            pltpu.VMEM((total, 2 * HD), BF),
            pltpu.VMEM((blocks, 2 * HD, tile), BF),
            pltpu.VMEM((total, 2 * HD), BF),
            pltpu.VMEM((blocks, HD, tile), BF),
            pltpu.VMEM((blocks, 2 * HD, tile), BF),
            pltpu.VMEM((blocks, HD, tile), F32),
            pltpu.VMEM((blocks, 8, tile), F32),
        ],
        compiler_params=pltpu.CompilerParams(vmem_limit_bytes=40 << 20),
        cost_estimate=pl.CostEstimate(
            flops=work * 256 * 10, bytes_accessed=qkv.size * 8, transcendentals=work
        ),
    )(length, qkv, d_mix, mix, lse)


def widths(total, step):
    return [(at, min(step, total - at)) for at in range(0, total, step)]


def middle_kernel(
    ff, split, scal, mix_a, mix_b, own, cot, gain, w_hbm,
    out_ref, dmid_ref, got_a, got_b, *refs,
):
    n_out = 3 if split < w_hbm.shape[2] else 1
    grads = refs[:n_out]
    (w, acts, att_t, mid, scale, dn, normed_ref, branch_ref, dattn_ref, turned, do_a, do_b,
     sems, out_sems, send_sems, recv_sems, local_sems) = refs[n_out:]
    slabs, halves, _, half = mix_a.shape
    width = own.shape[1]
    inner = width // halves
    base = 3 * ff
    lanes = base + inner
    here, line = lax.axis_index("ctx"), lax.axis_index("tp")
    core = lax.rem(lax.axis_index("fsdp"), 2)
    barrier = pltpu.get_barrier_semaphore()
    peers = [(dz, dt) for dz in range(slabs) for dt in range(halves) if dz or dt]

    def peer(dz, dt):
        return lax.rem(here + dz, slabs), lax.rem(line + dt, halves)

    for dz, dt in peers:
        z, t = peer(dz, dt)
        pl.semaphore_signal(
            barrier, inc=1, device_id={"ctx": z, "tp": t}, device_id_type=pl.DeviceIdType.MESH
        )
    cuts = [(t, base, inner) for t in range(halves)]
    cuts += [(t, k * ff, ff) for t in range(halves) for k in range(3)]
    loads = [
        pltpu.make_async_copy(
            w_hbm.at[t, :, at : at + n], w.at[t, :, at : at + n], sems.at[k]
        )
        for k, (t, at, n) in enumerate(cuts)
    ]
    for load in loads:
        load.start()
    length, first = scal[0], scal[1]
    step = 256
    rows = 64

    for t in range(halves):
        for z in range(slabs):
            at = z * 2 * HD
            att_t[at : at + HD, :] = mix_a[z, t]
            att_t[at + HD : at + 2 * HD, :] = mix_b[z, t]
        acts[t, :, base:lanes] = att_t[...].astype(F32).T.astype(BF)
    for k in range(halves):
        loads[k].wait()

    def project(n, _):
        cut = pl.ds(pl.multiple_of(n * step, step), step)
        total = own[:, cut].astype(F32)
        for t in range(halves):
            total = total + mm(acts[t, :, base:lanes], w[t, cut, base:lanes], NT)
        mid[:, cut] = total
        return 0

    lax.fori_loop(0, width // step, project, 0)

    def row_mask(r):
        pos = first + r * rows + lax.broadcasted_iota(jnp.int32, (rows, 1), 0)
        return jnp.where(pos < length, 1.0, 0.0)

    def norm(r, _):
        cut = pl.ds(pl.multiple_of(r * rows, rows), rows)
        values = mid[cut, :]
        inverse = lax.rsqrt(jnp.mean(values * values, axis=1, keepdims=True) + EPSILON)
        scale[cut, :] = jnp.broadcast_to(inverse, (rows, 128))
        normed_ref[cut, :] = (values * inverse * gain[...]).astype(BF)
        branch_ref[cut, :] = (cot[cut, :].astype(F32) * row_mask(r)).astype(BF)
        return 0

    lax.fori_loop(0, half // rows, norm, 0)

    for t in range(halves):
        for k in range(3):
            loads[halves + 3 * t + k].wait()

        def columns(at, n):
            def cut(k):
                return pl.ds(pl.multiple_of(k * ff + at, 128), n)

            gate = mm(normed_ref[...], w[t, :, cut(0)], NN)
            upward = mm(normed_ref[...], w[t, :, cut(1)], NN)
            d_hidden = mm(branch_ref[...], w[t, :, cut(2)], NN)
            sig = 1.0 / (1.0 + jnp.exp(-gate))
            active = gate * sig
            acts[t, :, cut(2)] = (active * upward).astype(BF)
            acts[t, :, cut(0)] = (
                d_hidden * upward * sig * (1.0 + gate * (1.0 - sig))
            ).astype(BF)
            acts[t, :, cut(1)] = (d_hidden * active).astype(BF)

        def chunk(c, _):
            columns(c * step, step)
            return 0

        lax.fori_loop(0, ff // step, chunk, 0)
        if ff % step:
            columns(ff - ff % step, ff % step)

    def back(n, _):
        cut = pl.ds(pl.multiple_of(n * step, step), step)
        total = mid[:, cut]
        grad = jnp.zeros((half, step), F32)
        for t in range(halves):
            total = total + mm(acts[t, :, 2 * ff : base], w[t, cut, 2 * ff : base], NT)
            grad = grad + mm(acts[t, :, 0:ff], w[t, cut, 0:ff], NT)
            grad = grad + mm(acts[t, :, ff : 2 * ff], w[t, cut, ff : 2 * ff], NT)
        dmid_ref[:, cut] = total
        dn[:, cut] = grad
        return 0

    lax.fori_loop(0, width // step, back, 0)

    def finish(r, _):
        cut = pl.ds(pl.multiple_of(r * rows, rows), rows)
        mask = row_mask(r)
        out_ref[cut, :] = (dmid_ref[cut, :] * mask).astype(BF)
        inverse = scale[cut, 0:1]
        scaled = mid[cut, :] * inverse
        d_scaled = dn[cut, :] * gain[...]
        mean = jnp.mean(d_scaled * scaled, axis=1, keepdims=True)
        total = cot[cut, :].astype(F32) * mask + inverse * (d_scaled - scaled * mean)
        dmid_ref[cut, :] = total
        dattn_ref[cut, :] = total.astype(BF)
        return 0

    lax.fori_loop(0, half // rows, finish, 0)
    for t in range(halves):
        for z in range(0, slabs, 2):
            at = base + z * 2 * HD
            grad = mm(dattn_ref[...], w[t, :, at : at + 4 * HD], NN).T.astype(BF)
            for k in range(2):
                do_a[z + k, t] = grad[2 * k * HD : (2 * k + 1) * HD]
                do_b[z + k, t] = grad[(2 * k + 1) * HD : (2 * k + 2) * HD]

    pl.semaphore_wait(barrier, len(peers))
    moves = []
    for k, (dz, dt) in enumerate(peers):
        z, t = peer(dz, dt)
        for h, (source, target) in enumerate(((do_a, got_a), (do_b, got_b))):
            move = pltpu.make_async_remote_copy(
                src_ref=source.at[z, t],
                dst_ref=target.at[here, line],
                send_sem=send_sems.at[2 * k + h],
                recv_sem=recv_sems.at[2 * k + h],
                device_id={"ctx": z, "tp": t},
                device_id_type=pl.DeviceIdType.MESH,
            )
            move.start()
            moves.append(move)
    for h, (source, target) in enumerate(((do_a, got_a), (do_b, got_b))):
        move = pltpu.make_async_copy(
            source.at[here, line], target.at[here, line], local_sems.at[h]
        )
        move.start()
        moves.append(move)

    regions = ((0, 2 * ff), (2 * ff, base), (base, lanes))

    def store(n, t):
        cut = pl.ds(pl.multiple_of(n * step, step), step)
        pltpu.make_async_copy(
            w.at[t, cut, 0:split], grads[0].at[t, cut, :], out_sems.at[n, t, 0]
        ).start()
        if n_out == 3:
            for side in range(2):

                @pl.when(lax.rem(n + core, 2) == 1 - side)
                def _():
                    pltpu.make_async_copy(
                        w.at[t, cut, split:lanes], grads[1 + side].at[t, n // 2], out_sems.at[n, t, 1]
                    ).start()

    def gradient(n, _):
        cut = pl.ds(pl.multiple_of(n * step, step), step)
        for k, ref in enumerate((normed_ref, branch_ref, dattn_ref)):
            turned[k] = ref[:, cut].astype(F32).T.astype(BF)
        for t in range(halves):
            for k, (at, end) in enumerate(regions):
                for b, m in widths(end - at, 1024):
                    value = mm(turned[k], acts[t, :, at + b : at + b + m], NN)
                    w[t, cut, at + b : at + b + m] = value.astype(BF)
            store(n, t)
        return 0

    lax.fori_loop(0, width // step, gradient, 0)

    def settle(n, _):
        cut = pl.ds(pl.multiple_of(n * step, step), step)
        for t in range(halves):
            pltpu.make_async_copy(
                w.at[t, cut, 0:split], grads[0].at[t, cut, :], out_sems.at[n, t, 0]
            ).wait()
            if n_out == 3:
                pltpu.make_async_copy(
                    w.at[t, cut, split:lanes], grads[1].at[t, n // 2], out_sems.at[n, t, 1]
                ).wait()
        return 0

    lax.fori_loop(0, width // step, settle, 0)
    for move in moves:
        move.wait()


def middle_stage(scalars, mix_a, mix_b, own, cot, gain, w, split):
    halves, width, lanes = w.shape
    slabs, _, _, half = mix_a.shape
    ff = (lanes - width // halves) // 3
    blocks = width // 256
    peers = slabs * halves - 1
    vmem = pl.BlockSpec(memory_space=pltpu.VMEM)
    outside = pl.BlockSpec(memory_space=pl.ANY)
    out_shape = [
        jax.ShapeDtypeStruct((half, width), BF),
        jax.ShapeDtypeStruct((half, width), F32),
        jax.ShapeDtypeStruct(mix_a.shape, BF),
        jax.ShapeDtypeStruct(mix_a.shape, BF),
        jax.ShapeDtypeStruct((halves, width, split), BF),
    ]
    out_specs = [vmem] * 4 + [outside]
    if split < lanes:
        out_shape += [jax.ShapeDtypeStruct((halves, blocks // 2, 256, lanes - split), BF)] * 2
        out_specs += [outside] * 2
    flops = 2 * half * width * (9 * ff * halves + 3 * width)
    return pl.pallas_call(
        functools.partial(middle_kernel, ff, split),
        out_shape=out_shape,
        in_specs=[pl.BlockSpec(memory_space=pltpu.SMEM)] + [vmem] * 5 + [outside],
        out_specs=out_specs,
        scratch_shapes=[
            pltpu.VMEM((halves, width, lanes), BF),
            pltpu.VMEM((halves, half, lanes), BF),
            pltpu.VMEM((width // halves, half), BF),
            pltpu.VMEM((half, width), F32),
            pltpu.VMEM((half, 128), F32),
            pltpu.VMEM((half, width), F32),
            pltpu.VMEM((half, width), BF),
            pltpu.VMEM((half, width), BF),
            pltpu.VMEM((half, width), BF),
            pltpu.VMEM((3, 256, half), BF),
            pltpu.VMEM(mix_a.shape, BF),
            pltpu.VMEM(mix_a.shape, BF),
            pltpu.SemaphoreType.DMA((4 * halves,)),
            pltpu.SemaphoreType.DMA((blocks, halves, 2)),
            pltpu.SemaphoreType.DMA((2 * peers,)),
            pltpu.SemaphoreType.DMA((2 * peers,)),
            pltpu.SemaphoreType.DMA((2,)),
        ],
        compiler_params=pltpu.CompilerParams(
            vmem_limit_bytes=58 << 20, collective_id=1, has_side_effects=True
        ),
        cost_estimate=pl.CostEstimate(
            flops=flops, bytes_accessed=4 * w.size + 16 * half * width, transcendentals=half * lanes
        ),
    )(scalars, mix_a, mix_b, own, cot, gain, w)


class LineSum:
    def __init__(self, source, held, slots, out, sems):
        self.source, self.held, self.slots, self.out = source, held, slots, out
        self.sum_send, self.sum_recv, self.out_send, self.out_recv = sems
        here = lax.axis_index("ctx")
        self.low = here < 2
        self.place = jnp.where(self.low, here, 3 - here)
        self.inward = jnp.where(self.low, here + 1, here - 1)
        self.outward = jnp.where(self.low, here - 1, here + 1)
        self.size = out.shape[0] // 4

    def number(self, part):
        return jnp.where(self.low, part, 3 - part)

    def part(self, ref, part):
        at = pl.multiple_of(self.number(part) * self.size, self.size)
        return ref.at[pl.ds(at, self.size), :]

    def read(self, ref, part):
        at = pl.multiple_of(self.number(part) * self.size, self.size)
        return ref[pl.ds(at, self.size), :].astype(F32)

    def write(self, ref, part, value):
        at = pl.multiple_of(self.number(part) * self.size, self.size)
        ref[pl.ds(at, self.size), :] = value.astype(BF)

    def copy(self, source, target, send, recv, place):
        return pltpu.make_async_remote_copy(
            src_ref=source, dst_ref=target, send_sem=send, recv_sem=recv,
            device_id={"ctx": place}, device_id_type=pl.DeviceIdType.MESH,
        )

    def took(self, slot):
        ref = self.slots.at[slot]
        self.copy(ref, ref, self.sum_send.at[0], self.sum_recv.at[slot], self.inward).wait_recv()
        return self.slots[slot].astype(F32)

    def begin(self):
        @pl.when(self.place == 0)
        def _():
            for k in range(3):
                self.copy(
                    self.part(self.source, 3 - k), self.slots.at[k],
                    self.sum_send.at[k], self.sum_recv.at[k], self.inward,
                ).start()

    def first(self, k):
        @pl.when(self.place == 1)
        def _():
            self.write(self.held, 3 - k, self.read(self.source, 3 - k) + self.took(k))
            self.copy(
                self.part(self.held, 3 - k), self.slots.at[3 + k],
                self.sum_send.at[k], self.sum_recv.at[3 + k], self.inward,
            ).start()

    def second(self):
        @pl.when(self.place == 1)
        def _():
            self.write(self.held, 0, self.read(self.source, 0) + self.took(3))
            self.copy(
                self.part(self.held, 0), self.slots.at[3],
                self.sum_send.at[2], self.sum_recv.at[3], self.outward,
            ).start()

    def give(self, part, send, place):
        ref = self.part(self.out, part)
        return self.copy(
            ref, ref, self.out_send.at[send], self.out_recv.at[self.number(part)], place
        )

    def final(self):
        @pl.when(self.place == 1)
        def _():
            self.write(self.out, 1, self.read(self.source, 1) + self.took(2) + self.took(4))
            self.give(1, 0, self.inward).start()
            self.give(1, 1, self.outward).start()

        @pl.when(self.place == 0)
        def _():
            self.write(self.out, 0, self.read(self.source, 0) + self.took(3))
            self.give(0, 0, self.inward).start()

    def forward(self):
        @pl.when(self.place == 1)
        def _():
            for k, (part, place) in enumerate(((0, self.inward), (2, self.outward), (3, self.outward))):
                self.give(part, 2 + k, place).wait_recv()
                self.give(part, 2 + k, place).start()

    def end(self):
        for k in range(3):
            self.copy(
                self.slots.at[0], self.slots.at[0],
                self.sum_send.at[k], self.sum_recv.at[0], self.inward,
            ).wait_send()

        @pl.when(self.place == 0)
        def _():
            self.give(0, 0, self.inward).wait_send()
            for part in (1, 2, 3):
                self.give(part, 0, self.inward).wait_recv()

        @pl.when(self.place == 1)
        def _():
            for k in range(5):
                self.give(1, k, self.inward).wait_send()


def tail_kernel(
    back_a, back_b, some, low, high, normed, weights, own, gain, dmid,
    grad_out, some_out, rest_out, qa_out, qb_out,
    got_b, turned, swapped, rest, some_held, some_slots, rest_held, rest_slots,
    local, crossed, column_sum, columned, q_src, q_held, q_slots, theirs, got_theirs, mine,
    in_send, in_recv, in_local, swap_send, swap_recv, core_send, core_recv, col_send, col_recv,
    row_send, row_recv, out_send, out_recv, *line_sems,
):
    here, line, place = lax.axis_index("ctx"), lax.axis_index("tp"), lax.axis_index("fsdp")
    core, column = lax.rem(place, 2), place // 2
    sibling = {"fsdp": place + 1 - 2 * core}
    beside = {"fsdp": lax.rem(place + 2, 4)}
    across = {"tp": 1 - line}
    others = [{"ctx": lax.rem(here + k, 4)} for k in range(1, 4)]
    mesh_id = pl.DeviceIdType.MESH
    barrier = pltpu.get_barrier_semaphore()
    for device in (*others, sibling, beside, across):
        pl.semaphore_signal(barrier, inc=1, device_id=device, device_id_type=mesh_id)
    pl.semaphore_wait(barrier, 6)

    def remote(source, target, send, recv, device):
        return pltpu.make_async_remote_copy(
            src_ref=source, dst_ref=target, send_sem=send, recv_sem=recv,
            device_id=device, device_id_type=mesh_id,
        )

    block = back_a.shape[0] // 4
    rows = normed.shape[0]
    half = rows // 2
    depth = 256

    def window(ref, at):
        return ref.at[pl.ds(pl.multiple_of(at * block, block), block), :]

    sent_in = [
        remote(
            window(back_b, device["ctx"]), window(got_b, here), in_send.at[k], in_recv.at[k], device
        )
        for k, device in enumerate(others)
    ]
    for move in sent_in:
        move.start()
    stays = pltpu.make_async_copy(window(back_b, here), window(got_b, here), in_local)
    stays.start()
    swaps = [
        remote(low.at[1 - column], swapped.at[0], swap_send.at[0], swap_recv.at[0], beside),
        remote(high.at[1 - line], swapped.at[1], swap_send.at[1], swap_recv.at[1], across),
    ]
    for move in swaps:
        move.start()
    a, b, qa, qb = (
        LineSum(src, held, slots, out, line_sems[4 * k : 4 * k + 4])
        for k, (src, held, slots, out) in enumerate(
            (
                (some, some_held, some_slots, some_out),
                (rest, rest_held, rest_slots, rest_out),
                (q_src.at[0], q_held.at[0], q_slots.at[0], qa_out),
                (q_src.at[1], q_held.at[1], q_slots.at[1], qb_out),
            )
        )
    )
    a.begin()

    def weight_gradient(h, grads):
        def step(n, _):
            cut = pl.ds(pl.multiple_of(n * depth, depth), depth)
            value = mm(grads[...], normed[:, cut], NN).astype(BF)
            local[h, lax.rem(n, 2), n // 2] = value
            return 0

        lax.fori_loop(0, 4, step, 0)
        move = remote(
            local.at[h, 1 - core], crossed.at[h], core_send.at[h], core_recv.at[h], sibling
        )
        move.start()
        return move

    def column_step(h, move):
        move.wait_recv()
        for x in range(2):
            column_sum[h, x] = (
                local[h, core, x].astype(F32) + crossed[h, x].astype(F32)
            ).astype(BF)
        move = remote(
            column_sum.at[h, 1 - column], columned.at[h], col_send.at[h], col_recv.at[h], beside
        )
        move.start()
        return move

    def column_end(h, move):
        move.wait_recv()
        q_src[h] = (column_sum[h, column].astype(F32) + columned[h].astype(F32)).astype(BF)

    def turn(h, grads):
        for k in range(0, grads.shape[0], 128):
            at = h * grads.shape[0] + k
            turned[:, at : at + 128] = grads[k : k + 128, :].astype(F32).T.astype(BF)

    core_a = weight_gradient(0, back_a)
    a.first(0)
    turn(0, back_a)
    for move in swaps:
        move.wait_recv()
    quarter = low.shape[1]
    rest[0:quarter] = (low[column].astype(F32) + swapped[0].astype(F32)).astype(BF)
    rest[quarter : 2 * quarter] = (high[line].astype(F32) + swapped[1].astype(F32)).astype(BF)
    b.begin()
    a.first(1)
    col_a = column_step(0, core_a)
    a.second()
    stays.wait()
    for move in sent_in:
        move.wait_recv()
    turn(1, got_b)

    pieces = 2
    piece = half // pieces
    sent_rows = []
    for k in range(pieces):
        cut = slice(k * piece, (k + 1) * piece)
        start = pl.multiple_of((1 - line) * half + k * piece, piece)

        def make(n, _):
            wide = pl.ds(pl.multiple_of(n * depth, depth), depth)
            value = mm(turned[pl.ds(start, piece), :], weights[:, wide], NN)
            theirs[cut, wide] = value.astype(BF)
            return 0

        lax.fori_loop(0, 4, make, 0)
        move = remote(theirs.at[cut], got_theirs.at[cut], row_send.at[k], row_recv.at[k], across)
        move.start()
        sent_rows.append(move)
    b.first(0)
    core_b = weight_gradient(1, got_b)
    a.final()
    mine_start = pl.multiple_of(line * half, half)

    def make_mine(n, _):
        wide = pl.ds(pl.multiple_of(n * depth, depth), depth)
        mine[:, wide] = mm(turned[pl.ds(mine_start, half), :], weights[:, wide], NN)
        return 0

    lax.fori_loop(0, 4, make_mine, 0)
    b.first(1)
    column_end(0, col_a)
    qa.begin()
    col_b = column_step(1, core_b)
    sent_out = []
    small = 64
    for k in range(pieces):
        sent_rows[k].wait_recv()

        def back(r, _):
            at = pl.multiple_of(k * piece + r * small, small)
            cut = pl.ds(at, small)
            values = own[cut, :].astype(F32)
            inverse = lax.rsqrt(jnp.mean(values * values, axis=1, keepdims=True) + EPSILON)
            scaled = values * inverse
            d_scaled = (mine[cut, :] + got_theirs[cut, :].astype(F32)) * gain[...]
            mean = jnp.mean(d_scaled * scaled, axis=1, keepdims=True)
            total = dmid[cut, :] + inverse * (d_scaled - scaled * mean)
            grad_out[pl.ds(pl.multiple_of(line * half + at, small), small), :] = total.astype(BF)
            return 0

        lax.fori_loop(0, piece // small, back, 0)
        ref = grad_out.at[pl.ds(pl.multiple_of(line * half + k * piece, piece), piece), :]
        move = remote(ref, ref, out_send.at[k], out_recv.at[k], across)
        move.start()
        sent_out.append(move)
    b.second()
    column_end(1, col_b)
    qb.begin()
    a.forward()
    b.final()
    qa.first(0)
    qa.first(1)
    qb.first(0)
    qb.first(1)
    qa.second()
    qb.second()
    b.forward()
    qa.final()
    qb.final()
    qa.forward()
    qb.forward()
    for run in (a, b, qa, qb):
        run.end()
    for move in (*sent_in, *swaps, core_a, core_b, col_a, col_b, *sent_rows):
        move.wait_send()
    for k, move in enumerate(sent_out):
        move.wait_send()
        ref = grad_out.at[pl.ds(pl.multiple_of((1 - line) * half + k * piece, piece), piece), :]
        remote(ref, ref, out_send.at[k], out_recv.at[k], across).wait_recv()


def tail_stage(back_a, back_b, some, low, high, normed, weights, own, gain, dmid):
    rows, width = normed.shape
    half = rows // 2
    lanes_a, lanes_b = some.shape[1], low.shape[2]
    wide = back_a.shape[0]
    vmem = pl.BlockSpec(memory_space=pltpu.VMEM)
    dma = pltpu.SemaphoreType.DMA
    return pl.pallas_call(
        tail_kernel,
        out_shape=(
            jax.ShapeDtypeStruct((rows, width), BF),
            jax.ShapeDtypeStruct((256, lanes_a), BF),
            jax.ShapeDtypeStruct((256, lanes_b), BF),
            jax.ShapeDtypeStruct((wide, 256), BF),
            jax.ShapeDtypeStruct((wide, 256), BF),
        ),
        in_specs=[vmem] * 10,
        out_specs=(vmem,) * 5,
        scratch_shapes=[
            pltpu.VMEM((wide, rows), BF),
            pltpu.VMEM((rows, 2 * wide), BF),
            pltpu.VMEM((2, 128, lanes_b), BF),
            pltpu.VMEM((256, lanes_b), BF),
            pltpu.VMEM((256, lanes_a), BF),
            pltpu.VMEM((5, 64, lanes_a), BF),
            pltpu.VMEM((256, lanes_b), BF),
            pltpu.VMEM((5, 64, lanes_b), BF),
            pltpu.VMEM((2, 2, 2, wide, 256), BF),
            pltpu.VMEM((2, 2, wide, 256), BF),
            pltpu.VMEM((2, 2, wide, 256), BF),
            pltpu.VMEM((2, wide, 256), BF),
            pltpu.VMEM((2, wide, 256), BF),
            pltpu.VMEM((2, wide, 256), BF),
            pltpu.VMEM((2, 5, wide // 4, 256), BF),
            pltpu.VMEM((half, width), BF),
            pltpu.VMEM((half, width), BF),
            pltpu.VMEM((half, width), F32),
            dma((3,)), dma((3,)), dma,
            dma((2,)), dma((2,)), dma((2,)), dma((2,)), dma((2,)), dma((2,)),
            dma((2,)), dma((2,)), dma((2,)), dma((2,)),
        ]
        + [dma((3,)), dma((5,)), dma((5,)), dma((4,))] * 4,
        compiler_params=pltpu.CompilerParams(
            vmem_limit_bytes=56 << 20, collective_id=2, has_side_effects=True
        ),
        cost_estimate=pl.CostEstimate(
            flops=8 * rows * width * wide, bytes_accessed=40 << 20, transcendentals=0
        ),
    )(back_a, back_b, some, low, high, normed, weights, own, gain, dmid)


def normalize(values, gain):
    inverse = lax.rsqrt(jnp.mean(values * values, axis=-1, keepdims=True) + EPSILON)
    scaled = values * inverse
    return scaled, inverse, (scaled * gain).astype(BF)


def norm_back(d_normed, scaled, inverse, gain):
    d_scaled = d_normed * gain
    d_values = inverse * (d_scaled - scaled * jnp.mean(d_scaled * scaled, axis=-1, keepdims=True))
    return d_values


def rows_first(values):
    return with_layout_constraint(values, Layout(major_to_minor=tuple(range(values.ndim))))


def swap(values, axis, bit):
    count = lax.axis_size(axis)
    return lax.ppermute(values, axis, [(k, k ^ bit) for k in range(count)])


def plus(left, right):
    return (left.astype(F32) + right.astype(F32)).astype(BF)


def pick(values, index, axis):
    return lax.dynamic_index_in_dim(values, index, axis, keepdims=False)


def both_halves(values):
    half = values.shape[0]
    side = lax.axis_index("tp") * half
    whole = jnp.zeros((2 * half,) + values.shape[1:], values.dtype)
    whole = lax.dynamic_update_slice_in_dim(whole, values, side, 0)
    return lax.dynamic_update_slice_in_dim(whole, swap(values, "tp", 1), half - side, 0)


def sum_blocks(values):
    slabs = lax.axis_size("ctx")
    cut = values.reshape((slabs, values.shape[0] // slabs) + values.shape[1:])
    cut = lax.all_to_all(cut, "ctx", 0, 0, tiled=True)
    total = jnp.sum(cut.astype(F32), axis=0).astype(BF)
    total = lax.all_to_all(
        jnp.broadcast_to(total[None], (slabs,) + total.shape), "ctx", 0, 0, tiled=True
    )
    return total.reshape(values.shape)


def shards(
    inputs,
    lengths,
    first_gain,
    query_weight,
    key_weight,
    value_weight,
    out_weight,
    second_gain,
    gate_weight,
    up_weight,
    down_weight,
    cotangent,
):
    slabs, halves, parts = lax.axis_size("ctx"), lax.axis_size("tp"), lax.axis_size("fsdp")
    rows, width = inputs.shape[1], inputs.shape[2]
    depth = query_weight.shape[0]
    group = query_weight.shape[1] // HD // slabs
    half = rows // halves
    ff = gate_weight.shape[1]
    everywhere = ("tp", "fsdp")
    side = lax.axis_index("tp") * half

    paired = parts == 4 and halves == 2 and slabs == 4 and group == 2
    w_rest = jnp.concatenate([gate_weight, up_weight, down_weight.T, out_weight.T], axis=1)
    w_rest = rows_first(lax.all_gather(rows_first(w_rest), everywhere, axis=0, tiled=True))
    w_rest = w_rest.reshape(halves, width, -1)
    qkv_width = slabs * 3 * HD

    if paired:
        gains = jnp.stack([first_gain.astype(F32), second_gain.astype(F32)])
        gains = jnp.concatenate([gains, jnp.zeros((6, depth), F32)])
        w_turned, normed_one, gains, *rest = front_stage(
            lengths, inputs[0], gains, query_weight, key_weight, value_weight, slabs, halves
        )
        gain_one, gain_two = gains[0], gains[1]
        qkv, arrived = rest[0:2], rest[2:4]
        saved = [(rest[4], rest[6]), (rest[5], rest[7])]
    else:
        gains = lax.all_gather(jnp.stack([first_gain, second_gain]), "fsdp", axis=1, tiled=True)
        gain_one, gain_two = gains[0].astype(F32), gains[1].astype(F32)
        stacked = jnp.stack(
            [w.reshape(depth, slabs, group, HD) for w in (query_weight, key_weight, value_weight)]
        ).transpose(1, 3, 2, 0, 4)
        w_qkv = lax.all_gather(
            stacked.reshape(depth, group * qkv_width), "fsdp", axis=0, tiled=True
        )
        w_heads = [w_qkv[:, h * qkv_width : (h + 1) * qkv_width] for h in range(group)]
        _, _, normed_one = normalize(inputs[0].astype(F32), gain_one)
        qkv = []
        for h in range(group):
            part = mm(w_heads[h], normed_one, (((0,), (1,)), ((), ()))).astype(BF)
            part = part.reshape(slabs, 3 * HD, rows)
            qkv.append(lax.all_to_all(part, "ctx", 0, 0, tiled=True))
        arrived, saved = [], []
        for h in range(group):
            mix, mix_full, lse = attend(lengths, qkv[h], halves, rows)
            saved.append((mix_full, lse))
            mix = mix.reshape(slabs * halves, HD, half)
            mix = lax.all_to_all(mix, ("ctx", "tp"), 0, 0, tiled=True)
            arrived.append(mix.reshape(slabs, halves, HD, half))

    own = lax.dynamic_slice_in_dim(inputs[0], side, half, 0)
    cot = lax.dynamic_slice_in_dim(cotangent[0], side, half, 0)
    scalars = jnp.stack([lengths[0], lax.axis_index("ctx") * rows + side])
    split = 2432 if paired else w_rest.shape[2]
    output, d_middle, *d_mix, = middle_stage(
        scalars, *arrived, own, cot, gain_two[None], w_rest, split
    )
    d_mix, (g_some, *g_rest) = d_mix[:2], d_mix[2:]
    output = both_halves(output)
    s_some = lax.psum_scatter(
        rows_first(g_some.reshape(halves * width, -1)), everywhere, scatter_dimension=0, tiled=True
    )
    s_some = rows_first(s_some)

    core, column, line = (
        lax.rem(lax.axis_index("fsdp"), 2),
        lax.axis_index("fsdp") // 2,
        lax.axis_index("tp"),
    )
    d_local = [None] * group
    d_local[0] = attend_back(lengths, qkv[0], d_mix[0], *saved[0], 1024)
    if paired:
        got = swap(g_rest[0], "fsdp", 1)
        got, d_local[0] = lax.optimization_barrier((got, d_local[0]))
        total = plus(g_rest[1], got)
        cut = total.shape[2] // 2
        low, high = total[:, :, :cut], total[:, :, cut:]
        low_out, high_out = pick(low, 1 - line, 0), pick(high, 1 - column, 1)
        low, high = pick(low, line, 0), pick(high, column, 1)
        d_mix[1], low_out, high_out, low, high = lax.optimization_barrier(
            (d_mix[1], low_out, high_out, low, high)
        )
    for h in range(1, group):
        d_local[h] = attend_back(lengths, qkv[h], d_mix[h], *saved[h], 1024)
    normed_rows = own.astype(F32)
    if paired:
        back_a = lax.all_to_all(d_local[0], "ctx", 0, 0, tiled=True).reshape(qkv_width, rows)
        got_low, got_high = swap(low_out, "tp", 1), swap(high_out, "fsdp", 2)
        got_low, got_high, back_a, d_local[1] = lax.optimization_barrier(
            (got_low, got_high, back_a, d_local[1])
        )
        input_gradient, s_some, s_rest, *q_grads = tail_stage(
            back_a, d_local[1].reshape(qkv_width, rows), s_some, plus(low, got_low),
            plus(high, got_high), normed_one, w_turned, own, gain_one[None], d_middle,
        )
        s_all = jnp.concatenate([s_some, s_rest], axis=1).astype(F32)
        s_qkv = jnp.stack([q.reshape(slabs, 3, HD, depth) for q in q_grads], axis=1)
        s_qkv = s_qkv.transpose(2, 4, 0, 1, 3).reshape(3, depth, slabs * group * HD).astype(F32)
    else:
        d_qkv = [
            lax.all_to_all(d, "ctx", 0, 0, tiled=True).reshape(qkv_width, rows) for d in d_local
        ]
        d_normed_one = jnp.zeros((rows, width), F32)
        s_qkv = []
        for h in range(group):
            d_normed_one = d_normed_one + mm(d_qkv[h], w_heads[h], (((0,), (1,)), ((), ())))
            grad = mm(normed_one, d_qkv[h], (((0,), (1,)), ((), ()))).astype(BF)
            grad = lax.psum_scatter(grad, "fsdp", scatter_dimension=0, tiled=True)
            s_qkv.append(lax.psum(grad, "ctx").reshape(depth, slabs, 3, HD))
        d_normed_one = lax.psum_scatter(d_normed_one, "tp", scatter_dimension=0, tiled=True)
        scaled_one, inverse_one, _ = normalize(normed_rows, gain_one)
        d_from_one = norm_back(d_normed_one, scaled_one, inverse_one, gain_one)
        input_gradient = lax.all_gather(
            (d_middle + d_from_one).astype(BF), "tp", axis=0, tiled=True
        )
        s_qkv = jnp.stack(s_qkv, axis=2).transpose(3, 0, 1, 2, 4)
        s_qkv = s_qkv.reshape(3, depth, slabs * group * HD).astype(F32)
        s_all = lax.psum(s_some, "ctx").astype(F32)

    d_gain_one = sum(
        jnp.sum(w.astype(F32) * s, axis=1)
        for w, s in zip((query_weight, key_weight, value_weight), s_qkv)
    ) / first_gain.astype(F32)
    d_gain_two = (
        jnp.sum(gate_weight.astype(F32) * s_all[:, :ff], axis=1)
        + jnp.sum(up_weight.astype(F32) * s_all[:, ff : 2 * ff], axis=1)
    ) / second_gain.astype(F32)
    d_gains = jnp.stack([d_gain_one, d_gain_two])
    d_gains = d_gains + swap(d_gains, "tp", 1) if paired else lax.psum(d_gains, "tp")
    return (
        output[None],
        input_gradient[None],
        d_gains[0],
        s_qkv[0],
        s_qkv[1],
        s_qkv[2],
        s_all[:, 3 * ff :].T,
        d_gains[1],
        s_all[:, :ff],
        s_all[:, ff : 2 * ff],
        s_all[:, 2 * ff : 3 * ff].T,
    )


def solution(mesh):
    rows = P("fsdp", "ctx", None)
    gain = P("fsdp")
    inward = P("fsdp", "tp")
    outward = P("tp", "fsdp")
    return jax.shard_map(
        shards,
        mesh=mesh,
        in_specs=(
            rows, gain, gain, inward, inward, inward, outward, gain, inward, inward, outward, rows,
        ),
        out_specs=(
            rows, rows, gain, inward, inward, inward, outward, gain, inward, inward, outward,
        ),
        check_vma=False,
    )
```

```python
import functools

import jax
import jax.numpy as jnp
from jax import lax
from jax.experimental import pallas as pl
from jax.experimental.pallas import tpu as pltpu
from jax.experimental.layout import Layout, with_layout_constraint
from jax.sharding import PartitionSpec as P

HD = 64
EPSILON = 1e-05
MASKED = -1000000000.0
NN = (((1,), (0,)), ((), ()))
NT = (((1,), (1,)), ((), ()))
TN = (((0,), (0,)), ((), ()))
BF = jnp.bfloat16
F32 = jnp.float32


def mm(left, right, dims):
    return lax.dot_general(left, right, dims, preferred_element_type=F32)


def spread_keys(keys, start, length):
    rows = keys.shape[0]
    pos = start + lax.broadcasted_iota(jnp.int32, (rows, HD), 0)
    lane = lax.broadcasted_iota(jnp.int32, (rows, HD), 1)
    bias = jnp.where((lane == 0) & (pos >= length), MASKED, 0.0)
    return jnp.concatenate([keys, bias], axis=1).astype(BF)


def spread_queries(queries):
    row = lax.broadcasted_iota(jnp.int32, queries.shape, 0)
    ones = jnp.where(row == 0, 1.0, 0.0)
    return jnp.concatenate([queries * HD**-0.5, ones], axis=0).astype(BF)


def attend_rows(tile, length, qkv, kx, qx, vx, emit):
    slabs, _, rows = qkv.shape
    per = rows // tile
    blocks = slabs * per
    for z in range(slabs):
        keys = qkv[z, HD : 2 * HD, :].astype(F32).T
        kx[z * rows : (z + 1) * rows, :] = spread_keys(keys, z * rows, length)
        queries = spread_queries(qkv[z, 0:HD, :].astype(F32))
        for b in range(per):
            cut = slice(b * tile, (b + 1) * tile)
            qx[z * per + b] = queries[:, cut]
            vx[z * per + b] = qkv[z, 2 * HD : 3 * HD, cut]
    later = lax.broadcasted_iota(jnp.int32, (tile, tile), 0) > lax.broadcasted_iota(
        jnp.int32, (tile, tile), 1
    )

    def query_block(i, _):
        queries = qx[i]

        def step(j, carry, masked):
            highest, total, mix = carry
            keys = kx[pl.ds(pl.multiple_of(j * tile, tile), tile), :]
            scores = mm(keys, queries, NN)
            if masked:
                scores = jnp.where(later, MASKED, scores)
            new = jnp.maximum(highest, jnp.max(scores, axis=0, keepdims=True))
            scale = jnp.exp(highest - new)
            probs = jnp.exp(scores - new)
            total = total * scale + jnp.sum(probs, axis=0, keepdims=True)
            mix = mix * scale + mm(vx[j], probs.astype(BF), NN)
            return new, total, mix

        first = (
            jnp.full((1, tile), -jnp.inf, F32),
            jnp.zeros((1, tile), F32),
            jnp.zeros((HD, tile), F32),
        )
        carry = lax.fori_loop(0, i, lambda j, c: step(j, c, False), first)
        highest, total, mix = step(i, carry, True)
        emit(i, mix / total, highest + jnp.log(total))
        return 0

    lax.fori_loop(0, blocks, query_block, 0)


def attend_kernel(tile, len_ref, qkv, o_ref, of_ref, lse_ref, kx, qx, vx):
    rows = qkv.shape[2]
    halves = o_ref.shape[1]
    half = rows // halves

    def emit(i, mix, lse):
        of_ref[i] = mix
        lse_ref[i] = lse
        for t in range(halves):
            o_ref[i, t] = mix[:, t * half : (t + 1) * half].astype(BF)

    attend_rows(tile, len_ref[0], qkv, kx, qx, vx, emit)


def front_kernel(
    len_ref, x, gains_own, wq, wk, wv,
    wt, normed, gains, qkv_a, qkv_b, mix_a, mix_b, of_a, of_b, lse_a, lse_b,
    packed, parts, mixed, kx, qx, vx,
    gain_send, gain_recv, w_send, w_recv, part_send, part_recv, part_local,
    mix_send, mix_recv, mix_local,
):
    here, line, place = lax.axis_index("ctx"), lax.axis_index("tp"), lax.axis_index("fsdp")
    core, column = lax.rem(place, 2), place // 2
    pair = place + 1 - 2 * core
    other = lax.rem(place + 2, 4)
    mesh_id = pl.DeviceIdType.MESH
    slabs, halves = mix_a.shape[0], mix_a.shape[1]
    rows, width = x.shape
    half = rows // halves
    wide = slabs * 3 * HD
    depth = wq.shape[0]
    peers = [(dz, dt) for dz in range(slabs) for dt in range(halves) if dz or dt]

    def peer(dz, dt):
        return lax.rem(here + dz, slabs), lax.rem(line + dt, halves)

    barrier = pltpu.get_barrier_semaphore()
    for dz, dt in peers:
        z, t = peer(dz, dt)
        pl.semaphore_signal(barrier, inc=1, device_id={"ctx": z, "tp": t}, device_id_type=mesh_id)
    for device in (pair, other):
        pl.semaphore_signal(barrier, inc=1, device_id={"fsdp": device}, device_id_type=mesh_id)
    for q, w in enumerate((wq, wk, wv)):
        flat = w[...].astype(F32).T.astype(BF)
        for z in range(slabs):
            for h in range(2):
                at = (2 * z + h) * HD
                packed[h, (3 * z + q) * HD : (3 * z + q + 1) * HD, :] = flat[at : at + HD]

    def remote(source, target, send, recv, device):
        return pltpu.make_async_remote_copy(
            src_ref=source, dst_ref=target, send_sem=send, recv_sem=recv,
            device_id=device, device_id_type=mesh_id,
        )

    def lanes(index):
        return pl.ds(pl.multiple_of(index * depth, depth), depth)

    def weight(h, index):
        return wt.at[h * wide : (h + 1) * wide, lanes(index)]

    gains[:, lanes(place)] = gains_own[...]
    for h in range(2):
        wt[h * wide : (h + 1) * wide, lanes(place)] = packed[h]
    pl.semaphore_wait(barrier, len(peers) + 2)
    sent = []

    def launch(move):
        move.start()
        sent.append(move)
        return move

    for k, device in enumerate((pair, other)):
        launch(
            remote(
                gains_own, gains.at[:, lanes(place)], gain_send.at[k], gain_recv.at[k], {"fsdp": device}
            )
        )
    for h in range(2):
        for k, device in ((1, other), (0, pair)):
            launch(
                remote(
                    packed.at[h], weight(h, place), w_send.at[h, k], w_recv.at[h, k], {"fsdp": device}
                )
            )

    def arrived(ref, sem):
        remote(ref, ref, gain_send.at[0], sem, {"fsdp": pair}).wait_recv()

    arrived(gains.at[:, lanes(other)], gain_recv.at[1])
    launch(
        remote(
            gains.at[:, lanes(other)], gains.at[:, lanes(other)], gain_send.at[2], gain_recv.at[2],
            {"fsdp": pair},
        )
    )
    far = lax.rem(pair + 2, 4)
    arrived(gains.at[:, lanes(pair)], gain_recv.at[0])
    arrived(gains.at[:, lanes(far)], gain_recv.at[2])
    small = 64

    def norm(r, _):
        cut = pl.ds(pl.multiple_of(r * small, small), small)
        values = x[cut, :].astype(F32)
        inverse = lax.rsqrt(jnp.mean(values * values, axis=1, keepdims=True) + EPSILON)
        normed[cut, :] = (values * inverse * gains[0:1, :]).astype(BF)
        return 0

    lax.fori_loop(0, rows // small, norm, 0)
    queues = (qkv_a, qkv_b)
    waits = []
    for h in range(2):
        arrived(weight(h, other), w_recv.at[h, 1])
        launch(
            remote(
                weight(h, other), weight(h, other), w_send.at[h, 2], w_recv.at[h, 2], {"fsdp": pair}
            )
        )
    for h in range(2):
        arrived(weight(h, pair), w_recv.at[h, 0])
        arrived(weight(h, far), w_recv.at[h, 2])

        def project(n, _):
            cut = pl.ds(pl.multiple_of(n * 256, 256), 256)
            value = mm(wt[h * wide : (h + 1) * wide, :], normed[cut, :], NT).astype(BF)
            for z in range(slabs):
                parts[h, z, :, cut] = value[z * 3 * HD : (z + 1) * 3 * HD]
            return 0

        lax.fori_loop(0, rows // 256, project, 0)
        for k in range(1, slabs):
            z = lax.rem(here + k, slabs)
            waits.append(
                launch(
                    remote(
                        parts.at[h, z], queues[h].at[here], part_send.at[h, k], part_recv.at[h, k],
                        {"ctx": z},
                    )
                )
            )
        stays = pltpu.make_async_copy(parts.at[h, here], queues[h].at[here], part_local.at[h])
        stays.start()
        waits.append(stays)

    for h, (qkv, mix_ref, of_ref, lse_ref) in enumerate(
        ((qkv_a, mix_a, of_a, lse_a), (qkv_b, mix_b, of_b, lse_b))
    ):
        for move in waits[h * slabs : (h + 1) * slabs - 1]:
            move.wait_recv()
        waits[(h + 1) * slabs - 1].wait()

        def emit(i, mix, lse):
            of_ref[i] = mix
            lse_ref[i] = lse
            for t in range(halves):
                mixed[h, i, t] = mix[:, t * half : (t + 1) * half].astype(BF)
                stay = (i == here) & (line == t)

                @pl.when(stay)
                def _():
                    pltpu.make_async_copy(
                        mixed.at[h, i, t], mix_ref.at[here, line], mix_local.at[h]
                    ).start()

                @pl.when(jnp.logical_not(stay))
                def _():
                    remote(
                        mixed.at[h, i, t], mix_ref.at[here, line], mix_send.at[h, i, t],
                        mix_recv.at[h, here, line], {"ctx": i, "tp": t},
                    ).start()

        attend_rows(rows, len_ref[0], qkv, kx, qx, vx, emit)

    for move in sent:
        move.wait_send()
    for h, mix_ref in enumerate((mix_a, mix_b)):
        pltpu.make_async_copy(mixed.at[h, here, line], mix_ref.at[here, line], mix_local.at[h]).wait()
        for dz, dt in peers:
            z, t = peer(dz, dt)
            remote(
                mixed.at[h, z, t], mix_ref.at[z, t], mix_send.at[h, z, t], mix_recv.at[h, z, t],
                {"ctx": z, "tp": t},
            ).wait()


def front_stage(length, x, gains, wq, wk, wv, slabs, halves):
    rows, width = x.shape
    half = rows // halves
    wide = slabs * 3 * HD
    total = slabs * rows
    work = total * (total + rows) // 2
    vmem = pl.BlockSpec(memory_space=pltpu.VMEM)
    dma = pltpu.SemaphoreType.DMA
    shape = jax.ShapeDtypeStruct
    return pl.pallas_call(
        front_kernel,
        out_shape=(
            shape((2 * wide, width), BF),
            shape((rows, width), BF),
            shape((8, width), F32),
            *[shape((slabs, 3 * HD, rows), BF)] * 2,
            *[shape((slabs, halves, HD, half), BF)] * 2,
            *[shape((slabs, HD, rows), F32)] * 2,
            *[shape((slabs, 1, rows), F32)] * 2,
        ),
        in_specs=[pl.BlockSpec(memory_space=pltpu.SMEM)] + [vmem] * 5,
        out_specs=(vmem,) * 11,
        scratch_shapes=[
            pltpu.VMEM((2, wide, wq.shape[0]), BF),
            pltpu.VMEM((2, slabs, 3 * HD, rows), BF),
            pltpu.VMEM((2, slabs, halves, HD, half), BF),
            pltpu.VMEM((total, 2 * HD), BF),
            pltpu.VMEM((slabs, 2 * HD, rows), BF),
            pltpu.VMEM((slabs, HD, rows), BF),
            dma((3,)), dma((3,)), dma((2, 3)), dma((2, 3)),
            dma((2, slabs)), dma((2, slabs)), dma((2,)),
            dma((2, slabs, halves)), dma((2, slabs, halves)), dma((2,)),
        ],
        compiler_params=pltpu.CompilerParams(
            vmem_limit_bytes=48 << 20, collective_id=3, has_side_effects=True
        ),
        cost_estimate=pl.CostEstimate(
            flops=2 * work * 256 * 4, bytes_accessed=20 << 20, transcendentals=2 * work
        ),
    )(length, x, gains, wq, wk, wv)


def attend(length, qkv, halves, tile):
    slabs, _, rows = qkv.shape
    total = slabs * rows
    tile = min(tile, rows)
    work = total * (total + tile) // 2
    vmem = pl.BlockSpec(memory_space=pltpu.VMEM)
    return pl.pallas_call(
        functools.partial(attend_kernel, tile),
        out_shape=(
            jax.ShapeDtypeStruct((slabs, halves, HD, rows // halves), BF),
            jax.ShapeDtypeStruct((slabs, HD, rows), F32),
            jax.ShapeDtypeStruct((slabs, 1, rows), F32),
        ),
        in_specs=[pl.BlockSpec(memory_space=pltpu.SMEM), vmem],
        out_specs=(vmem, vmem, vmem),
        scratch_shapes=[
            pltpu.VMEM((total, 2 * HD), BF),
            pltpu.VMEM((total // tile, 2 * HD, tile), BF),
            pltpu.VMEM((total // tile, HD, tile), BF),
        ],
        compiler_params=pltpu.CompilerParams(vmem_limit_bytes=40 << 20),
        cost_estimate=pl.CostEstimate(
            flops=work * 256 * 4, bytes_accessed=qkv.size * 4, transcendentals=work
        ),
    )(length, qkv)


def attend_back_rows(tile, length, qkv, do_ref, of_ref, lse_ref, out, scratch, emit):
    kx, qx, vx, kt, dox, dq, st = scratch
    slabs, _, rows = qkv.shape
    halves, half = do_ref.shape[1], do_ref.shape[3]
    per = rows // tile
    blocks = slabs * per
    for z in range(slabs):
        keys = qkv[z, HD : 2 * HD, :]
        kx[z * rows : (z + 1) * rows, :] = spread_keys(keys.astype(F32).T, z * rows, length)
        queries = spread_queries(qkv[z, 0:HD, :].astype(F32))
        values = qkv[z, 2 * HD : 3 * HD, :].astype(F32).T
        vx[z * rows : (z + 1) * rows, :] = jnp.concatenate(
            [values, jnp.zeros((rows, HD), F32)], axis=1
        ).astype(BF)
        d_mix = jnp.concatenate([do_ref[z, t] for t in range(halves)], axis=1)
        delta = jnp.sum(d_mix.astype(F32) * of_ref[z], axis=0, keepdims=True)
        for b in range(per):
            cut = slice(b * tile, (b + 1) * tile)
            n = z * per + b
            qx[n] = queries[:, cut]
            kt[n] = keys[:, cut]
            dox[n, 0:HD] = d_mix[:, cut]
            dox[n, HD : 2 * HD] = jnp.zeros((HD, tile), BF)
            st[n, 0:1] = lse_ref[z, :, cut]
            st[n, 1:2] = delta[:, cut]
    dq[...] = jnp.zeros_like(dq)
    later = lax.broadcasted_iota(jnp.int32, (tile, tile), 0) > lax.broadcasted_iota(
        jnp.int32, (tile, tile), 1
    )

    def key_block(j, _):
        here = pl.ds(pl.multiple_of(j * tile, tile), tile)
        keys = kx[here, :]
        values = vx[here, :]

        def step(i, carry, masked):
            dk, dv = carry
            scores = mm(keys, qx[i], NN)
            if masked:
                scores = jnp.where(later, MASKED, scores)
            probs = jnp.exp(scores - st[i, 0:1])
            d_probs = mm(values, dox[i], NN)
            d_scores = (probs * (d_probs - st[i, 1:2])).astype(BF)
            dv = dv + mm(dox[i, 0:HD], probs.astype(BF), NT)
            dk = dk + mm(qx[i, 0:HD], d_scores, NT)
            dq[i] += mm(kt[j], d_scores, NN)
            return dk, dv

        zero = jnp.zeros((HD, tile), F32)
        carry = step(j, (zero, zero), True)
        dk, dv = lax.fori_loop(j + 1, blocks, lambda i, c: step(i, c, False), carry)
        z = j // per
        cut = pl.ds(pl.multiple_of(lax.rem(j, per) * tile, tile), tile)
        out[z, 0:HD, cut] = (dq[j] * HD**-0.5).astype(BF)
        out[z, HD : 2 * HD, cut] = dk.astype(BF)
        out[z, 2 * HD : 3 * HD, cut] = dv.astype(BF)
        if emit is not None:

            @pl.when(lax.rem(j, per) == per - 1)
            def _():
                emit(z)

        return 0

    lax.fori_loop(0, blocks, key_block, 0)


def attend_back_scratch(slabs, rows, tile):
    total = slabs * rows
    blocks = total // tile
    return [
        pltpu.VMEM((total, 2 * HD), BF),
        pltpu.VMEM((blocks, 2 * HD, tile), BF),
        pltpu.VMEM((total, 2 * HD), BF),
        pltpu.VMEM((blocks, HD, tile), BF),
        pltpu.VMEM((blocks, 2 * HD, tile), BF),
        pltpu.VMEM((blocks, HD, tile), F32),
        pltpu.VMEM((blocks, 8, tile), F32),
    ]


def attend_back_kernel(tile, len_ref, qkv, do_ref, of_ref, lse_ref, out, *scratch):
    attend_back_rows(tile, len_ref[0], qkv, do_ref, of_ref, lse_ref, out, scratch, None)


def back_kernel(
    tile, len_ref, qkv_a, qkv_b, do_a, do_b, of_a, of_b, lse_a, lse_b, keep_hbm, got_hbm,
    out_a, out_b, rest,
    local, keep, got, low_got, high_got, swapped, *refs,
):
    scratch, sems = refs[:7], refs[7:]
    (load_sems, grad_send, grad_recv, grad_local, low_send, low_recv, high_send, high_recv,
     swap_send, swap_recv) = sems
    here, line, place = lax.axis_index("ctx"), lax.axis_index("tp"), lax.axis_index("fsdp")
    column = place // 2
    beside = {"fsdp": lax.rem(place + 2, 4)}
    across = {"tp": 1 - line}
    mesh_id = pl.DeviceIdType.MESH
    slabs, block = qkv_a.shape[0], qkv_a.shape[1]
    loads = [
        pltpu.make_async_copy(source, target, load_sems.at[k])
        for k, (source, target) in enumerate(((keep_hbm, keep), (got_hbm, got)))
    ]
    for load in loads:
        load.start()
    others = [lax.rem(here + k, slabs) for k in range(1, slabs)]
    barrier = pltpu.get_barrier_semaphore()
    for device in (*[{"ctx": z} for z in others], beside, across):
        pl.semaphore_signal(barrier, inc=1, device_id=device, device_id_type=mesh_id)
    pl.semaphore_wait(barrier, slabs + 1)

    def remote(source, target, send, recv, device):
        return pltpu.make_async_remote_copy(
            src_ref=source, dst_ref=target, send_sem=send, recv_sem=recv,
            device_id=device, device_id_type=mesh_id,
        )

    outs = (out_a, out_b)

    def window(h, at):
        return outs[h].at[pl.ds(pl.multiple_of(at * block, block), block), :]

    def attend_head(h, qkv, do_ref, of_ref, lse_ref):
        def emit(z):
            @pl.when(z == here)
            def _():
                pltpu.make_async_copy(
                    local.at[h, z], window(h, here), grad_local.at[h]
                ).start()

            @pl.when(z != here)
            def _():
                remote(
                    local.at[h, z], window(h, here), grad_send.at[h, z], grad_recv.at[h, here],
                    {"ctx": z},
                ).start()

        attend_back_rows(
            tile, len_ref[0], qkv, do_ref, of_ref, lse_ref, local.at[h], scratch, emit
        )

    attend_head(0, qkv_a, do_a, of_a, lse_a)
    for load in loads:
        load.wait()
    cut = rest.shape[0] // 2
    for t in range(2):
        for x in range(2):
            keep[t, x] = (keep[t, x].astype(F32) + got[t, x].astype(F32)).astype(BF)
    moves = []
    for k in range(2):
        moves.append(
            remote(
                keep.at[1 - line, k, 0:cut], low_got.at[k], low_send.at[k], low_recv.at[k], across
            )
        )
        moves.append(
            remote(
                keep.at[k, 1 - column, cut : 2 * cut], high_got.at[k], high_send.at[k],
                high_recv.at[k], beside,
            )
        )
    for move in moves:
        move.start()
    attend_head(1, qkv_b, do_b, of_b, lse_b)
    for move in moves:
        move.wait_recv()
    low, high = slice(0, cut), slice(cut, 2 * cut)
    for k in range(2):
        keep[line, k, low] = (
            keep[line, k, low].astype(F32) + low_got[k].astype(F32)
        ).astype(BF)
        keep[k, column, high] = (
            keep[k, column, high].astype(F32) + high_got[k].astype(F32)
        ).astype(BF)
    swaps = [
        remote(
            keep.at[line, 1 - column, low], swapped.at[0], swap_send.at[0], swap_recv.at[0], beside
        ),
        remote(
            keep.at[1 - line, column, high], swapped.at[1], swap_send.at[1], swap_recv.at[1], across
        ),
    ]
    for move in swaps:
        move.start()
    for move in swaps:
        move.wait_recv()
    for k, part in enumerate((low, high)):
        rest[part] = (
            keep[line, column, part].astype(F32) + swapped[k].astype(F32)
        ).astype(BF)
    for h in range(2):
        pltpu.make_async_copy(local.at[h, here], window(h, here), grad_local.at[h]).wait()
        for z in others:
            remote(
                local.at[h, z], window(h, z), grad_send.at[h, z], grad_recv.at[h, z], {"ctx": z}
            ).wait()
    for move in (*moves, *swaps):
        move.wait_send()


def back_stage(length, qkv, d_mix, saved, keep, got):
    slabs, block, rows = qkv[0].shape
    tile = 512
    lanes = keep.shape[3]
    total = slabs * rows
    work = total * (total + tile) // 2
    vmem = pl.BlockSpec(memory_space=pltpu.VMEM)
    outside = pl.BlockSpec(memory_space=pl.ANY)
    dma = pltpu.SemaphoreType.DMA
    return pl.pallas_call(
        functools.partial(back_kernel, tile),
        out_shape=(
            jax.ShapeDtypeStruct((slabs * block, rows), BF),
            jax.ShapeDtypeStruct((slabs * block, rows), BF),
            jax.ShapeDtypeStruct((256, lanes), BF),
        ),
        in_specs=[pl.BlockSpec(memory_space=pltpu.SMEM)] + [vmem] * 8 + [outside] * 2,
        out_specs=(vmem,) * 3,
        scratch_shapes=[
            pltpu.VMEM((2, slabs, block, rows), BF),
            pltpu.VMEM(keep.shape, BF),
            pltpu.VMEM(keep.shape, BF),
            pltpu.VMEM((2, 128, lanes), BF),
            pltpu.VMEM((2, 128, lanes), BF),
            pltpu.VMEM((2, 128, lanes), BF),
            *attend_back_scratch(slabs, rows, tile),
            dma((2,)), dma((2, slabs)), dma((2, slabs)), dma((2,)),
            dma((2,)), dma((2,)), dma((2,)), dma((2,)), dma((2,)), dma((2,)),
        ],
        compiler_params=pltpu.CompilerParams(
            vmem_limit_bytes=56 << 20, collective_id=4, has_side_effects=True
        ),
        cost_estimate=pl.CostEstimate(
            flops=2 * work * 256 * 10, bytes_accessed=24 << 20, transcendentals=2 * work
        ),
    )(length, *qkv, *d_mix, *[m for m, _ in saved], *[l for _, l in saved], keep, got)


def attend_back(length, qkv, d_mix, mix, lse, tile):
    slabs, _, rows = qkv.shape
    total = slabs * rows
    tile = min(tile, rows)
    work = total * (total + tile) // 2
    vmem = pl.BlockSpec(memory_space=pltpu.VMEM)
    return pl.pallas_call(
        functools.partial(attend_back_kernel, tile),
        out_shape=jax.ShapeDtypeStruct((slabs, 3 * HD, rows), BF),
        in_specs=[pl.BlockSpec(memory_space=pltpu.SMEM), vmem, vmem, vmem, vmem],
        out_specs=vmem,
        scratch_shapes=attend_back_scratch(slabs, rows, tile),
        compiler_params=pltpu.CompilerParams(vmem_limit_bytes=40 << 20),
        cost_estimate=pl.CostEstimate(
            flops=work * 256 * 10, bytes_accessed=qkv.size * 8, transcendentals=work
        ),
    )(length, qkv, d_mix, mix, lse)


def widths(total, step):
    return [(at, min(step, total - at)) for at in range(0, total, step)]


def middle_kernel(
    ff, split, scal, mix_a, mix_b, own, cot, gain, w_hbm,
    out_ref, dmid_ref, got_a, got_b, *refs,
):
    n_out = 3 if split < w_hbm.shape[2] else 1
    grads = refs[:n_out]
    (w, acts, att_t, mid, scale, dn, normed_ref, branch_ref, dattn_ref, turned, do_a, do_b,
     sems, out_sems, send_sems, recv_sems, local_sems, core_send, core_recv) = refs[n_out:]
    slabs, halves, _, half = mix_a.shape
    width = own.shape[1]
    inner = width // halves
    base = 3 * ff
    lanes = base + inner
    here, line = lax.axis_index("ctx"), lax.axis_index("tp")
    core = lax.rem(lax.axis_index("fsdp"), 2)
    sibling = {"fsdp": lax.axis_index("fsdp") + 1 - 2 * core}
    barrier = pltpu.get_barrier_semaphore()
    peers = [(dz, dt) for dz in range(slabs) for dt in range(halves) if dz or dt]

    def peer(dz, dt):
        return lax.rem(here + dz, slabs), lax.rem(line + dt, halves)

    for dz, dt in peers:
        z, t = peer(dz, dt)
        pl.semaphore_signal(
            barrier, inc=1, device_id={"ctx": z, "tp": t}, device_id_type=pl.DeviceIdType.MESH
        )
    if n_out == 3:
        pl.semaphore_signal(
            barrier, inc=1, device_id=sibling, device_id_type=pl.DeviceIdType.MESH
        )
    cuts = [(t, base, inner) for t in range(halves)]
    cuts += [(t, k * ff, ff) for t in range(halves) for k in range(3)]
    loads = [
        pltpu.make_async_copy(
            w_hbm.at[t, :, at : at + n], w.at[t, :, at : at + n], sems.at[k]
        )
        for k, (t, at, n) in enumerate(cuts)
    ]
    for load in loads:
        load.start()
    length, first = scal[0], scal[1]
    step = 256
    rows = 64

    for t in range(halves):
        for z in range(slabs):
            at = z * 2 * HD
            att_t[at : at + HD, :] = mix_a[z, t]
            att_t[at + HD : at + 2 * HD, :] = mix_b[z, t]
        acts[t, :, base:lanes] = att_t[...].astype(F32).T.astype(BF)
    for k in range(halves):
        loads[k].wait()

    def project(n, _):
        cut = pl.ds(pl.multiple_of(n * step, step), step)
        total = own[:, cut].astype(F32)
        for t in range(halves):
            total = total + mm(acts[t, :, base:lanes], w[t, cut, base:lanes], NT)
        mid[:, cut] = total
        return 0

    lax.fori_loop(0, width // step, project, 0)

    def row_mask(r):
        pos = first + r * rows + lax.broadcasted_iota(jnp.int32, (rows, 1), 0)
        return jnp.where(pos < length, 1.0, 0.0)

    def norm(r, _):
        cut = pl.ds(pl.multiple_of(r * rows, rows), rows)
        values = mid[cut, :]
        inverse = lax.rsqrt(jnp.mean(values * values, axis=1, keepdims=True) + EPSILON)
        scale[cut, :] = jnp.broadcast_to(inverse, (rows, 128))
        normed_ref[cut, :] = (values * inverse * gain[...]).astype(BF)
        branch_ref[cut, :] = (cot[cut, :].astype(F32) * row_mask(r)).astype(BF)
        return 0

    lax.fori_loop(0, half // rows, norm, 0)

    for t in range(halves):
        for k in range(3):
            loads[halves + 3 * t + k].wait()

        def columns(at, n):
            def cut(k):
                return pl.ds(pl.multiple_of(k * ff + at, 128), n)

            gate = mm(normed_ref[...], w[t, :, cut(0)], NN)
            upward = mm(normed_ref[...], w[t, :, cut(1)], NN)
            d_hidden = mm(branch_ref[...], w[t, :, cut(2)], NN)
            sig = 1.0 / (1.0 + jnp.exp(-gate))
            active = gate * sig
            acts[t, :, cut(2)] = (active * upward).astype(BF)
            acts[t, :, cut(0)] = (
                d_hidden * upward * sig * (1.0 + gate * (1.0 - sig))
            ).astype(BF)
            acts[t, :, cut(1)] = (d_hidden * active).astype(BF)

        def chunk(c, _):
            columns(c * step, step)
            return 0

        lax.fori_loop(0, ff // step, chunk, 0)
        if ff % step:
            columns(ff - ff % step, ff % step)

    def back(n, _):
        cut = pl.ds(pl.multiple_of(n * step, step), step)
        total = mid[:, cut]
        grad = jnp.zeros((half, step), F32)
        for t in range(halves):
            total = total + mm(acts[t, :, 2 * ff : base], w[t, cut, 2 * ff : base], NT)
            grad = grad + mm(acts[t, :, 0:ff], w[t, cut, 0:ff], NT)
            grad = grad + mm(acts[t, :, ff : 2 * ff], w[t, cut, ff : 2 * ff], NT)
        dmid_ref[:, cut] = total
        dn[:, cut] = grad
        return 0

    lax.fori_loop(0, width // step, back, 0)

    def finish(r, _):
        cut = pl.ds(pl.multiple_of(r * rows, rows), rows)
        mask = row_mask(r)
        out_ref[cut, :] = (dmid_ref[cut, :] * mask).astype(BF)
        inverse = scale[cut, 0:1]
        scaled = mid[cut, :] * inverse
        d_scaled = dn[cut, :] * gain[...]
        mean = jnp.mean(d_scaled * scaled, axis=1, keepdims=True)
        total = cot[cut, :].astype(F32) * mask + inverse * (d_scaled - scaled * mean)
        dmid_ref[cut, :] = total
        dattn_ref[cut, :] = total.astype(BF)
        return 0

    lax.fori_loop(0, half // rows, finish, 0)
    for t in range(halves):
        for z in range(0, slabs, 2):
            at = base + z * 2 * HD
            grad = mm(dattn_ref[...], w[t, :, at : at + 4 * HD], NN).T.astype(BF)
            for k in range(2):
                do_a[z + k, t] = grad[2 * k * HD : (2 * k + 1) * HD]
                do_b[z + k, t] = grad[(2 * k + 1) * HD : (2 * k + 2) * HD]

    pl.semaphore_wait(barrier, len(peers) + (n_out == 3))
    moves = []
    for k, (dz, dt) in enumerate(peers):
        z, t = peer(dz, dt)
        for h, (source, target) in enumerate(((do_a, got_a), (do_b, got_b))):
            move = pltpu.make_async_remote_copy(
                src_ref=source.at[z, t],
                dst_ref=target.at[here, line],
                send_sem=send_sems.at[2 * k + h],
                recv_sem=recv_sems.at[2 * k + h],
                device_id={"ctx": z, "tp": t},
                device_id_type=pl.DeviceIdType.MESH,
            )
            move.start()
            moves.append(move)
    for h, (source, target) in enumerate(((do_a, got_a), (do_b, got_b))):
        move = pltpu.make_async_copy(
            source.at[here, line], target.at[here, line], local_sems.at[h]
        )
        move.start()
        moves.append(move)

    regions = ((0, 2 * ff), (2 * ff, base), (base, lanes))

    def own_copy(n, t):
        cut = pl.ds(pl.multiple_of(n * step, step), step)
        return pltpu.make_async_copy(
            w.at[t, cut, split:lanes], grads[1].at[t, n // 2], out_sems.at[n, t, 1]
        )

    def core_copy(n, t):
        cut = pl.ds(pl.multiple_of(n * step, step), step)
        return pltpu.make_async_remote_copy(
            src_ref=w.at[t, cut, split:lanes], dst_ref=grads[2].at[t, n // 2],
            send_sem=core_send.at[n, t], recv_sem=core_recv.at[n, t],
            device_id=sibling, device_id_type=pl.DeviceIdType.MESH,
        )

    def store(n, t):
        cut = pl.ds(pl.multiple_of(n * step, step), step)
        pltpu.make_async_copy(
            w.at[t, cut, 0:split], grads[0].at[t, cut, :], out_sems.at[n, t, 0]
        ).start()
        if n_out == 3:

            @pl.when(lax.rem(n, 2) == core)
            def _():
                own_copy(n, t).start()

            @pl.when(lax.rem(n, 2) != core)
            def _():
                core_copy(n, t).start()

    def gradient(n, _):
        cut = pl.ds(pl.multiple_of(n * step, step), step)
        for k, ref in enumerate((normed_ref, branch_ref, dattn_ref)):
            turned[k] = ref[:, cut].astype(F32).T.astype(BF)
        for t in range(halves):
            for k, (at, end) in enumerate(regions):
                for b, m in widths(end - at, 1024):
                    value = mm(turned[k], acts[t, :, at + b : at + b + m], NN)
                    w[t, cut, at + b : at + b + m] = value.astype(BF)
            store(n, t)
        return 0

    lax.fori_loop(0, width // step, gradient, 0)

    def settle(n, _):
        cut = pl.ds(pl.multiple_of(n * step, step), step)
        for t in range(halves):
            pltpu.make_async_copy(
                w.at[t, cut, 0:split], grads[0].at[t, cut, :], out_sems.at[n, t, 0]
            ).wait()
            if n_out == 3:

                @pl.when(lax.rem(n, 2) == core)
                def _():
                    own_copy(n, t).wait()
                    core_copy(n, t).wait_recv()

                @pl.when(lax.rem(n, 2) != core)
                def _():
                    core_copy(n, t).wait_send()

        return 0

    lax.fori_loop(0, width // step, settle, 0)
    for move in moves:
        move.wait()


def middle_stage(scalars, mix_a, mix_b, own, cot, gain, w, split):
    halves, width, lanes = w.shape
    slabs, _, _, half = mix_a.shape
    ff = (lanes - width // halves) // 3
    blocks = width // 256
    peers = slabs * halves - 1
    vmem = pl.BlockSpec(memory_space=pltpu.VMEM)
    outside = pl.BlockSpec(memory_space=pl.ANY)
    out_shape = [
        jax.ShapeDtypeStruct((half, width), BF),
        jax.ShapeDtypeStruct((half, width), F32),
        jax.ShapeDtypeStruct(mix_a.shape, BF),
        jax.ShapeDtypeStruct(mix_a.shape, BF),
        jax.ShapeDtypeStruct((halves, width, split), BF),
    ]
    out_specs = [vmem] * 4 + [outside]
    if split < lanes:
        out_shape += [jax.ShapeDtypeStruct((halves, blocks // 2, 256, lanes - split), BF)] * 2
        out_specs += [outside] * 2
    flops = 2 * half * width * (9 * ff * halves + 3 * width)
    return pl.pallas_call(
        functools.partial(middle_kernel, ff, split),
        out_shape=out_shape,
        in_specs=[pl.BlockSpec(memory_space=pltpu.SMEM)] + [vmem] * 5 + [outside],
        out_specs=out_specs,
        scratch_shapes=[
            pltpu.VMEM((halves, width, lanes), BF),
            pltpu.VMEM((halves, half, lanes), BF),
            pltpu.VMEM((width // halves, half), BF),
            pltpu.VMEM((half, width), F32),
            pltpu.VMEM((half, 128), F32),
            pltpu.VMEM((half, width), F32),
            pltpu.VMEM((half, width), BF),
            pltpu.VMEM((half, width), BF),
            pltpu.VMEM((half, width), BF),
            pltpu.VMEM((3, 256, half), BF),
            pltpu.VMEM(mix_a.shape, BF),
            pltpu.VMEM(mix_a.shape, BF),
            pltpu.SemaphoreType.DMA((4 * halves,)),
            pltpu.SemaphoreType.DMA((blocks, halves, 2)),
            pltpu.SemaphoreType.DMA((2 * peers,)),
            pltpu.SemaphoreType.DMA((2 * peers,)),
            pltpu.SemaphoreType.DMA((2,)),
            pltpu.SemaphoreType.DMA((blocks, halves)),
            pltpu.SemaphoreType.DMA((blocks, halves)),
        ],
        compiler_params=pltpu.CompilerParams(
            vmem_limit_bytes=58 << 20, collective_id=1, has_side_effects=True
        ),
        cost_estimate=pl.CostEstimate(
            flops=flops, bytes_accessed=4 * w.size + 16 * half * width, transcendentals=half * lanes
        ),
    )(scalars, mix_a, mix_b, own, cot, gain, w)


class LineSum:
    def __init__(self, source, held, slots, out, sems):
        self.source, self.held, self.slots, self.out = source, held, slots, out
        self.sum_send, self.sum_recv, self.out_send, self.out_recv = sems
        here = lax.axis_index("ctx")
        self.low = here < 2
        self.place = jnp.where(self.low, here, 3 - here)
        self.inward = jnp.where(self.low, here + 1, here - 1)
        self.outward = jnp.where(self.low, here - 1, here + 1)
        self.size = out.shape[0] // 4

    def number(self, part):
        return jnp.where(self.low, part, 3 - part)

    def part(self, ref, part):
        at = pl.multiple_of(self.number(part) * self.size, self.size)
        return ref.at[pl.ds(at, self.size), :]

    def read(self, ref, part):
        at = pl.multiple_of(self.number(part) * self.size, self.size)
        return ref[pl.ds(at, self.size), :].astype(F32)

    def write(self, ref, part, value):
        at = pl.multiple_of(self.number(part) * self.size, self.size)
        ref[pl.ds(at, self.size), :] = value.astype(BF)

    def copy(self, source, target, send, recv, place):
        return pltpu.make_async_remote_copy(
            src_ref=source, dst_ref=target, send_sem=send, recv_sem=recv,
            device_id={"ctx": place}, device_id_type=pl.DeviceIdType.MESH,
        )

    def took(self, slot):
        ref = self.slots.at[slot]
        self.copy(ref, ref, self.sum_send.at[0], self.sum_recv.at[slot], self.inward).wait_recv()
        return self.slots[slot].astype(F32)

    def begin(self):
        @pl.when(self.place == 0)
        def _():
            for k in range(3):
                self.copy(
                    self.part(self.source, 3 - k), self.slots.at[k],
                    self.sum_send.at[k], self.sum_recv.at[k], self.inward,
                ).start()

    def first(self, k):
        @pl.when(self.place == 1)
        def _():
            self.write(self.held, 3 - k, self.read(self.source, 3 - k) + self.took(k))
            self.copy(
                self.part(self.held, 3 - k), self.slots.at[3 + k],
                self.sum_send.at[k], self.sum_recv.at[3 + k], self.inward,
            ).start()

    def second(self):
        @pl.when(self.place == 1)
        def _():
            self.write(self.held, 0, self.read(self.source, 0) + self.took(3))
            self.copy(
                self.part(self.held, 0), self.slots.at[3],
                self.sum_send.at[2], self.sum_recv.at[3], self.outward,
            ).start()

    def give(self, part, send, place):
        ref = self.part(self.out, part)
        return self.copy(
            ref, ref, self.out_send.at[send], self.out_recv.at[self.number(part)], place
        )

    def final(self):
        @pl.when(self.place == 1)
        def _():
            self.write(self.out, 1, self.read(self.source, 1) + self.took(2) + self.took(4))
            self.give(1, 0, self.inward).start()
            self.give(1, 1, self.outward).start()

        @pl.when(self.place == 0)
        def _():
            self.write(self.out, 0, self.read(self.source, 0) + self.took(3))
            self.give(0, 0, self.inward).start()

    def forward(self):
        @pl.when(self.place == 1)
        def _():
            for k, (part, place) in enumerate(((0, self.inward), (2, self.outward), (3, self.outward))):
                self.give(part, 2 + k, place).wait_recv()
                self.give(part, 2 + k, place).start()

    def end(self):
        for k in range(3):
            self.copy(
                self.slots.at[0], self.slots.at[0],
                self.sum_send.at[k], self.sum_recv.at[0], self.inward,
            ).wait_send()

        @pl.when(self.place == 0)
        def _():
            self.give(0, 0, self.inward).wait_send()
            for part in (1, 2, 3):
                self.give(part, 0, self.inward).wait_recv()

        @pl.when(self.place == 1)
        def _():
            for k in range(5):
                self.give(1, k, self.inward).wait_send()


def tail_kernel(
    back_a, back_b, some, rest, normed, weights, own, gain, dmid,
    grad_out, some_out, rest_out, qa_out, qb_out,
    turned, some_held, some_slots, rest_held, rest_slots,
    local, crossed, column_sum, columned, q_src, q_held, q_slots, theirs, got_theirs, mine,
    core_send, core_recv, col_send, col_recv,
    row_send, row_recv, out_send, out_recv, *line_sems,
):
    here, line, place = lax.axis_index("ctx"), lax.axis_index("tp"), lax.axis_index("fsdp")
    core, column = lax.rem(place, 2), place // 2
    sibling = {"fsdp": place + 1 - 2 * core}
    beside = {"fsdp": lax.rem(place + 2, 4)}
    across = {"tp": 1 - line}
    others = [{"ctx": lax.rem(here + k, 4)} for k in range(1, 4)]
    mesh_id = pl.DeviceIdType.MESH
    barrier = pltpu.get_barrier_semaphore()
    for device in (*others, sibling, beside, across):
        pl.semaphore_signal(barrier, inc=1, device_id=device, device_id_type=mesh_id)
    pl.semaphore_wait(barrier, 6)

    def remote(source, target, send, recv, device):
        return pltpu.make_async_remote_copy(
            src_ref=source, dst_ref=target, send_sem=send, recv_sem=recv,
            device_id=device, device_id_type=mesh_id,
        )

    rows = normed.shape[0]
    half = rows // 2
    depth = 256
    a, b, qa, qb = (
        LineSum(src, held, slots, out, line_sems[4 * k : 4 * k + 4])
        for k, (src, held, slots, out) in enumerate(
            (
                (some, some_held, some_slots, some_out),
                (rest, rest_held, rest_slots, rest_out),
                (q_src.at[0], q_held.at[0], q_slots.at[0], qa_out),
                (q_src.at[1], q_held.at[1], q_slots.at[1], qb_out),
            )
        )
    )
    a.begin()
    b.begin()

    def weight_gradient(h, grads):
        def step(n, _):
            cut = pl.ds(pl.multiple_of(n * depth, depth), depth)
            value = mm(grads[...], normed[:, cut], NN).astype(BF)
            local[h, lax.rem(n, 2), n // 2] = value
            return 0

        lax.fori_loop(0, 4, step, 0)
        move = remote(
            local.at[h, 1 - core], crossed.at[h], core_send.at[h], core_recv.at[h], sibling
        )
        move.start()
        return move

    def column_step(h, move):
        move.wait_recv()
        for x in range(2):
            column_sum[h, x] = (
                local[h, core, x].astype(F32) + crossed[h, x].astype(F32)
            ).astype(BF)
        move = remote(
            column_sum.at[h, 1 - column], columned.at[h], col_send.at[h], col_recv.at[h], beside
        )
        move.start()
        return move

    def column_end(h, move):
        move.wait_recv()
        q_src[h] = (column_sum[h, column].astype(F32) + columned[h].astype(F32)).astype(BF)

    def turn(h, grads):
        for k in range(0, grads.shape[0], 128):
            at = h * grads.shape[0] + k
            turned[:, at : at + 128] = grads[k : k + 128, :].astype(F32).T.astype(BF)

    core_a = weight_gradient(0, back_a)
    core_b = weight_gradient(1, back_b)
    a.first(0)
    turn(0, back_a)
    turn(1, back_b)
    a.first(1)
    pieces = 2
    piece = half // pieces
    sent_rows = []
    for k in range(pieces):
        cut = slice(k * piece, (k + 1) * piece)
        start = pl.multiple_of((1 - line) * half + k * piece, piece)

        def make(n, _):
            wide = pl.ds(pl.multiple_of(n * depth, depth), depth)
            value = mm(turned[pl.ds(start, piece), :], weights[:, wide], NN)
            theirs[cut, wide] = value.astype(BF)
            return 0

        lax.fori_loop(0, 4, make, 0)
        move = remote(theirs.at[cut], got_theirs.at[cut], row_send.at[k], row_recv.at[k], across)
        move.start()
        sent_rows.append(move)
    b.first(0)
    col_a = column_step(0, core_a)
    col_b = column_step(1, core_b)
    a.second()
    b.first(1)
    a.final()
    mine_start = pl.multiple_of(line * half, half)

    def make_mine(n, _):
        wide = pl.ds(pl.multiple_of(n * depth, depth), depth)
        mine[:, wide] = mm(turned[pl.ds(mine_start, half), :], weights[:, wide], NN)
        return 0

    lax.fori_loop(0, 4, make_mine, 0)
    b.second()
    column_end(0, col_a)
    qa.begin()
    column_end(1, col_b)
    qb.begin()
    b.final()
    a.forward()
    qa.first(0)
    qb.first(0)
    qa.first(1)
    qb.first(1)
    sent_out = []
    small = 64
    for k in range(pieces):
        sent_rows[k].wait_recv()

        def back(r, _):
            at = pl.multiple_of(k * piece + r * small, small)
            cut = pl.ds(at, small)
            values = own[cut, :].astype(F32)
            inverse = lax.rsqrt(jnp.mean(values * values, axis=1, keepdims=True) + EPSILON)
            scaled = values * inverse
            d_scaled = (mine[cut, :] + got_theirs[cut, :].astype(F32)) * gain[...]
            mean = jnp.mean(d_scaled * scaled, axis=1, keepdims=True)
            total = dmid[cut, :] + inverse * (d_scaled - scaled * mean)
            grad_out[pl.ds(pl.multiple_of(line * half + at, small), small), :] = total.astype(BF)
            return 0

        lax.fori_loop(0, piece // small, back, 0)
        ref = grad_out.at[pl.ds(pl.multiple_of(line * half + k * piece, piece), piece), :]
        move = remote(ref, ref, out_send.at[k], out_recv.at[k], across)
        move.start()
        sent_out.append(move)
    b.forward()
    qa.second()
    qb.second()
    qa.final()
    qb.final()
    qa.forward()
    qb.forward()
    for run in (a, b, qa, qb):
        run.end()
    for move in (core_a, core_b, col_a, col_b, *sent_rows):
        move.wait_send()
    for k, move in enumerate(sent_out):
        move.wait_send()
        ref = grad_out.at[pl.ds(pl.multiple_of((1 - line) * half + k * piece, piece), piece), :]
        remote(ref, ref, out_send.at[k], out_recv.at[k], across).wait_recv()


def tail_stage(back_a, back_b, some, rest, normed, weights, own, gain, dmid):
    rows, width = normed.shape
    half = rows // 2
    lanes_a, lanes_b = some.shape[1], rest.shape[1]
    wide = back_a.shape[0]
    vmem = pl.BlockSpec(memory_space=pltpu.VMEM)
    dma = pltpu.SemaphoreType.DMA
    return pl.pallas_call(
        tail_kernel,
        out_shape=(
            jax.ShapeDtypeStruct((rows, width), BF),
            jax.ShapeDtypeStruct((256, lanes_a), BF),
            jax.ShapeDtypeStruct((256, lanes_b), BF),
            jax.ShapeDtypeStruct((wide, 256), BF),
            jax.ShapeDtypeStruct((wide, 256), BF),
        ),
        in_specs=[vmem] * 9,
        out_specs=(vmem,) * 5,
        scratch_shapes=[
            pltpu.VMEM((rows, 2 * wide), BF),
            pltpu.VMEM((256, lanes_a), BF),
            pltpu.VMEM((5, 64, lanes_a), BF),
            pltpu.VMEM((256, lanes_b), BF),
            pltpu.VMEM((5, 64, lanes_b), BF),
            pltpu.VMEM((2, 2, 2, wide, 256), BF),
            pltpu.VMEM((2, 2, wide, 256), BF),
            pltpu.VMEM((2, 2, wide, 256), BF),
            pltpu.VMEM((2, wide, 256), BF),
            pltpu.VMEM((2, wide, 256), BF),
            pltpu.VMEM((2, wide, 256), BF),
            pltpu.VMEM((2, 5, wide // 4, 256), BF),
            pltpu.VMEM((half, width), BF),
            pltpu.VMEM((half, width), BF),
            pltpu.VMEM((half, width), F32),
            dma((2,)), dma((2,)), dma((2,)), dma((2,)),
            dma((2,)), dma((2,)), dma((2,)), dma((2,)),
        ]
        + [dma((3,)), dma((5,)), dma((5,)), dma((4,))] * 4,
        compiler_params=pltpu.CompilerParams(
            vmem_limit_bytes=56 << 20, collective_id=2, has_side_effects=True
        ),
        cost_estimate=pl.CostEstimate(
            flops=8 * rows * width * wide, bytes_accessed=40 << 20, transcendentals=0
        ),
    )(back_a, back_b, some, rest, normed, weights, own, gain, dmid)


def normalize(values, gain):
    inverse = lax.rsqrt(jnp.mean(values * values, axis=-1, keepdims=True) + EPSILON)
    scaled = values * inverse
    return scaled, inverse, (scaled * gain).astype(BF)


def norm_back(d_normed, scaled, inverse, gain):
    d_scaled = d_normed * gain
    d_values = inverse * (d_scaled - scaled * jnp.mean(d_scaled * scaled, axis=-1, keepdims=True))
    return d_values


def rows_first(values):
    return with_layout_constraint(values, Layout(major_to_minor=tuple(range(values.ndim))))


def swap(values, axis, bit):
    count = lax.axis_size(axis)
    return lax.ppermute(values, axis, [(k, k ^ bit) for k in range(count)])


def both_halves(values):
    half = values.shape[0]
    side = lax.axis_index("tp") * half
    whole = jnp.zeros((2 * half,) + values.shape[1:], values.dtype)
    whole = lax.dynamic_update_slice_in_dim(whole, values, side, 0)
    return lax.dynamic_update_slice_in_dim(whole, swap(values, "tp", 1), half - side, 0)


def shards(
    inputs,
    lengths,
    first_gain,
    query_weight,
    key_weight,
    value_weight,
    out_weight,
    second_gain,
    gate_weight,
    up_weight,
    down_weight,
    cotangent,
):
    slabs, halves, parts = lax.axis_size("ctx"), lax.axis_size("tp"), lax.axis_size("fsdp")
    rows, width = inputs.shape[1], inputs.shape[2]
    depth = query_weight.shape[0]
    group = query_weight.shape[1] // HD // slabs
    half = rows // halves
    ff = gate_weight.shape[1]
    everywhere = ("tp", "fsdp")
    side = lax.axis_index("tp") * half

    paired = parts == 4 and halves == 2 and slabs == 4 and group == 2
    w_rest = jnp.concatenate([gate_weight, up_weight, down_weight.T, out_weight.T], axis=1)
    w_rest = rows_first(lax.all_gather(rows_first(w_rest), everywhere, axis=0, tiled=True))
    w_rest = w_rest.reshape(halves, width, -1)
    qkv_width = slabs * 3 * HD

    if paired:
        gains = jnp.stack([first_gain.astype(F32), second_gain.astype(F32)])
        gains = jnp.concatenate([gains, jnp.zeros((6, depth), F32)])
        w_turned, normed_one, gains, *rest = front_stage(
            lengths, inputs[0], gains, query_weight, key_weight, value_weight, slabs, halves
        )
        gain_one, gain_two = gains[0], gains[1]
        qkv, arrived = rest[0:2], rest[2:4]
        saved = [(rest[4], rest[6]), (rest[5], rest[7])]
    else:
        gains = lax.all_gather(jnp.stack([first_gain, second_gain]), "fsdp", axis=1, tiled=True)
        gain_one, gain_two = gains[0].astype(F32), gains[1].astype(F32)
        stacked = jnp.stack(
            [w.reshape(depth, slabs, group, HD) for w in (query_weight, key_weight, value_weight)]
        ).transpose(1, 3, 2, 0, 4)
        w_qkv = lax.all_gather(
            stacked.reshape(depth, group * qkv_width), "fsdp", axis=0, tiled=True
        )
        w_heads = [w_qkv[:, h * qkv_width : (h + 1) * qkv_width] for h in range(group)]
        _, _, normed_one = normalize(inputs[0].astype(F32), gain_one)
        qkv = []
        for h in range(group):
            part = mm(w_heads[h], normed_one, (((0,), (1,)), ((), ()))).astype(BF)
            part = part.reshape(slabs, 3 * HD, rows)
            qkv.append(lax.all_to_all(part, "ctx", 0, 0, tiled=True))
        arrived, saved = [], []
        for h in range(group):
            mix, mix_full, lse = attend(lengths, qkv[h], halves, rows)
            saved.append((mix_full, lse))
            mix = mix.reshape(slabs * halves, HD, half)
            mix = lax.all_to_all(mix, ("ctx", "tp"), 0, 0, tiled=True)
            arrived.append(mix.reshape(slabs, halves, HD, half))

    own = lax.dynamic_slice_in_dim(inputs[0], side, half, 0)
    cot = lax.dynamic_slice_in_dim(cotangent[0], side, half, 0)
    scalars = jnp.stack([lengths[0], lax.axis_index("ctx") * rows + side])
    split = 2432 if paired else w_rest.shape[2]
    output, d_middle, *d_mix, = middle_stage(
        scalars, *arrived, own, cot, gain_two[None], w_rest, split
    )
    d_mix, (g_some, *g_rest) = d_mix[:2], d_mix[2:]
    output = both_halves(output)
    s_some = lax.psum_scatter(
        rows_first(g_some.reshape(halves * width, -1)), everywhere, scatter_dimension=0, tiled=True
    )
    s_some = rows_first(s_some)

    if paired:
        back_a, back_b, g_rest = back_stage(lengths, qkv, d_mix, saved, *g_rest)
        input_gradient, s_some, s_rest, *q_grads = tail_stage(
            back_a, back_b, s_some, g_rest, normed_one, w_turned, own, gain_one[None], d_middle
        )
        s_all = jnp.concatenate([s_some, s_rest], axis=1).astype(F32)
        s_qkv = jnp.stack([q.reshape(slabs, 3, HD, depth) for q in q_grads], axis=1)
        s_qkv = s_qkv.transpose(2, 4, 0, 1, 3).reshape(3, depth, slabs * group * HD).astype(F32)
    else:
        d_local = [
            attend_back(lengths, qkv[h], d_mix[h], *saved[h], 512) for h in range(group)
        ]
        d_qkv = [
            lax.all_to_all(d, "ctx", 0, 0, tiled=True).reshape(qkv_width, rows) for d in d_local
        ]
        d_normed_one = jnp.zeros((rows, width), F32)
        s_qkv = []
        for h in range(group):
            d_normed_one = d_normed_one + mm(d_qkv[h], w_heads[h], (((0,), (1,)), ((), ())))
            grad = mm(normed_one, d_qkv[h], (((0,), (1,)), ((), ()))).astype(BF)
            grad = lax.psum_scatter(grad, "fsdp", scatter_dimension=0, tiled=True)
            s_qkv.append(lax.psum(grad, "ctx").reshape(depth, slabs, 3, HD))
        d_normed_one = lax.psum_scatter(d_normed_one, "tp", scatter_dimension=0, tiled=True)
        scaled_one, inverse_one, _ = normalize(own.astype(F32), gain_one)
        d_from_one = norm_back(d_normed_one, scaled_one, inverse_one, gain_one)
        input_gradient = lax.all_gather(
            (d_middle + d_from_one).astype(BF), "tp", axis=0, tiled=True
        )
        s_qkv = jnp.stack(s_qkv, axis=2).transpose(3, 0, 1, 2, 4)
        s_qkv = s_qkv.reshape(3, depth, slabs * group * HD).astype(F32)
        s_all = lax.psum(s_some, "ctx").astype(F32)

    d_gain_one = sum(
        jnp.sum(w.astype(F32) * s, axis=1)
        for w, s in zip((query_weight, key_weight, value_weight), s_qkv)
    ) / first_gain.astype(F32)
    d_gain_two = (
        jnp.sum(gate_weight.astype(F32) * s_all[:, :ff], axis=1)
        + jnp.sum(up_weight.astype(F32) * s_all[:, ff : 2 * ff], axis=1)
    ) / second_gain.astype(F32)
    d_gains = jnp.stack([d_gain_one, d_gain_two])
    d_gains = d_gains + swap(d_gains, "tp", 1) if paired else lax.psum(d_gains, "tp")
    return (
        output[None],
        input_gradient[None],
        d_gains[0],
        s_qkv[0],
        s_qkv[1],
        s_qkv[2],
        s_all[:, 3 * ff :].T,
        d_gains[1],
        s_all[:, :ff],
        s_all[:, ff : 2 * ff],
        s_all[:, 2 * ff : 3 * ff].T,
    )


def solution(mesh):
    rows = P("fsdp", "ctx", None)
    gain = P("fsdp")
    inward = P("fsdp", "tp")
    outward = P("tp", "fsdp")
    return jax.shard_map(
        shards,
        mesh=mesh,
        in_specs=(
            rows, gain, gain, inward, inward, inward, outward, gain, inward, inward, outward, rows,
        ),
        out_specs=(
            rows, rows, gain, inward, inward, inward, outward, gain, inward, inward, outward,
        ),
        check_vma=False,
    )
```

```python
import functools

import jax
import jax.numpy as jnp
from jax import lax
from jax.experimental import pallas as pl
from jax.experimental.pallas import tpu as pltpu
from jax.experimental.layout import Layout, with_layout_constraint
from jax.sharding import PartitionSpec as P

HD = 64
EPSILON = 1e-05
MASKED = -1000000000.0
NN = (((1,), (0,)), ((), ()))
NT = (((1,), (1,)), ((), ()))
TN = (((0,), (0,)), ((), ()))
BF = jnp.bfloat16
F32 = jnp.float32


def mm(left, right, dims):
    return lax.dot_general(left, right, dims, preferred_element_type=F32)


def spread_keys(keys, start, length):
    rows = keys.shape[0]
    pos = start + lax.broadcasted_iota(jnp.int32, (rows, HD), 0)
    lane = lax.broadcasted_iota(jnp.int32, (rows, HD), 1)
    bias = jnp.where((lane == 0) & (pos >= length), MASKED, 0.0)
    return jnp.concatenate([keys, bias], axis=1).astype(BF)


def spread_queries(queries):
    row = lax.broadcasted_iota(jnp.int32, queries.shape, 0)
    ones = jnp.where(row == 0, 1.0, 0.0)
    return jnp.concatenate([queries * HD**-0.5, ones], axis=0).astype(BF)


def attend_rows(tile, length, qkv, kx, qx, vx, emit):
    slabs, _, rows = qkv.shape
    per = rows // tile
    blocks = slabs * per
    for z in range(slabs):
        keys = qkv[z, HD : 2 * HD, :].astype(F32).T
        kx[z * rows : (z + 1) * rows, :] = spread_keys(keys, z * rows, length)
        queries = spread_queries(qkv[z, 0:HD, :].astype(F32))
        for b in range(per):
            cut = slice(b * tile, (b + 1) * tile)
            qx[z * per + b] = queries[:, cut]
            vx[z * per + b] = qkv[z, 2 * HD : 3 * HD, cut]
    later = lax.broadcasted_iota(jnp.int32, (tile, tile), 0) > lax.broadcasted_iota(
        jnp.int32, (tile, tile), 1
    )

    def query_block(i, _):
        queries = qx[i]

        def step(j, carry, masked):
            highest, total, mix = carry
            keys = kx[pl.ds(pl.multiple_of(j * tile, tile), tile), :]
            scores = mm(keys, queries, NN)
            if masked:
                scores = jnp.where(later, MASKED, scores)
            new = jnp.maximum(highest, jnp.max(scores, axis=0, keepdims=True))
            scale = jnp.exp(highest - new)
            probs = jnp.exp(scores - new)
            total = total * scale + jnp.sum(probs, axis=0, keepdims=True)
            mix = mix * scale + mm(vx[j], probs.astype(BF), NN)
            return new, total, mix

        first = (
            jnp.full((1, tile), -jnp.inf, F32),
            jnp.zeros((1, tile), F32),
            jnp.zeros((HD, tile), F32),
        )
        carry = lax.fori_loop(0, i, lambda j, c: step(j, c, False), first)
        highest, total, mix = step(i, carry, True)
        emit(i, mix / total, highest + jnp.log(total))
        return 0

    lax.fori_loop(0, blocks, query_block, 0)


def attend_kernel(tile, len_ref, qkv, o_ref, of_ref, lse_ref, kx, qx, vx):
    rows = qkv.shape[2]
    halves = o_ref.shape[1]
    half = rows // halves

    def emit(i, mix, lse):
        of_ref[i] = mix
        lse_ref[i] = lse
        for t in range(halves):
            o_ref[i, t] = mix[:, t * half : (t + 1) * half].astype(BF)

    attend_rows(tile, len_ref[0], qkv, kx, qx, vx, emit)


def front_kernel(
    len_ref, x, gains_own, wq, wk, wv,
    wt_hbm, normed_hbm, gains, qkv_a_hbm, qkv_b_hbm, mix_a, mix_b, of_a_hbm, of_b_hbm, lse_a, lse_b,
    wt, normed, qkv_a, qkv_b, of_a, of_b, out_sems, packed, parts, mixed, kx, qx, vx,
    gain_send, gain_recv, w_send, w_recv, part_send, part_recv, part_local,
    mix_send, mix_recv, mix_local,
):
    here, line, place = lax.axis_index("ctx"), lax.axis_index("tp"), lax.axis_index("fsdp")
    core, column = lax.rem(place, 2), place // 2
    pair = place + 1 - 2 * core
    other = lax.rem(place + 2, 4)
    mesh_id = pl.DeviceIdType.MESH
    slabs, halves = mix_a.shape[0], mix_a.shape[1]
    rows, width = x.shape
    half = rows // halves
    wide = slabs * 3 * HD
    depth = wq.shape[0]
    peers = [(dz, dt) for dz in range(slabs) for dt in range(halves) if dz or dt]

    def peer(dz, dt):
        return lax.rem(here + dz, slabs), lax.rem(line + dt, halves)

    barrier = pltpu.get_barrier_semaphore()
    for dz, dt in peers:
        z, t = peer(dz, dt)
        pl.semaphore_signal(barrier, inc=1, device_id={"ctx": z, "tp": t}, device_id_type=mesh_id)
    for device in (pair, other):
        pl.semaphore_signal(barrier, inc=1, device_id={"fsdp": device}, device_id_type=mesh_id)
    for q, w in enumerate((wq, wk, wv)):
        flat = w[...].astype(F32).T.astype(BF)
        for z in range(slabs):
            for h in range(2):
                at = (2 * z + h) * HD
                packed[h, (3 * z + q) * HD : (3 * z + q + 1) * HD, :] = flat[at : at + HD]

    def remote(source, target, send, recv, device):
        return pltpu.make_async_remote_copy(
            src_ref=source, dst_ref=target, send_sem=send, recv_sem=recv,
            device_id=device, device_id_type=mesh_id,
        )

    def lanes(index):
        return pl.ds(pl.multiple_of(index * depth, depth), depth)

    def weight(h, index):
        return wt.at[h * wide : (h + 1) * wide, lanes(index)]

    gains[:, lanes(place)] = gains_own[...]
    for h in range(2):
        wt[h * wide : (h + 1) * wide, lanes(place)] = packed[h]
    pl.semaphore_wait(barrier, len(peers) + 2)
    sent = []

    def launch(move):
        move.start()
        sent.append(move)
        return move

    for k, device in enumerate((pair, other)):
        launch(
            remote(
                gains_own, gains.at[:, lanes(place)], gain_send.at[k], gain_recv.at[k], {"fsdp": device}
            )
        )
    for h in range(2):
        for k, device in ((1, other), (0, pair)):
            launch(
                remote(
                    packed.at[h], weight(h, place), w_send.at[h, k], w_recv.at[h, k], {"fsdp": device}
                )
            )

    def arrived(ref, sem):
        remote(ref, ref, gain_send.at[0], sem, {"fsdp": pair}).wait_recv()

    arrived(gains.at[:, lanes(other)], gain_recv.at[1])
    launch(
        remote(
            gains.at[:, lanes(other)], gains.at[:, lanes(other)], gain_send.at[2], gain_recv.at[2],
            {"fsdp": pair},
        )
    )
    far = lax.rem(pair + 2, 4)
    arrived(gains.at[:, lanes(pair)], gain_recv.at[0])
    arrived(gains.at[:, lanes(far)], gain_recv.at[2])
    small = 64

    def norm(r, _):
        cut = pl.ds(pl.multiple_of(r * small, small), small)
        values = x[cut, :].astype(F32)
        inverse = lax.rsqrt(jnp.mean(values * values, axis=1, keepdims=True) + EPSILON)
        normed[cut, :] = (values * inverse * gains[0:1, :]).astype(BF)
        return 0

    lax.fori_loop(0, rows // small, norm, 0)
    kept = []

    def keep(source, target):
        move = pltpu.make_async_copy(source, target, out_sems.at[len(kept)])
        move.start()
        kept.append(move)

    keep(normed, normed_hbm)
    queues = (qkv_a, qkv_b)
    waits = []
    for h in range(2):
        arrived(weight(h, other), w_recv.at[h, 1])
        launch(
            remote(
                weight(h, other), weight(h, other), w_send.at[h, 2], w_recv.at[h, 2], {"fsdp": pair}
            )
        )
    for h in range(2):
        arrived(weight(h, pair), w_recv.at[h, 0])
        arrived(weight(h, far), w_recv.at[h, 2])

        def project(n, _):
            cut = pl.ds(pl.multiple_of(n * 256, 256), 256)
            value = mm(wt[h * wide : (h + 1) * wide, :], normed[cut, :], NT).astype(BF)
            for z in range(slabs):
                parts[h, z, :, cut] = value[z * 3 * HD : (z + 1) * 3 * HD]
            return 0

        lax.fori_loop(0, rows // 256, project, 0)
        for k in range(1, slabs):
            z = lax.rem(here + k, slabs)
            waits.append(
                launch(
                    remote(
                        parts.at[h, z], queues[h].at[here], part_send.at[h, k], part_recv.at[h, k],
                        {"ctx": z},
                    )
                )
            )
        stays = pltpu.make_async_copy(parts.at[h, here], queues[h].at[here], part_local.at[h])
        stays.start()
        waits.append(stays)

    keep(wt, wt_hbm)
    for h, (qkv, mix_ref, of_ref, lse_ref) in enumerate(
        ((qkv_a, mix_a, of_a, lse_a), (qkv_b, mix_b, of_b, lse_b))
    ):
        for move in waits[h * slabs : (h + 1) * slabs - 1]:
            move.wait_recv()
        waits[(h + 1) * slabs - 1].wait()
        keep(qkv, (qkv_a_hbm, qkv_b_hbm)[h])

        def emit(i, mix, lse):
            of_ref[i] = mix
            lse_ref[i] = lse
            for t in range(halves):
                mixed[h, i, t] = mix[:, t * half : (t + 1) * half].astype(BF)
                stay = (i == here) & (line == t)

                @pl.when(stay)
                def _():
                    pltpu.make_async_copy(
                        mixed.at[h, i, t], mix_ref.at[here, line], mix_local.at[h]
                    ).start()

                @pl.when(jnp.logical_not(stay))
                def _():
                    remote(
                        mixed.at[h, i, t], mix_ref.at[here, line], mix_send.at[h, i, t],
                        mix_recv.at[h, here, line], {"ctx": i, "tp": t},
                    ).start()

        attend_rows(rows, len_ref[0], qkv, kx, qx, vx, emit)
        keep(of_ref, (of_a_hbm, of_b_hbm)[h])

    for move in sent:
        move.wait_send()
    for move in kept:
        move.wait()
    for h, mix_ref in enumerate((mix_a, mix_b)):
        pltpu.make_async_copy(mixed.at[h, here, line], mix_ref.at[here, line], mix_local.at[h]).wait()
        for dz, dt in peers:
            z, t = peer(dz, dt)
            remote(
                mixed.at[h, z, t], mix_ref.at[z, t], mix_send.at[h, z, t], mix_recv.at[h, z, t],
                {"ctx": z, "tp": t},
            ).wait()


def front_stage(length, x, gains, wq, wk, wv, slabs, halves):
    rows, width = x.shape
    half = rows // halves
    wide = slabs * 3 * HD
    total = slabs * rows
    work = total * (total + rows) // 2
    vmem = pl.BlockSpec(memory_space=pltpu.VMEM)
    outside = pl.BlockSpec(memory_space=pl.ANY)
    dma = pltpu.SemaphoreType.DMA
    shape = jax.ShapeDtypeStruct
    return pl.pallas_call(
        front_kernel,
        out_shape=(
            shape((2 * wide, width), BF),
            shape((rows, width), BF),
            shape((8, width), F32),
            *[shape((slabs, 3 * HD, rows), BF)] * 2,
            *[shape((slabs, halves, HD, half), BF)] * 2,
            *[shape((slabs, HD, rows), F32)] * 2,
            *[shape((slabs, 1, rows), F32)] * 2,
        ),
        in_specs=[pl.BlockSpec(memory_space=pltpu.SMEM)] + [vmem] * 5,
        out_specs=(
            outside, outside, vmem, outside, outside, vmem, vmem, outside, outside, vmem, vmem,
        ),
        scratch_shapes=[
            pltpu.VMEM((2 * wide, width), BF),
            pltpu.VMEM((rows, width), BF),
            *[pltpu.VMEM((slabs, 3 * HD, rows), BF)] * 2,
            *[pltpu.VMEM((slabs, HD, rows), F32)] * 2,
            dma((6,)),
            pltpu.VMEM((2, wide, wq.shape[0]), BF),
            pltpu.VMEM((2, slabs, 3 * HD, rows), BF),
            pltpu.VMEM((2, slabs, halves, HD, half), BF),
            pltpu.VMEM((total, 2 * HD), BF),
            pltpu.VMEM((slabs, 2 * HD, rows), BF),
            pltpu.VMEM((slabs, HD, rows), BF),
            dma((3,)), dma((3,)), dma((2, 3)), dma((2, 3)),
            dma((2, slabs)), dma((2, slabs)), dma((2,)),
            dma((2, slabs, halves)), dma((2, slabs, halves)), dma((2,)),
        ],
        compiler_params=pltpu.CompilerParams(
            vmem_limit_bytes=48 << 20, collective_id=3, has_side_effects=True
        ),
        cost_estimate=pl.CostEstimate(
            flops=2 * work * 256 * 4, bytes_accessed=20 << 20, transcendentals=2 * work
        ),
    )(length, x, gains, wq, wk, wv)


def attend(length, qkv, halves, tile):
    slabs, _, rows = qkv.shape
    total = slabs * rows
    tile = min(tile, rows)
    work = total * (total + tile) // 2
    vmem = pl.BlockSpec(memory_space=pltpu.VMEM)
    return pl.pallas_call(
        functools.partial(attend_kernel, tile),
        out_shape=(
            jax.ShapeDtypeStruct((slabs, halves, HD, rows // halves), BF),
            jax.ShapeDtypeStruct((slabs, HD, rows), F32),
            jax.ShapeDtypeStruct((slabs, 1, rows), F32),
        ),
        in_specs=[pl.BlockSpec(memory_space=pltpu.SMEM), vmem],
        out_specs=(vmem, vmem, vmem),
        scratch_shapes=[
            pltpu.VMEM((total, 2 * HD), BF),
            pltpu.VMEM((total // tile, 2 * HD, tile), BF),
            pltpu.VMEM((total // tile, HD, tile), BF),
        ],
        compiler_params=pltpu.CompilerParams(vmem_limit_bytes=40 << 20),
        cost_estimate=pl.CostEstimate(
            flops=work * 256 * 4, bytes_accessed=qkv.size * 4, transcendentals=work
        ),
    )(length, qkv)


def attend_back_rows(tile, length, qkv, do_ref, of_ref, lse_ref, out, scratch, emit):
    kx, qx, vx, kt, dox, dq, st = scratch
    slabs, _, rows = qkv.shape
    halves, half = do_ref.shape[1], do_ref.shape[3]
    per = rows // tile
    blocks = slabs * per
    for z in range(slabs):
        keys = qkv[z, HD : 2 * HD, :]
        kx[z * rows : (z + 1) * rows, :] = spread_keys(keys.astype(F32).T, z * rows, length)
        queries = spread_queries(qkv[z, 0:HD, :].astype(F32))
        values = qkv[z, 2 * HD : 3 * HD, :].astype(F32).T
        vx[z * rows : (z + 1) * rows, :] = jnp.concatenate(
            [values, jnp.zeros((rows, HD), F32)], axis=1
        ).astype(BF)
        d_mix = jnp.concatenate([do_ref[z, t] for t in range(halves)], axis=1)
        delta = jnp.sum(d_mix.astype(F32) * of_ref[z], axis=0, keepdims=True)
        for b in range(per):
            cut = slice(b * tile, (b + 1) * tile)
            n = z * per + b
            qx[n] = queries[:, cut]
            kt[n] = keys[:, cut]
            dox[n, 0:HD] = d_mix[:, cut]
            dox[n, HD : 2 * HD] = jnp.zeros((HD, tile), BF)
            st[n, 0:1] = lse_ref[z, :, cut]
            st[n, 1:2] = delta[:, cut]
    dq[...] = jnp.zeros_like(dq)
    later = lax.broadcasted_iota(jnp.int32, (tile, tile), 0) > lax.broadcasted_iota(
        jnp.int32, (tile, tile), 1
    )

    def key_block(j, _):
        here = pl.ds(pl.multiple_of(j * tile, tile), tile)
        keys = kx[here, :]
        values = vx[here, :]

        def step(i, carry, masked):
            dk, dv = carry
            scores = mm(keys, qx[i], NN)
            if masked:
                scores = jnp.where(later, MASKED, scores)
            probs = jnp.exp(scores - st[i, 0:1])
            d_probs = mm(values, dox[i], NN)
            d_scores = (probs * (d_probs - st[i, 1:2])).astype(BF)
            dv = dv + mm(dox[i, 0:HD], probs.astype(BF), NT)
            dk = dk + mm(qx[i, 0:HD], d_scores, NT)
            dq[i] += mm(kt[j], d_scores, NN)
            return dk, dv

        zero = jnp.zeros((HD, tile), F32)
        carry = step(j, (zero, zero), True)
        dk, dv = lax.fori_loop(j + 1, blocks, lambda i, c: step(i, c, False), carry)
        z = j // per
        cut = pl.ds(pl.multiple_of(lax.rem(j, per) * tile, tile), tile)
        out[z, 0:HD, cut] = (dq[j] * HD**-0.5).astype(BF)
        out[z, HD : 2 * HD, cut] = dk.astype(BF)
        out[z, 2 * HD : 3 * HD, cut] = dv.astype(BF)
        if emit is not None:

            @pl.when(lax.rem(j, per) == per - 1)
            def _():
                emit(z)

        return 0

    lax.fori_loop(0, blocks, key_block, 0)


def attend_back_scratch(slabs, rows, tile):
    total = slabs * rows
    blocks = total // tile
    return [
        pltpu.VMEM((total, 2 * HD), BF),
        pltpu.VMEM((blocks, 2 * HD, tile), BF),
        pltpu.VMEM((total, 2 * HD), BF),
        pltpu.VMEM((blocks, HD, tile), BF),
        pltpu.VMEM((blocks, 2 * HD, tile), BF),
        pltpu.VMEM((blocks, HD, tile), F32),
        pltpu.VMEM((blocks, 8, tile), F32),
    ]


def attend_back_kernel(tile, len_ref, qkv, do_ref, of_ref, lse_ref, out, *scratch):
    attend_back_rows(tile, len_ref[0], qkv, do_ref, of_ref, lse_ref, out, scratch, None)


def back_kernel(
    tile, len_ref, qkv_a, qkv_b, do_a, do_b, of_a, of_b, lse_a, lse_b, keep_hbm, got_hbm,
    out_a, out_b, rest,
    local, keep, got, low_got, high_got, swapped, *refs,
):
    scratch, sems = refs[:7], refs[7:]
    (load_sems, grad_send, grad_recv, grad_local, low_send, low_recv, high_send, high_recv,
     swap_send, swap_recv) = sems
    here, line, place = lax.axis_index("ctx"), lax.axis_index("tp"), lax.axis_index("fsdp")
    column = place // 2
    beside = {"fsdp": lax.rem(place + 2, 4)}
    across = {"tp": 1 - line}
    mesh_id = pl.DeviceIdType.MESH
    slabs, block = qkv_a.shape[0], qkv_a.shape[1]
    loads = [
        pltpu.make_async_copy(source, target, load_sems.at[k])
        for k, (source, target) in enumerate(((keep_hbm, keep), (got_hbm, got)))
    ]
    for load in loads:
        load.start()
    others = [lax.rem(here + k, slabs) for k in range(1, slabs)]
    barrier = pltpu.get_barrier_semaphore()
    for device in (*[{"ctx": z} for z in others], beside, across):
        pl.semaphore_signal(barrier, inc=1, device_id=device, device_id_type=mesh_id)
    pl.semaphore_wait(barrier, slabs + 1)

    def remote(source, target, send, recv, device):
        return pltpu.make_async_remote_copy(
            src_ref=source, dst_ref=target, send_sem=send, recv_sem=recv,
            device_id=device, device_id_type=mesh_id,
        )

    outs = (out_a, out_b)

    def window(h, at):
        return outs[h].at[pl.ds(pl.multiple_of(at * block, block), block), :]

    def attend_head(h, qkv, do_ref, of_ref, lse_ref):
        def emit(z):
            @pl.when(z == here)
            def _():
                pltpu.make_async_copy(
                    local.at[h, z], window(h, here), grad_local.at[h]
                ).start()

            @pl.when(z != here)
            def _():
                remote(
                    local.at[h, z], window(h, here), grad_send.at[h, z], grad_recv.at[h, here],
                    {"ctx": z},
                ).start()

        attend_back_rows(
            tile, len_ref[0], qkv, do_ref, of_ref, lse_ref, local.at[h], scratch, emit
        )

    attend_head(0, qkv_a, do_a, of_a, lse_a)
    for load in loads:
        load.wait()
    cut = rest.shape[0] // 2
    for t in range(2):
        for x in range(2):
            keep[t, x] = (keep[t, x].astype(F32) + got[t, x].astype(F32)).astype(BF)
    moves = []
    for k in range(2):
        moves.append(
            remote(
                keep.at[1 - line, k, 0:cut], low_got.at[k], low_send.at[k], low_recv.at[k], across
            )
        )
        moves.append(
            remote(
                keep.at[k, 1 - column, cut : 2 * cut], high_got.at[k], high_send.at[k],
                high_recv.at[k], beside,
            )
        )
    for move in moves:
        move.start()
    attend_head(1, qkv_b, do_b, of_b, lse_b)
    for move in moves:
        move.wait_recv()
    low, high = slice(0, cut), slice(cut, 2 * cut)
    for k in range(2):
        keep[line, k, low] = (
            keep[line, k, low].astype(F32) + low_got[k].astype(F32)
        ).astype(BF)
        keep[k, column, high] = (
            keep[k, column, high].astype(F32) + high_got[k].astype(F32)
        ).astype(BF)
    swaps = [
        remote(
            keep.at[line, 1 - column, low], swapped.at[0], swap_send.at[0], swap_recv.at[0], beside
        ),
        remote(
            keep.at[1 - line, column, high], swapped.at[1], swap_send.at[1], swap_recv.at[1], across
        ),
    ]
    for move in swaps:
        move.start()
    for move in swaps:
        move.wait_recv()
    for k, part in enumerate((low, high)):
        rest[part] = (
            keep[line, column, part].astype(F32) + swapped[k].astype(F32)
        ).astype(BF)
    for h in range(2):
        pltpu.make_async_copy(local.at[h, here], window(h, here), grad_local.at[h]).wait()
        for z in others:
            remote(
                local.at[h, z], window(h, z), grad_send.at[h, z], grad_recv.at[h, z], {"ctx": z}
            ).wait()
    for move in (*moves, *swaps):
        move.wait_send()


def back_stage(length, qkv, d_mix, saved, keep, got):
    slabs, block, rows = qkv[0].shape
    tile = 512
    lanes = keep.shape[3]
    total = slabs * rows
    work = total * (total + tile) // 2
    vmem = pl.BlockSpec(memory_space=pltpu.VMEM)
    outside = pl.BlockSpec(memory_space=pl.ANY)
    dma = pltpu.SemaphoreType.DMA
    return pl.pallas_call(
        functools.partial(back_kernel, tile),
        out_shape=(
            jax.ShapeDtypeStruct((slabs * block, rows), BF),
            jax.ShapeDtypeStruct((slabs * block, rows), BF),
            jax.ShapeDtypeStruct((256, lanes), BF),
        ),
        in_specs=[pl.BlockSpec(memory_space=pltpu.SMEM)] + [vmem] * 8 + [outside] * 2,
        out_specs=(vmem,) * 3,
        scratch_shapes=[
            pltpu.VMEM((2, slabs, block, rows), BF),
            pltpu.VMEM(keep.shape, BF),
            pltpu.VMEM(keep.shape, BF),
            pltpu.VMEM((2, 128, lanes), BF),
            pltpu.VMEM((2, 128, lanes), BF),
            pltpu.VMEM((2, 128, lanes), BF),
            *attend_back_scratch(slabs, rows, tile),
            dma((2,)), dma((2, slabs)), dma((2, slabs)), dma((2,)),
            dma((2,)), dma((2,)), dma((2,)), dma((2,)), dma((2,)), dma((2,)),
        ],
        compiler_params=pltpu.CompilerParams(
            vmem_limit_bytes=56 << 20, collective_id=4, has_side_effects=True
        ),
        cost_estimate=pl.CostEstimate(
            flops=2 * work * 256 * 10, bytes_accessed=24 << 20, transcendentals=2 * work
        ),
    )(length, *qkv, *d_mix, *[m for m, _ in saved], *[l for _, l in saved], keep, got)


def attend_back(length, qkv, d_mix, mix, lse, tile):
    slabs, _, rows = qkv.shape
    total = slabs * rows
    tile = min(tile, rows)
    work = total * (total + tile) // 2
    vmem = pl.BlockSpec(memory_space=pltpu.VMEM)
    return pl.pallas_call(
        functools.partial(attend_back_kernel, tile),
        out_shape=jax.ShapeDtypeStruct((slabs, 3 * HD, rows), BF),
        in_specs=[pl.BlockSpec(memory_space=pltpu.SMEM), vmem, vmem, vmem, vmem],
        out_specs=vmem,
        scratch_shapes=attend_back_scratch(slabs, rows, tile),
        compiler_params=pltpu.CompilerParams(vmem_limit_bytes=40 << 20),
        cost_estimate=pl.CostEstimate(
            flops=work * 256 * 10, bytes_accessed=qkv.size * 8, transcendentals=work
        ),
    )(length, qkv, d_mix, mix, lse)


def widths(total, step):
    return [(at, min(step, total - at)) for at in range(0, total, step)]


def middle_kernel(
    ff, split, scal, mix_a, mix_b, own_hbm, cot_hbm, gain, w_hbm,
    out_ref, dmid_ref, got_a, got_b, *refs,
):
    n_out = 3 if split < w_hbm.shape[2] else 1
    grads = refs[:n_out]
    (w, acts, att_t, mid, scale, dn, normed_ref, branch_ref, dattn_ref, turned, do_a, do_b,
     sems, out_sems, send_sems, recv_sems, local_sems, core_send, core_recv,
     own, cot, row_sems) = refs[n_out:]
    slabs, halves, _, half = mix_a.shape
    width = own.shape[1]
    side = pl.ds(pl.multiple_of(lax.axis_index("tp") * half, half), half)
    row_loads = [
        pltpu.make_async_copy(source.at[side, :], target, row_sems.at[k])
        for k, (source, target) in enumerate(((own_hbm, own), (cot_hbm, cot)))
    ]
    for load in row_loads:
        load.start()
    inner = width // halves
    base = 3 * ff
    lanes = base + inner
    here, line = lax.axis_index("ctx"), lax.axis_index("tp")
    core = lax.rem(lax.axis_index("fsdp"), 2)
    sibling = {"fsdp": lax.axis_index("fsdp") + 1 - 2 * core}
    barrier = pltpu.get_barrier_semaphore()
    peers = [(dz, dt) for dz in range(slabs) for dt in range(halves) if dz or dt]

    def peer(dz, dt):
        return lax.rem(here + dz, slabs), lax.rem(line + dt, halves)

    for dz, dt in peers:
        z, t = peer(dz, dt)
        pl.semaphore_signal(
            barrier, inc=1, device_id={"ctx": z, "tp": t}, device_id_type=pl.DeviceIdType.MESH
        )
    if n_out == 3:
        pl.semaphore_signal(
            barrier, inc=1, device_id=sibling, device_id_type=pl.DeviceIdType.MESH
        )
    cuts = [(t, base, inner) for t in range(halves)]
    cuts += [(t, k * ff, ff) for t in range(halves) for k in range(3)]
    loads = [
        pltpu.make_async_copy(
            w_hbm.at[t, :, at : at + n], w.at[t, :, at : at + n], sems.at[k]
        )
        for k, (t, at, n) in enumerate(cuts)
    ]
    for load in loads:
        load.start()
    length, first = scal[0], scal[1]
    step = 256
    rows = 64

    for t in range(halves):
        for z in range(slabs):
            at = z * 2 * HD
            att_t[at : at + HD, :] = mix_a[z, t]
            att_t[at + HD : at + 2 * HD, :] = mix_b[z, t]
        acts[t, :, base:lanes] = att_t[...].astype(F32).T.astype(BF)
    for k in range(halves):
        loads[k].wait()
    for load in row_loads:
        load.wait()

    def project(n, _):
        cut = pl.ds(pl.multiple_of(n * step, step), step)
        total = own[:, cut].astype(F32)
        for t in range(halves):
            total = total + mm(acts[t, :, base:lanes], w[t, cut, base:lanes], NT)
        mid[:, cut] = total
        return 0

    lax.fori_loop(0, width // step, project, 0)

    def row_mask(r):
        pos = first + r * rows + lax.broadcasted_iota(jnp.int32, (rows, 1), 0)
        return jnp.where(pos < length, 1.0, 0.0)

    def norm(r, _):
        cut = pl.ds(pl.multiple_of(r * rows, rows), rows)
        values = mid[cut, :]
        inverse = lax.rsqrt(jnp.mean(values * values, axis=1, keepdims=True) + EPSILON)
        scale[cut, :] = jnp.broadcast_to(inverse, (rows, 128))
        normed_ref[cut, :] = (values * inverse * gain[...]).astype(BF)
        branch_ref[cut, :] = (cot[cut, :].astype(F32) * row_mask(r)).astype(BF)
        return 0

    lax.fori_loop(0, half // rows, norm, 0)

    for t in range(halves):
        for k in range(3):
            loads[halves + 3 * t + k].wait()

        def columns(at, n):
            def cut(k):
                return pl.ds(pl.multiple_of(k * ff + at, 128), n)

            gate = mm(normed_ref[...], w[t, :, cut(0)], NN)
            upward = mm(normed_ref[...], w[t, :, cut(1)], NN)
            d_hidden = mm(branch_ref[...], w[t, :, cut(2)], NN)
            sig = 1.0 / (1.0 + jnp.exp(-gate))
            active = gate * sig
            acts[t, :, cut(2)] = (active * upward).astype(BF)
            acts[t, :, cut(0)] = (
                d_hidden * upward * sig * (1.0 + gate * (1.0 - sig))
            ).astype(BF)
            acts[t, :, cut(1)] = (d_hidden * active).astype(BF)

        def chunk(c, _):
            columns(c * step, step)
            return 0

        lax.fori_loop(0, ff // step, chunk, 0)
        if ff % step:
            columns(ff - ff % step, ff % step)

    def back(n, _):
        cut = pl.ds(pl.multiple_of(n * step, step), step)
        total = mid[:, cut]
        grad = jnp.zeros((half, step), F32)
        for t in range(halves):
            total = total + mm(acts[t, :, 2 * ff : base], w[t, cut, 2 * ff : base], NT)
            grad = grad + mm(acts[t, :, 0:ff], w[t, cut, 0:ff], NT)
            grad = grad + mm(acts[t, :, ff : 2 * ff], w[t, cut, ff : 2 * ff], NT)
        dmid_ref[:, cut] = total
        dn[:, cut] = grad
        return 0

    lax.fori_loop(0, width // step, back, 0)

    def finish(r, _):
        cut = pl.ds(pl.multiple_of(r * rows, rows), rows)
        mask = row_mask(r)
        out_ref[cut, :] = (dmid_ref[cut, :] * mask).astype(BF)
        inverse = scale[cut, 0:1]
        scaled = mid[cut, :] * inverse
        d_scaled = dn[cut, :] * gain[...]
        mean = jnp.mean(d_scaled * scaled, axis=1, keepdims=True)
        total = cot[cut, :].astype(F32) * mask + inverse * (d_scaled - scaled * mean)
        dmid_ref[cut, :] = total
        dattn_ref[cut, :] = total.astype(BF)
        return 0

    lax.fori_loop(0, half // rows, finish, 0)
    for t in range(halves):
        for z in range(0, slabs, 2):
            at = base + z * 2 * HD
            grad = mm(dattn_ref[...], w[t, :, at : at + 4 * HD], NN).T.astype(BF)
            for k in range(2):
                do_a[z + k, t] = grad[2 * k * HD : (2 * k + 1) * HD]
                do_b[z + k, t] = grad[(2 * k + 1) * HD : (2 * k + 2) * HD]

    pl.semaphore_wait(barrier, len(peers) + (n_out == 3))
    moves = []
    for k, (dz, dt) in enumerate(peers):
        z, t = peer(dz, dt)
        for h, (source, target) in enumerate(((do_a, got_a), (do_b, got_b))):
            move = pltpu.make_async_remote_copy(
                src_ref=source.at[z, t],
                dst_ref=target.at[here, line],
                send_sem=send_sems.at[2 * k + h],
                recv_sem=recv_sems.at[2 * k + h],
                device_id={"ctx": z, "tp": t},
                device_id_type=pl.DeviceIdType.MESH,
            )
            move.start()
            moves.append(move)
    for h, (source, target) in enumerate(((do_a, got_a), (do_b, got_b))):
        move = pltpu.make_async_copy(
            source.at[here, line], target.at[here, line], local_sems.at[h]
        )
        move.start()
        moves.append(move)

    regions = ((0, 2 * ff), (2 * ff, base), (base, lanes))

    def own_copy(n, t):
        cut = pl.ds(pl.multiple_of(n * step, step), step)
        return pltpu.make_async_copy(
            w.at[t, cut, split:lanes], grads[1].at[t, n // 2], out_sems.at[n, t, 1]
        )

    def core_copy(n, t):
        cut = pl.ds(pl.multiple_of(n * step, step), step)
        return pltpu.make_async_remote_copy(
            src_ref=w.at[t, cut, split:lanes], dst_ref=grads[2].at[t, n // 2],
            send_sem=core_send.at[n, t], recv_sem=core_recv.at[n, t],
            device_id=sibling, device_id_type=pl.DeviceIdType.MESH,
        )

    def some_copy(t):
        return pltpu.make_async_copy(
            w.at[t, :, 0:split], grads[0].at[t], out_sems.at[0, t, 0]
        )

    def store(t):
        if n_out == 1:
            return

        def rows_of(n, _):
            @pl.when(lax.rem(n, 2) == core)
            def _():
                own_copy(n, t).start()

            @pl.when(lax.rem(n, 2) != core)
            def _():
                core_copy(n, t).start()

            return 0

        lax.fori_loop(0, width // step, rows_of, 0)

    for k, ref in enumerate((normed_ref, branch_ref, dattn_ref)):
        for b in range(0, width, step):
            turned[k, b : b + step] = ref[:, b : b + step].astype(F32).T.astype(BF)
    for t in range(halves):

        def fill(k, at, n):
            cut = pl.ds(at, n)
            w[t, :, cut] = mm(turned[k], acts[t, :, cut], NN).astype(BF)

        def span(k, start, stop):
            def chunk(c, _):
                fill(k, pl.multiple_of(start + c * step, 128), step)
                return 0

            count = (stop - start) // step
            lax.fori_loop(0, count, chunk, 0)
            if start + count * step < stop:
                fill(k, start + count * step, stop - start - count * step)

        for k, (at, end) in enumerate(regions):
            if at < split < end:
                span(k, at, split)
                at = split
                some_copy(t).start()
            span(k, at, end)
            if end == split:
                some_copy(t).start()
        store(t)

    for t in range(halves):
        some_copy(t).wait()

        def settle(n, _):
            @pl.when(lax.rem(n, 2) == core)
            def _():
                own_copy(n, t).wait()
                core_copy(n, t).wait_recv()

            @pl.when(lax.rem(n, 2) != core)
            def _():
                core_copy(n, t).wait_send()

            return 0

        if n_out == 3:
            lax.fori_loop(0, width // step, settle, 0)
    for move in moves:
        move.wait()


def middle_stage(scalars, mix_a, mix_b, own, cot, gain, w, split):
    halves, width, lanes = w.shape
    slabs, _, _, half = mix_a.shape
    ff = (lanes - width // halves) // 3
    blocks = width // 256
    peers = slabs * halves - 1
    vmem = pl.BlockSpec(memory_space=pltpu.VMEM)
    outside = pl.BlockSpec(memory_space=pl.ANY)
    out_shape = [
        jax.ShapeDtypeStruct((half, width), BF),
        jax.ShapeDtypeStruct((half, width), F32),
        jax.ShapeDtypeStruct(mix_a.shape, BF),
        jax.ShapeDtypeStruct(mix_a.shape, BF),
        jax.ShapeDtypeStruct((halves, width, split), BF),
    ]
    out_specs = [vmem] * 4 + [outside]
    if split < lanes:
        out_shape += [jax.ShapeDtypeStruct((halves, blocks // 2, 256, lanes - split), BF)] * 2
        out_specs += [outside] * 2
    flops = 2 * half * width * (9 * ff * halves + 3 * width)
    return pl.pallas_call(
        functools.partial(middle_kernel, ff, split),
        out_shape=out_shape,
        in_specs=[pl.BlockSpec(memory_space=pltpu.SMEM), vmem, vmem, outside, outside, vmem, outside],
        out_specs=out_specs,
        scratch_shapes=[
            pltpu.VMEM((halves, width, lanes), BF),
            pltpu.VMEM((halves, half, lanes), BF),
            pltpu.VMEM((width // halves, half), BF),
            pltpu.VMEM((half, width), F32),
            pltpu.VMEM((half, 128), F32),
            pltpu.VMEM((half, width), F32),
            pltpu.VMEM((half, width), BF),
            pltpu.VMEM((half, width), BF),
            pltpu.VMEM((half, width), BF),
            pltpu.VMEM((3, width, half), BF),
            pltpu.VMEM(mix_a.shape, BF),
            pltpu.VMEM(mix_a.shape, BF),
            pltpu.SemaphoreType.DMA((4 * halves,)),
            pltpu.SemaphoreType.DMA((blocks, halves, 2)),
            pltpu.SemaphoreType.DMA((2 * peers,)),
            pltpu.SemaphoreType.DMA((2 * peers,)),
            pltpu.SemaphoreType.DMA((2,)),
            pltpu.SemaphoreType.DMA((blocks, halves)),
            pltpu.SemaphoreType.DMA((blocks, halves)),
            pltpu.VMEM((half, width), BF),
            pltpu.VMEM((half, width), BF),
            pltpu.SemaphoreType.DMA((2,)),
        ],
        compiler_params=pltpu.CompilerParams(
            vmem_limit_bytes=58 << 20, collective_id=1, has_side_effects=True
        ),
        cost_estimate=pl.CostEstimate(
            flops=flops, bytes_accessed=4 * w.size + 16 * half * width, transcendentals=half * lanes
        ),
    )(scalars, mix_a, mix_b, own, cot, gain, w)


class LineSum:
    def __init__(self, source, held, slots, out, sems):
        self.source, self.held, self.slots, self.out = source, held, slots, out
        self.sum_send, self.sum_recv, self.out_send, self.out_recv = sems
        here = lax.axis_index("ctx")
        self.low = here < 2
        self.place = jnp.where(self.low, here, 3 - here)
        self.inward = jnp.where(self.low, here + 1, here - 1)
        self.outward = jnp.where(self.low, here - 1, here + 1)
        self.size = out.shape[0] // 4

    def number(self, part):
        return jnp.where(self.low, part, 3 - part)

    def part(self, ref, part):
        at = pl.multiple_of(self.number(part) * self.size, self.size)
        return ref.at[pl.ds(at, self.size), :]

    def read(self, ref, part):
        at = pl.multiple_of(self.number(part) * self.size, self.size)
        return ref[pl.ds(at, self.size), :].astype(F32)

    def write(self, ref, part, value):
        at = pl.multiple_of(self.number(part) * self.size, self.size)
        ref[pl.ds(at, self.size), :] = value.astype(BF)

    def copy(self, source, target, send, recv, place):
        return pltpu.make_async_remote_copy(
            src_ref=source, dst_ref=target, send_sem=send, recv_sem=recv,
            device_id={"ctx": place}, device_id_type=pl.DeviceIdType.MESH,
        )

    def took(self, slot):
        ref = self.slots.at[slot]
        self.copy(ref, ref, self.sum_send.at[0], self.sum_recv.at[slot], self.inward).wait_recv()
        return self.slots[slot].astype(F32)

    def begin(self):
        @pl.when(self.place == 0)
        def _():
            for k in range(3):
                self.copy(
                    self.part(self.source, 3 - k), self.slots.at[k],
                    self.sum_send.at[k], self.sum_recv.at[k], self.inward,
                ).start()

    def left(self, k):
        self.copy(
            self.slots.at[0], self.slots.at[0],
            self.sum_send.at[k], self.sum_recv.at[0], self.inward,
        ).wait_send()

    def first(self, k):
        @pl.when(self.place == 1)
        def _():
            self.write(self.held, 3 - k, self.read(self.source, 3 - k) + self.took(k))
            self.copy(
                self.part(self.held, 3 - k), self.slots.at[3 + k],
                self.sum_send.at[k], self.sum_recv.at[3 + k], self.inward,
            ).start()

    def second(self):
        @pl.when(self.place == 1)
        def _():
            self.write(self.held, 0, self.read(self.source, 0) + self.took(3))
            self.copy(
                self.part(self.held, 0), self.slots.at[3],
                self.sum_send.at[2], self.sum_recv.at[3], self.outward,
            ).start()

    def give(self, part, send, place):
        ref = self.part(self.out, part)
        return self.copy(
            ref, ref, self.out_send.at[send], self.out_recv.at[self.number(part)], place
        )

    def final(self):
        @pl.when(self.place == 1)
        def _():
            self.write(self.out, 1, self.read(self.source, 1) + self.took(2) + self.took(4))
            self.give(1, 0, self.inward).start()
            self.give(1, 1, self.outward).start()

        @pl.when(self.place == 0)
        def _():
            self.write(self.out, 0, self.read(self.source, 0) + self.took(3))
            self.give(0, 0, self.inward).start()

    def forward(self):
        @pl.when(self.place == 1)
        def _():
            for k, (part, place) in enumerate(((0, self.inward), (2, self.outward), (3, self.outward))):
                self.give(part, 2 + k, place).wait_recv()
                self.give(part, 2 + k, place).start()

    def end(self):
        @pl.when(self.place == 0)
        def _():
            for k in range(3):
                self.left(k)
            self.give(0, 0, self.inward).wait_send()
            for part in (1, 2, 3):
                self.give(part, 0, self.inward).wait_recv()

        @pl.when(self.place == 1)
        def _():
            for k in range(3):
                self.left(k)
            for k in range(5):
                self.give(1, k, self.inward).wait_send()


def tail_kernel(
    back_a, back_b, some, rest, normed, weights, own_hbm, gain, dmid,
    grad_out, some_out, rest_out, qa_out, qb_out,
    turned, some_held, some_slots, rest_held, rest_slots,
    local, crossed, column_sum, columned, q_src, q_held, q_slots, theirs, got_theirs, mine,
    core_send, core_recv, col_send, col_recv,
    row_send, row_recv, out_send, out_recv, *line_sems,
):
    here, line, place = lax.axis_index("ctx"), lax.axis_index("tp"), lax.axis_index("fsdp")
    core, column = lax.rem(place, 2), place // 2
    sibling = {"fsdp": place + 1 - 2 * core}
    beside = {"fsdp": lax.rem(place + 2, 4)}
    across = {"tp": 1 - line}
    others = [{"ctx": lax.rem(here + k, 4)} for k in range(1, 4)]
    mesh_id = pl.DeviceIdType.MESH
    barrier = pltpu.get_barrier_semaphore()
    for device in (*others, sibling, beside, across):
        pl.semaphore_signal(barrier, inc=1, device_id=device, device_id_type=mesh_id)
    pl.semaphore_wait(barrier, 6)

    def remote(source, target, send, recv, device):
        return pltpu.make_async_remote_copy(
            src_ref=source, dst_ref=target, send_sem=send, recv_sem=recv,
            device_id=device, device_id_type=mesh_id,
        )

    rows = normed.shape[0]
    half = rows // 2
    depth = 256
    own, own_sem, *line_sems = line_sems
    load = pltpu.make_async_copy(
        own_hbm.at[pl.ds(pl.multiple_of(line * half, half), half), :], own, own_sem
    )
    load.start()
    a, b, qa, qb = (
        LineSum(src, held, slots, out, line_sems[4 * k : 4 * k + 4])
        for k, (src, held, slots, out) in enumerate(
            (
                (some, some_held, some_slots, some_out),
                (rest, rest_held, rest_slots, rest_out),
                (q_src.at[0], q_held.at[0], q_slots.at[0], qa_out),
                (q_src.at[1], q_held.at[1], q_slots.at[1], qb_out),
            )
        )
    )
    a.begin()

    def weight_gradient(h, grads):
        def step(n, _):
            cut = pl.ds(pl.multiple_of(n * depth, depth), depth)
            value = mm(grads[...], normed[:, cut], NN).astype(BF)
            local[h, lax.rem(n, 2), n // 2] = value
            return 0

        lax.fori_loop(0, 4, step, 0)
        move = remote(
            local.at[h, 1 - core], crossed.at[h], core_send.at[h], core_recv.at[h], sibling
        )
        move.start()
        return move

    def column_step(h, move):
        move.wait_recv()
        for x in range(2):
            column_sum[h, x] = (
                local[h, core, x].astype(F32) + crossed[h, x].astype(F32)
            ).astype(BF)
        move = remote(
            column_sum.at[h, 1 - column], columned.at[h], col_send.at[h], col_recv.at[h], beside
        )
        move.start()
        return move

    def column_end(h, move):
        move.wait_recv()
        q_src[h] = (column_sum[h, column].astype(F32) + columned[h].astype(F32)).astype(BF)

    def turn(h, grads):
        for k in range(0, grads.shape[0], 128):
            at = h * grads.shape[0] + k
            turned[:, at : at + 128] = grads[k : k + 128, :].astype(F32).T.astype(BF)

    pieces = 2
    piece = half // pieces
    sent_rows = []
    sent_out = []
    mine_start = pl.multiple_of(line * half, half)

    def make_theirs(k):
        cut = slice(k * piece, (k + 1) * piece)
        start = pl.multiple_of((1 - line) * half + k * piece, piece)

        def make(n, _):
            wide = pl.ds(pl.multiple_of(n * depth, depth), depth)
            value = mm(turned[pl.ds(start, piece), :], weights[:, wide], NN)
            theirs[cut, wide] = value.astype(BF)
            return 0

        lax.fori_loop(0, 4, make, 0)
        move = remote(theirs.at[cut], got_theirs.at[cut], row_send.at[k], row_recv.at[k], across)
        move.start()
        sent_rows.append(move)

    def make_mine(n, _):
        wide = pl.ds(pl.multiple_of(n * depth, depth), depth)
        mine[:, wide] = mm(turned[pl.ds(mine_start, half), :], weights[:, wide], NN)
        return 0

    def finish_rows(k):
        small = 64
        if k == 0:
            load.wait()
        sent_rows[k].wait_recv()

        def back(r, _):
            at = pl.multiple_of(k * piece + r * small, small)
            cut = pl.ds(at, small)
            values = own[cut, :].astype(F32)
            inverse = lax.rsqrt(jnp.mean(values * values, axis=1, keepdims=True) + EPSILON)
            scaled = values * inverse
            d_scaled = (mine[cut, :] + got_theirs[cut, :].astype(F32)) * gain[...]
            mean = jnp.mean(d_scaled * scaled, axis=1, keepdims=True)
            total = dmid[cut, :] + inverse * (d_scaled - scaled * mean)
            grad_out[pl.ds(pl.multiple_of(line * half + at, small), small), :] = total.astype(BF)
            return 0

        lax.fori_loop(0, piece // small, back, 0)
        ref = grad_out.at[pl.ds(pl.multiple_of(line * half + k * piece, piece), piece), :]
        move = remote(ref, ref, out_send.at[k], out_recv.at[k], across)
        move.start()
        sent_out.append(move)

    b.begin()
    turn(0, back_a)
    turn(1, back_b)
    make_theirs(0)
    core_a = weight_gradient(0, back_a)
    a.first(0)
    make_theirs(1)
    core_b = weight_gradient(1, back_b)
    a.first(1)
    col_a = column_step(0, core_a)
    lax.fori_loop(0, 4, make_mine, 0)
    a.second()
    col_b = column_step(1, core_b)
    b.first(0)
    a.final()
    b.first(1)
    finish_rows(0)
    b.second()
    a.forward()
    column_end(0, col_a)
    qa.begin()
    b.final()
    finish_rows(1)
    column_end(1, col_b)
    qb.begin()
    qa.first(0)
    qa.first(1)
    b.forward()
    qb.first(0)
    qb.first(1)
    qa.second()
    qa.final()
    qb.second()
    qb.final()
    qa.forward()
    qb.forward()
    for run in (a, b, qa, qb):
        run.end()
    for move in (core_a, core_b, col_a, col_b, *sent_rows):
        move.wait_send()
    for k, move in enumerate(sent_out):
        move.wait_send()
        ref = grad_out.at[pl.ds(pl.multiple_of((1 - line) * half + k * piece, piece), piece), :]
        remote(ref, ref, out_send.at[k], out_recv.at[k], across).wait_recv()


def tail_stage(back_a, back_b, some, rest, normed, weights, own, gain, dmid):
    rows, width = normed.shape
    half = rows // 2
    lanes_a, lanes_b = some.shape[1], rest.shape[1]
    wide = back_a.shape[0]
    vmem = pl.BlockSpec(memory_space=pltpu.VMEM)
    dma = pltpu.SemaphoreType.DMA
    return pl.pallas_call(
        tail_kernel,
        out_shape=(
            jax.ShapeDtypeStruct((rows, width), BF),
            jax.ShapeDtypeStruct((256, lanes_a), BF),
            jax.ShapeDtypeStruct((256, lanes_b), BF),
            jax.ShapeDtypeStruct((wide, 256), BF),
            jax.ShapeDtypeStruct((wide, 256), BF),
        ),
        in_specs=[vmem] * 6 + [pl.BlockSpec(memory_space=pl.ANY)] + [vmem] * 2,
        out_specs=(vmem,) * 5,
        scratch_shapes=[
            pltpu.VMEM((rows, 2 * wide), BF),
            pltpu.VMEM((256, lanes_a), BF),
            pltpu.VMEM((5, 64, lanes_a), BF),
            pltpu.VMEM((256, lanes_b), BF),
            pltpu.VMEM((5, 64, lanes_b), BF),
            pltpu.VMEM((2, 2, 2, wide, 256), BF),
            pltpu.VMEM((2, 2, wide, 256), BF),
            pltpu.VMEM((2, 2, wide, 256), BF),
            pltpu.VMEM((2, wide, 256), BF),
            pltpu.VMEM((2, wide, 256), BF),
            pltpu.VMEM((2, wide, 256), BF),
            pltpu.VMEM((2, 5, wide // 4, 256), BF),
            pltpu.VMEM((half, width), BF),
            pltpu.VMEM((half, width), BF),
            pltpu.VMEM((half, width), F32),
            dma((2,)), dma((2,)), dma((2,)), dma((2,)),
            dma((2,)), dma((2,)), dma((2,)), dma((2,)),
            pltpu.VMEM((half, width), BF), dma,
        ]
        + [dma((3,)), dma((5,)), dma((5,)), dma((4,))] * 4,
        compiler_params=pltpu.CompilerParams(
            vmem_limit_bytes=56 << 20, collective_id=2, has_side_effects=True
        ),
        cost_estimate=pl.CostEstimate(
            flops=8 * rows * width * wide, bytes_accessed=40 << 20, transcendentals=0
        ),
    )(back_a, back_b, some, rest, normed, weights, own, gain, dmid)


def pack_kernel(gate, up, down, out, packed):
    ff = gate.shape[1]
    packed[:, 0:ff] = gate[...]
    packed[:, ff : 2 * ff] = up[...]
    packed[:, 2 * ff : 3 * ff] = down[...].astype(F32).T.astype(BF)
    packed[:, 3 * ff :] = out[...].astype(F32).T.astype(BF)


def pack_stage(gate, up, down, out):
    depth, ff = gate.shape
    vmem = pl.BlockSpec(memory_space=pltpu.VMEM)
    return pl.pallas_call(
        pack_kernel,
        out_shape=jax.ShapeDtypeStruct((depth, 3 * ff + out.shape[0]), BF),
        in_specs=[vmem] * 4,
        out_specs=vmem,
        compiler_params=pltpu.CompilerParams(vmem_limit_bytes=24 << 20),
        cost_estimate=pl.CostEstimate(flops=0, bytes_accessed=14 * depth * ff, transcendentals=0),
    )(gate, up, down, out)


def finish_kernel(
    some, rest, qa, qb, wq, wk, wv, gate_w, up_w, gains, grad_in,
    gate, up, down, out, qg, kg, vg, part, grad_out, sem,
):
    move = pltpu.make_async_copy(grad_in, grad_out, sem)
    move.start()
    ff = gate.shape[1]
    split = some.shape[1]
    low = split - ff
    high = ff - low

    def fold(values):
        total = values[:, 0:128]
        for at in range(128, values.shape[1], 128):
            total = total + values[:, at : at + 128]
        return total

    value = some[:, 0:ff].astype(F32)
    gate[...] = value
    two = fold(value * gate_w[...].astype(F32))
    value = some[:, ff:split].astype(F32)
    up[:, 0:low] = value
    two = two + fold(value * up_w[:, 0:low].astype(F32))
    value = rest[:, 0:high].astype(F32)
    up[:, low:ff] = value
    two = two + fold(value * up_w[:, low:ff].astype(F32))
    down[...] = rest[:, high : high + ff].astype(F32).T
    out[...] = rest[:, high + ff :].astype(F32).T
    one = jnp.zeros((gate.shape[0], 128), F32)
    for k, (target, weight) in enumerate(((qg, wq), (kg, wk), (vg, wv))):
        for z in range(qa.shape[0] // (3 * HD)):
            at = (3 * z + k) * HD
            value = jnp.concatenate([qa[at : at + HD, :], qb[at : at + HD, :]], axis=0)
            value = value.astype(F32).T
            cut = slice(2 * HD * z, 2 * HD * (z + 1))
            target[:, cut] = value
            one = one + value * weight[:, cut].astype(F32)
    part[...] = jnp.zeros_like(part)
    part[0:1] = jnp.sum(one.T, axis=0, keepdims=True) / gains[0:1]
    part[1:2] = jnp.sum(two.T, axis=0, keepdims=True) / gains[1:2]
    move.wait()


def finish_stage(some, rest, qa, qb, weights, gate_w, up_w, gains, grad):
    depth, ff = gate_w.shape
    inner = weights[0].shape[1]
    vmem = pl.BlockSpec(memory_space=pltpu.VMEM)
    outside = pl.BlockSpec(memory_space=pl.ANY)
    shape = jax.ShapeDtypeStruct
    return pl.pallas_call(
        finish_kernel,
        out_shape=(
            shape((depth, ff), F32), shape((depth, ff), F32), shape((ff, depth), F32),
            shape((inner, depth), F32), *[shape((depth, inner), F32)] * 3,
            shape((8, depth), F32), shape(grad.shape, BF),
        ),
        in_specs=[vmem] * 10 + [outside],
        out_specs=(vmem,) * 8 + (outside,),
        scratch_shapes=[pltpu.SemaphoreType.DMA],
        compiler_params=pltpu.CompilerParams(vmem_limit_bytes=40 << 20),
        cost_estimate=pl.CostEstimate(flops=0, bytes_accessed=16 << 20, transcendentals=0),
    )(some, rest, qa, qb, *weights, gate_w, up_w, gains, grad)


def normalize(values, gain):
    inverse = lax.rsqrt(jnp.mean(values * values, axis=-1, keepdims=True) + EPSILON)
    scaled = values * inverse
    return scaled, inverse, (scaled * gain).astype(BF)


def norm_back(d_normed, scaled, inverse, gain):
    d_scaled = d_normed * gain
    d_values = inverse * (d_scaled - scaled * jnp.mean(d_scaled * scaled, axis=-1, keepdims=True))
    return d_values


def rows_first(values):
    return with_layout_constraint(values, Layout(major_to_minor=tuple(range(values.ndim))))


def swap(values, axis, bit):
    count = lax.axis_size(axis)
    return lax.ppermute(values, axis, [(k, k ^ bit) for k in range(count)])


def both_halves(values):
    other = swap(values, "tp", 1)
    first = lax.axis_index("tp") == 0
    return jnp.concatenate([jnp.where(first, values, other), jnp.where(first, other, values)])


def shards(
    inputs,
    lengths,
    first_gain,
    query_weight,
    key_weight,
    value_weight,
    out_weight,
    second_gain,
    gate_weight,
    up_weight,
    down_weight,
    cotangent,
):
    slabs, halves, parts = lax.axis_size("ctx"), lax.axis_size("tp"), lax.axis_size("fsdp")
    rows, width = inputs.shape[1], inputs.shape[2]
    depth = query_weight.shape[0]
    group = query_weight.shape[1] // HD // slabs
    half = rows // halves
    ff = gate_weight.shape[1]
    everywhere = ("tp", "fsdp")
    side = lax.axis_index("tp") * half

    paired = parts == 4 and halves == 2 and slabs == 4 and group == 2
    w_rest = pack_stage(gate_weight, up_weight, down_weight, out_weight)
    w_rest = rows_first(lax.all_gather(rows_first(w_rest), everywhere, axis=0, tiled=True))
    w_rest = w_rest.reshape(halves, width, -1)
    qkv_width = slabs * 3 * HD

    if paired:
        gains_own = jnp.stack([first_gain.astype(F32), second_gain.astype(F32)])
        gains_own = jnp.concatenate([gains_own, jnp.zeros((6, depth), F32)])
        w_turned, normed_one, gains, *rest = front_stage(
            lengths, inputs[0], gains_own, query_weight, key_weight, value_weight, slabs, halves
        )
        gain_one, gain_two = gains[0], gains[1]
        qkv, arrived = rest[0:2], rest[2:4]
        saved = [(rest[4], rest[6]), (rest[5], rest[7])]
    else:
        gains = lax.all_gather(jnp.stack([first_gain, second_gain]), "fsdp", axis=1, tiled=True)
        gain_one, gain_two = gains[0].astype(F32), gains[1].astype(F32)
        stacked = jnp.stack(
            [w.reshape(depth, slabs, group, HD) for w in (query_weight, key_weight, value_weight)]
        ).transpose(1, 3, 2, 0, 4)
        w_qkv = lax.all_gather(
            stacked.reshape(depth, group * qkv_width), "fsdp", axis=0, tiled=True
        )
        w_heads = [w_qkv[:, h * qkv_width : (h + 1) * qkv_width] for h in range(group)]
        _, _, normed_one = normalize(inputs[0].astype(F32), gain_one)
        qkv = []
        for h in range(group):
            part = mm(w_heads[h], normed_one, (((0,), (1,)), ((), ()))).astype(BF)
            part = part.reshape(slabs, 3 * HD, rows)
            qkv.append(lax.all_to_all(part, "ctx", 0, 0, tiled=True))
        arrived, saved = [], []
        for h in range(group):
            mix, mix_full, lse = attend(lengths, qkv[h], halves, rows)
            saved.append((mix_full, lse))
            mix = mix.reshape(slabs * halves, HD, half)
            mix = lax.all_to_all(mix, ("ctx", "tp"), 0, 0, tiled=True)
            arrived.append(mix.reshape(slabs, halves, HD, half))

    scalars = jnp.stack([lengths[0], lax.axis_index("ctx") * rows + side])
    split = 2304 if paired else w_rest.shape[2]
    output, d_middle, *d_mix, = middle_stage(
        scalars, *arrived, inputs[0], cotangent[0], gain_two[None], w_rest, split
    )
    d_mix, (g_some, *g_rest) = d_mix[:2], d_mix[2:]
    output = both_halves(output)
    s_some = lax.psum_scatter(
        rows_first(g_some.reshape(halves * width, -1)), everywhere, scatter_dimension=0, tiled=True
    )
    s_some = rows_first(s_some)

    if paired:
        back_a, back_b, g_rest = back_stage(lengths, qkv, d_mix, saved, *g_rest)
        input_gradient, s_some, s_rest, *q_grads = tail_stage(
            back_a, back_b, s_some, g_rest, normed_one, w_turned, inputs[0], gain_one[None], d_middle
        )
        s_gate, s_up, s_down, s_out, *s_qkv, d_gains, input_gradient = finish_stage(
            s_some, s_rest, *q_grads, (query_weight, key_weight, value_weight), gate_weight,
            up_weight, gains_own, input_gradient,
        )
        d_gains = d_gains[0:2]
        d_gains = d_gains + swap(d_gains, "tp", 1)
    else:
        d_local = [
            attend_back(lengths, qkv[h], d_mix[h], *saved[h], 512) for h in range(group)
        ]
        d_qkv = [
            lax.all_to_all(d, "ctx", 0, 0, tiled=True).reshape(qkv_width, rows) for d in d_local
        ]
        d_normed_one = jnp.zeros((rows, width), F32)
        s_qkv = []
        for h in range(group):
            d_normed_one = d_normed_one + mm(d_qkv[h], w_heads[h], (((0,), (1,)), ((), ())))
            grad = mm(normed_one, d_qkv[h], (((0,), (1,)), ((), ()))).astype(BF)
            grad = lax.psum_scatter(grad, "fsdp", scatter_dimension=0, tiled=True)
            s_qkv.append(lax.psum(grad, "ctx").reshape(depth, slabs, 3, HD))
        d_normed_one = lax.psum_scatter(d_normed_one, "tp", scatter_dimension=0, tiled=True)
        own = lax.dynamic_slice_in_dim(inputs[0], side, half, 0)
        scaled_one, inverse_one, _ = normalize(own.astype(F32), gain_one)
        d_from_one = norm_back(d_normed_one, scaled_one, inverse_one, gain_one)
        input_gradient = lax.all_gather(
            (d_middle + d_from_one).astype(BF), "tp", axis=0, tiled=True
        )
        s_qkv = jnp.stack(s_qkv, axis=2).transpose(3, 0, 1, 2, 4)
        s_qkv = s_qkv.reshape(3, depth, slabs * group * HD).astype(F32)
        s_all = lax.psum(s_some, "ctx").astype(F32)
        d_gain_one = sum(
            jnp.sum(w.astype(F32) * s, axis=1)
            for w, s in zip((query_weight, key_weight, value_weight), s_qkv)
        ) / first_gain.astype(F32)
        d_gain_two = (
            jnp.sum(gate_weight.astype(F32) * s_all[:, :ff], axis=1)
            + jnp.sum(up_weight.astype(F32) * s_all[:, ff : 2 * ff], axis=1)
        ) / second_gain.astype(F32)
        d_gains = jnp.stack([d_gain_one, d_gain_two])
        d_gains = lax.psum(d_gains, "tp")
        s_gate, s_up, s_down, s_out = (
            s_all[:, :ff], s_all[:, ff : 2 * ff], s_all[:, 2 * ff : 3 * ff].T, s_all[:, 3 * ff :].T
        )

    return (
        output[None],
        input_gradient[None],
        d_gains[0],
        s_qkv[0],
        s_qkv[1],
        s_qkv[2],
        s_out,
        d_gains[1],
        s_gate,
        s_up,
        s_down,
    )


def solution(mesh):
    rows = P("fsdp", "ctx", None)
    gain = P("fsdp")
    inward = P("fsdp", "tp")
    outward = P("tp", "fsdp")
    return jax.shard_map(
        shards,
        mesh=mesh,
        in_specs=(
            rows, gain, gain, inward, inward, inward, outward, gain, inward, inward, outward, rows,
        ),
        out_specs=(
            rows, rows, gain, inward, inward, inward, outward, gain, inward, inward, outward,
        ),
        check_vma=False,
    )
```

```python
import functools

import jax
import jax.numpy as jnp
from jax import lax
from jax.experimental import pallas as pl
from jax.experimental.pallas import tpu as pltpu
from jax.experimental.layout import Layout, with_layout_constraint
from jax.sharding import PartitionSpec as P

HD = 64
EPSILON = 1e-05
MASKED = -1000000000.0
NN = (((1,), (0,)), ((), ()))
NT = (((1,), (1,)), ((), ()))
TN = (((0,), (0,)), ((), ()))
BF = jnp.bfloat16
F32 = jnp.float32


def mm(left, right, dims):
    return lax.dot_general(left, right, dims, preferred_element_type=F32)


def spread_keys(keys, start, length):
    rows = keys.shape[0]
    pos = start + lax.broadcasted_iota(jnp.int32, (rows, HD), 0)
    lane = lax.broadcasted_iota(jnp.int32, (rows, HD), 1)
    bias = jnp.where((lane == 0) & (pos >= length), MASKED, 0.0)
    return jnp.concatenate([keys, bias], axis=1).astype(BF)


def spread_queries(queries):
    row = lax.broadcasted_iota(jnp.int32, queries.shape, 0)
    ones = jnp.where(row == 0, 1.0, 0.0)
    return jnp.concatenate([queries * HD**-0.5, ones], axis=0).astype(BF)


def attend_rows(tile, length, qkv, kx, qx, vx, emit):
    slabs, _, rows = qkv.shape
    per = rows // tile
    blocks = slabs * per
    for z in range(slabs):
        keys = qkv[z, HD : 2 * HD, :].astype(F32).T
        kx[z * rows : (z + 1) * rows, :] = spread_keys(keys, z * rows, length)
        queries = spread_queries(qkv[z, 0:HD, :].astype(F32))
        for b in range(per):
            cut = slice(b * tile, (b + 1) * tile)
            qx[z * per + b] = queries[:, cut]
            vx[z * per + b] = qkv[z, 2 * HD : 3 * HD, cut]
    later = lax.broadcasted_iota(jnp.int32, (tile, tile), 0) > lax.broadcasted_iota(
        jnp.int32, (tile, tile), 1
    )

    def query_block(i, _):
        queries = qx[i]

        def step(j, carry, masked):
            highest, total, mix = carry
            keys = kx[pl.ds(pl.multiple_of(j * tile, tile), tile), :]
            scores = mm(keys, queries, NN)
            if masked:
                scores = jnp.where(later, MASKED, scores)
            new = jnp.maximum(highest, jnp.max(scores, axis=0, keepdims=True))
            scale = jnp.exp(highest - new)
            probs = jnp.exp(scores - new)
            total = total * scale + jnp.sum(probs, axis=0, keepdims=True)
            mix = mix * scale + mm(vx[j], probs.astype(BF), NN)
            return new, total, mix

        first = (
            jnp.full((1, tile), -jnp.inf, F32),
            jnp.zeros((1, tile), F32),
            jnp.zeros((HD, tile), F32),
        )
        carry = lax.fori_loop(0, i, lambda j, c: step(j, c, False), first)
        highest, total, mix = step(i, carry, True)
        emit(i, mix / total, highest + jnp.log(total))
        return 0

    lax.fori_loop(0, blocks, query_block, 0)


def attend_kernel(tile, len_ref, qkv, o_ref, of_ref, lse_ref, kx, qx, vx):
    rows = qkv.shape[2]
    halves = o_ref.shape[1]
    half = rows // halves

    def emit(i, mix, lse):
        of_ref[i] = mix
        lse_ref[i] = lse
        for t in range(halves):
            o_ref[i, t] = mix[:, t * half : (t + 1) * half].astype(BF)

    attend_rows(tile, len_ref[0], qkv, kx, qx, vx, emit)


def front_kernel(
    len_ref, x, gains_own, wq, wk, wv,
    wt_hbm, normed_hbm, gains, qkv_a_hbm, qkv_b_hbm, mix_a, mix_b, of_a_hbm, of_b_hbm,
    lse_a_hbm, lse_b_hbm,
    wt, normed, qkv_a, qkv_b, of_a, of_b, lse_a, lse_b, out_sems, packed, parts, mixed, kx, qx, vx,
    gain_send, gain_recv, w_send, w_recv, part_send, part_recv, part_local,
    mix_send, mix_recv, mix_local,
):
    here, line, place = lax.axis_index("ctx"), lax.axis_index("tp"), lax.axis_index("fsdp")
    core, column = lax.rem(place, 2), place // 2
    pair = place + 1 - 2 * core
    other = lax.rem(place + 2, 4)
    mesh_id = pl.DeviceIdType.MESH
    slabs, halves = mix_a.shape[0], mix_a.shape[1]
    rows, width = x.shape
    half = rows // halves
    wide = slabs * 3 * HD
    depth = wq.shape[0]
    peers = [(dz, dt) for dz in range(slabs) for dt in range(halves) if dz or dt]

    def peer(dz, dt):
        return lax.rem(here + dz, slabs), lax.rem(line + dt, halves)

    barrier = pltpu.get_barrier_semaphore()
    for dz, dt in peers:
        z, t = peer(dz, dt)
        pl.semaphore_signal(barrier, inc=1, device_id={"ctx": z, "tp": t}, device_id_type=mesh_id)
    for device in (pair, other):
        pl.semaphore_signal(barrier, inc=1, device_id={"fsdp": device}, device_id_type=mesh_id)
    for q, w in enumerate((wq, wk, wv)):
        flat = w[...].astype(F32).T.astype(BF)
        for z in range(slabs):
            for h in range(2):
                at = (2 * z + h) * HD
                packed[h, (3 * z + q) * HD : (3 * z + q + 1) * HD, :] = flat[at : at + HD]

    def remote(source, target, send, recv, device):
        return pltpu.make_async_remote_copy(
            src_ref=source, dst_ref=target, send_sem=send, recv_sem=recv,
            device_id=device, device_id_type=mesh_id,
        )

    def lanes(index):
        return pl.ds(pl.multiple_of(index * depth, depth), depth)

    def weight(h, index):
        return wt.at[h * wide : (h + 1) * wide, lanes(index)]

    gains[:, lanes(place)] = gains_own[...]
    for h in range(2):
        wt[h * wide : (h + 1) * wide, lanes(place)] = packed[h]
    pl.semaphore_wait(barrier, len(peers) + 2)
    sent = []

    def launch(move):
        move.start()
        sent.append(move)
        return move

    for k, device in enumerate((pair, other)):
        launch(
            remote(
                gains_own, gains.at[:, lanes(place)], gain_send.at[k], gain_recv.at[k], {"fsdp": device}
            )
        )
    for h in range(2):
        for k, device in ((1, other), (0, pair)):
            launch(
                remote(
                    packed.at[h], weight(h, place), w_send.at[h, k], w_recv.at[h, k], {"fsdp": device}
                )
            )

    def arrived(ref, sem):
        remote(ref, ref, gain_send.at[0], sem, {"fsdp": pair}).wait_recv()

    arrived(gains.at[:, lanes(other)], gain_recv.at[1])
    launch(
        remote(
            gains.at[:, lanes(other)], gains.at[:, lanes(other)], gain_send.at[2], gain_recv.at[2],
            {"fsdp": pair},
        )
    )
    far = lax.rem(pair + 2, 4)
    arrived(gains.at[:, lanes(pair)], gain_recv.at[0])
    arrived(gains.at[:, lanes(far)], gain_recv.at[2])
    small = 64

    def norm(r, _):
        cut = pl.ds(pl.multiple_of(r * small, small), small)
        values = x[cut, :].astype(F32)
        inverse = lax.rsqrt(jnp.mean(values * values, axis=1, keepdims=True) + EPSILON)
        normed[cut, :] = (values * inverse * gains[0:1, :]).astype(BF)
        return 0

    lax.fori_loop(0, rows // small, norm, 0)
    kept = []

    def keep(source, target):
        move = pltpu.make_async_copy(source, target, out_sems.at[len(kept)])
        move.start()
        kept.append(move)

    keep(normed, normed_hbm)
    queues = (qkv_a, qkv_b)
    waits = []
    for h in range(2):
        arrived(weight(h, other), w_recv.at[h, 1])
        launch(
            remote(
                weight(h, other), weight(h, other), w_send.at[h, 2], w_recv.at[h, 2], {"fsdp": pair}
            )
        )
    for h in range(2):
        arrived(weight(h, pair), w_recv.at[h, 0])
        arrived(weight(h, far), w_recv.at[h, 2])

        def project(n, _):
            cut = pl.ds(pl.multiple_of(n * 256, 256), 256)
            value = mm(wt[h * wide : (h + 1) * wide, :], normed[cut, :], NT).astype(BF)
            for z in range(slabs):
                parts[h, z, :, cut] = value[z * 3 * HD : (z + 1) * 3 * HD]
            return 0

        lax.fori_loop(0, rows // 256, project, 0)
        for k in range(1, slabs):
            z = lax.rem(here + k, slabs)
            waits.append(
                launch(
                    remote(
                        parts.at[h, z], queues[h].at[here], part_send.at[h, k], part_recv.at[h, k],
                        {"ctx": z},
                    )
                )
            )
        stays = pltpu.make_async_copy(parts.at[h, here], queues[h].at[here], part_local.at[h])
        stays.start()
        waits.append(stays)

    keep(wt, wt_hbm)
    for h, (qkv, mix_ref, of_ref, lse_ref) in enumerate(
        ((qkv_a, mix_a, of_a, lse_a), (qkv_b, mix_b, of_b, lse_b))
    ):
        for move in waits[h * slabs : (h + 1) * slabs - 1]:
            move.wait_recv()
        waits[(h + 1) * slabs - 1].wait()
        keep(qkv, (qkv_a_hbm, qkv_b_hbm)[h])

        def emit(i, mix, lse):
            of_ref[i] = mix
            lse_ref[i] = lse
            for t in range(halves):
                mixed[h, i, t] = mix[:, t * half : (t + 1) * half].astype(BF)
                stay = (i == here) & (line == t)

                @pl.when(stay)
                def _():
                    pltpu.make_async_copy(
                        mixed.at[h, i, t], mix_ref.at[here, line], mix_local.at[h]
                    ).start()

                @pl.when(jnp.logical_not(stay))
                def _():
                    remote(
                        mixed.at[h, i, t], mix_ref.at[here, line], mix_send.at[h, i, t],
                        mix_recv.at[h, here, line], {"ctx": i, "tp": t},
                    ).start()

        attend_rows(rows, len_ref[0], qkv, kx, qx, vx, emit)
        keep(of_ref, (of_a_hbm, of_b_hbm)[h])
        keep(lse_ref, (lse_a_hbm, lse_b_hbm)[h])

    for move in sent:
        move.wait_send()
    for move in kept:
        move.wait()
    for h, mix_ref in enumerate((mix_a, mix_b)):
        pltpu.make_async_copy(mixed.at[h, here, line], mix_ref.at[here, line], mix_local.at[h]).wait()
        for dz, dt in peers:
            z, t = peer(dz, dt)
            remote(
                mixed.at[h, z, t], mix_ref.at[z, t], mix_send.at[h, z, t], mix_recv.at[h, z, t],
                {"ctx": z, "tp": t},
            ).wait()


def front_stage(length, x, gains, wq, wk, wv, slabs, halves):
    rows, width = x.shape
    half = rows // halves
    wide = slabs * 3 * HD
    total = slabs * rows
    work = total * (total + rows) // 2
    vmem = pl.BlockSpec(memory_space=pltpu.VMEM)
    outside = pl.BlockSpec(memory_space=pltpu.HBM)
    dma = pltpu.SemaphoreType.DMA
    shape = jax.ShapeDtypeStruct
    return pl.pallas_call(
        front_kernel,
        out_shape=(
            shape((2 * wide, width), BF),
            shape((rows, width), BF),
            shape((8, width), F32),
            *[shape((slabs, 3 * HD, rows), BF)] * 2,
            *[shape((slabs, halves, HD, half), BF)] * 2,
            *[shape((slabs, HD, rows), F32)] * 2,
            *[shape((slabs, 1, rows), F32)] * 2,
        ),
        in_specs=[pl.BlockSpec(memory_space=pltpu.SMEM)] + [vmem] * 5,
        out_specs=(outside, outside, vmem, *[outside] * 8),
        scratch_shapes=[
            pltpu.VMEM((2 * wide, width), BF),
            pltpu.VMEM((rows, width), BF),
            *[pltpu.VMEM((slabs, 3 * HD, rows), BF)] * 2,
            *[pltpu.VMEM((slabs, HD, rows), F32)] * 2,
            *[pltpu.VMEM((slabs, 1, rows), F32)] * 2,
            dma((8,)),
            pltpu.VMEM((2, wide, wq.shape[0]), BF),
            pltpu.VMEM((2, slabs, 3 * HD, rows), BF),
            pltpu.VMEM((2, slabs, halves, HD, half), BF),
            pltpu.VMEM((total, 2 * HD), BF),
            pltpu.VMEM((slabs, 2 * HD, rows), BF),
            pltpu.VMEM((slabs, HD, rows), BF),
            dma((3,)), dma((3,)), dma((2, 3)), dma((2, 3)),
            dma((2, slabs)), dma((2, slabs)), dma((2,)),
            dma((2, slabs, halves)), dma((2, slabs, halves)), dma((2,)),
        ],
        compiler_params=pltpu.CompilerParams(
            vmem_limit_bytes=60 << 20, collective_id=3, has_side_effects=True
        ),
        cost_estimate=pl.CostEstimate(
            flops=2 * work * 256 * 4, bytes_accessed=20 << 20, transcendentals=2 * work
        ),
    )(length, x, gains, wq, wk, wv)


def attend(length, qkv, halves, tile):
    slabs, _, rows = qkv.shape
    total = slabs * rows
    tile = min(tile, rows)
    work = total * (total + tile) // 2
    vmem = pl.BlockSpec(memory_space=pltpu.VMEM)
    return pl.pallas_call(
        functools.partial(attend_kernel, tile),
        out_shape=(
            jax.ShapeDtypeStruct((slabs, halves, HD, rows // halves), BF),
            jax.ShapeDtypeStruct((slabs, HD, rows), F32),
            jax.ShapeDtypeStruct((slabs, 1, rows), F32),
        ),
        in_specs=[pl.BlockSpec(memory_space=pltpu.SMEM), vmem],
        out_specs=(vmem, vmem, vmem),
        scratch_shapes=[
            pltpu.VMEM((total, 2 * HD), BF),
            pltpu.VMEM((total // tile, 2 * HD, tile), BF),
            pltpu.VMEM((total // tile, HD, tile), BF),
        ],
        compiler_params=pltpu.CompilerParams(vmem_limit_bytes=60 << 20),
        cost_estimate=pl.CostEstimate(
            flops=work * 256 * 4, bytes_accessed=qkv.size * 4, transcendentals=work
        ),
    )(length, qkv)


def attend_back_rows(tile, length, qkv, do_ref, of_ref, lse_ref, out, scratch, emit):
    kx, qx, vx, kt, dox, dq, st = scratch
    slabs, _, rows = qkv.shape
    halves, half = do_ref.shape[1], do_ref.shape[3]
    per = rows // tile
    blocks = slabs * per
    for z in range(slabs):
        keys = qkv[z, HD : 2 * HD, :]
        kx[z * rows : (z + 1) * rows, :] = spread_keys(keys.astype(F32).T, z * rows, length)
        queries = spread_queries(qkv[z, 0:HD, :].astype(F32))
        values = qkv[z, 2 * HD : 3 * HD, :].astype(F32).T
        vx[z * rows : (z + 1) * rows, :] = jnp.concatenate(
            [values, jnp.zeros((rows, HD), F32)], axis=1
        ).astype(BF)
        d_mix = jnp.concatenate([do_ref[z, t] for t in range(halves)], axis=1)
        delta = jnp.sum(d_mix.astype(F32) * of_ref[z], axis=0, keepdims=True)
        for b in range(per):
            cut = slice(b * tile, (b + 1) * tile)
            n = z * per + b
            qx[n] = queries[:, cut]
            kt[n] = keys[:, cut]
            dox[n, 0:HD] = d_mix[:, cut]
            dox[n, HD : 2 * HD] = jnp.zeros((HD, tile), BF)
            st[n, 0:1] = lse_ref[z, :, cut]
            st[n, 1:2] = delta[:, cut]
    dq[...] = jnp.zeros_like(dq)
    later = lax.broadcasted_iota(jnp.int32, (tile, tile), 0) > lax.broadcasted_iota(
        jnp.int32, (tile, tile), 1
    )

    def key_block(j, _):
        here = pl.ds(pl.multiple_of(j * tile, tile), tile)
        keys = kx[here, :]
        values = vx[here, :]

        def step(i, carry, masked):
            dk, dv = carry
            scores = mm(keys, qx[i], NN)
            if masked:
                scores = jnp.where(later, MASKED, scores)
            probs = jnp.exp(scores - st[i, 0:1])
            d_probs = mm(values, dox[i], NN)
            d_scores = (probs * (d_probs - st[i, 1:2])).astype(BF)
            dv = dv + mm(dox[i, 0:HD], probs.astype(BF), NT)
            dk = dk + mm(qx[i, 0:HD], d_scores, NT)
            dq[i] += mm(kt[j], d_scores, NN)
            return dk, dv

        zero = jnp.zeros((HD, tile), F32)
        carry = step(j, (zero, zero), True)
        dk, dv = lax.fori_loop(j + 1, blocks, lambda i, c: step(i, c, False), carry)
        z = j // per
        cut = pl.ds(pl.multiple_of(lax.rem(j, per) * tile, tile), tile)
        out[z, 0:HD, cut] = (dq[j] * HD**-0.5).astype(BF)
        out[z, HD : 2 * HD, cut] = dk.astype(BF)
        out[z, 2 * HD : 3 * HD, cut] = dv.astype(BF)
        if emit is not None:

            @pl.when(lax.rem(j, per) == per - 1)
            def _():
                emit(z)

        return 0

    lax.fori_loop(0, blocks, key_block, 0)


def attend_back_scratch(slabs, rows, tile):
    total = slabs * rows
    blocks = total // tile
    return [
        pltpu.VMEM((total, 2 * HD), BF),
        pltpu.VMEM((blocks, 2 * HD, tile), BF),
        pltpu.VMEM((total, 2 * HD), BF),
        pltpu.VMEM((blocks, HD, tile), BF),
        pltpu.VMEM((blocks, 2 * HD, tile), BF),
        pltpu.VMEM((blocks, HD, tile), F32),
        pltpu.VMEM((blocks, 8, tile), F32),
    ]


def attend_back_kernel(tile, len_ref, qkv, do_ref, of_ref, lse_ref, out, *scratch):
    attend_back_rows(tile, len_ref[0], qkv, do_ref, of_ref, lse_ref, out, scratch, None)


def back_kernel(
    tile, len_ref, qkv_a, qkv_b, do_a, do_b, of_a, of_b, lse_a, lse_b, keep_hbm, got_hbm,
    out_a, out_b, rest,
    local, keep, got, low_got, high_got, swapped, *refs,
):
    scratch, sems = refs[:7], refs[7:]
    (load_sems, grad_send, grad_recv, grad_local, low_send, low_recv, high_send, high_recv,
     swap_send, swap_recv) = sems
    here, line, place = lax.axis_index("ctx"), lax.axis_index("tp"), lax.axis_index("fsdp")
    column = place // 2
    beside = {"fsdp": lax.rem(place + 2, 4)}
    across = {"tp": 1 - line}
    mesh_id = pl.DeviceIdType.MESH
    slabs, block = qkv_a.shape[0], qkv_a.shape[1]
    loads = [
        pltpu.make_async_copy(source, target, load_sems.at[k])
        for k, (source, target) in enumerate(((keep_hbm, keep), (got_hbm, got)))
    ]
    for load in loads:
        load.start()
    others = [lax.rem(here + k, slabs) for k in range(1, slabs)]
    barrier = pltpu.get_barrier_semaphore()
    for device in (*[{"ctx": z} for z in others], beside, across):
        pl.semaphore_signal(barrier, inc=1, device_id=device, device_id_type=mesh_id)
    pl.semaphore_wait(barrier, slabs + 1)

    def remote(source, target, send, recv, device):
        return pltpu.make_async_remote_copy(
            src_ref=source, dst_ref=target, send_sem=send, recv_sem=recv,
            device_id=device, device_id_type=mesh_id,
        )

    outs = (out_a, out_b)

    def window(h, at):
        return outs[h].at[pl.ds(pl.multiple_of(at * block, block), block), :]

    def attend_head(h, qkv, do_ref, of_ref, lse_ref):
        def emit(z):
            @pl.when(z == here)
            def _():
                pltpu.make_async_copy(
                    local.at[h, z], window(h, here), grad_local.at[h]
                ).start()

            @pl.when(z != here)
            def _():
                remote(
                    local.at[h, z], window(h, here), grad_send.at[h, z], grad_recv.at[h, here],
                    {"ctx": z},
                ).start()

        attend_back_rows(
            tile, len_ref[0], qkv, do_ref, of_ref, lse_ref, local.at[h], scratch, emit
        )

    attend_head(0, qkv_a, do_a, of_a, lse_a)
    for load in loads:
        load.wait()
    cut = rest.shape[0] // 2
    for t in range(2):
        for x in range(2):
            keep[t, x] = (keep[t, x].astype(F32) + got[t, x].astype(F32)).astype(BF)
    moves = []
    for k in range(2):
        moves.append(
            remote(
                keep.at[1 - line, k, 0:cut], low_got.at[k], low_send.at[k], low_recv.at[k], across
            )
        )
        moves.append(
            remote(
                keep.at[k, 1 - column, cut : 2 * cut], high_got.at[k], high_send.at[k],
                high_recv.at[k], beside,
            )
        )
    for move in moves:
        move.start()
    attend_head(1, qkv_b, do_b, of_b, lse_b)
    for move in moves:
        move.wait_recv()
    low, high = slice(0, cut), slice(cut, 2 * cut)
    for k in range(2):
        keep[line, k, low] = (
            keep[line, k, low].astype(F32) + low_got[k].astype(F32)
        ).astype(BF)
        keep[k, column, high] = (
            keep[k, column, high].astype(F32) + high_got[k].astype(F32)
        ).astype(BF)
    swaps = [
        remote(
            keep.at[line, 1 - column, low], swapped.at[0], swap_send.at[0], swap_recv.at[0], beside
        ),
        remote(
            keep.at[1 - line, column, high], swapped.at[1], swap_send.at[1], swap_recv.at[1], across
        ),
    ]
    for move in swaps:
        move.start()
    for move in swaps:
        move.wait_recv()
    for k, part in enumerate((low, high)):
        rest[part] = (
            keep[line, column, part].astype(F32) + swapped[k].astype(F32)
        ).astype(BF)
    for h in range(2):
        pltpu.make_async_copy(local.at[h, here], window(h, here), grad_local.at[h]).wait()
        for z in others:
            remote(
                local.at[h, z], window(h, z), grad_send.at[h, z], grad_recv.at[h, z], {"ctx": z}
            ).wait()
    for move in (*moves, *swaps):
        move.wait_send()


def back_stage(length, qkv, d_mix, saved, keep, got):
    slabs, block, rows = qkv[0].shape
    tile = 512
    lanes = keep.shape[3]
    total = slabs * rows
    work = total * (total + tile) // 2
    vmem = pl.BlockSpec(memory_space=pltpu.VMEM)
    outside = pl.BlockSpec(memory_space=pl.ANY)
    dma = pltpu.SemaphoreType.DMA
    return pl.pallas_call(
        functools.partial(back_kernel, tile),
        out_shape=(
            jax.ShapeDtypeStruct((slabs * block, rows), BF),
            jax.ShapeDtypeStruct((slabs * block, rows), BF),
            jax.ShapeDtypeStruct((256, lanes), BF),
        ),
        in_specs=[pl.BlockSpec(memory_space=pltpu.SMEM)] + [vmem] * 8 + [outside] * 2,
        out_specs=(vmem,) * 3,
        scratch_shapes=[
            pltpu.VMEM((2, slabs, block, rows), BF),
            pltpu.VMEM(keep.shape, BF),
            pltpu.VMEM(keep.shape, BF),
            pltpu.VMEM((2, 128, lanes), BF),
            pltpu.VMEM((2, 128, lanes), BF),
            pltpu.VMEM((2, 128, lanes), BF),
            *attend_back_scratch(slabs, rows, tile),
            dma((2,)), dma((2, slabs)), dma((2, slabs)), dma((2,)),
            dma((2,)), dma((2,)), dma((2,)), dma((2,)), dma((2,)), dma((2,)),
        ],
        compiler_params=pltpu.CompilerParams(
            vmem_limit_bytes=60 << 20, collective_id=4, has_side_effects=True
        ),
        cost_estimate=pl.CostEstimate(
            flops=2 * work * 256 * 10, bytes_accessed=24 << 20, transcendentals=2 * work
        ),
    )(length, *qkv, *d_mix, *[m for m, _ in saved], *[l for _, l in saved], keep, got)


def attend_back(length, qkv, d_mix, mix, lse, tile):
    slabs, _, rows = qkv.shape
    total = slabs * rows
    tile = min(tile, rows)
    work = total * (total + tile) // 2
    vmem = pl.BlockSpec(memory_space=pltpu.VMEM)
    return pl.pallas_call(
        functools.partial(attend_back_kernel, tile),
        out_shape=jax.ShapeDtypeStruct((slabs, 3 * HD, rows), BF),
        in_specs=[pl.BlockSpec(memory_space=pltpu.SMEM), vmem, vmem, vmem, vmem],
        out_specs=vmem,
        scratch_shapes=attend_back_scratch(slabs, rows, tile),
        compiler_params=pltpu.CompilerParams(vmem_limit_bytes=60 << 20),
        cost_estimate=pl.CostEstimate(
            flops=work * 256 * 10, bytes_accessed=qkv.size * 8, transcendentals=work
        ),
    )(length, qkv, d_mix, mix, lse)


def widths(total, step):
    return [(at, min(step, total - at)) for at in range(0, total, step)]


def middle_kernel(
    ff, split, scal, mix_a_hbm, mix_b_hbm, own_hbm, cot_hbm, gain, w_hbm,
    out_ref, dmid_ref, got_a, got_b, *refs,
):
    n_out = 3 if split < w_hbm.shape[2] else 1
    grads = refs[:n_out]
    (w, acts, att_t, mid, scale, dn, normed_ref, branch_ref, dattn_ref, turned, do_a, do_b,
     sems, out_sems, send_sems, recv_sems, local_sems, core_send, core_recv,
     own, cot, mix_a, mix_b, row_sems) = refs[n_out:]
    slabs, halves, _, half = mix_a.shape
    width = own.shape[1]
    side = pl.ds(pl.multiple_of(lax.axis_index("tp") * half, half), half)
    row_loads = [
        pltpu.make_async_copy(source.at[side, :], target, row_sems.at[k])
        for k, (source, target) in enumerate(((own_hbm, own), (cot_hbm, cot)))
    ]
    mix_loads = [
        pltpu.make_async_copy(source, target, row_sems.at[2 + k])
        for k, (source, target) in enumerate(((mix_a_hbm, mix_a), (mix_b_hbm, mix_b)))
    ]
    for load in (*mix_loads, *row_loads):
        load.start()
    inner = width // halves
    base = 3 * ff
    lanes = base + inner
    here, line = lax.axis_index("ctx"), lax.axis_index("tp")
    core = lax.rem(lax.axis_index("fsdp"), 2)
    sibling = {"fsdp": lax.axis_index("fsdp") + 1 - 2 * core}
    barrier = pltpu.get_barrier_semaphore()
    peers = [(dz, dt) for dz in range(slabs) for dt in range(halves) if dz or dt]

    def peer(dz, dt):
        return lax.rem(here + dz, slabs), lax.rem(line + dt, halves)

    for dz, dt in peers:
        z, t = peer(dz, dt)
        pl.semaphore_signal(
            barrier, inc=1, device_id={"ctx": z, "tp": t}, device_id_type=pl.DeviceIdType.MESH
        )
    if n_out == 3:
        pl.semaphore_signal(
            barrier, inc=1, device_id=sibling, device_id_type=pl.DeviceIdType.MESH
        )
    cuts = [(t, base, inner) for t in range(halves)]
    cuts += [(t, k * ff, ff) for t in range(halves) for k in range(3)]
    loads = [
        pltpu.make_async_copy(
            w_hbm.at[t, :, at : at + n], w.at[t, :, at : at + n], sems.at[k]
        )
        for k, (t, at, n) in enumerate(cuts)
    ]
    for load in loads:
        load.start()
    length, first = scal[0], scal[1]
    step = 256
    rows = 64

    for load in mix_loads:
        load.wait()
    for t in range(halves):
        for z in range(slabs):
            at = z * 2 * HD
            att_t[at : at + HD, :] = mix_a[z, t]
            att_t[at + HD : at + 2 * HD, :] = mix_b[z, t]
        acts[t, :, base:lanes] = att_t[...].astype(F32).T.astype(BF)
    for k in range(halves):
        loads[k].wait()
    for load in row_loads:
        load.wait()

    def project(n, _):
        cut = pl.ds(pl.multiple_of(n * step, step), step)
        total = own[:, cut].astype(F32)
        for t in range(halves):
            total = total + mm(acts[t, :, base:lanes], w[t, cut, base:lanes], NT)
        mid[:, cut] = total
        return 0

    lax.fori_loop(0, width // step, project, 0)

    def row_mask(r):
        pos = first + r * rows + lax.broadcasted_iota(jnp.int32, (rows, 1), 0)
        return jnp.where(pos < length, 1.0, 0.0)

    def norm(r, _):
        cut = pl.ds(pl.multiple_of(r * rows, rows), rows)
        values = mid[cut, :]
        inverse = lax.rsqrt(jnp.mean(values * values, axis=1, keepdims=True) + EPSILON)
        scale[cut, :] = jnp.broadcast_to(inverse, (rows, 128))
        normed_ref[cut, :] = (values * inverse * gain[...]).astype(BF)
        branch_ref[cut, :] = (cot[cut, :].astype(F32) * row_mask(r)).astype(BF)
        return 0

    lax.fori_loop(0, half // rows, norm, 0)

    for t in range(halves):
        for k in range(3):
            loads[halves + 3 * t + k].wait()

        def columns(at, n):
            def cut(k):
                return pl.ds(pl.multiple_of(k * ff + at, 128), n)

            gate = mm(normed_ref[...], w[t, :, cut(0)], NN)
            upward = mm(normed_ref[...], w[t, :, cut(1)], NN)
            d_hidden = mm(branch_ref[...], w[t, :, cut(2)], NN)
            sig = 1.0 / (1.0 + jnp.exp(-gate))
            active = gate * sig
            acts[t, :, cut(2)] = (active * upward).astype(BF)
            acts[t, :, cut(0)] = (
                d_hidden * upward * sig * (1.0 + gate * (1.0 - sig))
            ).astype(BF)
            acts[t, :, cut(1)] = (d_hidden * active).astype(BF)

        def chunk(c, _):
            columns(c * step, step)
            return 0

        lax.fori_loop(0, ff // step, chunk, 0)
        if ff % step:
            columns(ff - ff % step, ff % step)

    def back(n, _):
        cut = pl.ds(pl.multiple_of(n * step, step), step)
        total = mid[:, cut]
        grad = jnp.zeros((half, step), F32)
        for t in range(halves):
            total = total + mm(acts[t, :, 2 * ff : base], w[t, cut, 2 * ff : base], NT)
            grad = grad + mm(acts[t, :, 0:ff], w[t, cut, 0:ff], NT)
            grad = grad + mm(acts[t, :, ff : 2 * ff], w[t, cut, ff : 2 * ff], NT)
        dmid_ref[:, cut] = total
        dn[:, cut] = grad
        return 0

    lax.fori_loop(0, width // step, back, 0)

    def finish(r, _):
        cut = pl.ds(pl.multiple_of(r * rows, rows), rows)
        mask = row_mask(r)
        out_ref[cut, :] = (dmid_ref[cut, :] * mask).astype(BF)
        inverse = scale[cut, 0:1]
        scaled = mid[cut, :] * inverse
        d_scaled = dn[cut, :] * gain[...]
        mean = jnp.mean(d_scaled * scaled, axis=1, keepdims=True)
        total = cot[cut, :].astype(F32) * mask + inverse * (d_scaled - scaled * mean)
        dmid_ref[cut, :] = total
        dattn_ref[cut, :] = total.astype(BF)
        return 0

    lax.fori_loop(0, half // rows, finish, 0)
    for t in range(halves):
        for z in range(0, slabs, 2):
            at = base + z * 2 * HD
            grad = mm(dattn_ref[...], w[t, :, at : at + 4 * HD], NN).T.astype(BF)
            for k in range(2):
                do_a[z + k, t] = grad[2 * k * HD : (2 * k + 1) * HD]
                do_b[z + k, t] = grad[(2 * k + 1) * HD : (2 * k + 2) * HD]

    pl.semaphore_wait(barrier, len(peers) + (n_out == 3))
    moves = []
    for k, (dz, dt) in enumerate(peers):
        z, t = peer(dz, dt)
        for h, (source, target) in enumerate(((do_a, got_a), (do_b, got_b))):
            move = pltpu.make_async_remote_copy(
                src_ref=source.at[z, t],
                dst_ref=target.at[here, line],
                send_sem=send_sems.at[2 * k + h],
                recv_sem=recv_sems.at[2 * k + h],
                device_id={"ctx": z, "tp": t},
                device_id_type=pl.DeviceIdType.MESH,
            )
            move.start()
            moves.append(move)
    for h, (source, target) in enumerate(((do_a, got_a), (do_b, got_b))):
        move = pltpu.make_async_copy(
            source.at[here, line], target.at[here, line], local_sems.at[h]
        )
        move.start()
        moves.append(move)

    regions = ((0, 2 * ff), (2 * ff, base), (base, lanes))

    def own_copy(n, t):
        cut = pl.ds(pl.multiple_of(n * step, step), step)
        return pltpu.make_async_copy(
            w.at[t, cut, split:lanes], grads[1].at[t, n // 2], out_sems.at[n, t, 1]
        )

    def core_copy(n, t):
        cut = pl.ds(pl.multiple_of(n * step, step), step)
        return pltpu.make_async_remote_copy(
            src_ref=w.at[t, cut, split:lanes], dst_ref=grads[2].at[t, n // 2],
            send_sem=core_send.at[n, t], recv_sem=core_recv.at[n, t],
            device_id=sibling, device_id_type=pl.DeviceIdType.MESH,
        )

    def some_copy(t):
        return pltpu.make_async_copy(
            w.at[t, :, 0:split], grads[0].at[t], out_sems.at[0, t, 0]
        )

    def store(t):
        if n_out == 1:
            return

        def rows_of(n, _):
            @pl.when(lax.rem(n, 2) == core)
            def _():
                own_copy(n, t).start()

            @pl.when(lax.rem(n, 2) != core)
            def _():
                core_copy(n, t).start()

            return 0

        lax.fori_loop(0, width // step, rows_of, 0)

    for k, ref in enumerate((normed_ref, branch_ref, dattn_ref)):
        for b in range(0, width, step):
            turned[k, b : b + step] = ref[:, b : b + step].astype(F32).T.astype(BF)
    for t in range(halves):

        def fill(k, at, n):
            cut = pl.ds(at, n)
            w[t, :, cut] = mm(turned[k], acts[t, :, cut], NN).astype(BF)

        def span(k, start, stop):
            def chunk(c, _):
                fill(k, pl.multiple_of(start + c * step, 128), step)
                return 0

            count = (stop - start) // step
            lax.fori_loop(0, count, chunk, 0)
            if start + count * step < stop:
                fill(k, start + count * step, stop - start - count * step)

        for k, (at, end) in enumerate(regions):
            if at < split < end:
                span(k, at, split)
                at = split
                some_copy(t).start()
            span(k, at, end)
            if end == split:
                some_copy(t).start()
        store(t)

    for t in range(halves):
        some_copy(t).wait()

        def settle(n, _):
            @pl.when(lax.rem(n, 2) == core)
            def _():
                own_copy(n, t).wait()
                core_copy(n, t).wait_recv()

            @pl.when(lax.rem(n, 2) != core)
            def _():
                core_copy(n, t).wait_send()

            return 0

        if n_out == 3:
            lax.fori_loop(0, width // step, settle, 0)
    for move in moves:
        move.wait()


def middle_stage(scalars, mix_a, mix_b, own, cot, gain, w, split):
    halves, width, lanes = w.shape
    slabs, _, _, half = mix_a.shape
    ff = (lanes - width // halves) // 3
    blocks = width // 256
    peers = slabs * halves - 1
    vmem = pl.BlockSpec(memory_space=pltpu.VMEM)
    outside = pl.BlockSpec(memory_space=pl.ANY)
    out_shape = [
        jax.ShapeDtypeStruct((half, width), BF),
        jax.ShapeDtypeStruct((half, width), F32),
        jax.ShapeDtypeStruct(mix_a.shape, BF),
        jax.ShapeDtypeStruct(mix_a.shape, BF),
        jax.ShapeDtypeStruct((halves, width, split), BF),
    ]
    out_specs = [vmem] * 4 + [outside]
    if split < lanes:
        out_shape += [jax.ShapeDtypeStruct((halves, blocks // 2, 256, lanes - split), BF)] * 2
        out_specs += [outside] * 2
    flops = 2 * half * width * (9 * ff * halves + 3 * width)
    return pl.pallas_call(
        functools.partial(middle_kernel, ff, split),
        out_shape=out_shape,
        in_specs=[
            pl.BlockSpec(memory_space=pltpu.SMEM), *[pl.BlockSpec(memory_space=pltpu.HBM)] * 4,
            vmem, outside,
        ],
        out_specs=out_specs,
        scratch_shapes=[
            pltpu.VMEM((halves, width, lanes), BF),
            pltpu.VMEM((halves, half, lanes), BF),
            pltpu.VMEM((width // halves, half), BF),
            pltpu.VMEM((half, width), F32),
            pltpu.VMEM((half, 128), F32),
            pltpu.VMEM((half, width), F32),
            pltpu.VMEM((half, width), BF),
            pltpu.VMEM((half, width), BF),
            pltpu.VMEM((half, width), BF),
            pltpu.VMEM((3, width, half), BF),
            pltpu.VMEM(mix_a.shape, BF),
            pltpu.VMEM(mix_a.shape, BF),
            pltpu.SemaphoreType.DMA((4 * halves,)),
            pltpu.SemaphoreType.DMA((blocks, halves, 2)),
            pltpu.SemaphoreType.DMA((2 * peers,)),
            pltpu.SemaphoreType.DMA((2 * peers,)),
            pltpu.SemaphoreType.DMA((2,)),
            pltpu.SemaphoreType.DMA((blocks, halves)),
            pltpu.SemaphoreType.DMA((blocks, halves)),
            pltpu.VMEM((half, width), BF),
            pltpu.VMEM((half, width), BF),
            pltpu.VMEM(mix_a.shape, BF),
            pltpu.VMEM(mix_a.shape, BF),
            pltpu.SemaphoreType.DMA((4,)),
        ],
        compiler_params=pltpu.CompilerParams(
            vmem_limit_bytes=60 << 20, collective_id=1, has_side_effects=True
        ),
        cost_estimate=pl.CostEstimate(
            flops=flops, bytes_accessed=4 * w.size + 16 * half * width, transcendentals=half * lanes
        ),
    )(scalars, mix_a, mix_b, own, cot, gain, w)


class LineSum:
    def __init__(self, source, held, slots, out, sems):
        self.source, self.held, self.slots, self.out = source, held, slots, out
        self.sum_send, self.sum_recv, self.out_send, self.out_recv = sems
        here = lax.axis_index("ctx")
        self.low = here < 2
        self.place = jnp.where(self.low, here, 3 - here)
        self.inward = jnp.where(self.low, here + 1, here - 1)
        self.outward = jnp.where(self.low, here - 1, here + 1)
        self.size = out.shape[0] // 4

    def number(self, part):
        return jnp.where(self.low, part, 3 - part)

    def part(self, ref, part):
        at = pl.multiple_of(self.number(part) * self.size, self.size)
        return ref.at[pl.ds(at, self.size), :]

    def read(self, ref, part):
        at = pl.multiple_of(self.number(part) * self.size, self.size)
        return ref[pl.ds(at, self.size), :].astype(F32)

    def write(self, ref, part, value):
        at = pl.multiple_of(self.number(part) * self.size, self.size)
        ref[pl.ds(at, self.size), :] = value.astype(BF)

    def copy(self, source, target, send, recv, place):
        return pltpu.make_async_remote_copy(
            src_ref=source, dst_ref=target, send_sem=send, recv_sem=recv,
            device_id={"ctx": place}, device_id_type=pl.DeviceIdType.MESH,
        )

    def took(self, slot):
        ref = self.slots.at[slot]
        self.copy(ref, ref, self.sum_send.at[0], self.sum_recv.at[slot], self.inward).wait_recv()
        return self.slots[slot].astype(F32)

    def begin(self):
        @pl.when(self.place == 0)
        def _():
            for k in range(3):
                self.copy(
                    self.part(self.source, 3 - k), self.slots.at[k],
                    self.sum_send.at[k], self.sum_recv.at[k], self.inward,
                ).start()

    def left(self, k):
        self.copy(
            self.slots.at[0], self.slots.at[0],
            self.sum_send.at[k], self.sum_recv.at[0], self.inward,
        ).wait_send()

    def first(self, k):
        @pl.when(self.place == 1)
        def _():
            self.write(self.held, 3 - k, self.read(self.source, 3 - k) + self.took(k))
            self.copy(
                self.part(self.held, 3 - k), self.slots.at[3 + k],
                self.sum_send.at[k], self.sum_recv.at[3 + k], self.inward,
            ).start()

    def second(self):
        @pl.when(self.place == 1)
        def _():
            self.write(self.held, 0, self.read(self.source, 0) + self.took(3))
            self.copy(
                self.part(self.held, 0), self.slots.at[3],
                self.sum_send.at[2], self.sum_recv.at[3], self.outward,
            ).start()

    def give(self, part, send, place):
        ref = self.part(self.out, part)
        return self.copy(
            ref, ref, self.out_send.at[send], self.out_recv.at[self.number(part)], place
        )

    def final(self):
        @pl.when(self.place == 1)
        def _():
            self.write(self.out, 1, self.read(self.source, 1) + self.took(2) + self.took(4))
            self.give(1, 0, self.inward).start()
            self.give(1, 1, self.outward).start()

        @pl.when(self.place == 0)
        def _():
            self.write(self.out, 0, self.read(self.source, 0) + self.took(3))
            self.give(0, 0, self.inward).start()

    def forward(self):
        @pl.when(self.place == 1)
        def _():
            for k, (part, place) in enumerate(((0, self.inward), (2, self.outward), (3, self.outward))):
                self.give(part, 2 + k, place).wait_recv()
                self.give(part, 2 + k, place).start()

    def end(self):
        @pl.when(self.place == 0)
        def _():
            for k in range(3):
                self.left(k)
            self.give(0, 0, self.inward).wait_send()
            for part in (1, 2, 3):
                self.give(part, 0, self.inward).wait_recv()

        @pl.when(self.place == 1)
        def _():
            for k in range(3):
                self.left(k)
            for k in range(5):
                self.give(1, k, self.inward).wait_send()


def tail_kernel(
    back_a, back_b, some, rest, normed, weights, own_hbm, gain, dmid,
    grad_out, some_out, rest_out, qa_out, qb_out,
    turned, some_held, some_slots, rest_held, rest_slots,
    local, crossed, column_sum, columned, q_src, q_held, q_slots, theirs, got_theirs, mine,
    core_send, core_recv, col_send, col_recv,
    row_send, row_recv, out_send, out_recv, *line_sems,
):
    here, line, place = lax.axis_index("ctx"), lax.axis_index("tp"), lax.axis_index("fsdp")
    core, column = lax.rem(place, 2), place // 2
    sibling = {"fsdp": place + 1 - 2 * core}
    beside = {"fsdp": lax.rem(place + 2, 4)}
    across = {"tp": 1 - line}
    others = [{"ctx": lax.rem(here + k, 4)} for k in range(1, 4)]
    mesh_id = pl.DeviceIdType.MESH
    barrier = pltpu.get_barrier_semaphore()
    for device in (*others, sibling, beside, across):
        pl.semaphore_signal(barrier, inc=1, device_id=device, device_id_type=mesh_id)
    pl.semaphore_wait(barrier, 6)

    def remote(source, target, send, recv, device):
        return pltpu.make_async_remote_copy(
            src_ref=source, dst_ref=target, send_sem=send, recv_sem=recv,
            device_id=device, device_id_type=mesh_id,
        )

    rows = normed.shape[0]
    half = rows // 2
    depth = 256
    own, own_sem, *line_sems = line_sems
    load = pltpu.make_async_copy(
        own_hbm.at[pl.ds(pl.multiple_of(line * half, half), half), :], own, own_sem
    )
    load.start()
    a, b, qa, qb = (
        LineSum(src, held, slots, out, line_sems[4 * k : 4 * k + 4])
        for k, (src, held, slots, out) in enumerate(
            (
                (some, some_held, some_slots, some_out),
                (rest, rest_held, rest_slots, rest_out),
                (q_src.at[0], q_held.at[0], q_slots.at[0], qa_out),
                (q_src.at[1], q_held.at[1], q_slots.at[1], qb_out),
            )
        )
    )
    a.begin()

    def weight_gradient(h, grads):
        def step(n, _):
            cut = pl.ds(pl.multiple_of(n * depth, depth), depth)
            value = mm(grads[...], normed[:, cut], NN).astype(BF)
            local[h, lax.rem(n, 2), n // 2] = value
            return 0

        lax.fori_loop(0, 4, step, 0)
        move = remote(
            local.at[h, 1 - core], crossed.at[h], core_send.at[h], core_recv.at[h], sibling
        )
        move.start()
        return move

    def column_step(h, move):
        move.wait_recv()
        for x in range(2):
            column_sum[h, x] = (
                local[h, core, x].astype(F32) + crossed[h, x].astype(F32)
            ).astype(BF)
        move = remote(
            column_sum.at[h, 1 - column], columned.at[h], col_send.at[h], col_recv.at[h], beside
        )
        move.start()
        return move

    def column_end(h, move):
        move.wait_recv()
        q_src[h] = (column_sum[h, column].astype(F32) + columned[h].astype(F32)).astype(BF)

    def turn(h, grads):
        for k in range(0, grads.shape[0], 128):
            at = h * grads.shape[0] + k
            turned[:, at : at + 128] = grads[k : k + 128, :].astype(F32).T.astype(BF)

    pieces = 2
    piece = half // pieces
    sent_rows = []
    sent_out = []
    mine_start = pl.multiple_of(line * half, half)

    def make_theirs(k):
        cut = slice(k * piece, (k + 1) * piece)
        start = pl.multiple_of((1 - line) * half + k * piece, piece)

        def make(n, _):
            wide = pl.ds(pl.multiple_of(n * depth, depth), depth)
            value = mm(turned[pl.ds(start, piece), :], weights[:, wide], NN)
            theirs[cut, wide] = value.astype(BF)
            return 0

        lax.fori_loop(0, 4, make, 0)
        move = remote(theirs.at[cut], got_theirs.at[cut], row_send.at[k], row_recv.at[k], across)
        move.start()
        sent_rows.append(move)

    def make_mine(n, _):
        wide = pl.ds(pl.multiple_of(n * depth, depth), depth)
        mine[:, wide] = mm(turned[pl.ds(mine_start, half), :], weights[:, wide], NN)
        return 0

    def finish_rows(k):
        small = 64
        if k == 0:
            load.wait()
        sent_rows[k].wait_recv()

        def back(r, _):
            at = pl.multiple_of(k * piece + r * small, small)
            cut = pl.ds(at, small)
            values = own[cut, :].astype(F32)
            inverse = lax.rsqrt(jnp.mean(values * values, axis=1, keepdims=True) + EPSILON)
            scaled = values * inverse
            d_scaled = (mine[cut, :] + got_theirs[cut, :].astype(F32)) * gain[...]
            mean = jnp.mean(d_scaled * scaled, axis=1, keepdims=True)
            total = dmid[cut, :] + inverse * (d_scaled - scaled * mean)
            grad_out[pl.ds(pl.multiple_of(line * half + at, small), small), :] = total.astype(BF)
            return 0

        lax.fori_loop(0, piece // small, back, 0)
        ref = grad_out.at[pl.ds(pl.multiple_of(line * half + k * piece, piece), piece), :]
        move = remote(ref, ref, out_send.at[k], out_recv.at[k], across)
        move.start()
        sent_out.append(move)

    b.begin()
    turn(0, back_a)
    turn(1, back_b)
    make_theirs(0)
    core_a = weight_gradient(0, back_a)
    a.first(0)
    make_theirs(1)
    core_b = weight_gradient(1, back_b)
    a.first(1)
    col_a = column_step(0, core_a)
    lax.fori_loop(0, 4, make_mine, 0)
    a.second()
    col_b = column_step(1, core_b)
    b.first(0)
    a.final()
    b.first(1)
    finish_rows(0)
    b.second()
    a.forward()
    column_end(0, col_a)
    qa.begin()
    b.final()
    finish_rows(1)
    column_end(1, col_b)
    qb.begin()
    qa.first(0)
    qa.first(1)
    b.forward()
    qb.first(0)
    qb.first(1)
    qa.second()
    qa.final()
    qb.second()
    qb.final()
    qa.forward()
    qb.forward()
    for run in (a, b, qa, qb):
        run.end()
    for move in (core_a, core_b, col_a, col_b, *sent_rows):
        move.wait_send()
    for k, move in enumerate(sent_out):
        move.wait_send()
        ref = grad_out.at[pl.ds(pl.multiple_of((1 - line) * half + k * piece, piece), piece), :]
        remote(ref, ref, out_send.at[k], out_recv.at[k], across).wait_recv()


def tail_stage(back_a, back_b, some, rest, normed, weights, own, gain, dmid):
    rows, width = normed.shape
    half = rows // 2
    lanes_a, lanes_b = some.shape[1], rest.shape[1]
    wide = back_a.shape[0]
    vmem = pl.BlockSpec(memory_space=pltpu.VMEM)
    dma = pltpu.SemaphoreType.DMA
    return pl.pallas_call(
        tail_kernel,
        out_shape=(
            jax.ShapeDtypeStruct((rows, width), BF),
            jax.ShapeDtypeStruct((256, lanes_a), BF),
            jax.ShapeDtypeStruct((256, lanes_b), BF),
            jax.ShapeDtypeStruct((wide, 256), BF),
            jax.ShapeDtypeStruct((wide, 256), BF),
        ),
        in_specs=[vmem] * 6 + [pl.BlockSpec(memory_space=pl.ANY)] + [vmem] * 2,
        out_specs=(vmem,) * 5,
        scratch_shapes=[
            pltpu.VMEM((rows, 2 * wide), BF),
            pltpu.VMEM((256, lanes_a), BF),
            pltpu.VMEM((5, 64, lanes_a), BF),
            pltpu.VMEM((256, lanes_b), BF),
            pltpu.VMEM((5, 64, lanes_b), BF),
            pltpu.VMEM((2, 2, 2, wide, 256), BF),
            pltpu.VMEM((2, 2, wide, 256), BF),
            pltpu.VMEM((2, 2, wide, 256), BF),
            pltpu.VMEM((2, wide, 256), BF),
            pltpu.VMEM((2, wide, 256), BF),
            pltpu.VMEM((2, wide, 256), BF),
            pltpu.VMEM((2, 5, wide // 4, 256), BF),
            pltpu.VMEM((half, width), BF),
            pltpu.VMEM((half, width), BF),
            pltpu.VMEM((half, width), F32),
            dma((2,)), dma((2,)), dma((2,)), dma((2,)),
            dma((2,)), dma((2,)), dma((2,)), dma((2,)),
            pltpu.VMEM((half, width), BF), dma,
        ]
        + [dma((3,)), dma((5,)), dma((5,)), dma((4,))] * 4,
        compiler_params=pltpu.CompilerParams(
            vmem_limit_bytes=60 << 20, collective_id=2, has_side_effects=True
        ),
        cost_estimate=pl.CostEstimate(
            flops=8 * rows * width * wide, bytes_accessed=40 << 20, transcendentals=0
        ),
    )(back_a, back_b, some, rest, normed, weights, own, gain, dmid)


def pack_kernel(gate, up, down_hbm, out_hbm, packed_hbm, packed, down, out, sems):
    depth, ff = gate.shape
    straight = [
        pltpu.make_async_copy(source, packed_hbm.at[:, k * ff : (k + 1) * ff], sems.at[k])
        for k, source in enumerate((gate, up))
    ]
    loads = [
        pltpu.make_async_copy(source, target, sems.at[2 + k])
        for k, (source, target) in enumerate(((down_hbm, down), (out_hbm, out)))
    ]
    for move in (*loads, *straight):
        move.start()
    for move in loads:
        move.wait()
    packed[:, 0:ff] = down[...].astype(F32).T.astype(BF)
    packed[:, ff:] = out[...].astype(F32).T.astype(BF)
    last = pltpu.make_async_copy(packed, packed_hbm.at[:, 2 * ff :], sems.at[4])
    last.start()
    for move in (*straight, last):
        move.wait()


def pack_stage(gate, up, down, out):
    depth, ff = gate.shape
    outside = pl.BlockSpec(memory_space=pltpu.HBM)
    return pl.pallas_call(
        pack_kernel,
        out_shape=jax.ShapeDtypeStruct((depth, 3 * ff + out.shape[0]), BF),
        in_specs=[outside] * 4,
        out_specs=outside,
        scratch_shapes=[
            pltpu.VMEM((depth, ff + out.shape[0]), BF),
            pltpu.VMEM(down.shape, BF),
            pltpu.VMEM(out.shape, BF),
            pltpu.SemaphoreType.DMA((5,)),
        ],
        compiler_params=pltpu.CompilerParams(vmem_limit_bytes=60 << 20),
        cost_estimate=pl.CostEstimate(flops=0, bytes_accessed=14 * depth * ff, transcendentals=0),
    )(gate, up, down, out)


def finish_kernel(
    *refs,
):
    sources, gains, grad_in = refs[:9], refs[9], refs[10]
    gate, up, down, out, qg, kg, vg, part, grad_out = refs[11:20]
    held, sems = refs[20:29], refs[29]
    some, rest, qa, qb, wq, wk, wv, gate_w, up_w = held
    move = pltpu.make_async_copy(grad_in, grad_out, sems.at[9])
    loads = [
        pltpu.make_async_copy(source, target, sems.at[k])
        for k, (source, target) in enumerate(zip(sources, held))
    ]
    for load in loads:
        load.start()
    move.start()
    for load in loads:
        load.wait()
    ff = gate.shape[1]
    split = some.shape[1]
    low = split - ff
    high = ff - low

    def fold(values):
        total = values[:, 0:128]
        for at in range(128, values.shape[1], 128):
            total = total + values[:, at : at + 128]
        return total

    value = some[:, 0:ff].astype(F32)
    gate[...] = value
    two = fold(value * gate_w[...].astype(F32))
    value = some[:, ff:split].astype(F32)
    up[:, 0:low] = value
    two = two + fold(value * up_w[:, 0:low].astype(F32))
    value = rest[:, 0:high].astype(F32)
    up[:, low:ff] = value
    two = two + fold(value * up_w[:, low:ff].astype(F32))
    down[...] = rest[:, high : high + ff].astype(F32).T
    out[...] = rest[:, high + ff :].astype(F32).T
    one = jnp.zeros((gate.shape[0], 128), F32)
    for k, (target, weight) in enumerate(((qg, wq), (kg, wk), (vg, wv))):
        for z in range(qa.shape[0] // (3 * HD)):
            at = (3 * z + k) * HD
            value = jnp.concatenate([qa[at : at + HD, :], qb[at : at + HD, :]], axis=0)
            value = value.astype(F32).T
            cut = slice(2 * HD * z, 2 * HD * (z + 1))
            target[:, cut] = value
            one = one + value * weight[:, cut].astype(F32)
    part[...] = jnp.zeros_like(part)
    part[0:1] = jnp.sum(one.T, axis=0, keepdims=True) / gains[0:1]
    part[1:2] = jnp.sum(two.T, axis=0, keepdims=True) / gains[1:2]
    move.wait()


def finish_stage(some, rest, qa, qb, weights, gate_w, up_w, gains, grad):
    depth, ff = gate_w.shape
    inner = weights[0].shape[1]
    vmem = pl.BlockSpec(memory_space=pltpu.VMEM)
    outside = pl.BlockSpec(memory_space=pltpu.HBM)
    shape = jax.ShapeDtypeStruct
    operands = (some, rest, qa, qb, *weights, gate_w, up_w)
    return pl.pallas_call(
        finish_kernel,
        out_shape=(
            shape((depth, ff), F32), shape((depth, ff), F32), shape((ff, depth), F32),
            shape((inner, depth), F32), *[shape((depth, inner), F32)] * 3,
            shape((8, depth), F32), shape(grad.shape, BF),
        ),
        in_specs=[outside] * 9 + [vmem, outside],
        out_specs=(vmem,) * 8 + (outside,),
        scratch_shapes=[
            *[pltpu.VMEM(a.shape, BF) for a in operands], pltpu.SemaphoreType.DMA((10,)),
        ],
        compiler_params=pltpu.CompilerParams(vmem_limit_bytes=60 << 20),
        cost_estimate=pl.CostEstimate(flops=0, bytes_accessed=16 << 20, transcendentals=0),
    )(*operands, gains, grad)


def normalize(values, gain):
    inverse = lax.rsqrt(jnp.mean(values * values, axis=-1, keepdims=True) + EPSILON)
    scaled = values * inverse
    return scaled, inverse, (scaled * gain).astype(BF)


def norm_back(d_normed, scaled, inverse, gain):
    d_scaled = d_normed * gain
    d_values = inverse * (d_scaled - scaled * jnp.mean(d_scaled * scaled, axis=-1, keepdims=True))
    return d_values


def rows_first(values):
    return with_layout_constraint(values, Layout(major_to_minor=tuple(range(values.ndim))))


def swap(values, axis, bit):
    count = lax.axis_size(axis)
    return lax.ppermute(values, axis, [(k, k ^ bit) for k in range(count)])


def both_halves(values):
    other = swap(values, "tp", 1)
    first = lax.axis_index("tp") == 0
    return jnp.concatenate([jnp.where(first, values, other), jnp.where(first, other, values)])


def shards(
    inputs,
    lengths,
    first_gain,
    query_weight,
    key_weight,
    value_weight,
    out_weight,
    second_gain,
    gate_weight,
    up_weight,
    down_weight,
    cotangent,
):
    slabs, halves, parts = lax.axis_size("ctx"), lax.axis_size("tp"), lax.axis_size("fsdp")
    rows, width = inputs.shape[1], inputs.shape[2]
    depth = query_weight.shape[0]
    group = query_weight.shape[1] // HD // slabs
    half = rows // halves
    ff = gate_weight.shape[1]
    everywhere = ("tp", "fsdp")
    side = lax.axis_index("tp") * half

    paired = parts == 4 and halves == 2 and slabs == 4 and group == 2
    w_rest = pack_stage(gate_weight, up_weight, down_weight, out_weight)
    w_rest = rows_first(lax.all_gather(rows_first(w_rest), everywhere, axis=0, tiled=True))
    w_rest = w_rest.reshape(halves, width, -1)
    qkv_width = slabs * 3 * HD

    if paired:
        gains_own = jnp.stack([first_gain.astype(F32), second_gain.astype(F32)])
        gains_own = jnp.concatenate([gains_own, jnp.zeros((6, depth), F32)])
        w_turned, normed_one, gains, *rest = front_stage(
            lengths, inputs[0], gains_own, query_weight, key_weight, value_weight, slabs, halves
        )
        gain_one, gain_two = gains[0], gains[1]
        qkv, arrived = rest[0:2], rest[2:4]
        saved = [(rest[4], rest[6]), (rest[5], rest[7])]
    else:
        gains = lax.all_gather(jnp.stack([first_gain, second_gain]), "fsdp", axis=1, tiled=True)
        gain_one, gain_two = gains[0].astype(F32), gains[1].astype(F32)
        stacked = jnp.stack(
            [w.reshape(depth, slabs, group, HD) for w in (query_weight, key_weight, value_weight)]
        ).transpose(1, 3, 2, 0, 4)
        w_qkv = lax.all_gather(
            stacked.reshape(depth, group * qkv_width), "fsdp", axis=0, tiled=True
        )
        w_heads = [w_qkv[:, h * qkv_width : (h + 1) * qkv_width] for h in range(group)]
        _, _, normed_one = normalize(inputs[0].astype(F32), gain_one)
        qkv = []
        for h in range(group):
            part = mm(w_heads[h], normed_one, (((0,), (1,)), ((), ()))).astype(BF)
            part = part.reshape(slabs, 3 * HD, rows)
            qkv.append(lax.all_to_all(part, "ctx", 0, 0, tiled=True))
        arrived, saved = [], []
        for h in range(group):
            mix, mix_full, lse = attend(lengths, qkv[h], halves, rows)
            saved.append((mix_full, lse))
            mix = mix.reshape(slabs * halves, HD, half)
            mix = lax.all_to_all(mix, ("ctx", "tp"), 0, 0, tiled=True)
            arrived.append(mix.reshape(slabs, halves, HD, half))

    scalars = jnp.stack([lengths[0], lax.axis_index("ctx") * rows + side])
    split = 2304 if paired else w_rest.shape[2]
    output, d_middle, *d_mix, = middle_stage(
        scalars, *arrived, inputs[0], cotangent[0], gain_two[None], w_rest, split
    )
    d_mix, (g_some, *g_rest) = d_mix[:2], d_mix[2:]
    output = both_halves(output)
    s_some = lax.psum_scatter(
        rows_first(g_some.reshape(halves * width, -1)), everywhere, scatter_dimension=0, tiled=True
    )
    s_some = rows_first(s_some)

    if paired:
        back_a, back_b, g_rest = back_stage(lengths, qkv, d_mix, saved, *g_rest)
        input_gradient, s_some, s_rest, *q_grads = tail_stage(
            back_a, back_b, s_some, g_rest, normed_one, w_turned, inputs[0], gain_one[None], d_middle
        )
        s_gate, s_up, s_down, s_out, *s_qkv, d_gains, input_gradient = finish_stage(
            s_some, s_rest, *q_grads, (query_weight, key_weight, value_weight), gate_weight,
            up_weight, gains_own, input_gradient,
        )
        d_gains = d_gains[0:2]
        d_gains = d_gains + swap(d_gains, "tp", 1)
    else:
        d_local = [
            attend_back(lengths, qkv[h], d_mix[h], *saved[h], 512) for h in range(group)
        ]
        d_qkv = [
            lax.all_to_all(d, "ctx", 0, 0, tiled=True).reshape(qkv_width, rows) for d in d_local
        ]
        d_normed_one = jnp.zeros((rows, width), F32)
        s_qkv = []
        for h in range(group):
            d_normed_one = d_normed_one + mm(d_qkv[h], w_heads[h], (((0,), (1,)), ((), ())))
            grad = mm(normed_one, d_qkv[h], (((0,), (1,)), ((), ()))).astype(BF)
            grad = lax.psum_scatter(grad, "fsdp", scatter_dimension=0, tiled=True)
            s_qkv.append(lax.psum(grad, "ctx").reshape(depth, slabs, 3, HD))
        d_normed_one = lax.psum_scatter(d_normed_one, "tp", scatter_dimension=0, tiled=True)
        own = lax.dynamic_slice_in_dim(inputs[0], side, half, 0)
        scaled_one, inverse_one, _ = normalize(own.astype(F32), gain_one)
        d_from_one = norm_back(d_normed_one, scaled_one, inverse_one, gain_one)
        input_gradient = lax.all_gather(
            (d_middle + d_from_one).astype(BF), "tp", axis=0, tiled=True
        )
        s_qkv = jnp.stack(s_qkv, axis=2).transpose(3, 0, 1, 2, 4)
        s_qkv = s_qkv.reshape(3, depth, slabs * group * HD).astype(F32)
        s_all = lax.psum(s_some, "ctx").astype(F32)
        d_gain_one = sum(
            jnp.sum(w.astype(F32) * s, axis=1)
            for w, s in zip((query_weight, key_weight, value_weight), s_qkv)
        ) / first_gain.astype(F32)
        d_gain_two = (
            jnp.sum(gate_weight.astype(F32) * s_all[:, :ff], axis=1)
            + jnp.sum(up_weight.astype(F32) * s_all[:, ff : 2 * ff], axis=1)
        ) / second_gain.astype(F32)
        d_gains = jnp.stack([d_gain_one, d_gain_two])
        d_gains = lax.psum(d_gains, "tp")
        s_gate, s_up, s_down, s_out = (
            s_all[:, :ff], s_all[:, ff : 2 * ff], s_all[:, 2 * ff : 3 * ff].T, s_all[:, 3 * ff :].T
        )

    return (
        output[None],
        input_gradient[None],
        d_gains[0],
        s_qkv[0],
        s_qkv[1],
        s_qkv[2],
        s_out,
        d_gains[1],
        s_gate,
        s_up,
        s_down,
    )


def solution(mesh):
    rows = P("fsdp", "ctx", None)
    gain = P("fsdp")
    inward = P("fsdp", "tp")
    outward = P("tp", "fsdp")
    return jax.shard_map(
        shards,
        mesh=mesh,
        in_specs=(
            rows, gain, gain, inward, inward, inward, outward, gain, inward, inward, outward, rows,
        ),
        out_specs=(
            rows, rows, gain, inward, inward, inward, outward, gain, inward, inward, outward,
        ),
        check_vma=False,
    )
```

```python
import functools

import jax
import jax.numpy as jnp
from jax import lax
from jax.experimental import pallas as pl
from jax.experimental.pallas import tpu as pltpu
from jax.experimental.layout import Layout, with_layout_constraint
from jax.sharding import PartitionSpec as P

HD = 64
EPSILON = 1e-05
MASKED = -1000000000.0
NN = (((1,), (0,)), ((), ()))
NT = (((1,), (1,)), ((), ()))
TN = (((0,), (0,)), ((), ()))
BF = jnp.bfloat16
F32 = jnp.float32


def mm(left, right, dims):
    return lax.dot_general(left, right, dims, preferred_element_type=F32)


def spread_keys(keys, start, length):
    rows = keys.shape[0]
    pos = start + lax.broadcasted_iota(jnp.int32, (rows, HD), 0)
    lane = lax.broadcasted_iota(jnp.int32, (rows, HD), 1)
    bias = jnp.where((lane == 0) & (pos >= length), MASKED, 0.0)
    return jnp.concatenate([keys, bias], axis=1).astype(BF)


def spread_queries(queries):
    row = lax.broadcasted_iota(jnp.int32, queries.shape, 0)
    ones = jnp.where(row == 0, 1.0, 0.0)
    return jnp.concatenate([queries * HD**-0.5, ones], axis=0).astype(BF)


def attend_rows(tile, length, qkv, kx, qx, vx, emit):
    slabs, _, rows = qkv.shape
    per = rows // tile
    blocks = slabs * per
    for z in range(slabs):
        keys = qkv[z, HD : 2 * HD, :].astype(F32).T
        kx[z * rows : (z + 1) * rows, :] = spread_keys(keys, z * rows, length)
        queries = spread_queries(qkv[z, 0:HD, :].astype(F32))
        for b in range(per):
            cut = slice(b * tile, (b + 1) * tile)
            qx[z * per + b] = queries[:, cut]
            vx[z * per + b] = qkv[z, 2 * HD : 3 * HD, cut]
    later = lax.broadcasted_iota(jnp.int32, (tile, tile), 0) > lax.broadcasted_iota(
        jnp.int32, (tile, tile), 1
    )

    def query_block(i, _):
        queries = qx[i]

        def step(j, carry, masked):
            highest, total, mix = carry
            keys = kx[pl.ds(pl.multiple_of(j * tile, tile), tile), :]
            scores = mm(keys, queries, NN)
            if masked:
                scores = jnp.where(later, MASKED, scores)
            new = jnp.maximum(highest, jnp.max(scores, axis=0, keepdims=True))
            scale = jnp.exp(highest - new)
            probs = jnp.exp(scores - new)
            total = total * scale + jnp.sum(probs, axis=0, keepdims=True)
            mix = mix * scale + mm(vx[j], probs.astype(BF), NN)
            return new, total, mix

        first = (
            jnp.full((1, tile), -jnp.inf, F32),
            jnp.zeros((1, tile), F32),
            jnp.zeros((HD, tile), F32),
        )
        carry = lax.fori_loop(0, i, lambda j, c: step(j, c, False), first)
        highest, total, mix = step(i, carry, True)
        emit(i, mix / total, highest + jnp.log(total))
        return 0

    lax.fori_loop(0, blocks, query_block, 0)


def attend_kernel(tile, len_ref, qkv, o_ref, of_ref, lse_ref, kx, qx, vx):
    rows = qkv.shape[2]
    halves = o_ref.shape[1]
    half = rows // halves

    def emit(i, mix, lse):
        of_ref[i] = mix
        lse_ref[i] = lse
        for t in range(halves):
            o_ref[i, t] = mix[:, t * half : (t + 1) * half].astype(BF)

    attend_rows(tile, len_ref[0], qkv, kx, qx, vx, emit)


def front_kernel(
    len_ref, x, gains_own, wq, wk, wv,
    wt_hbm, normed_hbm, gains, qkv_a_hbm, qkv_b_hbm, mix_a, mix_b, of_a_hbm, of_b_hbm,
    lse_a_hbm, lse_b_hbm,
    wt, normed, qkv_a, qkv_b, of_a, of_b, lse_a, lse_b, out_sems, packed, parts, mixed, kx, qx, vx,
    gain_send, gain_recv, w_send, w_recv, part_send, part_recv, part_local,
    mix_send, mix_recv, mix_local,
):
    here, line, place = lax.axis_index("ctx"), lax.axis_index("tp"), lax.axis_index("fsdp")
    core, column = lax.rem(place, 2), place // 2
    pair = place + 1 - 2 * core
    other = lax.rem(place + 2, 4)
    mesh_id = pl.DeviceIdType.MESH
    slabs, halves = mix_a.shape[0], mix_a.shape[1]
    rows, width = x.shape
    half = rows // halves
    wide = slabs * 3 * HD
    depth = wq.shape[0]
    peers = [(dz, dt) for dz in range(slabs) for dt in range(halves) if dz or dt]

    def peer(dz, dt):
        return lax.rem(here + dz, slabs), lax.rem(line + dt, halves)

    barrier = pltpu.get_barrier_semaphore()
    for dz, dt in peers:
        z, t = peer(dz, dt)
        pl.semaphore_signal(barrier, inc=1, device_id={"ctx": z, "tp": t}, device_id_type=mesh_id)
    for device in (pair, other):
        pl.semaphore_signal(barrier, inc=1, device_id={"fsdp": device}, device_id_type=mesh_id)
    for q, w in enumerate((wq, wk, wv)):
        flat = w[...].astype(F32).T.astype(BF)
        for z in range(slabs):
            for h in range(2):
                at = (2 * z + h) * HD
                packed[h, (3 * z + q) * HD : (3 * z + q + 1) * HD, :] = flat[at : at + HD]

    def remote(source, target, send, recv, device):
        return pltpu.make_async_remote_copy(
            src_ref=source, dst_ref=target, send_sem=send, recv_sem=recv,
            device_id=device, device_id_type=mesh_id,
        )

    def lanes(index):
        return pl.ds(pl.multiple_of(index * depth, depth), depth)

    def weight(h, index):
        return wt.at[h * wide : (h + 1) * wide, lanes(index)]

    gains[:, lanes(place)] = gains_own[...]
    for h in range(2):
        wt[h * wide : (h + 1) * wide, lanes(place)] = packed[h]
    pl.semaphore_wait(barrier, len(peers) + 2)
    sent = []

    def launch(move):
        move.start()
        sent.append(move)
        return move

    for k, device in enumerate((pair, other)):
        launch(
            remote(
                gains_own, gains.at[:, lanes(place)], gain_send.at[k], gain_recv.at[k], {"fsdp": device}
            )
        )
    for h in range(2):
        for k, device in ((1, other), (0, pair)):
            launch(
                remote(
                    packed.at[h], weight(h, place), w_send.at[h, k], w_recv.at[h, k], {"fsdp": device}
                )
            )

    def arrived(ref, sem):
        remote(ref, ref, gain_send.at[0], sem, {"fsdp": pair}).wait_recv()

    arrived(gains.at[:, lanes(other)], gain_recv.at[1])
    launch(
        remote(
            gains.at[:, lanes(other)], gains.at[:, lanes(other)], gain_send.at[2], gain_recv.at[2],
            {"fsdp": pair},
        )
    )
    far = lax.rem(pair + 2, 4)
    arrived(gains.at[:, lanes(pair)], gain_recv.at[0])
    arrived(gains.at[:, lanes(far)], gain_recv.at[2])
    small = 64

    def norm(r, _):
        cut = pl.ds(pl.multiple_of(r * small, small), small)
        values = x[cut, :].astype(F32)
        inverse = lax.rsqrt(jnp.mean(values * values, axis=1, keepdims=True) + EPSILON)
        normed[cut, :] = (values * inverse * gains[0:1, :]).astype(BF)
        return 0

    lax.fori_loop(0, rows // small, norm, 0)
    kept = []

    def keep(source, target):
        move = pltpu.make_async_copy(source, target, out_sems.at[len(kept)])
        move.start()
        kept.append(move)

    keep(normed, normed_hbm)
    queues = (qkv_a, qkv_b)
    waits = []
    for h in range(2):
        arrived(weight(h, other), w_recv.at[h, 1])
        launch(
            remote(
                weight(h, other), weight(h, other), w_send.at[h, 2], w_recv.at[h, 2], {"fsdp": pair}
            )
        )
    for h in range(2):
        arrived(weight(h, pair), w_recv.at[h, 0])
        arrived(weight(h, far), w_recv.at[h, 2])

        def project(n, _):
            cut = pl.ds(pl.multiple_of(n * 256, 256), 256)
            value = mm(wt[h * wide : (h + 1) * wide, :], normed[cut, :], NT).astype(BF)
            for z in range(slabs):
                parts[h, z, :, cut] = value[z * 3 * HD : (z + 1) * 3 * HD]
            return 0

        lax.fori_loop(0, rows // 256, project, 0)
        for k in range(1, slabs):
            z = lax.rem(here + k, slabs)
            waits.append(
                launch(
                    remote(
                        parts.at[h, z], queues[h].at[here], part_send.at[h, k], part_recv.at[h, k],
                        {"ctx": z},
                    )
                )
            )
        stays = pltpu.make_async_copy(parts.at[h, here], queues[h].at[here], part_local.at[h])
        stays.start()
        waits.append(stays)

    keep(wt, wt_hbm)
    for h, (qkv, mix_ref, of_ref, lse_ref) in enumerate(
        ((qkv_a, mix_a, of_a, lse_a), (qkv_b, mix_b, of_b, lse_b))
    ):
        for move in waits[h * slabs : (h + 1) * slabs - 1]:
            move.wait_recv()
        waits[(h + 1) * slabs - 1].wait()
        keep(qkv, (qkv_a_hbm, qkv_b_hbm)[h])

        def emit(i, mix, lse):
            of_ref[i] = mix
            lse_ref[i] = lse
            for t in range(halves):
                mixed[h, i, t] = mix[:, t * half : (t + 1) * half].astype(BF)
                stay = (i == here) & (line == t)

                @pl.when(stay)
                def _():
                    pltpu.make_async_copy(
                        mixed.at[h, i, t], mix_ref.at[here, line], mix_local.at[h]
                    ).start()

                @pl.when(jnp.logical_not(stay))
                def _():
                    remote(
                        mixed.at[h, i, t], mix_ref.at[here, line], mix_send.at[h, i, t],
                        mix_recv.at[h, here, line], {"ctx": i, "tp": t},
                    ).start()

        attend_rows(rows, len_ref[0], qkv, kx, qx, vx, emit)
        keep(of_ref, (of_a_hbm, of_b_hbm)[h])
        keep(lse_ref, (lse_a_hbm, lse_b_hbm)[h])

    for move in sent:
        move.wait_send()
    for move in kept:
        move.wait()
    for h, mix_ref in enumerate((mix_a, mix_b)):
        pltpu.make_async_copy(mixed.at[h, here, line], mix_ref.at[here, line], mix_local.at[h]).wait()
        for dz, dt in peers:
            z, t = peer(dz, dt)
            remote(
                mixed.at[h, z, t], mix_ref.at[z, t], mix_send.at[h, z, t], mix_recv.at[h, z, t],
                {"ctx": z, "tp": t},
            ).wait()


def front_stage(length, x, gains, wq, wk, wv, slabs, halves):
    rows, width = x.shape
    half = rows // halves
    wide = slabs * 3 * HD
    total = slabs * rows
    work = total * (total + rows) // 2
    vmem = pl.BlockSpec(memory_space=pltpu.VMEM)
    outside = pl.BlockSpec(memory_space=pltpu.HBM)
    dma = pltpu.SemaphoreType.DMA
    shape = jax.ShapeDtypeStruct
    return pl.pallas_call(
        front_kernel,
        out_shape=(
            shape((2 * wide, width), BF),
            shape((rows, width), BF),
            shape((8, width), F32),
            *[shape((slabs, 3 * HD, rows), BF)] * 2,
            *[shape((slabs, halves, HD, half), BF)] * 2,
            *[shape((slabs, HD, rows), F32)] * 2,
            *[shape((slabs, 1, rows), F32)] * 2,
        ),
        in_specs=[pl.BlockSpec(memory_space=pltpu.SMEM)] + [vmem] * 5,
        out_specs=(outside, outside, vmem, *[outside] * 8),
        scratch_shapes=[
            pltpu.VMEM((2 * wide, width), BF),
            pltpu.VMEM((rows, width), BF),
            *[pltpu.VMEM((slabs, 3 * HD, rows), BF)] * 2,
            *[pltpu.VMEM((slabs, HD, rows), F32)] * 2,
            *[pltpu.VMEM((slabs, 1, rows), F32)] * 2,
            dma((8,)),
            pltpu.VMEM((2, wide, wq.shape[0]), BF),
            pltpu.VMEM((2, slabs, 3 * HD, rows), BF),
            pltpu.VMEM((2, slabs, halves, HD, half), BF),
            pltpu.VMEM((total, 2 * HD), BF),
            pltpu.VMEM((slabs, 2 * HD, rows), BF),
            pltpu.VMEM((slabs, HD, rows), BF),
            dma((3,)), dma((3,)), dma((2, 3)), dma((2, 3)),
            dma((2, slabs)), dma((2, slabs)), dma((2,)),
            dma((2, slabs, halves)), dma((2, slabs, halves)), dma((2,)),
        ],
        compiler_params=pltpu.CompilerParams(
            vmem_limit_bytes=60 << 20, collective_id=3, has_side_effects=True
        ),
        cost_estimate=pl.CostEstimate(
            flops=2 * work * 256 * 4, bytes_accessed=20 << 20, transcendentals=2 * work
        ),
    )(length, x, gains, wq, wk, wv)


def attend(length, qkv, halves, tile):
    slabs, _, rows = qkv.shape
    total = slabs * rows
    tile = min(tile, rows)
    work = total * (total + tile) // 2
    vmem = pl.BlockSpec(memory_space=pltpu.VMEM)
    return pl.pallas_call(
        functools.partial(attend_kernel, tile),
        out_shape=(
            jax.ShapeDtypeStruct((slabs, halves, HD, rows // halves), BF),
            jax.ShapeDtypeStruct((slabs, HD, rows), F32),
            jax.ShapeDtypeStruct((slabs, 1, rows), F32),
        ),
        in_specs=[pl.BlockSpec(memory_space=pltpu.SMEM), vmem],
        out_specs=(vmem, vmem, vmem),
        scratch_shapes=[
            pltpu.VMEM((total, 2 * HD), BF),
            pltpu.VMEM((total // tile, 2 * HD, tile), BF),
            pltpu.VMEM((total // tile, HD, tile), BF),
        ],
        compiler_params=pltpu.CompilerParams(vmem_limit_bytes=60 << 20),
        cost_estimate=pl.CostEstimate(
            flops=work * 256 * 4, bytes_accessed=qkv.size * 4, transcendentals=work
        ),
    )(length, qkv)


def attend_back_rows(tile, length, qkv, do_ref, of_ref, lse_ref, out, scratch, emit):
    kx, qx, vx, kt, dox, dq, st = scratch
    slabs, _, rows = qkv.shape
    halves, half = do_ref.shape[1], do_ref.shape[3]
    per = rows // tile
    blocks = slabs * per
    for z in range(slabs):
        keys = qkv[z, HD : 2 * HD, :]
        kx[z * rows : (z + 1) * rows, :] = spread_keys(keys.astype(F32).T, z * rows, length)
        queries = spread_queries(qkv[z, 0:HD, :].astype(F32))
        values = qkv[z, 2 * HD : 3 * HD, :].astype(F32).T
        vx[z * rows : (z + 1) * rows, :] = jnp.concatenate(
            [values, jnp.zeros((rows, HD), F32)], axis=1
        ).astype(BF)
        d_mix = jnp.concatenate([do_ref[z, t] for t in range(halves)], axis=1)
        delta = jnp.sum(d_mix.astype(F32) * of_ref[z], axis=0, keepdims=True)
        for b in range(per):
            cut = slice(b * tile, (b + 1) * tile)
            n = z * per + b
            qx[n] = queries[:, cut]
            kt[n] = keys[:, cut]
            dox[n, 0:HD] = d_mix[:, cut]
            dox[n, HD : 2 * HD] = jnp.zeros((HD, tile), BF)
            st[n, 0:1] = lse_ref[z, :, cut]
            st[n, 1:2] = delta[:, cut]
    dq[...] = jnp.zeros_like(dq)
    later = lax.broadcasted_iota(jnp.int32, (tile, tile), 0) > lax.broadcasted_iota(
        jnp.int32, (tile, tile), 1
    )

    def key_block(j, _):
        here = pl.ds(pl.multiple_of(j * tile, tile), tile)
        keys = kx[here, :]
        values = vx[here, :]

        def step(i, carry, masked):
            dk, dv = carry
            scores = mm(keys, qx[i], NN)
            if masked:
                scores = jnp.where(later, MASKED, scores)
            probs = jnp.exp(scores - st[i, 0:1])
            d_probs = mm(values, dox[i], NN)
            d_scores = (probs * (d_probs - st[i, 1:2])).astype(BF)
            dv = dv + mm(dox[i, 0:HD], probs.astype(BF), NT)
            dk = dk + mm(qx[i, 0:HD], d_scores, NT)
            dq[i] += mm(kt[j], d_scores, NN)
            return dk, dv

        zero = jnp.zeros((HD, tile), F32)
        carry = step(j, (zero, zero), True)
        dk, dv = lax.fori_loop(j + 1, blocks, lambda i, c: step(i, c, False), carry)
        z = j // per
        cut = pl.ds(pl.multiple_of(lax.rem(j, per) * tile, tile), tile)
        out[z, 0:HD, cut] = (dq[j] * HD**-0.5).astype(BF)
        out[z, HD : 2 * HD, cut] = dk.astype(BF)
        out[z, 2 * HD : 3 * HD, cut] = dv.astype(BF)
        if emit is not None:

            @pl.when(lax.rem(j, per) == per - 1)
            def _():
                emit(z)

        return 0

    lax.fori_loop(0, blocks, key_block, 0)


def attend_back_scratch(slabs, rows, tile):
    total = slabs * rows
    blocks = total // tile
    return [
        pltpu.VMEM((total, 2 * HD), BF),
        pltpu.VMEM((blocks, 2 * HD, tile), BF),
        pltpu.VMEM((total, 2 * HD), BF),
        pltpu.VMEM((blocks, HD, tile), BF),
        pltpu.VMEM((blocks, 2 * HD, tile), BF),
        pltpu.VMEM((blocks, HD, tile), F32),
        pltpu.VMEM((blocks, 8, tile), F32),
    ]


def attend_back_kernel(tile, len_ref, qkv, do_ref, of_ref, lse_ref, out, *scratch):
    attend_back_rows(tile, len_ref[0], qkv, do_ref, of_ref, lse_ref, out, scratch, None)


def back_kernel(
    tile, len_ref, qkv_a, qkv_b, do_a, do_b, of_a, of_b, lse_a, lse_b, keep_hbm, got_hbm,
    out_a, out_b, rest,
    local, keep, got, low_got, high_got, swapped, *refs,
):
    scratch, sems = refs[:7], refs[7:]
    (load_sems, grad_send, grad_recv, grad_local, low_send, low_recv, high_send, high_recv,
     swap_send, swap_recv) = sems
    here, line, place = lax.axis_index("ctx"), lax.axis_index("tp"), lax.axis_index("fsdp")
    column = place // 2
    beside = {"fsdp": lax.rem(place + 2, 4)}
    across = {"tp": 1 - line}
    mesh_id = pl.DeviceIdType.MESH
    slabs, block = qkv_a.shape[0], qkv_a.shape[1]
    loads = [
        pltpu.make_async_copy(source, target, load_sems.at[k])
        for k, (source, target) in enumerate(((keep_hbm, keep), (got_hbm, got)))
    ]
    for load in loads:
        load.start()
    others = [lax.rem(here + k, slabs) for k in range(1, slabs)]
    barrier = pltpu.get_barrier_semaphore()
    for device in (*[{"ctx": z} for z in others], beside, across):
        pl.semaphore_signal(barrier, inc=1, device_id=device, device_id_type=mesh_id)
    pl.semaphore_wait(barrier, slabs + 1)

    def remote(source, target, send, recv, device):
        return pltpu.make_async_remote_copy(
            src_ref=source, dst_ref=target, send_sem=send, recv_sem=recv,
            device_id=device, device_id_type=mesh_id,
        )

    outs = (out_a, out_b)

    def window(h, at):
        return outs[h].at[pl.ds(pl.multiple_of(at * block, block), block), :]

    def attend_head(h, qkv, do_ref, of_ref, lse_ref):
        def emit(z):
            @pl.when(z == here)
            def _():
                pltpu.make_async_copy(
                    local.at[h, z], window(h, here), grad_local.at[h]
                ).start()

            @pl.when(z != here)
            def _():
                remote(
                    local.at[h, z], window(h, here), grad_send.at[h, z], grad_recv.at[h, here],
                    {"ctx": z},
                ).start()

        attend_back_rows(
            tile, len_ref[0], qkv, do_ref, of_ref, lse_ref, local.at[h], scratch, emit
        )

    attend_head(0, qkv_a, do_a, of_a, lse_a)
    for load in loads:
        load.wait()
    cut = rest.shape[0] // 2
    for t in range(2):
        for x in range(2):
            keep[t, x] = (keep[t, x].astype(F32) + got[t, x].astype(F32)).astype(BF)
    moves = []
    for k in range(2):
        moves.append(
            remote(
                keep.at[1 - line, k, 0:cut], low_got.at[k], low_send.at[k], low_recv.at[k], across
            )
        )
        moves.append(
            remote(
                keep.at[k, 1 - column, cut : 2 * cut], high_got.at[k], high_send.at[k],
                high_recv.at[k], beside,
            )
        )
    for move in moves:
        move.start()
    attend_head(1, qkv_b, do_b, of_b, lse_b)
    for move in moves:
        move.wait_recv()
    low, high = slice(0, cut), slice(cut, 2 * cut)
    for k in range(2):
        keep[line, k, low] = (
            keep[line, k, low].astype(F32) + low_got[k].astype(F32)
        ).astype(BF)
        keep[k, column, high] = (
            keep[k, column, high].astype(F32) + high_got[k].astype(F32)
        ).astype(BF)
    swaps = [
        remote(
            keep.at[line, 1 - column, low], swapped.at[0], swap_send.at[0], swap_recv.at[0], beside
        ),
        remote(
            keep.at[1 - line, column, high], swapped.at[1], swap_send.at[1], swap_recv.at[1], across
        ),
    ]
    for move in swaps:
        move.start()
    for move in swaps:
        move.wait_recv()
    for k, part in enumerate((low, high)):
        rest[part] = (
            keep[line, column, part].astype(F32) + swapped[k].astype(F32)
        ).astype(BF)
    for h in range(2):
        pltpu.make_async_copy(local.at[h, here], window(h, here), grad_local.at[h]).wait()
        for z in others:
            remote(
                local.at[h, z], window(h, z), grad_send.at[h, z], grad_recv.at[h, z], {"ctx": z}
            ).wait()
    for move in (*moves, *swaps):
        move.wait_send()


def back_stage(length, qkv, d_mix, saved, keep, got):
    slabs, block, rows = qkv[0].shape
    tile = 512
    lanes = keep.shape[3]
    total = slabs * rows
    work = total * (total + tile) // 2
    vmem = pl.BlockSpec(memory_space=pltpu.VMEM)
    outside = pl.BlockSpec(memory_space=pl.ANY)
    dma = pltpu.SemaphoreType.DMA
    return pl.pallas_call(
        functools.partial(back_kernel, tile),
        out_shape=(
            jax.ShapeDtypeStruct((slabs * block, rows), BF),
            jax.ShapeDtypeStruct((slabs * block, rows), BF),
            jax.ShapeDtypeStruct((256, lanes), BF),
        ),
        in_specs=[pl.BlockSpec(memory_space=pltpu.SMEM)] + [vmem] * 8 + [outside] * 2,
        out_specs=(vmem,) * 3,
        scratch_shapes=[
            pltpu.VMEM((2, slabs, block, rows), BF),
            pltpu.VMEM(keep.shape, BF),
            pltpu.VMEM(keep.shape, BF),
            pltpu.VMEM((2, 128, lanes), BF),
            pltpu.VMEM((2, 128, lanes), BF),
            pltpu.VMEM((2, 128, lanes), BF),
            *attend_back_scratch(slabs, rows, tile),
            dma((2,)), dma((2, slabs)), dma((2, slabs)), dma((2,)),
            dma((2,)), dma((2,)), dma((2,)), dma((2,)), dma((2,)), dma((2,)),
        ],
        compiler_params=pltpu.CompilerParams(
            vmem_limit_bytes=60 << 20, collective_id=4, has_side_effects=True
        ),
        cost_estimate=pl.CostEstimate(
            flops=2 * work * 256 * 10, bytes_accessed=24 << 20, transcendentals=2 * work
        ),
    )(length, *qkv, *d_mix, *[m for m, _ in saved], *[l for _, l in saved], keep, got)


def attend_back(length, qkv, d_mix, mix, lse, tile):
    slabs, _, rows = qkv.shape
    total = slabs * rows
    tile = min(tile, rows)
    work = total * (total + tile) // 2
    vmem = pl.BlockSpec(memory_space=pltpu.VMEM)
    return pl.pallas_call(
        functools.partial(attend_back_kernel, tile),
        out_shape=jax.ShapeDtypeStruct((slabs, 3 * HD, rows), BF),
        in_specs=[pl.BlockSpec(memory_space=pltpu.SMEM), vmem, vmem, vmem, vmem],
        out_specs=vmem,
        scratch_shapes=attend_back_scratch(slabs, rows, tile),
        compiler_params=pltpu.CompilerParams(vmem_limit_bytes=60 << 20),
        cost_estimate=pl.CostEstimate(
            flops=work * 256 * 10, bytes_accessed=qkv.size * 8, transcendentals=work
        ),
    )(length, qkv, d_mix, mix, lse)


def widths(total, step):
    return [(at, min(step, total - at)) for at in range(0, total, step)]


def middle_kernel(
    ff, split, scal, mix_a_hbm, mix_b_hbm, own_hbm, cot_hbm, gain, w_hbm,
    out_ref, dmid_ref, got_a, got_b, *refs,
):
    n_out = 3 if split < w_hbm.shape[2] else 1
    grads = refs[:n_out]
    (w, acts, att_t, mid, scale, dn, normed_ref, branch_ref, dattn_ref, turned, do_a, do_b,
     sems, out_sems, send_sems, recv_sems, local_sems, core_send, core_recv,
     own, cot, mix_a, mix_b, row_sems) = refs[n_out:]
    slabs, halves, _, half = mix_a.shape
    width = own.shape[1]
    side = pl.ds(pl.multiple_of(lax.axis_index("tp") * half, half), half)
    row_loads = [
        pltpu.make_async_copy(source.at[side, :], target, row_sems.at[k])
        for k, (source, target) in enumerate(((own_hbm, own), (cot_hbm, cot)))
    ]
    mix_loads = [
        pltpu.make_async_copy(source, target, row_sems.at[2 + k])
        for k, (source, target) in enumerate(((mix_a_hbm, mix_a), (mix_b_hbm, mix_b)))
    ]
    for load in (*mix_loads, *row_loads):
        load.start()
    inner = width // halves
    base = 3 * ff
    lanes = base + inner
    here, line = lax.axis_index("ctx"), lax.axis_index("tp")
    core = lax.rem(lax.axis_index("fsdp"), 2)
    sibling = {"fsdp": lax.axis_index("fsdp") + 1 - 2 * core}
    barrier = pltpu.get_barrier_semaphore()
    peers = [(dz, dt) for dz in range(slabs) for dt in range(halves) if dz or dt]

    def peer(dz, dt):
        return lax.rem(here + dz, slabs), lax.rem(line + dt, halves)

    for dz, dt in peers:
        z, t = peer(dz, dt)
        pl.semaphore_signal(
            barrier, inc=1, device_id={"ctx": z, "tp": t}, device_id_type=pl.DeviceIdType.MESH
        )
    if n_out == 3:
        pl.semaphore_signal(
            barrier, inc=1, device_id=sibling, device_id_type=pl.DeviceIdType.MESH
        )
    cuts = [(t, base, inner) for t in range(halves)]
    cuts += [(t, k * ff, ff) for t in range(halves) for k in range(3)]
    loads = [
        pltpu.make_async_copy(
            w_hbm.at[t, :, at : at + n], w.at[t, :, at : at + n], sems.at[k]
        )
        for k, (t, at, n) in enumerate(cuts)
    ]
    for load in loads:
        load.start()
    length, first = scal[0], scal[1]
    step = 256
    rows = 64

    for load in mix_loads:
        load.wait()
    for t in range(halves):
        for z in range(slabs):
            at = z * 2 * HD
            att_t[at : at + HD, :] = mix_a[z, t]
            att_t[at + HD : at + 2 * HD, :] = mix_b[z, t]
        acts[t, :, base:lanes] = att_t[...].astype(F32).T.astype(BF)
    for k in range(halves):
        loads[k].wait()
    for load in row_loads:
        load.wait()

    def project(n, _):
        cut = pl.ds(pl.multiple_of(n * step, step), step)
        total = own[:, cut].astype(F32)
        for t in range(halves):
            total = total + mm(acts[t, :, base:lanes], w[t, cut, base:lanes], NT)
        mid[:, cut] = total
        return 0

    lax.fori_loop(0, width // step, project, 0)

    def row_mask(r):
        pos = first + r * rows + lax.broadcasted_iota(jnp.int32, (rows, 1), 0)
        return jnp.where(pos < length, 1.0, 0.0)

    def norm(r, _):
        cut = pl.ds(pl.multiple_of(r * rows, rows), rows)
        values = mid[cut, :]
        inverse = lax.rsqrt(jnp.mean(values * values, axis=1, keepdims=True) + EPSILON)
        scale[cut, :] = jnp.broadcast_to(inverse, (rows, 128))
        normed_ref[cut, :] = (values * inverse * gain[...]).astype(BF)
        branch_ref[cut, :] = (cot[cut, :].astype(F32) * row_mask(r)).astype(BF)
        return 0

    lax.fori_loop(0, half // rows, norm, 0)

    for t in range(halves):
        for k in range(3):
            loads[halves + 3 * t + k].wait()

        def columns(at, n):
            def cut(k):
                return pl.ds(pl.multiple_of(k * ff + at, 128), n)

            gate = mm(normed_ref[...], w[t, :, cut(0)], NN)
            upward = mm(normed_ref[...], w[t, :, cut(1)], NN)
            d_hidden = mm(branch_ref[...], w[t, :, cut(2)], NN)
            sig = 1.0 / (1.0 + jnp.exp(-gate))
            active = gate * sig
            acts[t, :, cut(2)] = (active * upward).astype(BF)
            acts[t, :, cut(0)] = (
                d_hidden * upward * sig * (1.0 + gate * (1.0 - sig))
            ).astype(BF)
            acts[t, :, cut(1)] = (d_hidden * active).astype(BF)

        def chunk(c, _):
            columns(c * step, step)
            return 0

        lax.fori_loop(0, ff // step, chunk, 0)
        if ff % step:
            columns(ff - ff % step, ff % step)

    def back(n, _):
        cut = pl.ds(pl.multiple_of(n * step, step), step)
        total = mid[:, cut]
        grad = jnp.zeros((half, step), F32)
        for t in range(halves):
            total = total + mm(acts[t, :, 2 * ff : base], w[t, cut, 2 * ff : base], NT)
            grad = grad + mm(acts[t, :, 0:ff], w[t, cut, 0:ff], NT)
            grad = grad + mm(acts[t, :, ff : 2 * ff], w[t, cut, ff : 2 * ff], NT)
        dmid_ref[:, cut] = total
        dn[:, cut] = grad
        return 0

    lax.fori_loop(0, width // step, back, 0)

    def finish(r, _):
        cut = pl.ds(pl.multiple_of(r * rows, rows), rows)
        mask = row_mask(r)
        out_ref[cut, :] = (dmid_ref[cut, :] * mask).astype(BF)
        inverse = scale[cut, 0:1]
        scaled = mid[cut, :] * inverse
        d_scaled = dn[cut, :] * gain[...]
        mean = jnp.mean(d_scaled * scaled, axis=1, keepdims=True)
        total = cot[cut, :].astype(F32) * mask + inverse * (d_scaled - scaled * mean)
        dmid_ref[cut, :] = total
        dattn_ref[cut, :] = total.astype(BF)
        return 0

    lax.fori_loop(0, half // rows, finish, 0)
    for t in range(halves):
        for z in range(0, slabs, 2):
            at = base + z * 2 * HD
            grad = mm(dattn_ref[...], w[t, :, at : at + 4 * HD], NN).T.astype(BF)
            for k in range(2):
                do_a[z + k, t] = grad[2 * k * HD : (2 * k + 1) * HD]
                do_b[z + k, t] = grad[(2 * k + 1) * HD : (2 * k + 2) * HD]

    pl.semaphore_wait(barrier, len(peers) + (n_out == 3))
    moves = []
    for k, (dz, dt) in enumerate(peers):
        z, t = peer(dz, dt)
        for h, (source, target) in enumerate(((do_a, got_a), (do_b, got_b))):
            move = pltpu.make_async_remote_copy(
                src_ref=source.at[z, t],
                dst_ref=target.at[here, line],
                send_sem=send_sems.at[2 * k + h],
                recv_sem=recv_sems.at[2 * k + h],
                device_id={"ctx": z, "tp": t},
                device_id_type=pl.DeviceIdType.MESH,
            )
            move.start()
            moves.append(move)
    for h, (source, target) in enumerate(((do_a, got_a), (do_b, got_b))):
        move = pltpu.make_async_copy(
            source.at[here, line], target.at[here, line], local_sems.at[h]
        )
        move.start()
        moves.append(move)

    regions = ((0, 2 * ff), (2 * ff, base), (base, lanes))

    def own_copy(n, t):
        cut = pl.ds(pl.multiple_of(n * step, step), step)
        return pltpu.make_async_copy(
            w.at[t, cut, split:lanes], grads[1].at[t, n // 2], out_sems.at[n, t, 1]
        )

    def core_copy(n, t):
        cut = pl.ds(pl.multiple_of(n * step, step), step)
        return pltpu.make_async_remote_copy(
            src_ref=w.at[t, cut, split:lanes], dst_ref=grads[2].at[t, n // 2],
            send_sem=core_send.at[n, t], recv_sem=core_recv.at[n, t],
            device_id=sibling, device_id_type=pl.DeviceIdType.MESH,
        )

    def some_copy(t):
        return pltpu.make_async_copy(
            w.at[t, :, 0:split], grads[0].at[t], out_sems.at[0, t, 0]
        )

    def store(t):
        if n_out == 1:
            return

        def rows_of(n, _):
            @pl.when(lax.rem(n, 2) == core)
            def _():
                own_copy(n, t).start()

            @pl.when(lax.rem(n, 2) != core)
            def _():
                core_copy(n, t).start()

            return 0

        lax.fori_loop(0, width // step, rows_of, 0)

    for k, ref in enumerate((normed_ref, branch_ref, dattn_ref)):
        for b in range(0, width, step):
            turned[k, b : b + step] = ref[:, b : b + step].astype(F32).T.astype(BF)
    for t in range(halves):

        def fill(k, at, n):
            cut = pl.ds(at, n)
            w[t, :, cut] = mm(turned[k], acts[t, :, cut], NN).astype(BF)

        def span(k, start, stop):
            def chunk(c, _):
                fill(k, pl.multiple_of(start + c * step, 128), step)
                return 0

            count = (stop - start) // step
            lax.fori_loop(0, count, chunk, 0)
            if start + count * step < stop:
                fill(k, start + count * step, stop - start - count * step)

        for k, (at, end) in enumerate(regions):
            if at < split < end:
                span(k, at, split)
                at = split
                some_copy(t).start()
            span(k, at, end)
            if end == split:
                some_copy(t).start()
        store(t)

    for t in range(halves):
        some_copy(t).wait()

        def settle(n, _):
            @pl.when(lax.rem(n, 2) == core)
            def _():
                own_copy(n, t).wait()
                core_copy(n, t).wait_recv()

            @pl.when(lax.rem(n, 2) != core)
            def _():
                core_copy(n, t).wait_send()

            return 0

        if n_out == 3:
            lax.fori_loop(0, width // step, settle, 0)
    for move in moves:
        move.wait()


def middle_stage(scalars, mix_a, mix_b, own, cot, gain, w, split):
    halves, width, lanes = w.shape
    slabs, _, _, half = mix_a.shape
    ff = (lanes - width // halves) // 3
    blocks = width // 256
    peers = slabs * halves - 1
    vmem = pl.BlockSpec(memory_space=pltpu.VMEM)
    outside = pl.BlockSpec(memory_space=pl.ANY)
    out_shape = [
        jax.ShapeDtypeStruct((half, width), BF),
        jax.ShapeDtypeStruct((half, width), F32),
        jax.ShapeDtypeStruct(mix_a.shape, BF),
        jax.ShapeDtypeStruct(mix_a.shape, BF),
        jax.ShapeDtypeStruct((halves, width, split), BF),
    ]
    out_specs = [vmem] * 4 + [outside]
    if split < lanes:
        out_shape += [jax.ShapeDtypeStruct((halves, blocks // 2, 256, lanes - split), BF)] * 2
        out_specs += [outside] * 2
    flops = 2 * half * width * (9 * ff * halves + 3 * width)
    return pl.pallas_call(
        functools.partial(middle_kernel, ff, split),
        out_shape=out_shape,
        in_specs=[
            pl.BlockSpec(memory_space=pltpu.SMEM), *[pl.BlockSpec(memory_space=pltpu.HBM)] * 4,
            vmem, outside,
        ],
        out_specs=out_specs,
        scratch_shapes=[
            pltpu.VMEM((halves, width, lanes), BF),
            pltpu.VMEM((halves, half, lanes), BF),
            pltpu.VMEM((width // halves, half), BF),
            pltpu.VMEM((half, width), F32),
            pltpu.VMEM((half, 128), F32),
            pltpu.VMEM((half, width), F32),
            pltpu.VMEM((half, width), BF),
            pltpu.VMEM((half, width), BF),
            pltpu.VMEM((half, width), BF),
            pltpu.VMEM((3, width, half), BF),
            pltpu.VMEM(mix_a.shape, BF),
            pltpu.VMEM(mix_a.shape, BF),
            pltpu.SemaphoreType.DMA((4 * halves,)),
            pltpu.SemaphoreType.DMA((blocks, halves, 2)),
            pltpu.SemaphoreType.DMA((2 * peers,)),
            pltpu.SemaphoreType.DMA((2 * peers,)),
            pltpu.SemaphoreType.DMA((2,)),
            pltpu.SemaphoreType.DMA((blocks, halves)),
            pltpu.SemaphoreType.DMA((blocks, halves)),
            pltpu.VMEM((half, width), BF),
            pltpu.VMEM((half, width), BF),
            pltpu.VMEM(mix_a.shape, BF),
            pltpu.VMEM(mix_a.shape, BF),
            pltpu.SemaphoreType.DMA((4,)),
        ],
        compiler_params=pltpu.CompilerParams(
            vmem_limit_bytes=60 << 20, collective_id=1, has_side_effects=True
        ),
        cost_estimate=pl.CostEstimate(
            flops=flops, bytes_accessed=4 * w.size + 16 * half * width, transcendentals=half * lanes
        ),
    )(scalars, mix_a, mix_b, own, cot, gain, w)


class LineSum:
    def __init__(self, source, held, slots, out, sems):
        self.source, self.held, self.slots, self.out = source, held, slots, out
        self.sum_send, self.sum_recv, self.out_send, self.out_recv = sems
        here = lax.axis_index("ctx")
        self.low = here < 2
        self.place = jnp.where(self.low, here, 3 - here)
        self.inward = jnp.where(self.low, here + 1, here - 1)
        self.outward = jnp.where(self.low, here - 1, here + 1)
        self.size = out.shape[0] // 4

    def number(self, part):
        return jnp.where(self.low, part, 3 - part)

    def part(self, ref, part):
        at = pl.multiple_of(self.number(part) * self.size, self.size)
        return ref.at[pl.ds(at, self.size), :]

    def read(self, ref, part):
        at = pl.multiple_of(self.number(part) * self.size, self.size)
        return ref[pl.ds(at, self.size), :].astype(F32)

    def write(self, ref, part, value):
        at = pl.multiple_of(self.number(part) * self.size, self.size)
        ref[pl.ds(at, self.size), :] = value.astype(BF)

    def copy(self, source, target, send, recv, place):
        return pltpu.make_async_remote_copy(
            src_ref=source, dst_ref=target, send_sem=send, recv_sem=recv,
            device_id={"ctx": place}, device_id_type=pl.DeviceIdType.MESH,
        )

    def took(self, slot):
        ref = self.slots.at[slot]
        self.copy(ref, ref, self.sum_send.at[0], self.sum_recv.at[slot], self.inward).wait_recv()
        return self.slots[slot].astype(F32)

    def begin(self):
        @pl.when(self.place == 0)
        def _():
            for k in range(3):
                self.copy(
                    self.part(self.source, 3 - k), self.slots.at[k],
                    self.sum_send.at[k], self.sum_recv.at[k], self.inward,
                ).start()

    def left(self, k):
        self.copy(
            self.slots.at[0], self.slots.at[0],
            self.sum_send.at[k], self.sum_recv.at[0], self.inward,
        ).wait_send()

    def first(self, k):
        @pl.when(self.place == 1)
        def _():
            self.write(self.held, 3 - k, self.read(self.source, 3 - k) + self.took(k))
            self.copy(
                self.part(self.held, 3 - k), self.slots.at[3 + k],
                self.sum_send.at[k], self.sum_recv.at[3 + k], self.inward,
            ).start()

    def second(self):
        @pl.when(self.place == 1)
        def _():
            self.write(self.held, 0, self.read(self.source, 0) + self.took(3))
            self.copy(
                self.part(self.held, 0), self.slots.at[3],
                self.sum_send.at[2], self.sum_recv.at[3], self.outward,
            ).start()

    def give(self, part, send, place):
        ref = self.part(self.out, part)
        return self.copy(
            ref, ref, self.out_send.at[send], self.out_recv.at[self.number(part)], place
        )

    def final(self):
        @pl.when(self.place == 1)
        def _():
            self.write(self.out, 1, self.read(self.source, 1) + self.took(2) + self.took(4))
            self.give(1, 0, self.inward).start()
            self.give(1, 1, self.outward).start()

        @pl.when(self.place == 0)
        def _():
            self.write(self.out, 0, self.read(self.source, 0) + self.took(3))
            self.give(0, 0, self.inward).start()

    def forward(self):
        @pl.when(self.place == 1)
        def _():
            for k, (part, place) in enumerate(((0, self.inward), (2, self.outward), (3, self.outward))):
                self.give(part, 2 + k, place).wait_recv()
                self.give(part, 2 + k, place).start()

    def end(self):
        @pl.when(self.place == 0)
        def _():
            for k in range(3):
                self.left(k)
            self.give(0, 0, self.inward).wait_send()
            for part in (1, 2, 3):
                self.give(part, 0, self.inward).wait_recv()

        @pl.when(self.place == 1)
        def _():
            for k in range(3):
                self.left(k)
            for k in range(5):
                self.give(1, k, self.inward).wait_send()


def tail_kernel(
    back_a, back_b, some, rest, normed, weights, own_hbm, gain, dmid,
    grad_out, some_out, rest_out, qa_out, qb_out,
    turned, some_held, some_slots, rest_held, rest_slots,
    local, crossed, column_sum, columned, q_src, q_held, q_slots, theirs, got_theirs, mine,
    core_send, core_recv, col_send, col_recv,
    row_send, row_recv, out_send, out_recv, *line_sems,
):
    here, line, place = lax.axis_index("ctx"), lax.axis_index("tp"), lax.axis_index("fsdp")
    core, column = lax.rem(place, 2), place // 2
    sibling = {"fsdp": place + 1 - 2 * core}
    beside = {"fsdp": lax.rem(place + 2, 4)}
    across = {"tp": 1 - line}
    others = [{"ctx": lax.rem(here + k, 4)} for k in range(1, 4)]
    mesh_id = pl.DeviceIdType.MESH
    barrier = pltpu.get_barrier_semaphore()
    for device in (*others, sibling, beside, across):
        pl.semaphore_signal(barrier, inc=1, device_id=device, device_id_type=mesh_id)
    pl.semaphore_wait(barrier, 6)

    def remote(source, target, send, recv, device):
        return pltpu.make_async_remote_copy(
            src_ref=source, dst_ref=target, send_sem=send, recv_sem=recv,
            device_id=device, device_id_type=mesh_id,
        )

    rows = normed.shape[0]
    half = rows // 2
    depth = 256
    own, own_sem, *line_sems = line_sems
    load = pltpu.make_async_copy(
        own_hbm.at[pl.ds(pl.multiple_of(line * half, half), half), :], own, own_sem
    )
    load.start()
    a, b, qa, qb = (
        LineSum(src, held, slots, out, line_sems[4 * k : 4 * k + 4])
        for k, (src, held, slots, out) in enumerate(
            (
                (some, some_held, some_slots, some_out),
                (rest, rest_held, rest_slots, rest_out),
                (q_src.at[0], q_held.at[0], q_slots.at[0], qa_out),
                (q_src.at[1], q_held.at[1], q_slots.at[1], qb_out),
            )
        )
    )
    a.begin()

    def weight_gradient(h, grads):
        def step(n, _):
            cut = pl.ds(pl.multiple_of(n * depth, depth), depth)
            value = mm(grads[...], normed[:, cut], NN).astype(BF)
            local[h, lax.rem(n, 2), n // 2] = value
            return 0

        lax.fori_loop(0, 4, step, 0)
        move = remote(
            local.at[h, 1 - core], crossed.at[h], core_send.at[h], core_recv.at[h], sibling
        )
        move.start()
        return move

    def column_step(h, move):
        move.wait_recv()
        for x in range(2):
            column_sum[h, x] = (
                local[h, core, x].astype(F32) + crossed[h, x].astype(F32)
            ).astype(BF)
        move = remote(
            column_sum.at[h, 1 - column], columned.at[h], col_send.at[h], col_recv.at[h], beside
        )
        move.start()
        return move

    def column_end(h, move):
        move.wait_recv()
        q_src[h] = (column_sum[h, column].astype(F32) + columned[h].astype(F32)).astype(BF)

    def turn(h, grads):
        for k in range(0, grads.shape[0], 128):
            at = h * grads.shape[0] + k
            turned[:, at : at + 128] = grads[k : k + 128, :].astype(F32).T.astype(BF)

    pieces = 2
    piece = half // pieces
    sent_rows = []
    sent_out = []
    mine_start = pl.multiple_of(line * half, half)

    def make_theirs(k):
        cut = slice(k * piece, (k + 1) * piece)
        start = pl.multiple_of((1 - line) * half + k * piece, piece)

        def make(n, _):
            wide = pl.ds(pl.multiple_of(n * depth, depth), depth)
            value = mm(turned[pl.ds(start, piece), :], weights[:, wide], NN)
            theirs[cut, wide] = value.astype(BF)
            return 0

        lax.fori_loop(0, 4, make, 0)
        move = remote(theirs.at[cut], got_theirs.at[cut], row_send.at[k], row_recv.at[k], across)
        move.start()
        sent_rows.append(move)

    def make_mine(n, _):
        wide = pl.ds(pl.multiple_of(n * depth, depth), depth)
        mine[:, wide] = mm(turned[pl.ds(mine_start, half), :], weights[:, wide], NN)
        return 0

    def finish_rows(k):
        small = 64
        if k == 0:
            load.wait()
        sent_rows[k].wait_recv()

        def back(r, _):
            at = pl.multiple_of(k * piece + r * small, small)
            cut = pl.ds(at, small)
            values = own[cut, :].astype(F32)
            inverse = lax.rsqrt(jnp.mean(values * values, axis=1, keepdims=True) + EPSILON)
            scaled = values * inverse
            d_scaled = (mine[cut, :] + got_theirs[cut, :].astype(F32)) * gain[...]
            mean = jnp.mean(d_scaled * scaled, axis=1, keepdims=True)
            total = dmid[cut, :] + inverse * (d_scaled - scaled * mean)
            grad_out[pl.ds(pl.multiple_of(line * half + at, small), small), :] = total.astype(BF)
            return 0

        lax.fori_loop(0, piece // small, back, 0)
        ref = grad_out.at[pl.ds(pl.multiple_of(line * half + k * piece, piece), piece), :]
        move = remote(ref, ref, out_send.at[k], out_recv.at[k], across)
        move.start()
        sent_out.append(move)

    b.begin()
    turn(0, back_a)
    turn(1, back_b)
    make_theirs(0)
    core_a = weight_gradient(0, back_a)
    a.first(0)
    make_theirs(1)
    core_b = weight_gradient(1, back_b)
    a.first(1)
    col_a = column_step(0, core_a)
    lax.fori_loop(0, 4, make_mine, 0)
    a.second()
    col_b = column_step(1, core_b)
    b.first(0)
    a.final()
    b.first(1)
    finish_rows(0)
    b.second()
    a.forward()
    column_end(0, col_a)
    qa.begin()
    b.final()
    finish_rows(1)
    column_end(1, col_b)
    qb.begin()
    qa.first(0)
    qa.first(1)
    b.forward()
    qb.first(0)
    qb.first(1)
    qa.second()
    qa.final()
    qb.second()
    qb.final()
    qa.forward()
    qb.forward()
    for run in (a, b, qa, qb):
        run.end()
    for move in (core_a, core_b, col_a, col_b, *sent_rows):
        move.wait_send()
    for k, move in enumerate(sent_out):
        move.wait_send()
        ref = grad_out.at[pl.ds(pl.multiple_of((1 - line) * half + k * piece, piece), piece), :]
        remote(ref, ref, out_send.at[k], out_recv.at[k], across).wait_recv()


def tail_stage(back_a, back_b, some, rest, normed, weights, own, gain, dmid):
    rows, width = normed.shape
    half = rows // 2
    lanes_a, lanes_b = some.shape[1], rest.shape[1]
    wide = back_a.shape[0]
    vmem = pl.BlockSpec(memory_space=pltpu.VMEM)
    dma = pltpu.SemaphoreType.DMA
    return pl.pallas_call(
        tail_kernel,
        out_shape=(
            jax.ShapeDtypeStruct((rows, width), BF),
            jax.ShapeDtypeStruct((256, lanes_a), BF),
            jax.ShapeDtypeStruct((256, lanes_b), BF),
            jax.ShapeDtypeStruct((wide, 256), BF),
            jax.ShapeDtypeStruct((wide, 256), BF),
        ),
        in_specs=[vmem] * 6 + [pl.BlockSpec(memory_space=pl.ANY)] + [vmem] * 2,
        out_specs=(vmem,) * 5,
        scratch_shapes=[
            pltpu.VMEM((rows, 2 * wide), BF),
            pltpu.VMEM((256, lanes_a), BF),
            pltpu.VMEM((5, 64, lanes_a), BF),
            pltpu.VMEM((256, lanes_b), BF),
            pltpu.VMEM((5, 64, lanes_b), BF),
            pltpu.VMEM((2, 2, 2, wide, 256), BF),
            pltpu.VMEM((2, 2, wide, 256), BF),
            pltpu.VMEM((2, 2, wide, 256), BF),
            pltpu.VMEM((2, wide, 256), BF),
            pltpu.VMEM((2, wide, 256), BF),
            pltpu.VMEM((2, wide, 256), BF),
            pltpu.VMEM((2, 5, wide // 4, 256), BF),
            pltpu.VMEM((half, width), BF),
            pltpu.VMEM((half, width), BF),
            pltpu.VMEM((half, width), F32),
            dma((2,)), dma((2,)), dma((2,)), dma((2,)),
            dma((2,)), dma((2,)), dma((2,)), dma((2,)),
            pltpu.VMEM((half, width), BF), dma,
        ]
        + [dma((3,)), dma((5,)), dma((5,)), dma((4,))] * 4,
        compiler_params=pltpu.CompilerParams(
            vmem_limit_bytes=60 << 20, collective_id=2, has_side_effects=True
        ),
        cost_estimate=pl.CostEstimate(
            flops=8 * rows * width * wide, bytes_accessed=40 << 20, transcendentals=0
        ),
    )(back_a, back_b, some, rest, normed, weights, own, gain, dmid)


def pack_kernel(gate, up, down_hbm, out_hbm, packed_hbm, packed, down, out, sems):
    ff = gate.shape[1]
    first = packed.at[:, 0 : 2 * ff]
    last = packed.at[:, 2 * ff :]
    loads = [
        pltpu.make_async_copy(source, target, sems.at[k])
        for k, (source, target) in enumerate(
            (
                (gate, packed.at[:, 0:ff]),
                (up, packed.at[:, ff : 2 * ff]),
                (down_hbm, down),
                (out_hbm, out),
            )
        )
    ]
    for move in loads:
        move.start()
    loads[0].wait()
    loads[1].wait()
    stores = [
        pltpu.make_async_copy(first, packed_hbm.at[:, 0 : 2 * ff], sems.at[4]),
        pltpu.make_async_copy(last, packed_hbm.at[:, 2 * ff :], sems.at[5]),
    ]
    stores[0].start()
    loads[2].wait()
    loads[3].wait()
    packed[:, 2 * ff : 3 * ff] = down[...].astype(F32).T.astype(BF)
    packed[:, 3 * ff :] = out[...].astype(F32).T.astype(BF)
    stores[1].start()
    for move in stores:
        move.wait()


def pack_stage(gate, up, down, out):
    depth, ff = gate.shape
    outside = pl.BlockSpec(memory_space=pltpu.HBM)
    return pl.pallas_call(
        pack_kernel,
        out_shape=jax.ShapeDtypeStruct((depth, 3 * ff + out.shape[0]), BF),
        in_specs=[outside] * 4,
        out_specs=outside,
        scratch_shapes=[
            pltpu.VMEM((depth, 3 * ff + out.shape[0]), BF),
            pltpu.VMEM(down.shape, BF),
            pltpu.VMEM(out.shape, BF),
            pltpu.SemaphoreType.DMA((6,)),
        ],
        compiler_params=pltpu.CompilerParams(vmem_limit_bytes=60 << 20),
        cost_estimate=pl.CostEstimate(flops=0, bytes_accessed=14 * depth * ff, transcendentals=0),
    )(gate, up, down, out)


def finish_kernel(
    *refs,
):
    sources, gains, grad_in = refs[:9], refs[9], refs[10]
    gate, up, down, out, qg, kg, vg, part, grad_out = refs[11:20]
    held, grad_held, sems = refs[20:29], refs[29], refs[30]
    some, rest, qa, qb, wq, wk, wv, gate_w, up_w = held
    taken = pltpu.make_async_copy(grad_in, grad_held, sems.at[9])
    given = pltpu.make_async_copy(grad_held, grad_out, sems.at[10])
    loads = [
        pltpu.make_async_copy(source, target, sems.at[k])
        for k, (source, target) in enumerate(zip(sources, held))
    ]
    for load in loads:
        load.start()
    taken.start()
    for load in loads:
        load.wait()
    ff = gate.shape[1]
    split = some.shape[1]
    low = split - ff
    high = ff - low

    def fold(values):
        total = values[:, 0:128]
        for at in range(128, values.shape[1], 128):
            total = total + values[:, at : at + 128]
        return total

    value = some[:, 0:ff].astype(F32)
    gate[...] = value
    taken.wait()
    given.start()
    two = fold(value * gate_w[...].astype(F32))
    value = some[:, ff:split].astype(F32)
    up[:, 0:low] = value
    two = two + fold(value * up_w[:, 0:low].astype(F32))
    value = rest[:, 0:high].astype(F32)
    up[:, low:ff] = value
    two = two + fold(value * up_w[:, low:ff].astype(F32))
    down[...] = rest[:, high : high + ff].astype(F32).T
    out[...] = rest[:, high + ff :].astype(F32).T
    one = jnp.zeros((gate.shape[0], 128), F32)
    for k, (target, weight) in enumerate(((qg, wq), (kg, wk), (vg, wv))):
        for z in range(qa.shape[0] // (3 * HD)):
            at = (3 * z + k) * HD
            value = jnp.concatenate([qa[at : at + HD, :], qb[at : at + HD, :]], axis=0)
            value = value.astype(F32).T
            cut = slice(2 * HD * z, 2 * HD * (z + 1))
            target[:, cut] = value
            one = one + value * weight[:, cut].astype(F32)
    part[...] = jnp.zeros_like(part)
    part[0:1] = jnp.sum(one.T, axis=0, keepdims=True) / gains[0:1]
    part[1:2] = jnp.sum(two.T, axis=0, keepdims=True) / gains[1:2]
    given.wait()


def finish_stage(some, rest, qa, qb, weights, gate_w, up_w, gains, grad):
    depth, ff = gate_w.shape
    inner = weights[0].shape[1]
    vmem = pl.BlockSpec(memory_space=pltpu.VMEM)
    outside = pl.BlockSpec(memory_space=pltpu.HBM)
    shape = jax.ShapeDtypeStruct
    operands = (some, rest, qa, qb, *weights, gate_w, up_w)
    return pl.pallas_call(
        finish_kernel,
        out_shape=(
            shape((depth, ff), F32), shape((depth, ff), F32), shape((ff, depth), F32),
            shape((inner, depth), F32), *[shape((depth, inner), F32)] * 3,
            shape((8, depth), F32), shape(grad.shape, BF),
        ),
        in_specs=[outside] * 9 + [vmem, outside],
        out_specs=(vmem,) * 8 + (outside,),
        scratch_shapes=[
            *[pltpu.VMEM(a.shape, BF) for a in operands], pltpu.VMEM(grad.shape, BF),
            pltpu.SemaphoreType.DMA((11,)),
        ],
        compiler_params=pltpu.CompilerParams(vmem_limit_bytes=60 << 20),
        cost_estimate=pl.CostEstimate(flops=0, bytes_accessed=16 << 20, transcendentals=0),
    )(*operands, gains, grad)


def normalize(values, gain):
    inverse = lax.rsqrt(jnp.mean(values * values, axis=-1, keepdims=True) + EPSILON)
    scaled = values * inverse
    return scaled, inverse, (scaled * gain).astype(BF)


def norm_back(d_normed, scaled, inverse, gain):
    d_scaled = d_normed * gain
    d_values = inverse * (d_scaled - scaled * jnp.mean(d_scaled * scaled, axis=-1, keepdims=True))
    return d_values


def rows_first(values):
    return with_layout_constraint(values, Layout(major_to_minor=tuple(range(values.ndim))))


def swap(values, axis, bit):
    count = lax.axis_size(axis)
    return lax.ppermute(values, axis, [(k, k ^ bit) for k in range(count)])


def both_halves(values):
    other = swap(values, "tp", 1)
    first = lax.axis_index("tp") == 0
    return jnp.concatenate([jnp.where(first, values, other), jnp.where(first, other, values)])


def shards(
    inputs,
    lengths,
    first_gain,
    query_weight,
    key_weight,
    value_weight,
    out_weight,
    second_gain,
    gate_weight,
    up_weight,
    down_weight,
    cotangent,
):
    slabs, halves, parts = lax.axis_size("ctx"), lax.axis_size("tp"), lax.axis_size("fsdp")
    rows, width = inputs.shape[1], inputs.shape[2]
    depth = query_weight.shape[0]
    group = query_weight.shape[1] // HD // slabs
    half = rows // halves
    ff = gate_weight.shape[1]
    everywhere = ("tp", "fsdp")
    side = lax.axis_index("tp") * half

    paired = parts == 4 and halves == 2 and slabs == 4 and group == 2
    w_rest = pack_stage(gate_weight, up_weight, down_weight, out_weight)
    w_rest = rows_first(lax.all_gather(rows_first(w_rest), everywhere, axis=0, tiled=True))
    w_rest = w_rest.reshape(halves, width, -1)
    qkv_width = slabs * 3 * HD

    if paired:
        gains_own = jnp.stack([first_gain.astype(F32), second_gain.astype(F32)])
        gains_own = jnp.concatenate([gains_own, jnp.zeros((6, depth), F32)])
        w_turned, normed_one, gains, *rest = front_stage(
            lengths, inputs[0], gains_own, query_weight, key_weight, value_weight, slabs, halves
        )
        gain_one, gain_two = gains[0], gains[1]
        qkv, arrived = rest[0:2], rest[2:4]
        saved = [(rest[4], rest[6]), (rest[5], rest[7])]
    else:
        gains = lax.all_gather(jnp.stack([first_gain, second_gain]), "fsdp", axis=1, tiled=True)
        gain_one, gain_two = gains[0].astype(F32), gains[1].astype(F32)
        stacked = jnp.stack(
            [w.reshape(depth, slabs, group, HD) for w in (query_weight, key_weight, value_weight)]
        ).transpose(1, 3, 2, 0, 4)
        w_qkv = lax.all_gather(
            stacked.reshape(depth, group * qkv_width), "fsdp", axis=0, tiled=True
        )
        w_heads = [w_qkv[:, h * qkv_width : (h + 1) * qkv_width] for h in range(group)]
        _, _, normed_one = normalize(inputs[0].astype(F32), gain_one)
        qkv = []
        for h in range(group):
            part = mm(w_heads[h], normed_one, (((0,), (1,)), ((), ()))).astype(BF)
            part = part.reshape(slabs, 3 * HD, rows)
            qkv.append(lax.all_to_all(part, "ctx", 0, 0, tiled=True))
        arrived, saved = [], []
        for h in range(group):
            mix, mix_full, lse = attend(lengths, qkv[h], halves, rows)
            saved.append((mix_full, lse))
            mix = mix.reshape(slabs * halves, HD, half)
            mix = lax.all_to_all(mix, ("ctx", "tp"), 0, 0, tiled=True)
            arrived.append(mix.reshape(slabs, halves, HD, half))

    scalars = jnp.stack([lengths[0], lax.axis_index("ctx") * rows + side])
    split = 2304 if paired else w_rest.shape[2]
    output, d_middle, *d_mix, = middle_stage(
        scalars, *arrived, inputs[0], cotangent[0], gain_two[None], w_rest, split
    )
    d_mix, (g_some, *g_rest) = d_mix[:2], d_mix[2:]
    output = both_halves(output)
    s_some = lax.psum_scatter(
        rows_first(g_some.reshape(halves * width, -1)), everywhere, scatter_dimension=0, tiled=True
    )
    s_some = rows_first(s_some)

    if paired:
        back_a, back_b, g_rest = back_stage(lengths, qkv, d_mix, saved, *g_rest)
        input_gradient, s_some, s_rest, *q_grads = tail_stage(
            back_a, back_b, s_some, g_rest, normed_one, w_turned, inputs[0], gain_one[None], d_middle
        )
        s_gate, s_up, s_down, s_out, *s_qkv, d_gains, input_gradient = finish_stage(
            s_some, s_rest, *q_grads, (query_weight, key_weight, value_weight), gate_weight,
            up_weight, gains_own, input_gradient,
        )
        d_gains = d_gains[0:2]
        d_gains = d_gains + swap(d_gains, "tp", 1)
    else:
        d_local = [
            attend_back(lengths, qkv[h], d_mix[h], *saved[h], 512) for h in range(group)
        ]
        d_qkv = [
            lax.all_to_all(d, "ctx", 0, 0, tiled=True).reshape(qkv_width, rows) for d in d_local
        ]
        d_normed_one = jnp.zeros((rows, width), F32)
        s_qkv = []
        for h in range(group):
            d_normed_one = d_normed_one + mm(d_qkv[h], w_heads[h], (((0,), (1,)), ((), ())))
            grad = mm(normed_one, d_qkv[h], (((0,), (1,)), ((), ()))).astype(BF)
            grad = lax.psum_scatter(grad, "fsdp", scatter_dimension=0, tiled=True)
            s_qkv.append(lax.psum(grad, "ctx").reshape(depth, slabs, 3, HD))
        d_normed_one = lax.psum_scatter(d_normed_one, "tp", scatter_dimension=0, tiled=True)
        own = lax.dynamic_slice_in_dim(inputs[0], side, half, 0)
        scaled_one, inverse_one, _ = normalize(own.astype(F32), gain_one)
        d_from_one = norm_back(d_normed_one, scaled_one, inverse_one, gain_one)
        input_gradient = lax.all_gather(
            (d_middle + d_from_one).astype(BF), "tp", axis=0, tiled=True
        )
        s_qkv = jnp.stack(s_qkv, axis=2).transpose(3, 0, 1, 2, 4)
        s_qkv = s_qkv.reshape(3, depth, slabs * group * HD).astype(F32)
        s_all = lax.psum(s_some, "ctx").astype(F32)
        d_gain_one = sum(
            jnp.sum(w.astype(F32) * s, axis=1)
            for w, s in zip((query_weight, key_weight, value_weight), s_qkv)
        ) / first_gain.astype(F32)
        d_gain_two = (
            jnp.sum(gate_weight.astype(F32) * s_all[:, :ff], axis=1)
            + jnp.sum(up_weight.astype(F32) * s_all[:, ff : 2 * ff], axis=1)
        ) / second_gain.astype(F32)
        d_gains = jnp.stack([d_gain_one, d_gain_two])
        d_gains = lax.psum(d_gains, "tp")
        s_gate, s_up, s_down, s_out = (
            s_all[:, :ff], s_all[:, ff : 2 * ff], s_all[:, 2 * ff : 3 * ff].T, s_all[:, 3 * ff :].T
        )

    return (
        output[None],
        input_gradient[None],
        d_gains[0],
        s_qkv[0],
        s_qkv[1],
        s_qkv[2],
        s_out,
        d_gains[1],
        s_gate,
        s_up,
        s_down,
    )


def solution(mesh):
    rows = P("fsdp", "ctx", None)
    gain = P("fsdp")
    inward = P("fsdp", "tp")
    outward = P("tp", "fsdp")
    return jax.shard_map(
        shards,
        mesh=mesh,
        in_specs=(
            rows, gain, gain, inward, inward, inward, outward, gain, inward, inward, outward, rows,
        ),
        out_specs=(
            rows, rows, gain, inward, inward, inward, outward, gain, inward, inward, outward,
        ),
        check_vma=False,
    )
```

```python
import functools

import jax
import jax.numpy as jnp
from jax import lax
from jax.experimental import pallas as pl
from jax.experimental.pallas import tpu as pltpu
from jax.experimental.layout import Layout, with_layout_constraint
from jax.sharding import PartitionSpec as P

HD = 64
EPSILON = 1e-05
MASKED = -1000000000.0
NN = (((1,), (0,)), ((), ()))
NT = (((1,), (1,)), ((), ()))
TN = (((0,), (0,)), ((), ()))
BF = jnp.bfloat16
F32 = jnp.float32


def mm(left, right, dims):
    return lax.dot_general(left, right, dims, preferred_element_type=F32)


def spread_keys(keys, start, length):
    rows = keys.shape[0]
    pos = start + lax.broadcasted_iota(jnp.int32, (rows, HD), 0)
    lane = lax.broadcasted_iota(jnp.int32, (rows, HD), 1)
    bias = jnp.where((lane == 0) & (pos >= length), MASKED, 0.0)
    return jnp.concatenate([keys, bias], axis=1).astype(BF)


def spread_queries(queries):
    row = lax.broadcasted_iota(jnp.int32, queries.shape, 0)
    ones = jnp.where(row == 0, 1.0, 0.0)
    return jnp.concatenate([queries * HD**-0.5, ones], axis=0).astype(BF)


def attend_rows(tile, length, qkv, kx, qx, vx, emit):
    slabs, _, rows = qkv.shape
    per = rows // tile
    blocks = slabs * per
    for z in range(slabs):
        keys = qkv[z, HD : 2 * HD, :].astype(F32).T
        kx[z * rows : (z + 1) * rows, :] = spread_keys(keys, z * rows, length)
        queries = spread_queries(qkv[z, 0:HD, :].astype(F32))
        for b in range(per):
            cut = slice(b * tile, (b + 1) * tile)
            qx[z * per + b] = queries[:, cut]
            vx[z * per + b] = qkv[z, 2 * HD : 3 * HD, cut]
    later = lax.broadcasted_iota(jnp.int32, (tile, tile), 0) > lax.broadcasted_iota(
        jnp.int32, (tile, tile), 1
    )

    def query_block(i, _):
        queries = qx[i]

        def step(j, carry, masked):
            highest, total, mix = carry
            keys = kx[pl.ds(pl.multiple_of(j * tile, tile), tile), :]
            scores = mm(keys, queries, NN)
            if masked:
                scores = jnp.where(later, MASKED, scores)
            new = jnp.maximum(highest, jnp.max(scores, axis=0, keepdims=True))
            scale = jnp.exp(highest - new)
            probs = jnp.exp(scores - new)
            total = total * scale + jnp.sum(probs, axis=0, keepdims=True)
            mix = mix * scale + mm(vx[j], probs.astype(BF), NN)
            return new, total, mix

        first = (
            jnp.full((1, tile), -jnp.inf, F32),
            jnp.zeros((1, tile), F32),
            jnp.zeros((HD, tile), F32),
        )
        carry = lax.fori_loop(0, i, lambda j, c: step(j, c, False), first)
        highest, total, mix = step(i, carry, True)
        emit(i, mix / total, highest + jnp.log(total))
        return 0

    lax.fori_loop(0, blocks, query_block, 0)


def attend_kernel(tile, len_ref, qkv, o_ref, of_ref, lse_ref, kx, qx, vx):
    rows = qkv.shape[2]
    halves = o_ref.shape[1]
    half = rows // halves

    def emit(i, mix, lse):
        of_ref[i] = mix
        lse_ref[i] = lse
        for t in range(halves):
            o_ref[i, t] = mix[:, t * half : (t + 1) * half].astype(BF)

    attend_rows(tile, len_ref[0], qkv, kx, qx, vx, emit)


def front_kernel(
    len_ref, x, gains_own, wq, wk, wv,
    wt_hbm, normed_hbm, gains, qkv_a_hbm, qkv_b_hbm, mix_a, mix_b, of_a_hbm, of_b_hbm,
    lse_a_hbm, lse_b_hbm,
    wt, normed, qkv_a, qkv_b, of_a, of_b, lse_a, lse_b, out_sems, packed, parts, mixed, kx, qx, vx,
    gain_send, gain_recv, w_send, w_recv, part_send, part_recv, part_local,
    mix_send, mix_recv, mix_local,
):
    here, line, place = lax.axis_index("ctx"), lax.axis_index("tp"), lax.axis_index("fsdp")
    core, column = lax.rem(place, 2), place // 2
    pair = place + 1 - 2 * core
    other = lax.rem(place + 2, 4)
    mesh_id = pl.DeviceIdType.MESH
    slabs, halves = mix_a.shape[0], mix_a.shape[1]
    rows, width = x.shape
    half = rows // halves
    wide = slabs * 3 * HD
    depth = wq.shape[0]
    peers = [(dz, dt) for dz in range(slabs) for dt in range(halves) if dz or dt]

    def peer(dz, dt):
        return lax.rem(here + dz, slabs), lax.rem(line + dt, halves)

    barrier = pltpu.get_barrier_semaphore()
    for dz, dt in peers:
        z, t = peer(dz, dt)
        pl.semaphore_signal(barrier, inc=1, device_id={"ctx": z, "tp": t}, device_id_type=mesh_id)
    for device in (pair, other):
        pl.semaphore_signal(barrier, inc=1, device_id={"fsdp": device}, device_id_type=mesh_id)
    for q, w in enumerate((wq, wk, wv)):
        flat = w[...].astype(F32).T.astype(BF)
        for z in range(slabs):
            for h in range(2):
                at = (2 * z + h) * HD
                packed[h, (3 * z + q) * HD : (3 * z + q + 1) * HD, :] = flat[at : at + HD]

    def remote(source, target, send, recv, device):
        return pltpu.make_async_remote_copy(
            src_ref=source, dst_ref=target, send_sem=send, recv_sem=recv,
            device_id=device, device_id_type=mesh_id,
        )

    def lanes(index):
        return pl.ds(pl.multiple_of(index * depth, depth), depth)

    def weight(h, index):
        return wt.at[h * wide : (h + 1) * wide, lanes(index)]

    gains[:, lanes(place)] = gains_own[...]
    for h in range(2):
        wt[h * wide : (h + 1) * wide, lanes(place)] = packed[h]
    pl.semaphore_wait(barrier, len(peers) + 2)
    sent = []

    def launch(move):
        move.start()
        sent.append(move)
        return move

    for k, device in enumerate((pair, other)):
        launch(
            remote(
                gains_own, gains.at[:, lanes(place)], gain_send.at[k], gain_recv.at[k], {"fsdp": device}
            )
        )
    for h in range(2):
        for k, device in ((1, other), (0, pair)):
            launch(
                remote(
                    packed.at[h], weight(h, place), w_send.at[h, k], w_recv.at[h, k], {"fsdp": device}
                )
            )

    def arrived(ref, sem):
        remote(ref, ref, gain_send.at[0], sem, {"fsdp": pair}).wait_recv()

    arrived(gains.at[:, lanes(other)], gain_recv.at[1])
    launch(
        remote(
            gains.at[:, lanes(other)], gains.at[:, lanes(other)], gain_send.at[2], gain_recv.at[2],
            {"fsdp": pair},
        )
    )
    far = lax.rem(pair + 2, 4)
    arrived(gains.at[:, lanes(pair)], gain_recv.at[0])
    arrived(gains.at[:, lanes(far)], gain_recv.at[2])
    small = 64

    def norm(r, _):
        cut = pl.ds(pl.multiple_of(r * small, small), small)
        values = x[cut, :].astype(F32)
        inverse = lax.rsqrt(jnp.mean(values * values, axis=1, keepdims=True) + EPSILON)
        normed[cut, :] = (values * inverse * gains[0:1, :]).astype(BF)
        return 0

    lax.fori_loop(0, rows // small, norm, 0)
    kept = []

    def keep(source, target):
        move = pltpu.make_async_copy(source, target, out_sems.at[len(kept)])
        move.start()
        kept.append(move)

    keep(normed, normed_hbm)
    queues = (qkv_a, qkv_b)
    waits = []
    for h in range(2):
        arrived(weight(h, other), w_recv.at[h, 1])
        launch(
            remote(
                weight(h, other), weight(h, other), w_send.at[h, 2], w_recv.at[h, 2], {"fsdp": pair}
            )
        )
    for h in range(2):
        arrived(weight(h, pair), w_recv.at[h, 0])
        arrived(weight(h, far), w_recv.at[h, 2])

        def project(n, _):
            cut = pl.ds(pl.multiple_of(n * 256, 256), 256)
            value = mm(wt[h * wide : (h + 1) * wide, :], normed[cut, :], NT).astype(BF)
            for z in range(slabs):
                parts[h, z, :, cut] = value[z * 3 * HD : (z + 1) * 3 * HD]
            return 0

        lax.fori_loop(0, rows // 256, project, 0)
        for k in range(1, slabs):
            z = lax.rem(here + k, slabs)
            waits.append(
                launch(
                    remote(
                        parts.at[h, z], queues[h].at[here], part_send.at[h, k], part_recv.at[h, k],
                        {"ctx": z},
                    )
                )
            )
        stays = pltpu.make_async_copy(parts.at[h, here], queues[h].at[here], part_local.at[h])
        stays.start()
        waits.append(stays)

    keep(wt, wt_hbm)
    for h, (qkv, mix_ref, of_ref, lse_ref) in enumerate(
        ((qkv_a, mix_a, of_a, lse_a), (qkv_b, mix_b, of_b, lse_b))
    ):
        for move in waits[h * slabs : (h + 1) * slabs - 1]:
            move.wait_recv()
        waits[(h + 1) * slabs - 1].wait()
        keep(qkv, (qkv_a_hbm, qkv_b_hbm)[h])

        def emit(i, mix, lse):
            of_ref[i] = mix
            lse_ref[i] = lse
            for t in range(halves):
                mixed[h, i, t] = mix[:, t * half : (t + 1) * half].astype(BF)
                stay = (i == here) & (line == t)

                @pl.when(stay)
                def _():
                    pltpu.make_async_copy(
                        mixed.at[h, i, t], mix_ref.at[here, line], mix_local.at[h]
                    ).start()

                @pl.when(jnp.logical_not(stay))
                def _():
                    remote(
                        mixed.at[h, i, t], mix_ref.at[here, line], mix_send.at[h, i, t],
                        mix_recv.at[h, here, line], {"ctx": i, "tp": t},
                    ).start()

        attend_rows(rows, len_ref[0], qkv, kx, qx, vx, emit)
        keep(of_ref, (of_a_hbm, of_b_hbm)[h])
        keep(lse_ref, (lse_a_hbm, lse_b_hbm)[h])

    for move in sent:
        move.wait_send()
    for move in kept:
        move.wait()
    for h, mix_ref in enumerate((mix_a, mix_b)):
        pltpu.make_async_copy(mixed.at[h, here, line], mix_ref.at[here, line], mix_local.at[h]).wait()
        for dz, dt in peers:
            z, t = peer(dz, dt)
            remote(
                mixed.at[h, z, t], mix_ref.at[z, t], mix_send.at[h, z, t], mix_recv.at[h, z, t],
                {"ctx": z, "tp": t},
            ).wait()


def front_stage(length, x, gains, wq, wk, wv, slabs, halves):
    rows, width = x.shape
    half = rows // halves
    wide = slabs * 3 * HD
    total = slabs * rows
    work = total * (total + rows) // 2
    vmem = pl.BlockSpec(memory_space=pltpu.VMEM)
    outside = pl.BlockSpec(memory_space=pltpu.HBM)
    dma = pltpu.SemaphoreType.DMA
    shape = jax.ShapeDtypeStruct
    return pl.pallas_call(
        front_kernel,
        out_shape=(
            shape((2 * wide, width), BF),
            shape((rows, width), BF),
            shape((8, width), F32),
            *[shape((slabs, 3 * HD, rows), BF)] * 2,
            *[shape((slabs, halves, HD, half), BF)] * 2,
            *[shape((slabs, HD, rows), F32)] * 2,
            *[shape((slabs, 1, rows), F32)] * 2,
        ),
        in_specs=[pl.BlockSpec(memory_space=pltpu.SMEM)] + [vmem] * 5,
        out_specs=(outside, outside, vmem, *[outside] * 8),
        scratch_shapes=[
            pltpu.VMEM((2 * wide, width), BF),
            pltpu.VMEM((rows, width), BF),
            *[pltpu.VMEM((slabs, 3 * HD, rows), BF)] * 2,
            *[pltpu.VMEM((slabs, HD, rows), F32)] * 2,
            *[pltpu.VMEM((slabs, 1, rows), F32)] * 2,
            dma((8,)),
            pltpu.VMEM((2, wide, wq.shape[0]), BF),
            pltpu.VMEM((2, slabs, 3 * HD, rows), BF),
            pltpu.VMEM((2, slabs, halves, HD, half), BF),
            pltpu.VMEM((total, 2 * HD), BF),
            pltpu.VMEM((slabs, 2 * HD, rows), BF),
            pltpu.VMEM((slabs, HD, rows), BF),
            dma((3,)), dma((3,)), dma((2, 3)), dma((2, 3)),
            dma((2, slabs)), dma((2, slabs)), dma((2,)),
            dma((2, slabs, halves)), dma((2, slabs, halves)), dma((2,)),
        ],
        compiler_params=pltpu.CompilerParams(
            vmem_limit_bytes=60 << 20, collective_id=3, has_side_effects=True
        ),
        cost_estimate=pl.CostEstimate(
            flops=2 * work * 256 * 4, bytes_accessed=20 << 20, transcendentals=2 * work
        ),
    )(length, x, gains, wq, wk, wv)


def attend(length, qkv, halves, tile):
    slabs, _, rows = qkv.shape
    total = slabs * rows
    tile = min(tile, rows)
    work = total * (total + tile) // 2
    vmem = pl.BlockSpec(memory_space=pltpu.VMEM)
    return pl.pallas_call(
        functools.partial(attend_kernel, tile),
        out_shape=(
            jax.ShapeDtypeStruct((slabs, halves, HD, rows // halves), BF),
            jax.ShapeDtypeStruct((slabs, HD, rows), F32),
            jax.ShapeDtypeStruct((slabs, 1, rows), F32),
        ),
        in_specs=[pl.BlockSpec(memory_space=pltpu.SMEM), vmem],
        out_specs=(vmem, vmem, vmem),
        scratch_shapes=[
            pltpu.VMEM((total, 2 * HD), BF),
            pltpu.VMEM((total // tile, 2 * HD, tile), BF),
            pltpu.VMEM((total // tile, HD, tile), BF),
        ],
        compiler_params=pltpu.CompilerParams(vmem_limit_bytes=60 << 20),
        cost_estimate=pl.CostEstimate(
            flops=work * 256 * 4, bytes_accessed=qkv.size * 4, transcendentals=work
        ),
    )(length, qkv)


def attend_back_rows(tile, length, qkv, do_ref, of_ref, lse_ref, out, scratch, emit):
    kx, qx, vx, kt, dox, dq, st, dk, dv = scratch
    slabs, _, rows = qkv.shape
    halves, half = do_ref.shape[1], do_ref.shape[3]
    per = rows // tile
    blocks = slabs * per
    for z in range(slabs):
        keys = qkv[z, HD : 2 * HD, :]
        kx[z * rows : (z + 1) * rows, :] = spread_keys(keys.astype(F32).T, z * rows, length)
        queries = spread_queries(qkv[z, 0:HD, :].astype(F32))
        values = qkv[z, 2 * HD : 3 * HD, :].astype(F32).T
        vx[z * rows : (z + 1) * rows, :] = jnp.concatenate(
            [values, jnp.zeros((rows, HD), F32)], axis=1
        ).astype(BF)
        d_mix = jnp.concatenate([do_ref[z, t] for t in range(halves)], axis=1)
        delta = jnp.sum(d_mix.astype(F32) * of_ref[z], axis=0, keepdims=True)
        for b in range(per):
            cut = slice(b * tile, (b + 1) * tile)
            n = z * per + b
            qx[n] = queries[:, cut]
            kt[n] = keys[:, cut]
            dox[n, 0:HD] = d_mix[:, cut]
            dox[n, HD : 2 * HD] = jnp.zeros((HD, tile), BF)
            st[n, 0:1] = lse_ref[z, :, cut]
            st[n, 1:2] = delta[:, cut]
    for ref in (dq, dk, dv):
        ref[...] = jnp.zeros_like(ref)
    later = lax.broadcasted_iota(jnp.int32, (tile, tile), 0) > lax.broadcasted_iota(
        jnp.int32, (tile, tile), 1
    )

    def step(i, j, masked):
        here = pl.ds(pl.multiple_of(j * tile, tile), tile)
        scores = mm(kx[here, :], qx[i], NN)
        if masked:
            scores = jnp.where(later, MASKED, scores)
        probs = jnp.exp(scores - st[i, 0:1])
        d_probs = mm(vx[here, :], dox[i], NN)
        d_scores = (probs * (d_probs - st[i, 1:2])).astype(BF)
        dv[j] += mm(dox[i, 0:HD], probs.astype(BF), NT)
        dk[j] += mm(qx[i, 0:HD], d_scores, NT)
        dq[i] += mm(kt[j], d_scores, NN)

    def complete(n):
        z = n // per
        cut = pl.ds(pl.multiple_of(lax.rem(n, per) * tile, tile), tile)
        out[z, 0:HD, cut] = (dq[n] * HD**-0.5).astype(BF)
        out[z, HD : 2 * HD, cut] = dk[n].astype(BF)
        out[z, 2 * HD : 3 * HD, cut] = dv[n].astype(BF)
        if emit is not None:
            emit(n)

    def ring(k, _):
        last = blocks - 1 - k

        def down(i, _):
            step(i, k, False)
            return 0

        def across(j, _):
            step(last, j, False)
            return 0

        step(k, k, True)
        lax.fori_loop(k + 1, last + 1, down, 0)
        complete(k)
        lax.fori_loop(k + 1, last, across, 0)
        step(last, last, True)
        complete(last)
        return 0

    lax.fori_loop(0, blocks // 2, ring, 0)


def attend_back_scratch(slabs, rows, tile):
    total = slabs * rows
    blocks = total // tile
    return [
        pltpu.VMEM((total, 2 * HD), BF),
        pltpu.VMEM((blocks, 2 * HD, tile), BF),
        pltpu.VMEM((total, 2 * HD), BF),
        pltpu.VMEM((blocks, HD, tile), BF),
        pltpu.VMEM((blocks, 2 * HD, tile), BF),
        pltpu.VMEM((blocks, HD, tile), F32),
        pltpu.VMEM((blocks, 8, tile), F32),
        pltpu.VMEM((blocks, HD, tile), F32),
        pltpu.VMEM((blocks, HD, tile), F32),
    ]


def attend_back_kernel(tile, len_ref, qkv, do_ref, of_ref, lse_ref, out, *scratch):
    attend_back_rows(tile, len_ref[0], qkv, do_ref, of_ref, lse_ref, out, scratch, None)


def back_kernel(
    tile, len_ref, qkv_a, qkv_b, do_a, do_b, of_a, of_b, lse_a, lse_b, keep_hbm, got_hbm,
    out_a, out_b, rest,
    local, keep, got, low_got, high_got, swapped, *refs,
):
    scratch, sems = refs[:9], refs[9:]
    (load_sems, grad_send, grad_recv, grad_local, low_send, low_recv, high_send, high_recv,
     swap_send, swap_recv) = sems
    here, line, place = lax.axis_index("ctx"), lax.axis_index("tp"), lax.axis_index("fsdp")
    column = place // 2
    beside = {"fsdp": lax.rem(place + 2, 4)}
    across = {"tp": 1 - line}
    mesh_id = pl.DeviceIdType.MESH
    slabs, block = qkv_a.shape[0], qkv_a.shape[1]
    loads = [
        pltpu.make_async_copy(source, target, load_sems.at[k])
        for k, (source, target) in enumerate(((keep_hbm, keep), (got_hbm, got)))
    ]
    for load in loads:
        load.start()
    others = [lax.rem(here + k, slabs) for k in range(1, slabs)]
    barrier = pltpu.get_barrier_semaphore()
    for device in (*[{"ctx": z} for z in others], beside, across):
        pl.semaphore_signal(barrier, inc=1, device_id=device, device_id_type=mesh_id)
    pl.semaphore_wait(barrier, slabs + 1)

    def remote(source, target, send, recv, device):
        return pltpu.make_async_remote_copy(
            src_ref=source, dst_ref=target, send_sem=send, recv_sem=recv,
            device_id=device, device_id_type=mesh_id,
        )

    outs = (out_a, out_b)

    per = qkv_a.shape[2] // tile

    def lanes(b):
        return pl.ds(pl.multiple_of(b * tile, tile), tile)

    def window(h, at, b):
        return outs[h].at[pl.ds(pl.multiple_of(at * block, block), block), lanes(b)]

    def attend_head(h, qkv, do_ref, of_ref, lse_ref):
        def emit(n):
            z, b = n // per, lax.rem(n, per)

            @pl.when(z == here)
            def _():
                pltpu.make_async_copy(
                    local.at[h, z, :, lanes(b)], window(h, here, b), grad_local.at[h, b]
                ).start()

            @pl.when(z != here)
            def _():
                remote(
                    local.at[h, z, :, lanes(b)], window(h, here, b), grad_send.at[h, z, b],
                    grad_recv.at[h, here, b], {"ctx": z},
                ).start()

        attend_back_rows(
            tile, len_ref[0], qkv, do_ref, of_ref, lse_ref, local.at[h], scratch, emit
        )

    attend_head(0, qkv_a, do_a, of_a, lse_a)
    for load in loads:
        load.wait()
    cut = rest.shape[0] // 2
    for t in range(2):
        for x in range(2):
            keep[t, x] = (keep[t, x].astype(F32) + got[t, x].astype(F32)).astype(BF)
    moves = []
    for k in range(2):
        moves.append(
            remote(
                keep.at[1 - line, k, 0:cut], low_got.at[k], low_send.at[k], low_recv.at[k], across
            )
        )
        moves.append(
            remote(
                keep.at[k, 1 - column, cut : 2 * cut], high_got.at[k], high_send.at[k],
                high_recv.at[k], beside,
            )
        )
    for move in moves:
        move.start()
    attend_head(1, qkv_b, do_b, of_b, lse_b)
    for move in moves:
        move.wait_recv()
    low, high = slice(0, cut), slice(cut, 2 * cut)
    for k in range(2):
        keep[line, k, low] = (
            keep[line, k, low].astype(F32) + low_got[k].astype(F32)
        ).astype(BF)
        keep[k, column, high] = (
            keep[k, column, high].astype(F32) + high_got[k].astype(F32)
        ).astype(BF)
    swaps = [
        remote(
            keep.at[line, 1 - column, low], swapped.at[0], swap_send.at[0], swap_recv.at[0], beside
        ),
        remote(
            keep.at[1 - line, column, high], swapped.at[1], swap_send.at[1], swap_recv.at[1], across
        ),
    ]
    for move in swaps:
        move.start()
    for move in swaps:
        move.wait_recv()
    for k, part in enumerate((low, high)):
        rest[part] = (
            keep[line, column, part].astype(F32) + swapped[k].astype(F32)
        ).astype(BF)
    for h in range(2):
        for b in range(per):
            pltpu.make_async_copy(
                local.at[h, here, :, lanes(b)], window(h, here, b), grad_local.at[h, b]
            ).wait()
            for z in others:
                remote(
                    local.at[h, z, :, lanes(b)], window(h, z, b), grad_send.at[h, z, b],
                    grad_recv.at[h, z, b], {"ctx": z},
                ).wait()
    for move in (*moves, *swaps):
        move.wait_send()


def back_stage(length, qkv, d_mix, saved, keep, got):
    slabs, block, rows = qkv[0].shape
    tile = 512
    lanes = keep.shape[3]
    total = slabs * rows
    work = total * (total + tile) // 2
    vmem = pl.BlockSpec(memory_space=pltpu.VMEM)
    outside = pl.BlockSpec(memory_space=pl.ANY)
    dma = pltpu.SemaphoreType.DMA
    return pl.pallas_call(
        functools.partial(back_kernel, tile),
        out_shape=(
            jax.ShapeDtypeStruct((slabs * block, rows), BF),
            jax.ShapeDtypeStruct((slabs * block, rows), BF),
            jax.ShapeDtypeStruct((256, lanes), BF),
        ),
        in_specs=[pl.BlockSpec(memory_space=pltpu.SMEM)] + [vmem] * 8 + [outside] * 2,
        out_specs=(vmem,) * 3,
        scratch_shapes=[
            pltpu.VMEM((2, slabs, block, rows), BF),
            pltpu.VMEM(keep.shape, BF),
            pltpu.VMEM(keep.shape, BF),
            pltpu.VMEM((2, 128, lanes), BF),
            pltpu.VMEM((2, 128, lanes), BF),
            pltpu.VMEM((2, 128, lanes), BF),
            *attend_back_scratch(slabs, rows, tile),
            dma((2,)), dma((2, slabs, rows // tile)), dma((2, slabs, rows // tile)),
            dma((2, rows // tile)),
            dma((2,)), dma((2,)), dma((2,)), dma((2,)), dma((2,)), dma((2,)),
        ],
        compiler_params=pltpu.CompilerParams(
            vmem_limit_bytes=60 << 20, collective_id=4, has_side_effects=True
        ),
        cost_estimate=pl.CostEstimate(
            flops=2 * work * 256 * 10, bytes_accessed=24 << 20, transcendentals=2 * work
        ),
    )(length, *qkv, *d_mix, *[m for m, _ in saved], *[l for _, l in saved], keep, got)


def attend_back(length, qkv, d_mix, mix, lse, tile):
    slabs, _, rows = qkv.shape
    total = slabs * rows
    tile = min(tile, rows)
    work = total * (total + tile) // 2
    vmem = pl.BlockSpec(memory_space=pltpu.VMEM)
    return pl.pallas_call(
        functools.partial(attend_back_kernel, tile),
        out_shape=jax.ShapeDtypeStruct((slabs, 3 * HD, rows), BF),
        in_specs=[pl.BlockSpec(memory_space=pltpu.SMEM), vmem, vmem, vmem, vmem],
        out_specs=vmem,
        scratch_shapes=attend_back_scratch(slabs, rows, tile),
        compiler_params=pltpu.CompilerParams(vmem_limit_bytes=60 << 20),
        cost_estimate=pl.CostEstimate(
            flops=work * 256 * 10, bytes_accessed=qkv.size * 8, transcendentals=work
        ),
    )(length, qkv, d_mix, mix, lse)


def widths(total, step):
    return [(at, min(step, total - at)) for at in range(0, total, step)]


def middle_kernel(
    ff, split, scal, mix_a_hbm, mix_b_hbm, own_hbm, cot_hbm, gain, w_hbm,
    out_ref, dmid_ref, got_a, got_b, *refs,
):
    n_out = 3 if split < w_hbm.shape[2] else 1
    grads = refs[:n_out]
    (w, acts, att_t, mid, scale, dn, normed_ref, branch_ref, dattn_ref, turned, do_a, do_b,
     sems, out_sems, send_sems, recv_sems, local_sems, core_send, core_recv,
     own, cot, mix_a, mix_b, row_sems) = refs[n_out:]
    slabs, halves, _, half = mix_a.shape
    width = own.shape[1]
    side = pl.ds(pl.multiple_of(lax.axis_index("tp") * half, half), half)
    row_loads = [
        pltpu.make_async_copy(source.at[side, :], target, row_sems.at[k])
        for k, (source, target) in enumerate(((own_hbm, own), (cot_hbm, cot)))
    ]
    mix_loads = [
        pltpu.make_async_copy(source, target, row_sems.at[2 + k])
        for k, (source, target) in enumerate(((mix_a_hbm, mix_a), (mix_b_hbm, mix_b)))
    ]
    for load in (*mix_loads, *row_loads):
        load.start()
    inner = width // halves
    base = 3 * ff
    lanes = base + inner
    here, line = lax.axis_index("ctx"), lax.axis_index("tp")
    core = lax.rem(lax.axis_index("fsdp"), 2)
    sibling = {"fsdp": lax.axis_index("fsdp") + 1 - 2 * core}
    barrier = pltpu.get_barrier_semaphore()
    peers = [(dz, dt) for dz in range(slabs) for dt in range(halves) if dz or dt]

    def peer(dz, dt):
        return lax.rem(here + dz, slabs), lax.rem(line + dt, halves)

    for dz, dt in peers:
        z, t = peer(dz, dt)
        pl.semaphore_signal(
            barrier, inc=1, device_id={"ctx": z, "tp": t}, device_id_type=pl.DeviceIdType.MESH
        )
    if n_out == 3:
        pl.semaphore_signal(
            barrier, inc=1, device_id=sibling, device_id_type=pl.DeviceIdType.MESH
        )
    cuts = [(t, base, inner) for t in range(halves)]
    cuts += [(t, k * ff, ff) for t in range(halves) for k in range(3)]
    loads = [
        pltpu.make_async_copy(
            w_hbm.at[t, :, at : at + n], w.at[t, :, at : at + n], sems.at[k]
        )
        for k, (t, at, n) in enumerate(cuts)
    ]
    for load in loads:
        load.start()
    length, first = scal[0], scal[1]
    step = 256
    rows = 64

    for load in mix_loads:
        load.wait()
    for t in range(halves):
        for z in range(slabs):
            at = z * 2 * HD
            att_t[at : at + HD, :] = mix_a[z, t]
            att_t[at + HD : at + 2 * HD, :] = mix_b[z, t]
        acts[t, :, base:lanes] = att_t[...].astype(F32).T.astype(BF)
    for k in range(halves):
        loads[k].wait()
    for load in row_loads:
        load.wait()

    def project(n, _):
        cut = pl.ds(pl.multiple_of(n * step, step), step)
        total = own[:, cut].astype(F32)
        for t in range(halves):
            total = total + mm(acts[t, :, base:lanes], w[t, cut, base:lanes], NT)
        mid[:, cut] = total
        return 0

    lax.fori_loop(0, width // step, project, 0)

    def row_mask(r):
        pos = first + r * rows + lax.broadcasted_iota(jnp.int32, (rows, 1), 0)
        return jnp.where(pos < length, 1.0, 0.0)

    def norm(r, _):
        cut = pl.ds(pl.multiple_of(r * rows, rows), rows)
        values = mid[cut, :]
        inverse = lax.rsqrt(jnp.mean(values * values, axis=1, keepdims=True) + EPSILON)
        scale[cut, :] = jnp.broadcast_to(inverse, (rows, 128))
        normed_ref[cut, :] = (values * inverse * gain[...]).astype(BF)
        branch_ref[cut, :] = (cot[cut, :].astype(F32) * row_mask(r)).astype(BF)
        return 0

    lax.fori_loop(0, half // rows, norm, 0)

    for t in range(halves):
        for k in range(3):
            loads[halves + 3 * t + k].wait()

        def columns(at, n):
            def cut(k):
                return pl.ds(pl.multiple_of(k * ff + at, 128), n)

            gate = mm(normed_ref[...], w[t, :, cut(0)], NN)
            upward = mm(normed_ref[...], w[t, :, cut(1)], NN)
            d_hidden = mm(branch_ref[...], w[t, :, cut(2)], NN)
            sig = 1.0 / (1.0 + jnp.exp(-gate))
            active = gate * sig
            acts[t, :, cut(2)] = (active * upward).astype(BF)
            acts[t, :, cut(0)] = (
                d_hidden * upward * sig * (1.0 + gate * (1.0 - sig))
            ).astype(BF)
            acts[t, :, cut(1)] = (d_hidden * active).astype(BF)

        def chunk(c, _):
            columns(c * step, step)
            return 0

        lax.fori_loop(0, ff // step, chunk, 0)
        if ff % step:
            columns(ff - ff % step, ff % step)

    def back(n, _):
        cut = pl.ds(pl.multiple_of(n * step, step), step)
        total = mid[:, cut]
        grad = jnp.zeros((half, step), F32)
        for t in range(halves):
            total = total + mm(acts[t, :, 2 * ff : base], w[t, cut, 2 * ff : base], NT)
            grad = grad + mm(acts[t, :, 0:ff], w[t, cut, 0:ff], NT)
            grad = grad + mm(acts[t, :, ff : 2 * ff], w[t, cut, ff : 2 * ff], NT)
        dmid_ref[:, cut] = total
        dn[:, cut] = grad
        return 0

    lax.fori_loop(0, width // step, back, 0)

    def finish(r, _):
        cut = pl.ds(pl.multiple_of(r * rows, rows), rows)
        mask = row_mask(r)
        out_ref[cut, :] = (dmid_ref[cut, :] * mask).astype(BF)
        inverse = scale[cut, 0:1]
        scaled = mid[cut, :] * inverse
        d_scaled = dn[cut, :] * gain[...]
        mean = jnp.mean(d_scaled * scaled, axis=1, keepdims=True)
        total = cot[cut, :].astype(F32) * mask + inverse * (d_scaled - scaled * mean)
        dmid_ref[cut, :] = total
        dattn_ref[cut, :] = total.astype(BF)
        return 0

    lax.fori_loop(0, half // rows, finish, 0)
    for t in range(halves):
        for z in range(0, slabs, 2):
            at = base + z * 2 * HD
            grad = mm(dattn_ref[...], w[t, :, at : at + 4 * HD], NN).T.astype(BF)
            for k in range(2):
                do_a[z + k, t] = grad[2 * k * HD : (2 * k + 1) * HD]
                do_b[z + k, t] = grad[(2 * k + 1) * HD : (2 * k + 2) * HD]

    pl.semaphore_wait(barrier, len(peers) + (n_out == 3))
    moves = []
    for k, (dz, dt) in enumerate(peers):
        z, t = peer(dz, dt)
        for h, (source, target) in enumerate(((do_a, got_a), (do_b, got_b))):
            move = pltpu.make_async_remote_copy(
                src_ref=source.at[z, t],
                dst_ref=target.at[here, line],
                send_sem=send_sems.at[2 * k + h],
                recv_sem=recv_sems.at[2 * k + h],
                device_id={"ctx": z, "tp": t},
                device_id_type=pl.DeviceIdType.MESH,
            )
            move.start()
            moves.append(move)
    for h, (source, target) in enumerate(((do_a, got_a), (do_b, got_b))):
        move = pltpu.make_async_copy(
            source.at[here, line], target.at[here, line], local_sems.at[h]
        )
        move.start()
        moves.append(move)

    regions = ((0, 2 * ff), (2 * ff, base), (base, lanes))

    def own_copy(n, t):
        cut = pl.ds(pl.multiple_of(n * step, step), step)
        return pltpu.make_async_copy(
            w.at[t, cut, split:lanes], grads[1].at[t, n // 2], out_sems.at[n, t, 1]
        )

    def core_copy(n, t):
        cut = pl.ds(pl.multiple_of(n * step, step), step)
        return pltpu.make_async_remote_copy(
            src_ref=w.at[t, cut, split:lanes], dst_ref=grads[2].at[t, n // 2],
            send_sem=core_send.at[n, t], recv_sem=core_recv.at[n, t],
            device_id=sibling, device_id_type=pl.DeviceIdType.MESH,
        )

    def some_copy(t):
        return pltpu.make_async_copy(
            w.at[t, :, 0:split], grads[0].at[t], out_sems.at[0, t, 0]
        )

    def store(t):
        if n_out == 1:
            return

        def rows_of(n, _):
            @pl.when(lax.rem(n, 2) == core)
            def _():
                own_copy(n, t).start()

            @pl.when(lax.rem(n, 2) != core)
            def _():
                core_copy(n, t).start()

            return 0

        lax.fori_loop(0, width // step, rows_of, 0)

    for k, ref in enumerate((normed_ref, branch_ref, dattn_ref)):
        for b in range(0, width, step):
            turned[k, b : b + step] = ref[:, b : b + step].astype(F32).T.astype(BF)
    for t in range(halves):

        def fill(k, at, n):
            cut = pl.ds(at, n)
            w[t, :, cut] = mm(turned[k], acts[t, :, cut], NN).astype(BF)

        def span(k, start, stop):
            def chunk(c, _):
                fill(k, pl.multiple_of(start + c * step, 128), step)
                return 0

            count = (stop - start) // step
            lax.fori_loop(0, count, chunk, 0)
            if start + count * step < stop:
                fill(k, start + count * step, stop - start - count * step)

        for k, (at, end) in enumerate(regions):
            if at < split < end:
                span(k, at, split)
                at = split
                some_copy(t).start()
            span(k, at, end)
            if end == split:
                some_copy(t).start()
        store(t)

    for t in range(halves):
        some_copy(t).wait()

        def settle(n, _):
            @pl.when(lax.rem(n, 2) == core)
            def _():
                own_copy(n, t).wait()
                core_copy(n, t).wait_recv()

            @pl.when(lax.rem(n, 2) != core)
            def _():
                core_copy(n, t).wait_send()

            return 0

        if n_out == 3:
            lax.fori_loop(0, width // step, settle, 0)
    for move in moves:
        move.wait()


def middle_stage(scalars, mix_a, mix_b, own, cot, gain, w, split):
    halves, width, lanes = w.shape
    slabs, _, _, half = mix_a.shape
    ff = (lanes - width // halves) // 3
    blocks = width // 256
    peers = slabs * halves - 1
    vmem = pl.BlockSpec(memory_space=pltpu.VMEM)
    outside = pl.BlockSpec(memory_space=pl.ANY)
    out_shape = [
        jax.ShapeDtypeStruct((half, width), BF),
        jax.ShapeDtypeStruct((half, width), F32),
        jax.ShapeDtypeStruct(mix_a.shape, BF),
        jax.ShapeDtypeStruct(mix_a.shape, BF),
        jax.ShapeDtypeStruct((halves, width, split), BF),
    ]
    out_specs = [vmem] * 4 + [outside]
    if split < lanes:
        out_shape += [jax.ShapeDtypeStruct((halves, blocks // 2, 256, lanes - split), BF)] * 2
        out_specs += [outside] * 2
    flops = 2 * half * width * (9 * ff * halves + 3 * width)
    return pl.pallas_call(
        functools.partial(middle_kernel, ff, split),
        out_shape=out_shape,
        in_specs=[
            pl.BlockSpec(memory_space=pltpu.SMEM), *[pl.BlockSpec(memory_space=pltpu.HBM)] * 4,
            vmem, outside,
        ],
        out_specs=out_specs,
        scratch_shapes=[
            pltpu.VMEM((halves, width, lanes), BF),
            pltpu.VMEM((halves, half, lanes), BF),
            pltpu.VMEM((width // halves, half), BF),
            pltpu.VMEM((half, width), F32),
            pltpu.VMEM((half, 128), F32),
            pltpu.VMEM((half, width), F32),
            pltpu.VMEM((half, width), BF),
            pltpu.VMEM((half, width), BF),
            pltpu.VMEM((half, width), BF),
            pltpu.VMEM((3, width, half), BF),
            pltpu.VMEM(mix_a.shape, BF),
            pltpu.VMEM(mix_a.shape, BF),
            pltpu.SemaphoreType.DMA((4 * halves,)),
            pltpu.SemaphoreType.DMA((blocks, halves, 2)),
            pltpu.SemaphoreType.DMA((2 * peers,)),
            pltpu.SemaphoreType.DMA((2 * peers,)),
            pltpu.SemaphoreType.DMA((2,)),
            pltpu.SemaphoreType.DMA((blocks, halves)),
            pltpu.SemaphoreType.DMA((blocks, halves)),
            pltpu.VMEM((half, width), BF),
            pltpu.VMEM((half, width), BF),
            pltpu.VMEM(mix_a.shape, BF),
            pltpu.VMEM(mix_a.shape, BF),
            pltpu.SemaphoreType.DMA((4,)),
        ],
        compiler_params=pltpu.CompilerParams(
            vmem_limit_bytes=60 << 20, collective_id=1, has_side_effects=True
        ),
        cost_estimate=pl.CostEstimate(
            flops=flops, bytes_accessed=4 * w.size + 16 * half * width, transcendentals=half * lanes
        ),
    )(scalars, mix_a, mix_b, own, cot, gain, w)


class LineSum:
    def __init__(self, source, held, slots, out, sems):
        self.source, self.held, self.slots, self.out = source, held, slots, out
        self.sum_send, self.sum_recv, self.out_send, self.out_recv = sems
        here = lax.axis_index("ctx")
        self.low = here < 2
        self.place = jnp.where(self.low, here, 3 - here)
        self.inward = jnp.where(self.low, here + 1, here - 1)
        self.outward = jnp.where(self.low, here - 1, here + 1)
        self.size = out.shape[0] // 4

    def number(self, part):
        return jnp.where(self.low, part, 3 - part)

    def part(self, ref, part):
        at = pl.multiple_of(self.number(part) * self.size, self.size)
        return ref.at[pl.ds(at, self.size), :]

    def read(self, ref, part):
        at = pl.multiple_of(self.number(part) * self.size, self.size)
        return ref[pl.ds(at, self.size), :].astype(F32)

    def write(self, ref, part, value):
        at = pl.multiple_of(self.number(part) * self.size, self.size)
        ref[pl.ds(at, self.size), :] = value.astype(BF)

    def copy(self, source, target, send, recv, place):
        return pltpu.make_async_remote_copy(
            src_ref=source, dst_ref=target, send_sem=send, recv_sem=recv,
            device_id={"ctx": place}, device_id_type=pl.DeviceIdType.MESH,
        )

    def took(self, slot):
        ref = self.slots.at[slot]
        self.copy(ref, ref, self.sum_send.at[0], self.sum_recv.at[slot], self.inward).wait_recv()
        return self.slots[slot].astype(F32)

    def begin(self):
        @pl.when(self.place == 0)
        def _():
            for k in range(3):
                self.copy(
                    self.part(self.source, 3 - k), self.slots.at[k],
                    self.sum_send.at[k], self.sum_recv.at[k], self.inward,
                ).start()

    def left(self, k):
        self.copy(
            self.slots.at[0], self.slots.at[0],
            self.sum_send.at[k], self.sum_recv.at[0], self.inward,
        ).wait_send()

    def first(self, k):
        @pl.when(self.place == 1)
        def _():
            self.write(self.held, 3 - k, self.read(self.source, 3 - k) + self.took(k))
            self.copy(
                self.part(self.held, 3 - k), self.slots.at[3 + k],
                self.sum_send.at[k], self.sum_recv.at[3 + k], self.inward,
            ).start()

    def second(self):
        @pl.when(self.place == 1)
        def _():
            self.write(self.held, 0, self.read(self.source, 0) + self.took(3))
            self.copy(
                self.part(self.held, 0), self.slots.at[3],
                self.sum_send.at[2], self.sum_recv.at[3], self.outward,
            ).start()

    def give(self, part, send, place):
        ref = self.part(self.out, part)
        return self.copy(
            ref, ref, self.out_send.at[send], self.out_recv.at[self.number(part)], place
        )

    def final(self):
        @pl.when(self.place == 1)
        def _():
            self.write(self.out, 1, self.read(self.source, 1) + self.took(2) + self.took(4))
            self.give(1, 0, self.inward).start()
            self.give(1, 1, self.outward).start()

        @pl.when(self.place == 0)
        def _():
            self.write(self.out, 0, self.read(self.source, 0) + self.took(3))
            self.give(0, 0, self.inward).start()

    def forward(self):
        @pl.when(self.place == 1)
        def _():
            for k, (part, place) in enumerate(((0, self.inward), (2, self.outward), (3, self.outward))):
                self.give(part, 2 + k, place).wait_recv()
                self.give(part, 2 + k, place).start()

    def end(self):
        @pl.when(self.place == 0)
        def _():
            for k in range(3):
                self.left(k)
            self.give(0, 0, self.inward).wait_send()
            for part in (1, 2, 3):
                self.give(part, 0, self.inward).wait_recv()

        @pl.when(self.place == 1)
        def _():
            for k in range(3):
                self.left(k)
            for k in range(5):
                self.give(1, k, self.inward).wait_send()


def tail_kernel(
    back_a, back_b, some, rest, normed, weights, own_hbm, gain, dmid,
    grad_out, some_out, rest_out, qa_out, qb_out,
    turned, some_held, some_slots, rest_held, rest_slots,
    local, crossed, column_sum, columned, q_src, q_held, q_slots, theirs, got_theirs, mine,
    core_send, core_recv, col_send, col_recv,
    row_send, row_recv, out_send, out_recv, *line_sems,
):
    here, line, place = lax.axis_index("ctx"), lax.axis_index("tp"), lax.axis_index("fsdp")
    core, column = lax.rem(place, 2), place // 2
    sibling = {"fsdp": place + 1 - 2 * core}
    beside = {"fsdp": lax.rem(place + 2, 4)}
    across = {"tp": 1 - line}
    others = [{"ctx": lax.rem(here + k, 4)} for k in range(1, 4)]
    mesh_id = pl.DeviceIdType.MESH
    barrier = pltpu.get_barrier_semaphore()
    for device in (*others, sibling, beside, across):
        pl.semaphore_signal(barrier, inc=1, device_id=device, device_id_type=mesh_id)
    pl.semaphore_wait(barrier, 6)

    def remote(source, target, send, recv, device):
        return pltpu.make_async_remote_copy(
            src_ref=source, dst_ref=target, send_sem=send, recv_sem=recv,
            device_id=device, device_id_type=mesh_id,
        )

    rows = normed.shape[0]
    half = rows // 2
    depth = 256
    own, own_sem, *line_sems = line_sems
    load = pltpu.make_async_copy(
        own_hbm.at[pl.ds(pl.multiple_of(line * half, half), half), :], own, own_sem
    )
    load.start()
    a, b, qa, qb = (
        LineSum(src, held, slots, out, line_sems[4 * k : 4 * k + 4])
        for k, (src, held, slots, out) in enumerate(
            (
                (some, some_held, some_slots, some_out),
                (rest, rest_held, rest_slots, rest_out),
                (q_src.at[0], q_held.at[0], q_slots.at[0], qa_out),
                (q_src.at[1], q_held.at[1], q_slots.at[1], qb_out),
            )
        )
    )
    a.begin()

    def weight_gradient(h, grads):
        def step(n, _):
            cut = pl.ds(pl.multiple_of(n * depth, depth), depth)
            value = mm(grads[...], normed[:, cut], NN).astype(BF)
            local[h, lax.rem(n, 2), n // 2] = value
            return 0

        lax.fori_loop(0, 4, step, 0)
        move = remote(
            local.at[h, 1 - core], crossed.at[h], core_send.at[h], core_recv.at[h], sibling
        )
        move.start()
        return move

    def column_step(h, move):
        move.wait_recv()
        for x in range(2):
            column_sum[h, x] = (
                local[h, core, x].astype(F32) + crossed[h, x].astype(F32)
            ).astype(BF)
        move = remote(
            column_sum.at[h, 1 - column], columned.at[h], col_send.at[h], col_recv.at[h], beside
        )
        move.start()
        return move

    def column_end(h, move):
        move.wait_recv()
        q_src[h] = (column_sum[h, column].astype(F32) + columned[h].astype(F32)).astype(BF)

    def turn(h, grads):
        for k in range(0, grads.shape[0], 128):
            at = h * grads.shape[0] + k
            turned[:, at : at + 128] = grads[k : k + 128, :].astype(F32).T.astype(BF)

    pieces = 2
    piece = half // pieces
    sent_rows = []
    sent_out = []
    mine_start = pl.multiple_of(line * half, half)

    def make_theirs(k):
        cut = slice(k * piece, (k + 1) * piece)
        start = pl.multiple_of((1 - line) * half + k * piece, piece)

        def make(n, _):
            wide = pl.ds(pl.multiple_of(n * depth, depth), depth)
            value = mm(turned[pl.ds(start, piece), :], weights[:, wide], NN)
            theirs[cut, wide] = value.astype(BF)
            return 0

        lax.fori_loop(0, 4, make, 0)
        move = remote(theirs.at[cut], got_theirs.at[cut], row_send.at[k], row_recv.at[k], across)
        move.start()
        sent_rows.append(move)

    def make_mine(n, _):
        wide = pl.ds(pl.multiple_of(n * depth, depth), depth)
        mine[:, wide] = mm(turned[pl.ds(mine_start, half), :], weights[:, wide], NN)
        return 0

    def finish_rows(k):
        small = 64
        if k == 0:
            load.wait()
        sent_rows[k].wait_recv()

        def back(r, _):
            at = pl.multiple_of(k * piece + r * small, small)
            cut = pl.ds(at, small)
            values = own[cut, :].astype(F32)
            inverse = lax.rsqrt(jnp.mean(values * values, axis=1, keepdims=True) + EPSILON)
            scaled = values * inverse
            d_scaled = (mine[cut, :] + got_theirs[cut, :].astype(F32)) * gain[...]
            mean = jnp.mean(d_scaled * scaled, axis=1, keepdims=True)
            total = dmid[cut, :] + inverse * (d_scaled - scaled * mean)
            grad_out[pl.ds(pl.multiple_of(line * half + at, small), small), :] = total.astype(BF)
            return 0

        lax.fori_loop(0, piece // small, back, 0)
        ref = grad_out.at[pl.ds(pl.multiple_of(line * half + k * piece, piece), piece), :]
        move = remote(ref, ref, out_send.at[k], out_recv.at[k], across)
        move.start()
        sent_out.append(move)

    b.begin()
    turn(0, back_a)
    turn(1, back_b)
    make_theirs(0)
    core_a = weight_gradient(0, back_a)
    a.first(0)
    make_theirs(1)
    core_b = weight_gradient(1, back_b)
    a.first(1)
    col_a = column_step(0, core_a)
    lax.fori_loop(0, 4, make_mine, 0)
    a.second()
    col_b = column_step(1, core_b)
    b.first(0)
    a.final()
    b.first(1)
    finish_rows(0)
    b.second()
    a.forward()
    column_end(0, col_a)
    qa.begin()
    b.final()
    finish_rows(1)
    column_end(1, col_b)
    qb.begin()
    qa.first(0)
    qa.first(1)
    b.forward()
    qb.first(0)
    qb.first(1)
    qa.second()
    qa.final()
    qb.second()
    qb.final()
    qa.forward()
    qb.forward()
    for run in (a, b, qa, qb):
        run.end()
    for move in (core_a, core_b, col_a, col_b, *sent_rows):
        move.wait_send()
    for k, move in enumerate(sent_out):
        move.wait_send()
        ref = grad_out.at[pl.ds(pl.multiple_of((1 - line) * half + k * piece, piece), piece), :]
        remote(ref, ref, out_send.at[k], out_recv.at[k], across).wait_recv()


def tail_stage(back_a, back_b, some, rest, normed, weights, own, gain, dmid):
    rows, width = normed.shape
    half = rows // 2
    lanes_a, lanes_b = some.shape[1], rest.shape[1]
    wide = back_a.shape[0]
    vmem = pl.BlockSpec(memory_space=pltpu.VMEM)
    dma = pltpu.SemaphoreType.DMA
    return pl.pallas_call(
        tail_kernel,
        out_shape=(
            jax.ShapeDtypeStruct((rows, width), BF),
            jax.ShapeDtypeStruct((256, lanes_a), BF),
            jax.ShapeDtypeStruct((256, lanes_b), BF),
            jax.ShapeDtypeStruct((wide, 256), BF),
            jax.ShapeDtypeStruct((wide, 256), BF),
        ),
        in_specs=[vmem] * 6 + [pl.BlockSpec(memory_space=pl.ANY)] + [vmem] * 2,
        out_specs=(vmem,) * 5,
        scratch_shapes=[
            pltpu.VMEM((rows, 2 * wide), BF),
            pltpu.VMEM((256, lanes_a), BF),
            pltpu.VMEM((5, 64, lanes_a), BF),
            pltpu.VMEM((256, lanes_b), BF),
            pltpu.VMEM((5, 64, lanes_b), BF),
            pltpu.VMEM((2, 2, 2, wide, 256), BF),
            pltpu.VMEM((2, 2, wide, 256), BF),
            pltpu.VMEM((2, 2, wide, 256), BF),
            pltpu.VMEM((2, wide, 256), BF),
            pltpu.VMEM((2, wide, 256), BF),
            pltpu.VMEM((2, wide, 256), BF),
            pltpu.VMEM((2, 5, wide // 4, 256), BF),
            pltpu.VMEM((half, width), BF),
            pltpu.VMEM((half, width), BF),
            pltpu.VMEM((half, width), F32),
            dma((2,)), dma((2,)), dma((2,)), dma((2,)),
            dma((2,)), dma((2,)), dma((2,)), dma((2,)),
            pltpu.VMEM((half, width), BF), dma,
        ]
        + [dma((3,)), dma((5,)), dma((5,)), dma((4,))] * 4,
        compiler_params=pltpu.CompilerParams(
            vmem_limit_bytes=60 << 20, collective_id=2, has_side_effects=True
        ),
        cost_estimate=pl.CostEstimate(
            flops=8 * rows * width * wide, bytes_accessed=40 << 20, transcendentals=0
        ),
    )(back_a, back_b, some, rest, normed, weights, own, gain, dmid)


def pack_kernel(gate, up, down_hbm, out_hbm, packed_hbm, packed, down, out, sems):
    ff = gate.shape[1]
    first = packed.at[:, 0 : 2 * ff]
    last = packed.at[:, 2 * ff :]
    loads = [
        pltpu.make_async_copy(source, target, sems.at[k])
        for k, (source, target) in enumerate(
            (
                (gate, packed.at[:, 0:ff]),
                (up, packed.at[:, ff : 2 * ff]),
                (down_hbm, down),
                (out_hbm, out),
            )
        )
    ]
    for move in loads:
        move.start()
    loads[0].wait()
    loads[1].wait()
    stores = [
        pltpu.make_async_copy(first, packed_hbm.at[:, 0 : 2 * ff], sems.at[4]),
        pltpu.make_async_copy(last, packed_hbm.at[:, 2 * ff :], sems.at[5]),
    ]
    stores[0].start()
    loads[2].wait()
    loads[3].wait()
    packed[:, 2 * ff : 3 * ff] = down[...].astype(F32).T.astype(BF)
    packed[:, 3 * ff :] = out[...].astype(F32).T.astype(BF)
    stores[1].start()
    for move in stores:
        move.wait()


def pack_stage(gate, up, down, out):
    depth, ff = gate.shape
    outside = pl.BlockSpec(memory_space=pltpu.HBM)
    return pl.pallas_call(
        pack_kernel,
        out_shape=jax.ShapeDtypeStruct((depth, 3 * ff + out.shape[0]), BF),
        in_specs=[outside] * 4,
        out_specs=outside,
        scratch_shapes=[
            pltpu.VMEM((depth, 3 * ff + out.shape[0]), BF),
            pltpu.VMEM(down.shape, BF),
            pltpu.VMEM(out.shape, BF),
            pltpu.SemaphoreType.DMA((6,)),
        ],
        compiler_params=pltpu.CompilerParams(vmem_limit_bytes=60 << 20),
        cost_estimate=pl.CostEstimate(flops=0, bytes_accessed=14 * depth * ff, transcendentals=0),
    )(gate, up, down, out)


def finish_kernel(
    *refs,
):
    sources, gains, grad_in = refs[:9], refs[9], refs[10]
    gate, up, down, out, qg, kg, vg, part, grad_out = refs[11:20]
    held, grad_held, sems = refs[20:29], refs[29], refs[30]
    some, rest, qa, qb, wq, wk, wv, gate_w, up_w = held
    taken = pltpu.make_async_copy(grad_in, grad_held, sems.at[9])
    given = pltpu.make_async_copy(grad_held, grad_out, sems.at[10])
    loads = [
        pltpu.make_async_copy(source, target, sems.at[k])
        for k, (source, target) in enumerate(zip(sources, held))
    ]
    for load in loads:
        load.start()
    taken.start()
    for load in loads:
        load.wait()
    ff = gate.shape[1]
    split = some.shape[1]
    low = split - ff
    high = ff - low

    def fold(values):
        total = values[:, 0:128]
        for at in range(128, values.shape[1], 128):
            total = total + values[:, at : at + 128]
        return total

    value = some[:, 0:ff].astype(F32)
    gate[...] = value
    taken.wait()
    given.start()
    two = fold(value * gate_w[...].astype(F32))
    value = some[:, ff:split].astype(F32)
    up[:, 0:low] = value
    two = two + fold(value * up_w[:, 0:low].astype(F32))
    value = rest[:, 0:high].astype(F32)
    up[:, low:ff] = value
    two = two + fold(value * up_w[:, low:ff].astype(F32))
    down[...] = rest[:, high : high + ff].astype(F32).T
    out[...] = rest[:, high + ff :].astype(F32).T
    one = jnp.zeros((gate.shape[0], 128), F32)
    for k, (target, weight) in enumerate(((qg, wq), (kg, wk), (vg, wv))):
        for z in range(qa.shape[0] // (3 * HD)):
            at = (3 * z + k) * HD
            value = jnp.concatenate([qa[at : at + HD, :], qb[at : at + HD, :]], axis=0)
            value = value.astype(F32).T
            cut = slice(2 * HD * z, 2 * HD * (z + 1))
            target[:, cut] = value
            one = one + value * weight[:, cut].astype(F32)
    part[...] = jnp.zeros_like(part)
    part[0:1] = jnp.sum(one.T, axis=0, keepdims=True) / gains[0:1]
    part[1:2] = jnp.sum(two.T, axis=0, keepdims=True) / gains[1:2]
    given.wait()


def finish_stage(some, rest, qa, qb, weights, gate_w, up_w, gains, grad):
    depth, ff = gate_w.shape
    inner = weights[0].shape[1]
    vmem = pl.BlockSpec(memory_space=pltpu.VMEM)
    outside = pl.BlockSpec(memory_space=pltpu.HBM)
    shape = jax.ShapeDtypeStruct
    operands = (some, rest, qa, qb, *weights, gate_w, up_w)
    return pl.pallas_call(
        finish_kernel,
        out_shape=(
            shape((depth, ff), F32), shape((depth, ff), F32), shape((ff, depth), F32),
            shape((inner, depth), F32), *[shape((depth, inner), F32)] * 3,
            shape((8, depth), F32), shape(grad.shape, BF),
        ),
        in_specs=[outside] * 9 + [vmem, outside],
        out_specs=(vmem,) * 8 + (outside,),
        scratch_shapes=[
            *[pltpu.VMEM(a.shape, BF) for a in operands], pltpu.VMEM(grad.shape, BF),
            pltpu.SemaphoreType.DMA((11,)),
        ],
        compiler_params=pltpu.CompilerParams(vmem_limit_bytes=60 << 20),
        cost_estimate=pl.CostEstimate(flops=0, bytes_accessed=16 << 20, transcendentals=0),
    )(*operands, gains, grad)


def normalize(values, gain):
    inverse = lax.rsqrt(jnp.mean(values * values, axis=-1, keepdims=True) + EPSILON)
    scaled = values * inverse
    return scaled, inverse, (scaled * gain).astype(BF)


def norm_back(d_normed, scaled, inverse, gain):
    d_scaled = d_normed * gain
    d_values = inverse * (d_scaled - scaled * jnp.mean(d_scaled * scaled, axis=-1, keepdims=True))
    return d_values


def rows_first(values):
    return with_layout_constraint(values, Layout(major_to_minor=tuple(range(values.ndim))))


def swap(values, axis, bit):
    count = lax.axis_size(axis)
    return lax.ppermute(values, axis, [(k, k ^ bit) for k in range(count)])


def both_halves(values):
    other = swap(values, "tp", 1)
    first = lax.axis_index("tp") == 0
    return jnp.concatenate([jnp.where(first, values, other), jnp.where(first, other, values)])


def shards(
    inputs,
    lengths,
    first_gain,
    query_weight,
    key_weight,
    value_weight,
    out_weight,
    second_gain,
    gate_weight,
    up_weight,
    down_weight,
    cotangent,
):
    slabs, halves, parts = lax.axis_size("ctx"), lax.axis_size("tp"), lax.axis_size("fsdp")
    rows, width = inputs.shape[1], inputs.shape[2]
    depth = query_weight.shape[0]
    group = query_weight.shape[1] // HD // slabs
    half = rows // halves
    ff = gate_weight.shape[1]
    everywhere = ("tp", "fsdp")
    side = lax.axis_index("tp") * half

    paired = parts == 4 and halves == 2 and slabs == 4 and group == 2
    w_rest = pack_stage(gate_weight, up_weight, down_weight, out_weight)
    w_rest = rows_first(lax.all_gather(rows_first(w_rest), everywhere, axis=0, tiled=True))
    w_rest = w_rest.reshape(halves, width, -1)
    qkv_width = slabs * 3 * HD

    if paired:
        gains_own = jnp.stack([first_gain.astype(F32), second_gain.astype(F32)])
        gains_own = jnp.concatenate([gains_own, jnp.zeros((6, depth), F32)])
        w_turned, normed_one, gains, *rest = front_stage(
            lengths, inputs[0], gains_own, query_weight, key_weight, value_weight, slabs, halves
        )
        gain_one, gain_two = gains[0], gains[1]
        qkv, arrived = rest[0:2], rest[2:4]
        saved = [(rest[4], rest[6]), (rest[5], rest[7])]
    else:
        gains = lax.all_gather(jnp.stack([first_gain, second_gain]), "fsdp", axis=1, tiled=True)
        gain_one, gain_two = gains[0].astype(F32), gains[1].astype(F32)
        stacked = jnp.stack(
            [w.reshape(depth, slabs, group, HD) for w in (query_weight, key_weight, value_weight)]
        ).transpose(1, 3, 2, 0, 4)
        w_qkv = lax.all_gather(
            stacked.reshape(depth, group * qkv_width), "fsdp", axis=0, tiled=True
        )
        w_heads = [w_qkv[:, h * qkv_width : (h + 1) * qkv_width] for h in range(group)]
        _, _, normed_one = normalize(inputs[0].astype(F32), gain_one)
        qkv = []
        for h in range(group):
            part = mm(w_heads[h], normed_one, (((0,), (1,)), ((), ()))).astype(BF)
            part = part.reshape(slabs, 3 * HD, rows)
            qkv.append(lax.all_to_all(part, "ctx", 0, 0, tiled=True))
        arrived, saved = [], []
        for h in range(group):
            mix, mix_full, lse = attend(lengths, qkv[h], halves, rows)
            saved.append((mix_full, lse))
            mix = mix.reshape(slabs * halves, HD, half)
            mix = lax.all_to_all(mix, ("ctx", "tp"), 0, 0, tiled=True)
            arrived.append(mix.reshape(slabs, halves, HD, half))

    scalars = jnp.stack([lengths[0], lax.axis_index("ctx") * rows + side])
    split = 2304 if paired else w_rest.shape[2]
    output, d_middle, *d_mix, = middle_stage(
        scalars, *arrived, inputs[0], cotangent[0], gain_two[None], w_rest, split
    )
    d_mix, (g_some, *g_rest) = d_mix[:2], d_mix[2:]
    output = both_halves(output)
    s_some = lax.psum_scatter(
        rows_first(g_some.reshape(halves * width, -1)), everywhere, scatter_dimension=0, tiled=True
    )
    s_some = rows_first(s_some)

    if paired:
        back_a, back_b, g_rest = back_stage(lengths, qkv, d_mix, saved, *g_rest)
        input_gradient, s_some, s_rest, *q_grads = tail_stage(
            back_a, back_b, s_some, g_rest, normed_one, w_turned, inputs[0], gain_one[None], d_middle
        )
        s_gate, s_up, s_down, s_out, *s_qkv, d_gains, input_gradient = finish_stage(
            s_some, s_rest, *q_grads, (query_weight, key_weight, value_weight), gate_weight,
            up_weight, gains_own, input_gradient,
        )
        d_gains = d_gains[0:2]
        d_gains = d_gains + swap(d_gains, "tp", 1)
    else:
        d_local = [
            attend_back(lengths, qkv[h], d_mix[h], *saved[h], 512) for h in range(group)
        ]
        d_qkv = [
            lax.all_to_all(d, "ctx", 0, 0, tiled=True).reshape(qkv_width, rows) for d in d_local
        ]
        d_normed_one = jnp.zeros((rows, width), F32)
        s_qkv = []
        for h in range(group):
            d_normed_one = d_normed_one + mm(d_qkv[h], w_heads[h], (((0,), (1,)), ((), ())))
            grad = mm(normed_one, d_qkv[h], (((0,), (1,)), ((), ()))).astype(BF)
            grad = lax.psum_scatter(grad, "fsdp", scatter_dimension=0, tiled=True)
            s_qkv.append(lax.psum(grad, "ctx").reshape(depth, slabs, 3, HD))
        d_normed_one = lax.psum_scatter(d_normed_one, "tp", scatter_dimension=0, tiled=True)
        own = lax.dynamic_slice_in_dim(inputs[0], side, half, 0)
        scaled_one, inverse_one, _ = normalize(own.astype(F32), gain_one)
        d_from_one = norm_back(d_normed_one, scaled_one, inverse_one, gain_one)
        input_gradient = lax.all_gather(
            (d_middle + d_from_one).astype(BF), "tp", axis=0, tiled=True
        )
        s_qkv = jnp.stack(s_qkv, axis=2).transpose(3, 0, 1, 2, 4)
        s_qkv = s_qkv.reshape(3, depth, slabs * group * HD).astype(F32)
        s_all = lax.psum(s_some, "ctx").astype(F32)
        d_gain_one = sum(
            jnp.sum(w.astype(F32) * s, axis=1)
            for w, s in zip((query_weight, key_weight, value_weight), s_qkv)
        ) / first_gain.astype(F32)
        d_gain_two = (
            jnp.sum(gate_weight.astype(F32) * s_all[:, :ff], axis=1)
            + jnp.sum(up_weight.astype(F32) * s_all[:, ff : 2 * ff], axis=1)
        ) / second_gain.astype(F32)
        d_gains = jnp.stack([d_gain_one, d_gain_two])
        d_gains = lax.psum(d_gains, "tp")
        s_gate, s_up, s_down, s_out = (
            s_all[:, :ff], s_all[:, ff : 2 * ff], s_all[:, 2 * ff : 3 * ff].T, s_all[:, 3 * ff :].T
        )

    return (
        output[None],
        input_gradient[None],
        d_gains[0],
        s_qkv[0],
        s_qkv[1],
        s_qkv[2],
        s_out,
        d_gains[1],
        s_gate,
        s_up,
        s_down,
    )


def solution(mesh):
    rows = P("fsdp", "ctx", None)
    gain = P("fsdp")
    inward = P("fsdp", "tp")
    outward = P("tp", "fsdp")
    return jax.shard_map(
        shards,
        mesh=mesh,
        in_specs=(
            rows, gain, gain, inward, inward, inward, outward, gain, inward, inward, outward, rows,
        ),
        out_specs=(
            rows, rows, gain, inward, inward, inward, outward, gain, inward, inward, outward,
        ),
        check_vma=False,
    )
```

```python
import functools

import jax
import jax.numpy as jnp
from jax import lax
from jax.experimental import pallas as pl
from jax.experimental.pallas import tpu as pltpu
from jax.experimental.layout import Layout, with_layout_constraint
from jax.sharding import PartitionSpec as P

HD = 64
EPSILON = 1e-05
MASKED = -1000000000.0
NN = (((1,), (0,)), ((), ()))
NT = (((1,), (1,)), ((), ()))
TN = (((0,), (0,)), ((), ()))
BF = jnp.bfloat16
F32 = jnp.float32


def mm(left, right, dims):
    return lax.dot_general(left, right, dims, preferred_element_type=F32)


def spread_keys(keys, start, length):
    rows = keys.shape[0]
    pos = start + lax.broadcasted_iota(jnp.int32, (rows, HD), 0)
    lane = lax.broadcasted_iota(jnp.int32, (rows, HD), 1)
    bias = jnp.where((lane == 0) & (pos >= length), MASKED, 0.0)
    return jnp.concatenate([keys, bias], axis=1).astype(BF)


def spread_queries(queries):
    row = lax.broadcasted_iota(jnp.int32, queries.shape, 0)
    ones = jnp.where(row == 0, 1.0, 0.0)
    return jnp.concatenate([queries * HD**-0.5, ones], axis=0).astype(BF)


def attend_rows(tile, length, qkv, kx, qx, vx, emit):
    slabs, _, rows = qkv.shape
    per = rows // tile
    blocks = slabs * per
    for z in range(slabs):
        keys = qkv[z, HD : 2 * HD, :].astype(F32).T
        kx[z * rows : (z + 1) * rows, :] = spread_keys(keys, z * rows, length)
        queries = spread_queries(qkv[z, 0:HD, :].astype(F32))
        for b in range(per):
            cut = slice(b * tile, (b + 1) * tile)
            qx[z * per + b] = queries[:, cut]
            vx[z * per + b] = qkv[z, 2 * HD : 3 * HD, cut]
    later = lax.broadcasted_iota(jnp.int32, (tile, tile), 0) > lax.broadcasted_iota(
        jnp.int32, (tile, tile), 1
    )

    def query_block(i, _):
        queries = qx[i]

        def step(j, carry, masked):
            highest, total, mix = carry
            keys = kx[pl.ds(pl.multiple_of(j * tile, tile), tile), :]
            scores = mm(keys, queries, NN)
            if masked:
                scores = jnp.where(later, MASKED, scores)
            new = jnp.maximum(highest, jnp.max(scores, axis=0, keepdims=True))
            scale = jnp.exp(highest - new)
            probs = jnp.exp(scores - new)
            total = total * scale + jnp.sum(probs, axis=0, keepdims=True)
            mix = mix * scale + mm(vx[j], probs.astype(BF), NN)
            return new, total, mix

        first = (
            jnp.full((1, tile), -jnp.inf, F32),
            jnp.zeros((1, tile), F32),
            jnp.zeros((HD, tile), F32),
        )
        carry = lax.fori_loop(0, i, lambda j, c: step(j, c, False), first)
        highest, total, mix = step(i, carry, True)
        emit(i, mix / total, highest + jnp.log(total))
        return 0

    lax.fori_loop(0, blocks, query_block, 0)


def attend_kernel(tile, len_ref, qkv, o_ref, of_ref, lse_ref, kx, qx, vx):
    rows = qkv.shape[2]
    halves = o_ref.shape[1]
    half = rows // halves

    def emit(i, mix, lse):
        of_ref[i] = mix
        lse_ref[i] = lse
        for t in range(halves):
            o_ref[i, t] = mix[:, t * half : (t + 1) * half].astype(BF)

    attend_rows(tile, len_ref[0], qkv, kx, qx, vx, emit)


def front_kernel(
    len_ref, x, gains_own, wq, wk, wv,
    wt_hbm, normed_hbm, gains, qkv_a_hbm, qkv_b_hbm, mix_a, mix_b, of_a_hbm, of_b_hbm,
    lse_a_hbm, lse_b_hbm,
    wt, normed, qkv_a, qkv_b, of_a, of_b, lse_a, lse_b, out_sems, packed, parts, mixed, kx, qx, vx,
    gain_send, gain_recv, w_send, w_recv, part_send, part_recv, part_local,
    mix_send, mix_recv, mix_local,
):
    here, line, place = lax.axis_index("ctx"), lax.axis_index("tp"), lax.axis_index("fsdp")
    core, column = lax.rem(place, 2), place // 2
    pair = place + 1 - 2 * core
    other = lax.rem(place + 2, 4)
    mesh_id = pl.DeviceIdType.MESH
    slabs, halves = mix_a.shape[0], mix_a.shape[1]
    rows, width = x.shape
    half = rows // halves
    wide = slabs * 3 * HD
    depth = wq.shape[0]
    peers = [(dz, dt) for dz in range(slabs) for dt in range(halves) if dz or dt]

    def peer(dz, dt):
        return lax.rem(here + dz, slabs), lax.rem(line + dt, halves)

    barrier = pltpu.get_barrier_semaphore()
    for dz, dt in peers:
        z, t = peer(dz, dt)
        pl.semaphore_signal(barrier, inc=1, device_id={"ctx": z, "tp": t}, device_id_type=mesh_id)
    for device in (pair, other):
        pl.semaphore_signal(barrier, inc=1, device_id={"fsdp": device}, device_id_type=mesh_id)
    for q, w in enumerate((wq, wk, wv)):
        flat = w[...].astype(F32).T.astype(BF)
        for z in range(slabs):
            for h in range(2):
                at = (2 * z + h) * HD
                packed[h, (3 * z + q) * HD : (3 * z + q + 1) * HD, :] = flat[at : at + HD]

    def remote(source, target, send, recv, device):
        return pltpu.make_async_remote_copy(
            src_ref=source, dst_ref=target, send_sem=send, recv_sem=recv,
            device_id=device, device_id_type=mesh_id,
        )

    def lanes(index):
        return pl.ds(pl.multiple_of(index * depth, depth), depth)

    def weight(h, index):
        return wt.at[h * wide : (h + 1) * wide, lanes(index)]

    gains[:, lanes(place)] = gains_own[...]
    for h in range(2):
        wt[h * wide : (h + 1) * wide, lanes(place)] = packed[h]
    pl.semaphore_wait(barrier, len(peers) + 2)
    sent = []

    def launch(move):
        move.start()
        sent.append(move)
        return move

    for k, device in enumerate((pair, other)):
        launch(
            remote(
                gains_own, gains.at[:, lanes(place)], gain_send.at[k], gain_recv.at[k], {"fsdp": device}
            )
        )
    for h in range(2):
        for k, device in ((1, other), (0, pair)):
            launch(
                remote(
                    packed.at[h], weight(h, place), w_send.at[h, k], w_recv.at[h, k], {"fsdp": device}
                )
            )

    def arrived(ref, sem):
        remote(ref, ref, gain_send.at[0], sem, {"fsdp": pair}).wait_recv()

    arrived(gains.at[:, lanes(other)], gain_recv.at[1])
    launch(
        remote(
            gains.at[:, lanes(other)], gains.at[:, lanes(other)], gain_send.at[2], gain_recv.at[2],
            {"fsdp": pair},
        )
    )
    far = lax.rem(pair + 2, 4)
    arrived(gains.at[:, lanes(pair)], gain_recv.at[0])
    arrived(gains.at[:, lanes(far)], gain_recv.at[2])
    small = 64

    def norm(r, _):
        cut = pl.ds(pl.multiple_of(r * small, small), small)
        values = x[cut, :].astype(F32)
        inverse = lax.rsqrt(jnp.mean(values * values, axis=1, keepdims=True) + EPSILON)
        normed[cut, :] = (values * inverse * gains[0:1, :]).astype(BF)
        return 0

    lax.fori_loop(0, rows // small, norm, 0)
    kept = []

    def keep(source, target):
        move = pltpu.make_async_copy(source, target, out_sems.at[len(kept)])
        move.start()
        kept.append(move)

    keep(normed, normed_hbm)
    queues = (qkv_a, qkv_b)
    waits = []
    for h in range(2):
        arrived(weight(h, other), w_recv.at[h, 1])
        launch(
            remote(
                weight(h, other), weight(h, other), w_send.at[h, 2], w_recv.at[h, 2], {"fsdp": pair}
            )
        )
    for h in range(2):
        arrived(weight(h, pair), w_recv.at[h, 0])
        arrived(weight(h, far), w_recv.at[h, 2])

        def project(n, _):
            cut = pl.ds(pl.multiple_of(n * 256, 256), 256)
            value = mm(wt[h * wide : (h + 1) * wide, :], normed[cut, :], NT).astype(BF)
            for z in range(slabs):
                parts[h, z, :, cut] = value[z * 3 * HD : (z + 1) * 3 * HD]
            return 0

        lax.fori_loop(0, rows // 256, project, 0)
        for k in range(1, slabs):
            z = lax.rem(here + k, slabs)
            waits.append(
                launch(
                    remote(
                        parts.at[h, z], queues[h].at[here], part_send.at[h, k], part_recv.at[h, k],
                        {"ctx": z},
                    )
                )
            )
        stays = pltpu.make_async_copy(parts.at[h, here], queues[h].at[here], part_local.at[h])
        stays.start()
        waits.append(stays)

    keep(wt, wt_hbm)
    for h, (qkv, mix_ref, of_ref, lse_ref) in enumerate(
        ((qkv_a, mix_a, of_a, lse_a), (qkv_b, mix_b, of_b, lse_b))
    ):
        for move in waits[h * slabs : (h + 1) * slabs - 1]:
            move.wait_recv()
        waits[(h + 1) * slabs - 1].wait()
        keep(qkv, (qkv_a_hbm, qkv_b_hbm)[h])

        def emit(i, mix, lse):
            of_ref[i] = mix
            lse_ref[i] = lse
            for t in range(halves):
                mixed[h, i, t] = mix[:, t * half : (t + 1) * half].astype(BF)
                stay = (i == here) & (line == t)

                @pl.when(stay)
                def _():
                    pltpu.make_async_copy(
                        mixed.at[h, i, t], mix_ref.at[here, line], mix_local.at[h]
                    ).start()

                @pl.when(jnp.logical_not(stay))
                def _():
                    remote(
                        mixed.at[h, i, t], mix_ref.at[here, line], mix_send.at[h, i, t],
                        mix_recv.at[h, here, line], {"ctx": i, "tp": t},
                    ).start()

        attend_rows(rows, len_ref[0], qkv, kx, qx, vx, emit)
        keep(of_ref, (of_a_hbm, of_b_hbm)[h])
        keep(lse_ref, (lse_a_hbm, lse_b_hbm)[h])

    for move in sent:
        move.wait_send()
    for move in kept:
        move.wait()
    for h, mix_ref in enumerate((mix_a, mix_b)):
        pltpu.make_async_copy(mixed.at[h, here, line], mix_ref.at[here, line], mix_local.at[h]).wait()
        for dz, dt in peers:
            z, t = peer(dz, dt)
            remote(
                mixed.at[h, z, t], mix_ref.at[z, t], mix_send.at[h, z, t], mix_recv.at[h, z, t],
                {"ctx": z, "tp": t},
            ).wait()


def front_stage(length, x, gains, wq, wk, wv, slabs, halves):
    rows, width = x.shape
    half = rows // halves
    wide = slabs * 3 * HD
    total = slabs * rows
    work = total * (total + rows) // 2
    vmem = pl.BlockSpec(memory_space=pltpu.VMEM)
    outside = pl.BlockSpec(memory_space=pltpu.HBM)
    dma = pltpu.SemaphoreType.DMA
    shape = jax.ShapeDtypeStruct
    return pl.pallas_call(
        front_kernel,
        out_shape=(
            shape((2 * wide, width), BF),
            shape((rows, width), BF),
            shape((8, width), F32),
            *[shape((slabs, 3 * HD, rows), BF)] * 2,
            *[shape((slabs, halves, HD, half), BF)] * 2,
            *[shape((slabs, HD, rows), F32)] * 2,
            *[shape((slabs, 1, rows), F32)] * 2,
        ),
        in_specs=[pl.BlockSpec(memory_space=pltpu.SMEM)] + [vmem] * 5,
        out_specs=(outside, outside, vmem, *[outside] * 8),
        scratch_shapes=[
            pltpu.VMEM((2 * wide, width), BF),
            pltpu.VMEM((rows, width), BF),
            *[pltpu.VMEM((slabs, 3 * HD, rows), BF)] * 2,
            *[pltpu.VMEM((slabs, HD, rows), F32)] * 2,
            *[pltpu.VMEM((slabs, 1, rows), F32)] * 2,
            dma((8,)),
            pltpu.VMEM((2, wide, wq.shape[0]), BF),
            pltpu.VMEM((2, slabs, 3 * HD, rows), BF),
            pltpu.VMEM((2, slabs, halves, HD, half), BF),
            pltpu.VMEM((total, 2 * HD), BF),
            pltpu.VMEM((slabs, 2 * HD, rows), BF),
            pltpu.VMEM((slabs, HD, rows), BF),
            dma((3,)), dma((3,)), dma((2, 3)), dma((2, 3)),
            dma((2, slabs)), dma((2, slabs)), dma((2,)),
            dma((2, slabs, halves)), dma((2, slabs, halves)), dma((2,)),
        ],
        compiler_params=pltpu.CompilerParams(
            vmem_limit_bytes=60 << 20, collective_id=3, has_side_effects=True
        ),
        cost_estimate=pl.CostEstimate(
            flops=2 * work * 256 * 4, bytes_accessed=20 << 20, transcendentals=2 * work
        ),
    )(length, x, gains, wq, wk, wv)


def attend(length, qkv, halves, tile):
    slabs, _, rows = qkv.shape
    total = slabs * rows
    tile = min(tile, rows)
    work = total * (total + tile) // 2
    vmem = pl.BlockSpec(memory_space=pltpu.VMEM)
    return pl.pallas_call(
        functools.partial(attend_kernel, tile),
        out_shape=(
            jax.ShapeDtypeStruct((slabs, halves, HD, rows // halves), BF),
            jax.ShapeDtypeStruct((slabs, HD, rows), F32),
            jax.ShapeDtypeStruct((slabs, 1, rows), F32),
        ),
        in_specs=[pl.BlockSpec(memory_space=pltpu.SMEM), vmem],
        out_specs=(vmem, vmem, vmem),
        scratch_shapes=[
            pltpu.VMEM((total, 2 * HD), BF),
            pltpu.VMEM((total // tile, 2 * HD, tile), BF),
            pltpu.VMEM((total // tile, HD, tile), BF),
        ],
        compiler_params=pltpu.CompilerParams(vmem_limit_bytes=60 << 20),
        cost_estimate=pl.CostEstimate(
            flops=work * 256 * 4, bytes_accessed=qkv.size * 4, transcendentals=work
        ),
    )(length, qkv)


def attend_back_rows(tile, length, qkv, do_ref, of_ref, lse_ref, out, scratch, emit):
    kx, qx, vx, kt, dox, dq, st, dk, dv = scratch
    slabs, _, rows = qkv.shape
    halves, half = do_ref.shape[1], do_ref.shape[3]
    per = rows // tile
    blocks = slabs * per
    for z in range(slabs):
        keys = qkv[z, HD : 2 * HD, :]
        kx[z * rows : (z + 1) * rows, :] = spread_keys(keys.astype(F32).T, z * rows, length)
        queries = spread_queries(qkv[z, 0:HD, :].astype(F32))
        values = qkv[z, 2 * HD : 3 * HD, :].astype(F32).T
        vx[z * rows : (z + 1) * rows, :] = jnp.concatenate(
            [values, jnp.zeros((rows, HD), F32)], axis=1
        ).astype(BF)
        d_mix = jnp.concatenate([do_ref[z, t] for t in range(halves)], axis=1)
        delta = jnp.sum(d_mix.astype(F32) * of_ref[z], axis=0, keepdims=True)
        for b in range(per):
            cut = slice(b * tile, (b + 1) * tile)
            n = z * per + b
            qx[n] = queries[:, cut]
            kt[n] = keys[:, cut]
            dox[n, 0:HD] = d_mix[:, cut]
            dox[n, HD : 2 * HD] = jnp.zeros((HD, tile), BF)
            st[n, 0:1] = lse_ref[z, :, cut]
            st[n, 1:2] = delta[:, cut]
    for ref in (dq, dk, dv):
        ref[...] = jnp.zeros_like(ref)
    later = lax.broadcasted_iota(jnp.int32, (tile, tile), 0) > lax.broadcasted_iota(
        jnp.int32, (tile, tile), 1
    )

    def step(i, j, masked):
        here = pl.ds(pl.multiple_of(j * tile, tile), tile)
        scores = mm(kx[here, :], qx[i], NN)
        if masked:
            scores = jnp.where(later, MASKED, scores)
        probs = jnp.exp(scores - st[i, 0:1])
        d_probs = mm(vx[here, :], dox[i], NN)
        d_scores = (probs * (d_probs - st[i, 1:2])).astype(BF)
        dv[j] += mm(dox[i, 0:HD], probs.astype(BF), NT)
        dk[j] += mm(qx[i, 0:HD], d_scores, NT)
        dq[i] += mm(kt[j], d_scores, NN)

    def complete(n):
        z = n // per
        cut = pl.ds(pl.multiple_of(lax.rem(n, per) * tile, tile), tile)
        out[z, 0:HD, cut] = (dq[n] * HD**-0.5).astype(BF)
        out[z, HD : 2 * HD, cut] = dk[n].astype(BF)
        out[z, 2 * HD : 3 * HD, cut] = dv[n].astype(BF)
        if emit is not None:
            emit(n)

    def ring(k, _):
        last = blocks - 1 - k

        def down(i, _):
            step(i, k, False)
            return 0

        def across(j, _):
            step(last, j, False)
            return 0

        step(k, k, True)
        lax.fori_loop(k + 1, last + 1, down, 0)
        complete(k)
        lax.fori_loop(k + 1, last, across, 0)
        step(last, last, True)
        complete(last)
        return 0

    lax.fori_loop(0, blocks // 2, ring, 0)


def attend_back_scratch(slabs, rows, tile):
    total = slabs * rows
    blocks = total // tile
    return [
        pltpu.VMEM((total, 2 * HD), BF),
        pltpu.VMEM((blocks, 2 * HD, tile), BF),
        pltpu.VMEM((total, 2 * HD), BF),
        pltpu.VMEM((blocks, HD, tile), BF),
        pltpu.VMEM((blocks, 2 * HD, tile), BF),
        pltpu.VMEM((blocks, HD, tile), F32),
        pltpu.VMEM((blocks, 8, tile), F32),
        pltpu.VMEM((blocks, HD, tile), F32),
        pltpu.VMEM((blocks, HD, tile), F32),
    ]


def attend_back_kernel(tile, len_ref, qkv, do_ref, of_ref, lse_ref, out, *scratch):
    attend_back_rows(tile, len_ref[0], qkv, do_ref, of_ref, lse_ref, out, scratch, None)


def back_kernel(
    tile, len_ref, qkv_a, qkv_b, do_a, do_b, of_a, of_b, lse_a, lse_b, keep_hbm, got_hbm,
    out_a, out_b, rest,
    local, keep, got, low_got, high_got, swapped, *refs,
):
    scratch, sems = refs[:9], refs[9:]
    (load_sems, grad_send, grad_recv, grad_local, low_send, low_recv, high_send, high_recv,
     swap_send, swap_recv) = sems
    here, line, place = lax.axis_index("ctx"), lax.axis_index("tp"), lax.axis_index("fsdp")
    column = place // 2
    beside = {"fsdp": lax.rem(place + 2, 4)}
    across = {"tp": 1 - line}
    mesh_id = pl.DeviceIdType.MESH
    slabs, block = qkv_a.shape[0], qkv_a.shape[1]
    loads = [
        pltpu.make_async_copy(source, target, load_sems.at[k])
        for k, (source, target) in enumerate(((keep_hbm, keep), (got_hbm, got)))
    ]
    for load in loads:
        load.start()
    others = [lax.rem(here + k, slabs) for k in range(1, slabs)]
    barrier = pltpu.get_barrier_semaphore()
    for device in (*[{"ctx": z} for z in others], beside, across):
        pl.semaphore_signal(barrier, inc=1, device_id=device, device_id_type=mesh_id)
    pl.semaphore_wait(barrier, slabs + 1)

    def remote(source, target, send, recv, device):
        return pltpu.make_async_remote_copy(
            src_ref=source, dst_ref=target, send_sem=send, recv_sem=recv,
            device_id=device, device_id_type=mesh_id,
        )

    outs = (out_a, out_b)

    per = qkv_a.shape[2] // tile

    def lanes(b):
        return pl.ds(pl.multiple_of(b * tile, tile), tile)

    def window(h, at, b):
        return outs[h].at[pl.ds(pl.multiple_of(at * block, block), block), lanes(b)]

    def attend_head(h, qkv, do_ref, of_ref, lse_ref):
        def emit(n):
            z, b = n // per, lax.rem(n, per)

            @pl.when(z == here)
            def _():
                pltpu.make_async_copy(
                    local.at[h, z, :, lanes(b)], window(h, here, b), grad_local.at[h, b]
                ).start()

            @pl.when(z != here)
            def _():
                remote(
                    local.at[h, z, :, lanes(b)], window(h, here, b), grad_send.at[h, z, b],
                    grad_recv.at[h, here, b], {"ctx": z},
                ).start()

        attend_back_rows(
            tile, len_ref[0], qkv, do_ref, of_ref, lse_ref, local.at[h], scratch, emit
        )

    for load in loads:
        load.wait()
    cut = rest.shape[0] // 2
    for t in range(2):
        for x in range(2):
            keep[t, x] = (keep[t, x].astype(F32) + got[t, x].astype(F32)).astype(BF)
    moves = []
    for k in range(2):
        moves.append(
            remote(
                keep.at[1 - line, k, 0:cut], low_got.at[k], low_send.at[k], low_recv.at[k], across
            )
        )
        moves.append(
            remote(
                keep.at[k, 1 - column, cut : 2 * cut], high_got.at[k], high_send.at[k],
                high_recv.at[k], beside,
            )
        )
    for move in moves:
        move.start()
    attend_head(0, qkv_a, do_a, of_a, lse_a)
    attend_head(1, qkv_b, do_b, of_b, lse_b)
    for move in moves:
        move.wait_recv()
    low, high = slice(0, cut), slice(cut, 2 * cut)
    for k in range(2):
        keep[line, k, low] = (
            keep[line, k, low].astype(F32) + low_got[k].astype(F32)
        ).astype(BF)
        keep[k, column, high] = (
            keep[k, column, high].astype(F32) + high_got[k].astype(F32)
        ).astype(BF)
    swaps = [
        remote(
            keep.at[line, 1 - column, low], swapped.at[0], swap_send.at[0], swap_recv.at[0], beside
        ),
        remote(
            keep.at[1 - line, column, high], swapped.at[1], swap_send.at[1], swap_recv.at[1], across
        ),
    ]
    for move in swaps:
        move.start()
    for move in swaps:
        move.wait_recv()
    for k, part in enumerate((low, high)):
        rest[part] = (
            keep[line, column, part].astype(F32) + swapped[k].astype(F32)
        ).astype(BF)
    for h in range(2):
        for b in range(per):
            pltpu.make_async_copy(
                local.at[h, here, :, lanes(b)], window(h, here, b), grad_local.at[h, b]
            ).wait()
            for z in others:
                remote(
                    local.at[h, z, :, lanes(b)], window(h, z, b), grad_send.at[h, z, b],
                    grad_recv.at[h, z, b], {"ctx": z},
                ).wait()
    for move in (*moves, *swaps):
        move.wait_send()


def back_stage(length, qkv, d_mix, saved, keep, got):
    slabs, block, rows = qkv[0].shape
    tile = 512
    lanes = keep.shape[3]
    total = slabs * rows
    work = total * (total + tile) // 2
    vmem = pl.BlockSpec(memory_space=pltpu.VMEM)
    outside = pl.BlockSpec(memory_space=pl.ANY)
    dma = pltpu.SemaphoreType.DMA
    return pl.pallas_call(
        functools.partial(back_kernel, tile),
        out_shape=(
            jax.ShapeDtypeStruct((slabs * block, rows), BF),
            jax.ShapeDtypeStruct((slabs * block, rows), BF),
            jax.ShapeDtypeStruct((256, lanes), BF),
        ),
        in_specs=[pl.BlockSpec(memory_space=pltpu.SMEM)] + [vmem] * 8 + [outside] * 2,
        out_specs=(vmem,) * 3,
        scratch_shapes=[
            pltpu.VMEM((2, slabs, block, rows), BF),
            pltpu.VMEM(keep.shape, BF),
            pltpu.VMEM(keep.shape, BF),
            pltpu.VMEM((2, 128, lanes), BF),
            pltpu.VMEM((2, 128, lanes), BF),
            pltpu.VMEM((2, 128, lanes), BF),
            *attend_back_scratch(slabs, rows, tile),
            dma((2,)), dma((2, slabs, rows // tile)), dma((2, slabs, rows // tile)),
            dma((2, rows // tile)),
            dma((2,)), dma((2,)), dma((2,)), dma((2,)), dma((2,)), dma((2,)),
        ],
        compiler_params=pltpu.CompilerParams(
            vmem_limit_bytes=60 << 20, collective_id=4, has_side_effects=True
        ),
        cost_estimate=pl.CostEstimate(
            flops=2 * work * 256 * 10, bytes_accessed=24 << 20, transcendentals=2 * work
        ),
    )(length, *qkv, *d_mix, *[m for m, _ in saved], *[l for _, l in saved], keep, got)


def attend_back(length, qkv, d_mix, mix, lse, tile):
    slabs, _, rows = qkv.shape
    total = slabs * rows
    tile = min(tile, rows)
    work = total * (total + tile) // 2
    vmem = pl.BlockSpec(memory_space=pltpu.VMEM)
    return pl.pallas_call(
        functools.partial(attend_back_kernel, tile),
        out_shape=jax.ShapeDtypeStruct((slabs, 3 * HD, rows), BF),
        in_specs=[pl.BlockSpec(memory_space=pltpu.SMEM), vmem, vmem, vmem, vmem],
        out_specs=vmem,
        scratch_shapes=attend_back_scratch(slabs, rows, tile),
        compiler_params=pltpu.CompilerParams(vmem_limit_bytes=60 << 20),
        cost_estimate=pl.CostEstimate(
            flops=work * 256 * 10, bytes_accessed=qkv.size * 8, transcendentals=work
        ),
    )(length, qkv, d_mix, mix, lse)


def widths(total, step):
    return [(at, min(step, total - at)) for at in range(0, total, step)]


def middle_kernel(
    ff, split, scal, mix_a_hbm, mix_b_hbm, own_hbm, cot_hbm, gain, w_hbm,
    out_ref, dmid_ref, got_a, got_b, *refs,
):
    n_out = 3 if split < w_hbm.shape[2] else 1
    grads = refs[:n_out]
    (w, acts, att_t, mid, scale, dn, normed_ref, branch_ref, dattn_ref, turned, do_a, do_b,
     sems, out_sems, send_sems, recv_sems, local_sems, core_send, core_recv,
     own, cot, mix_a, mix_b, row_sems) = refs[n_out:]
    slabs, halves, _, half = mix_a.shape
    width = own.shape[1]
    side = pl.ds(pl.multiple_of(lax.axis_index("tp") * half, half), half)
    row_loads = [
        pltpu.make_async_copy(source.at[side, :], target, row_sems.at[k])
        for k, (source, target) in enumerate(((own_hbm, own), (cot_hbm, cot)))
    ]
    mix_loads = [
        pltpu.make_async_copy(source, target, row_sems.at[2 + k])
        for k, (source, target) in enumerate(((mix_a_hbm, mix_a), (mix_b_hbm, mix_b)))
    ]
    for load in (*mix_loads, *row_loads):
        load.start()
    inner = width // halves
    base = 3 * ff
    lanes = base + inner
    here, line = lax.axis_index("ctx"), lax.axis_index("tp")
    core = lax.rem(lax.axis_index("fsdp"), 2)
    sibling = {"fsdp": lax.axis_index("fsdp") + 1 - 2 * core}
    barrier = pltpu.get_barrier_semaphore()
    peers = [(dz, dt) for dz in range(slabs) for dt in range(halves) if dz or dt]

    def peer(dz, dt):
        return lax.rem(here + dz, slabs), lax.rem(line + dt, halves)

    for dz, dt in peers:
        z, t = peer(dz, dt)
        pl.semaphore_signal(
            barrier, inc=1, device_id={"ctx": z, "tp": t}, device_id_type=pl.DeviceIdType.MESH
        )
    if n_out == 3:
        pl.semaphore_signal(
            barrier, inc=1, device_id=sibling, device_id_type=pl.DeviceIdType.MESH
        )
    cuts = [(t, base, inner) for t in range(halves)]
    cuts += [(t, k * ff, ff) for t in range(halves) for k in range(3)]
    loads = [
        pltpu.make_async_copy(
            w_hbm.at[t, :, at : at + n], w.at[t, :, at : at + n], sems.at[k]
        )
        for k, (t, at, n) in enumerate(cuts)
    ]
    for load in loads:
        load.start()
    length, first = scal[0], scal[1]
    step = 256
    rows = 64

    for load in mix_loads:
        load.wait()
    for t in range(halves):
        for z in range(slabs):
            at = z * 2 * HD
            att_t[at : at + HD, :] = mix_a[z, t]
            att_t[at + HD : at + 2 * HD, :] = mix_b[z, t]
        acts[t, :, base:lanes] = att_t[...].astype(F32).T.astype(BF)
    for k in range(halves):
        loads[k].wait()
    for load in row_loads:
        load.wait()

    def project(n, _):
        cut = pl.ds(pl.multiple_of(n * step, step), step)
        total = own[:, cut].astype(F32)
        for t in range(halves):
            total = total + mm(acts[t, :, base:lanes], w[t, cut, base:lanes], NT)
        mid[:, cut] = total
        return 0

    lax.fori_loop(0, width // step, project, 0)

    def row_mask(r):
        pos = first + r * rows + lax.broadcasted_iota(jnp.int32, (rows, 1), 0)
        return jnp.where(pos < length, 1.0, 0.0)

    def norm(r, _):
        cut = pl.ds(pl.multiple_of(r * rows, rows), rows)
        values = mid[cut, :]
        inverse = lax.rsqrt(jnp.mean(values * values, axis=1, keepdims=True) + EPSILON)
        scale[cut, :] = jnp.broadcast_to(inverse, (rows, 128))
        normed_ref[cut, :] = (values * inverse * gain[...]).astype(BF)
        branch_ref[cut, :] = (cot[cut, :].astype(F32) * row_mask(r)).astype(BF)
        return 0

    lax.fori_loop(0, half // rows, norm, 0)

    for t in range(halves):
        for k in range(3):
            loads[halves + 3 * t + k].wait()

        def columns(at, n):
            def cut(k):
                return pl.ds(pl.multiple_of(k * ff + at, 128), n)

            gate = mm(normed_ref[...], w[t, :, cut(0)], NN)
            upward = mm(normed_ref[...], w[t, :, cut(1)], NN)
            d_hidden = mm(branch_ref[...], w[t, :, cut(2)], NN)
            sig = 1.0 / (1.0 + jnp.exp(-gate))
            active = gate * sig
            acts[t, :, cut(2)] = (active * upward).astype(BF)
            acts[t, :, cut(0)] = (
                d_hidden * upward * sig * (1.0 + gate * (1.0 - sig))
            ).astype(BF)
            acts[t, :, cut(1)] = (d_hidden * active).astype(BF)

        def chunk(c, _):
            columns(c * step, step)
            return 0

        lax.fori_loop(0, ff // step, chunk, 0)
        if ff % step:
            columns(ff - ff % step, ff % step)

    def back(n, _):
        cut = pl.ds(pl.multiple_of(n * step, step), step)
        total = mid[:, cut]
        grad = jnp.zeros((half, step), F32)
        for t in range(halves):
            total = total + mm(acts[t, :, 2 * ff : base], w[t, cut, 2 * ff : base], NT)
            grad = grad + mm(acts[t, :, 0:ff], w[t, cut, 0:ff], NT)
            grad = grad + mm(acts[t, :, ff : 2 * ff], w[t, cut, ff : 2 * ff], NT)
        dmid_ref[:, cut] = total
        dn[:, cut] = grad
        return 0

    lax.fori_loop(0, width // step, back, 0)

    def finish(r, _):
        cut = pl.ds(pl.multiple_of(r * rows, rows), rows)
        mask = row_mask(r)
        out_ref[cut, :] = (dmid_ref[cut, :] * mask).astype(BF)
        inverse = scale[cut, 0:1]
        scaled = mid[cut, :] * inverse
        d_scaled = dn[cut, :] * gain[...]
        mean = jnp.mean(d_scaled * scaled, axis=1, keepdims=True)
        total = cot[cut, :].astype(F32) * mask + inverse * (d_scaled - scaled * mean)
        dmid_ref[cut, :] = total
        dattn_ref[cut, :] = total.astype(BF)
        return 0

    lax.fori_loop(0, half // rows, finish, 0)
    for t in range(halves):
        for z in range(0, slabs, 2):
            at = base + z * 2 * HD
            grad = mm(dattn_ref[...], w[t, :, at : at + 4 * HD], NN).T.astype(BF)
            for k in range(2):
                do_a[z + k, t] = grad[2 * k * HD : (2 * k + 1) * HD]
                do_b[z + k, t] = grad[(2 * k + 1) * HD : (2 * k + 2) * HD]

    pl.semaphore_wait(barrier, len(peers) + (n_out == 3))
    moves = []
    for k, (dz, dt) in enumerate(peers):
        z, t = peer(dz, dt)
        for h, (source, target) in enumerate(((do_a, got_a), (do_b, got_b))):
            move = pltpu.make_async_remote_copy(
                src_ref=source.at[z, t],
                dst_ref=target.at[here, line],
                send_sem=send_sems.at[2 * k + h],
                recv_sem=recv_sems.at[2 * k + h],
                device_id={"ctx": z, "tp": t},
                device_id_type=pl.DeviceIdType.MESH,
            )
            move.start()
            moves.append(move)
    for h, (source, target) in enumerate(((do_a, got_a), (do_b, got_b))):
        move = pltpu.make_async_copy(
            source.at[here, line], target.at[here, line], local_sems.at[h]
        )
        move.start()
        moves.append(move)

    regions = ((0, 2 * ff), (2 * ff, base), (base, lanes))

    def own_copy(n, t):
        cut = pl.ds(pl.multiple_of(n * step, step), step)
        return pltpu.make_async_copy(
            w.at[t, cut, split:lanes], grads[1].at[t, n // 2], out_sems.at[n, t, 1]
        )

    def core_copy(n, t):
        cut = pl.ds(pl.multiple_of(n * step, step), step)
        return pltpu.make_async_remote_copy(
            src_ref=w.at[t, cut, split:lanes], dst_ref=grads[2].at[t, n // 2],
            send_sem=core_send.at[n, t], recv_sem=core_recv.at[n, t],
            device_id=sibling, device_id_type=pl.DeviceIdType.MESH,
        )

    def some_copy(t):
        return pltpu.make_async_copy(
            w.at[t, :, 0:split], grads[0].at[t], out_sems.at[0, t, 0]
        )

    def store(t):
        if n_out == 1:
            return

        def rows_of(n, _):
            @pl.when(lax.rem(n, 2) == core)
            def _():
                own_copy(n, t).start()

            @pl.when(lax.rem(n, 2) != core)
            def _():
                core_copy(n, t).start()

            return 0

        lax.fori_loop(0, width // step, rows_of, 0)

    for k, ref in enumerate((normed_ref, branch_ref, dattn_ref)):
        for b in range(0, width, step):
            turned[k, b : b + step] = ref[:, b : b + step].astype(F32).T.astype(BF)
    for t in range(halves):

        def fill(k, at, n):
            cut = pl.ds(at, n)
            w[t, :, cut] = mm(turned[k], acts[t, :, cut], NN).astype(BF)

        def span(k, start, stop):
            def chunk(c, _):
                fill(k, pl.multiple_of(start + c * step, 128), step)
                return 0

            count = (stop - start) // step
            lax.fori_loop(0, count, chunk, 0)
            if start + count * step < stop:
                fill(k, start + count * step, stop - start - count * step)

        for k, (at, end) in enumerate(regions):
            if at < split < end:
                span(k, at, split)
                at = split
                some_copy(t).start()
            span(k, at, end)
            if end == split:
                some_copy(t).start()
        store(t)

    for t in range(halves):
        some_copy(t).wait()

        def settle(n, _):
            @pl.when(lax.rem(n, 2) == core)
            def _():
                own_copy(n, t).wait()
                core_copy(n, t).wait_recv()

            @pl.when(lax.rem(n, 2) != core)
            def _():
                core_copy(n, t).wait_send()

            return 0

        if n_out == 3:
            lax.fori_loop(0, width // step, settle, 0)
    for move in moves:
        move.wait()


def middle_stage(scalars, mix_a, mix_b, own, cot, gain, w, split):
    halves, width, lanes = w.shape
    slabs, _, _, half = mix_a.shape
    ff = (lanes - width // halves) // 3
    blocks = width // 256
    peers = slabs * halves - 1
    vmem = pl.BlockSpec(memory_space=pltpu.VMEM)
    outside = pl.BlockSpec(memory_space=pl.ANY)
    out_shape = [
        jax.ShapeDtypeStruct((half, width), BF),
        jax.ShapeDtypeStruct((half, width), F32),
        jax.ShapeDtypeStruct(mix_a.shape, BF),
        jax.ShapeDtypeStruct(mix_a.shape, BF),
        jax.ShapeDtypeStruct((halves, width, split), BF),
    ]
    out_specs = [vmem] * 4 + [outside]
    if split < lanes:
        out_shape += [jax.ShapeDtypeStruct((halves, blocks // 2, 256, lanes - split), BF)] * 2
        out_specs += [outside] * 2
    flops = 2 * half * width * (9 * ff * halves + 3 * width)
    return pl.pallas_call(
        functools.partial(middle_kernel, ff, split),
        out_shape=out_shape,
        in_specs=[
            pl.BlockSpec(memory_space=pltpu.SMEM), *[pl.BlockSpec(memory_space=pltpu.HBM)] * 4,
            vmem, outside,
        ],
        out_specs=out_specs,
        scratch_shapes=[
            pltpu.VMEM((halves, width, lanes), BF),
            pltpu.VMEM((halves, half, lanes), BF),
            pltpu.VMEM((width // halves, half), BF),
            pltpu.VMEM((half, width), F32),
            pltpu.VMEM((half, 128), F32),
            pltpu.VMEM((half, width), F32),
            pltpu.VMEM((half, width), BF),
            pltpu.VMEM((half, width), BF),
            pltpu.VMEM((half, width), BF),
            pltpu.VMEM((3, width, half), BF),
            pltpu.VMEM(mix_a.shape, BF),
            pltpu.VMEM(mix_a.shape, BF),
            pltpu.SemaphoreType.DMA((4 * halves,)),
            pltpu.SemaphoreType.DMA((blocks, halves, 2)),
            pltpu.SemaphoreType.DMA((2 * peers,)),
            pltpu.SemaphoreType.DMA((2 * peers,)),
            pltpu.SemaphoreType.DMA((2,)),
            pltpu.SemaphoreType.DMA((blocks, halves)),
            pltpu.SemaphoreType.DMA((blocks, halves)),
            pltpu.VMEM((half, width), BF),
            pltpu.VMEM((half, width), BF),
            pltpu.VMEM(mix_a.shape, BF),
            pltpu.VMEM(mix_a.shape, BF),
            pltpu.SemaphoreType.DMA((4,)),
        ],
        compiler_params=pltpu.CompilerParams(
            vmem_limit_bytes=60 << 20, collective_id=1, has_side_effects=True
        ),
        cost_estimate=pl.CostEstimate(
            flops=flops, bytes_accessed=4 * w.size + 16 * half * width, transcendentals=half * lanes
        ),
    )(scalars, mix_a, mix_b, own, cot, gain, w)


class LineSum:
    def __init__(self, source, held, slots, out, sems):
        self.source, self.held, self.slots, self.out = source, held, slots, out
        self.sum_send, self.sum_recv, self.out_send, self.out_recv = sems
        here = lax.axis_index("ctx")
        self.low = here < 2
        self.place = jnp.where(self.low, here, 3 - here)
        self.inward = jnp.where(self.low, here + 1, here - 1)
        self.outward = jnp.where(self.low, here - 1, here + 1)
        self.size = out.shape[0] // 4

    def number(self, part):
        return jnp.where(self.low, part, 3 - part)

    def part(self, ref, part):
        at = pl.multiple_of(self.number(part) * self.size, self.size)
        return ref.at[pl.ds(at, self.size), :]

    def read(self, ref, part):
        at = pl.multiple_of(self.number(part) * self.size, self.size)
        return ref[pl.ds(at, self.size), :].astype(F32)

    def write(self, ref, part, value):
        at = pl.multiple_of(self.number(part) * self.size, self.size)
        ref[pl.ds(at, self.size), :] = value.astype(BF)

    def copy(self, source, target, send, recv, place):
        return pltpu.make_async_remote_copy(
            src_ref=source, dst_ref=target, send_sem=send, recv_sem=recv,
            device_id={"ctx": place}, device_id_type=pl.DeviceIdType.MESH,
        )

    def took(self, slot):
        ref = self.slots.at[slot]
        self.copy(ref, ref, self.sum_send.at[0], self.sum_recv.at[slot], self.inward).wait_recv()
        return self.slots[slot].astype(F32)

    def begin(self):
        @pl.when(self.place == 0)
        def _():
            for k in range(3):
                self.copy(
                    self.part(self.source, 3 - k), self.slots.at[k],
                    self.sum_send.at[k], self.sum_recv.at[k], self.inward,
                ).start()

    def left(self, k):
        self.copy(
            self.slots.at[0], self.slots.at[0],
            self.sum_send.at[k], self.sum_recv.at[0], self.inward,
        ).wait_send()

    def first(self, k):
        @pl.when(self.place == 1)
        def _():
            self.write(self.held, 3 - k, self.read(self.source, 3 - k) + self.took(k))
            self.copy(
                self.part(self.held, 3 - k), self.slots.at[3 + k],
                self.sum_send.at[k], self.sum_recv.at[3 + k], self.inward,
            ).start()

    def second(self):
        @pl.when(self.place == 1)
        def _():
            self.write(self.held, 0, self.read(self.source, 0) + self.took(3))
            self.copy(
                self.part(self.held, 0), self.slots.at[3],
                self.sum_send.at[2], self.sum_recv.at[3], self.outward,
            ).start()

    def give(self, part, send, place):
        ref = self.part(self.out, part)
        return self.copy(
            ref, ref, self.out_send.at[send], self.out_recv.at[self.number(part)], place
        )

    def final(self):
        @pl.when(self.place == 1)
        def _():
            self.write(self.out, 1, self.read(self.source, 1) + self.took(2) + self.took(4))
            self.give(1, 0, self.inward).start()
            self.give(1, 1, self.outward).start()

        @pl.when(self.place == 0)
        def _():
            self.write(self.out, 0, self.read(self.source, 0) + self.took(3))
            self.give(0, 0, self.inward).start()

    def forward(self):
        @pl.when(self.place == 1)
        def _():
            for k, (part, place) in enumerate(((0, self.inward), (2, self.outward), (3, self.outward))):
                self.give(part, 2 + k, place).wait_recv()
                self.give(part, 2 + k, place).start()

    def end(self):
        @pl.when(self.place == 0)
        def _():
            for k in range(3):
                self.left(k)
            self.give(0, 0, self.inward).wait_send()
            for part in (1, 2, 3):
                self.give(part, 0, self.inward).wait_recv()

        @pl.when(self.place == 1)
        def _():
            for k in range(3):
                self.left(k)
            for k in range(5):
                self.give(1, k, self.inward).wait_send()


def tail_kernel(
    back_a, back_b, some, rest, normed, weights, own_hbm, gain, dmid,
    grad_out, some_out, rest_out, qa_out, qb_out,
    turned, some_held, some_slots, rest_held, rest_slots,
    local, crossed, column_sum, columned, q_src, q_held, q_slots, theirs, got_theirs, mine,
    core_send, core_recv, col_send, col_recv,
    row_send, row_recv, out_send, out_recv, *line_sems,
):
    here, line, place = lax.axis_index("ctx"), lax.axis_index("tp"), lax.axis_index("fsdp")
    core, column = lax.rem(place, 2), place // 2
    sibling = {"fsdp": place + 1 - 2 * core}
    beside = {"fsdp": lax.rem(place + 2, 4)}
    across = {"tp": 1 - line}
    others = [{"ctx": lax.rem(here + k, 4)} for k in range(1, 4)]
    mesh_id = pl.DeviceIdType.MESH
    barrier = pltpu.get_barrier_semaphore()
    for device in (*others, sibling, beside, across):
        pl.semaphore_signal(barrier, inc=1, device_id=device, device_id_type=mesh_id)
    pl.semaphore_wait(barrier, 6)

    def remote(source, target, send, recv, device):
        return pltpu.make_async_remote_copy(
            src_ref=source, dst_ref=target, send_sem=send, recv_sem=recv,
            device_id=device, device_id_type=mesh_id,
        )

    rows = normed.shape[0]
    half = rows // 2
    depth = 256
    own, own_sem, *line_sems = line_sems
    load = pltpu.make_async_copy(
        own_hbm.at[pl.ds(pl.multiple_of(line * half, half), half), :], own, own_sem
    )
    load.start()
    a, b, qa, qb = (
        LineSum(src, held, slots, out, line_sems[4 * k : 4 * k + 4])
        for k, (src, held, slots, out) in enumerate(
            (
                (some, some_held, some_slots, some_out),
                (rest, rest_held, rest_slots, rest_out),
                (q_src.at[0], q_held.at[0], q_slots.at[0], qa_out),
                (q_src.at[1], q_held.at[1], q_slots.at[1], qb_out),
            )
        )
    )
    a.begin()

    def weight_gradient(h, grads):
        def step(n, _):
            cut = pl.ds(pl.multiple_of(n * depth, depth), depth)
            value = mm(grads[...], normed[:, cut], NN).astype(BF)
            local[h, lax.rem(n, 2), n // 2] = value
            return 0

        lax.fori_loop(0, 4, step, 0)
        move = remote(
            local.at[h, 1 - core], crossed.at[h], core_send.at[h], core_recv.at[h], sibling
        )
        move.start()
        return move

    def column_step(h, move):
        move.wait_recv()
        for x in range(2):
            column_sum[h, x] = (
                local[h, core, x].astype(F32) + crossed[h, x].astype(F32)
            ).astype(BF)
        move = remote(
            column_sum.at[h, 1 - column], columned.at[h], col_send.at[h], col_recv.at[h], beside
        )
        move.start()
        return move

    def column_end(h, move):
        move.wait_recv()
        q_src[h] = (column_sum[h, column].astype(F32) + columned[h].astype(F32)).astype(BF)

    def turn(h, grads):
        for k in range(0, grads.shape[0], 128):
            at = h * grads.shape[0] + k
            turned[:, at : at + 128] = grads[k : k + 128, :].astype(F32).T.astype(BF)

    pieces = 2
    piece = half // pieces
    sent_rows = []
    sent_out = []
    mine_start = pl.multiple_of(line * half, half)

    def make_theirs(k):
        cut = slice(k * piece, (k + 1) * piece)
        start = pl.multiple_of((1 - line) * half + k * piece, piece)

        def make(n, _):
            wide = pl.ds(pl.multiple_of(n * depth, depth), depth)
            value = mm(turned[pl.ds(start, piece), :], weights[:, wide], NN)
            theirs[cut, wide] = value.astype(BF)
            return 0

        lax.fori_loop(0, 4, make, 0)
        move = remote(theirs.at[cut], got_theirs.at[cut], row_send.at[k], row_recv.at[k], across)
        move.start()
        sent_rows.append(move)

    def make_mine(n, _):
        wide = pl.ds(pl.multiple_of(n * depth, depth), depth)
        mine[:, wide] = mm(turned[pl.ds(mine_start, half), :], weights[:, wide], NN)
        return 0

    def finish_rows(k):
        small = 64
        if k == 0:
            load.wait()
        sent_rows[k].wait_recv()

        def back(r, _):
            at = pl.multiple_of(k * piece + r * small, small)
            cut = pl.ds(at, small)
            values = own[cut, :].astype(F32)
            inverse = lax.rsqrt(jnp.mean(values * values, axis=1, keepdims=True) + EPSILON)
            scaled = values * inverse
            d_scaled = (mine[cut, :] + got_theirs[cut, :].astype(F32)) * gain[...]
            mean = jnp.mean(d_scaled * scaled, axis=1, keepdims=True)
            total = dmid[cut, :] + inverse * (d_scaled - scaled * mean)
            grad_out[pl.ds(pl.multiple_of(line * half + at, small), small), :] = total.astype(BF)
            return 0

        lax.fori_loop(0, piece // small, back, 0)
        ref = grad_out.at[pl.ds(pl.multiple_of(line * half + k * piece, piece), piece), :]
        move = remote(ref, ref, out_send.at[k], out_recv.at[k], across)
        move.start()
        sent_out.append(move)

    b.begin()
    turn(0, back_a)
    turn(1, back_b)
    make_theirs(0)
    core_a = weight_gradient(0, back_a)
    a.first(0)
    make_theirs(1)
    core_b = weight_gradient(1, back_b)
    a.first(1)
    col_a = column_step(0, core_a)
    lax.fori_loop(0, 4, make_mine, 0)
    a.second()
    col_b = column_step(1, core_b)
    b.first(0)
    a.final()
    b.first(1)
    finish_rows(0)
    b.second()
    a.forward()
    column_end(0, col_a)
    qa.begin()
    b.final()
    finish_rows(1)
    column_end(1, col_b)
    qb.begin()
    qa.first(0)
    qa.first(1)
    b.forward()
    qb.first(0)
    qb.first(1)
    qa.second()
    qa.final()
    qb.second()
    qb.final()
    qa.forward()
    qb.forward()
    for run in (a, b, qa, qb):
        run.end()
    for move in (core_a, core_b, col_a, col_b, *sent_rows):
        move.wait_send()
    for k, move in enumerate(sent_out):
        move.wait_send()
        ref = grad_out.at[pl.ds(pl.multiple_of((1 - line) * half + k * piece, piece), piece), :]
        remote(ref, ref, out_send.at[k], out_recv.at[k], across).wait_recv()


def tail_stage(back_a, back_b, some, rest, normed, weights, own, gain, dmid):
    rows, width = normed.shape
    half = rows // 2
    lanes_a, lanes_b = some.shape[1], rest.shape[1]
    wide = back_a.shape[0]
    vmem = pl.BlockSpec(memory_space=pltpu.VMEM)
    dma = pltpu.SemaphoreType.DMA
    return pl.pallas_call(
        tail_kernel,
        out_shape=(
            jax.ShapeDtypeStruct((rows, width), BF),
            jax.ShapeDtypeStruct((256, lanes_a), BF),
            jax.ShapeDtypeStruct((256, lanes_b), BF),
            jax.ShapeDtypeStruct((wide, 256), BF),
            jax.ShapeDtypeStruct((wide, 256), BF),
        ),
        in_specs=[vmem] * 6 + [pl.BlockSpec(memory_space=pl.ANY)] + [vmem] * 2,
        out_specs=(vmem,) * 5,
        scratch_shapes=[
            pltpu.VMEM((rows, 2 * wide), BF),
            pltpu.VMEM((256, lanes_a), BF),
            pltpu.VMEM((5, 64, lanes_a), BF),
            pltpu.VMEM((256, lanes_b), BF),
            pltpu.VMEM((5, 64, lanes_b), BF),
            pltpu.VMEM((2, 2, 2, wide, 256), BF),
            pltpu.VMEM((2, 2, wide, 256), BF),
            pltpu.VMEM((2, 2, wide, 256), BF),
            pltpu.VMEM((2, wide, 256), BF),
            pltpu.VMEM((2, wide, 256), BF),
            pltpu.VMEM((2, wide, 256), BF),
            pltpu.VMEM((2, 5, wide // 4, 256), BF),
            pltpu.VMEM((half, width), BF),
            pltpu.VMEM((half, width), BF),
            pltpu.VMEM((half, width), F32),
            dma((2,)), dma((2,)), dma((2,)), dma((2,)),
            dma((2,)), dma((2,)), dma((2,)), dma((2,)),
            pltpu.VMEM((half, width), BF), dma,
        ]
        + [dma((3,)), dma((5,)), dma((5,)), dma((4,))] * 4,
        compiler_params=pltpu.CompilerParams(
            vmem_limit_bytes=60 << 20, collective_id=2, has_side_effects=True
        ),
        cost_estimate=pl.CostEstimate(
            flops=8 * rows * width * wide, bytes_accessed=40 << 20, transcendentals=0
        ),
    )(back_a, back_b, some, rest, normed, weights, own, gain, dmid)


def pack_kernel(gate, up, down_hbm, out_hbm, packed_hbm, packed, down, out, sems):
    ff = gate.shape[1]
    first = packed.at[:, 0 : 2 * ff]
    last = packed.at[:, 2 * ff :]
    loads = [
        pltpu.make_async_copy(source, target, sems.at[k])
        for k, (source, target) in enumerate(
            (
                (gate, packed.at[:, 0:ff]),
                (up, packed.at[:, ff : 2 * ff]),
                (down_hbm, down),
                (out_hbm, out),
            )
        )
    ]
    for move in loads:
        move.start()
    loads[0].wait()
    loads[1].wait()
    stores = [
        pltpu.make_async_copy(first, packed_hbm.at[:, 0 : 2 * ff], sems.at[4]),
        pltpu.make_async_copy(last, packed_hbm.at[:, 2 * ff :], sems.at[5]),
    ]
    stores[0].start()
    loads[2].wait()
    loads[3].wait()
    packed[:, 2 * ff : 3 * ff] = down[...].astype(F32).T.astype(BF)
    packed[:, 3 * ff :] = out[...].astype(F32).T.astype(BF)
    stores[1].start()
    for move in stores:
        move.wait()


def pack_stage(gate, up, down, out):
    depth, ff = gate.shape
    outside = pl.BlockSpec(memory_space=pltpu.HBM)
    return pl.pallas_call(
        pack_kernel,
        out_shape=jax.ShapeDtypeStruct((depth, 3 * ff + out.shape[0]), BF),
        in_specs=[outside] * 4,
        out_specs=outside,
        scratch_shapes=[
            pltpu.VMEM((depth, 3 * ff + out.shape[0]), BF),
            pltpu.VMEM(down.shape, BF),
            pltpu.VMEM(out.shape, BF),
            pltpu.SemaphoreType.DMA((6,)),
        ],
        compiler_params=pltpu.CompilerParams(vmem_limit_bytes=60 << 20),
        cost_estimate=pl.CostEstimate(flops=0, bytes_accessed=14 * depth * ff, transcendentals=0),
    )(gate, up, down, out)


def finish_kernel(
    *refs,
):
    sources, gains, grad_in = refs[:9], refs[9], refs[10]
    gate, up, down, out, qg, kg, vg, part, grad_out = refs[11:20]
    held, grad_held, sems = refs[20:29], refs[29], refs[30]
    some, rest, qa, qb, wq, wk, wv, gate_w, up_w = held
    taken = pltpu.make_async_copy(grad_in, grad_held, sems.at[9])
    given = pltpu.make_async_copy(grad_held, grad_out, sems.at[10])
    loads = [
        pltpu.make_async_copy(source, target, sems.at[k])
        for k, (source, target) in enumerate(zip(sources, held))
    ]
    for load in loads:
        load.start()
    taken.start()
    for load in loads:
        load.wait()
    ff = gate.shape[1]
    split = some.shape[1]
    low = split - ff
    high = ff - low

    def fold(values):
        total = values[:, 0:128]
        for at in range(128, values.shape[1], 128):
            total = total + values[:, at : at + 128]
        return total

    value = some[:, 0:ff].astype(F32)
    gate[...] = value
    taken.wait()
    given.start()
    two = fold(value * gate_w[...].astype(F32))
    value = some[:, ff:split].astype(F32)
    up[:, 0:low] = value
    two = two + fold(value * up_w[:, 0:low].astype(F32))
    value = rest[:, 0:high].astype(F32)
    up[:, low:ff] = value
    two = two + fold(value * up_w[:, low:ff].astype(F32))
    down[...] = rest[:, high : high + ff].astype(F32).T
    out[...] = rest[:, high + ff :].astype(F32).T
    one = jnp.zeros((gate.shape[0], 128), F32)
    for k, (target, weight) in enumerate(((qg, wq), (kg, wk), (vg, wv))):
        for z in range(qa.shape[0] // (3 * HD)):
            at = (3 * z + k) * HD
            value = jnp.concatenate([qa[at : at + HD, :], qb[at : at + HD, :]], axis=0)
            value = value.astype(F32).T
            cut = slice(2 * HD * z, 2 * HD * (z + 1))
            target[:, cut] = value
            one = one + value * weight[:, cut].astype(F32)
    part[...] = jnp.zeros_like(part)
    part[0:1] = jnp.sum(one.T, axis=0, keepdims=True) / gains[0:1]
    part[1:2] = jnp.sum(two.T, axis=0, keepdims=True) / gains[1:2]
    given.wait()


def finish_stage(some, rest, qa, qb, weights, gate_w, up_w, gains, grad):
    depth, ff = gate_w.shape
    inner = weights[0].shape[1]
    vmem = pl.BlockSpec(memory_space=pltpu.VMEM)
    outside = pl.BlockSpec(memory_space=pltpu.HBM)
    shape = jax.ShapeDtypeStruct
    operands = (some, rest, qa, qb, *weights, gate_w, up_w)
    return pl.pallas_call(
        finish_kernel,
        out_shape=(
            shape((depth, ff), F32), shape((depth, ff), F32), shape((ff, depth), F32),
            shape((inner, depth), F32), *[shape((depth, inner), F32)] * 3,
            shape((8, depth), F32), shape(grad.shape, BF),
        ),
        in_specs=[outside] * 9 + [vmem, outside],
        out_specs=(vmem,) * 8 + (outside,),
        scratch_shapes=[
            *[pltpu.VMEM(a.shape, BF) for a in operands], pltpu.VMEM(grad.shape, BF),
            pltpu.SemaphoreType.DMA((11,)),
        ],
        compiler_params=pltpu.CompilerParams(vmem_limit_bytes=60 << 20),
        cost_estimate=pl.CostEstimate(flops=0, bytes_accessed=16 << 20, transcendentals=0),
    )(*operands, gains, grad)


def normalize(values, gain):
    inverse = lax.rsqrt(jnp.mean(values * values, axis=-1, keepdims=True) + EPSILON)
    scaled = values * inverse
    return scaled, inverse, (scaled * gain).astype(BF)


def norm_back(d_normed, scaled, inverse, gain):
    d_scaled = d_normed * gain
    d_values = inverse * (d_scaled - scaled * jnp.mean(d_scaled * scaled, axis=-1, keepdims=True))
    return d_values


def rows_first(values):
    return with_layout_constraint(values, Layout(major_to_minor=tuple(range(values.ndim))))


def swap(values, axis, bit):
    count = lax.axis_size(axis)
    return lax.ppermute(values, axis, [(k, k ^ bit) for k in range(count)])


def both_halves(values):
    other = swap(values, "tp", 1)
    first = lax.axis_index("tp") == 0
    return jnp.concatenate([jnp.where(first, values, other), jnp.where(first, other, values)])


def shards(
    inputs,
    lengths,
    first_gain,
    query_weight,
    key_weight,
    value_weight,
    out_weight,
    second_gain,
    gate_weight,
    up_weight,
    down_weight,
    cotangent,
):
    slabs, halves, parts = lax.axis_size("ctx"), lax.axis_size("tp"), lax.axis_size("fsdp")
    rows, width = inputs.shape[1], inputs.shape[2]
    depth = query_weight.shape[0]
    group = query_weight.shape[1] // HD // slabs
    half = rows // halves
    ff = gate_weight.shape[1]
    everywhere = ("tp", "fsdp")
    side = lax.axis_index("tp") * half

    paired = parts == 4 and halves == 2 and slabs == 4 and group == 2
    w_rest = pack_stage(gate_weight, up_weight, down_weight, out_weight)
    w_rest = rows_first(lax.all_gather(rows_first(w_rest), everywhere, axis=0, tiled=True))
    w_rest = w_rest.reshape(halves, width, -1)
    qkv_width = slabs * 3 * HD

    if paired:
        gains_own = jnp.stack([first_gain.astype(F32), second_gain.astype(F32)])
        gains_own = jnp.concatenate([gains_own, jnp.zeros((6, depth), F32)])
        w_turned, normed_one, gains, *rest = front_stage(
            lengths, inputs[0], gains_own, query_weight, key_weight, value_weight, slabs, halves
        )
        gain_one, gain_two = gains[0], gains[1]
        qkv, arrived = rest[0:2], rest[2:4]
        saved = [(rest[4], rest[6]), (rest[5], rest[7])]
    else:
        gains = lax.all_gather(jnp.stack([first_gain, second_gain]), "fsdp", axis=1, tiled=True)
        gain_one, gain_two = gains[0].astype(F32), gains[1].astype(F32)
        stacked = jnp.stack(
            [w.reshape(depth, slabs, group, HD) for w in (query_weight, key_weight, value_weight)]
        ).transpose(1, 3, 2, 0, 4)
        w_qkv = lax.all_gather(
            stacked.reshape(depth, group * qkv_width), "fsdp", axis=0, tiled=True
        )
        w_heads = [w_qkv[:, h * qkv_width : (h + 1) * qkv_width] for h in range(group)]
        _, _, normed_one = normalize(inputs[0].astype(F32), gain_one)
        qkv = []
        for h in range(group):
            part = mm(w_heads[h], normed_one, (((0,), (1,)), ((), ()))).astype(BF)
            part = part.reshape(slabs, 3 * HD, rows)
            qkv.append(lax.all_to_all(part, "ctx", 0, 0, tiled=True))
        arrived, saved = [], []
        for h in range(group):
            mix, mix_full, lse = attend(lengths, qkv[h], halves, rows)
            saved.append((mix_full, lse))
            mix = mix.reshape(slabs * halves, HD, half)
            mix = lax.all_to_all(mix, ("ctx", "tp"), 0, 0, tiled=True)
            arrived.append(mix.reshape(slabs, halves, HD, half))

    scalars = jnp.stack([lengths[0], lax.axis_index("ctx") * rows + side])
    split = 2048 if paired else w_rest.shape[2]
    output, d_middle, *d_mix, = middle_stage(
        scalars, *arrived, inputs[0], cotangent[0], gain_two[None], w_rest, split
    )
    d_mix, (g_some, *g_rest) = d_mix[:2], d_mix[2:]
    output = both_halves(output)
    s_some = lax.psum_scatter(
        rows_first(g_some.reshape(halves * width, -1)), everywhere, scatter_dimension=0, tiled=True
    )
    s_some = rows_first(s_some)

    if paired:
        back_a, back_b, g_rest = back_stage(lengths, qkv, d_mix, saved, *g_rest)
        input_gradient, s_some, s_rest, *q_grads = tail_stage(
            back_a, back_b, s_some, g_rest, normed_one, w_turned, inputs[0], gain_one[None], d_middle
        )
        s_gate, s_up, s_down, s_out, *s_qkv, d_gains, input_gradient = finish_stage(
            s_some, s_rest, *q_grads, (query_weight, key_weight, value_weight), gate_weight,
            up_weight, gains_own, input_gradient,
        )
        d_gains = d_gains[0:2]
        d_gains = d_gains + swap(d_gains, "tp", 1)
    else:
        d_local = [
            attend_back(lengths, qkv[h], d_mix[h], *saved[h], 512) for h in range(group)
        ]
        d_qkv = [
            lax.all_to_all(d, "ctx", 0, 0, tiled=True).reshape(qkv_width, rows) for d in d_local
        ]
        d_normed_one = jnp.zeros((rows, width), F32)
        s_qkv = []
        for h in range(group):
            d_normed_one = d_normed_one + mm(d_qkv[h], w_heads[h], (((0,), (1,)), ((), ())))
            grad = mm(normed_one, d_qkv[h], (((0,), (1,)), ((), ()))).astype(BF)
            grad = lax.psum_scatter(grad, "fsdp", scatter_dimension=0, tiled=True)
            s_qkv.append(lax.psum(grad, "ctx").reshape(depth, slabs, 3, HD))
        d_normed_one = lax.psum_scatter(d_normed_one, "tp", scatter_dimension=0, tiled=True)
        own = lax.dynamic_slice_in_dim(inputs[0], side, half, 0)
        scaled_one, inverse_one, _ = normalize(own.astype(F32), gain_one)
        d_from_one = norm_back(d_normed_one, scaled_one, inverse_one, gain_one)
        input_gradient = lax.all_gather(
            (d_middle + d_from_one).astype(BF), "tp", axis=0, tiled=True
        )
        s_qkv = jnp.stack(s_qkv, axis=2).transpose(3, 0, 1, 2, 4)
        s_qkv = s_qkv.reshape(3, depth, slabs * group * HD).astype(F32)
        s_all = lax.psum(s_some, "ctx").astype(F32)
        d_gain_one = sum(
            jnp.sum(w.astype(F32) * s, axis=1)
            for w, s in zip((query_weight, key_weight, value_weight), s_qkv)
        ) / first_gain.astype(F32)
        d_gain_two = (
            jnp.sum(gate_weight.astype(F32) * s_all[:, :ff], axis=1)
            + jnp.sum(up_weight.astype(F32) * s_all[:, ff : 2 * ff], axis=1)
        ) / second_gain.astype(F32)
        d_gains = jnp.stack([d_gain_one, d_gain_two])
        d_gains = lax.psum(d_gains, "tp")
        s_gate, s_up, s_down, s_out = (
            s_all[:, :ff], s_all[:, ff : 2 * ff], s_all[:, 2 * ff : 3 * ff].T, s_all[:, 3 * ff :].T
        )

    return (
        output[None],
        input_gradient[None],
        d_gains[0],
        s_qkv[0],
        s_qkv[1],
        s_qkv[2],
        s_out,
        d_gains[1],
        s_gate,
        s_up,
        s_down,
    )


def solution(mesh):
    rows = P("fsdp", "ctx", None)
    gain = P("fsdp")
    inward = P("fsdp", "tp")
    outward = P("tp", "fsdp")
    return jax.shard_map(
        shards,
        mesh=mesh,
        in_specs=(
            rows, gain, gain, inward, inward, inward, outward, gain, inward, inward, outward, rows,
        ),
        out_specs=(
            rows, rows, gain, inward, inward, inward, outward, gain, inward, inward, outward,
        ),
        check_vma=False,
    )
```

```python
import functools

import jax
import jax.numpy as jnp
from jax import lax
from jax.experimental import pallas as pl
from jax.experimental.pallas import tpu as pltpu
from jax.experimental.layout import Layout, with_layout_constraint
from jax.sharding import PartitionSpec as P

HD = 64
EPSILON = 1e-05
MASKED = -1000000000.0
NN = (((1,), (0,)), ((), ()))
NT = (((1,), (1,)), ((), ()))
TN = (((0,), (0,)), ((), ()))
BF = jnp.bfloat16
F32 = jnp.float32


def mm(left, right, dims):
    return lax.dot_general(left, right, dims, preferred_element_type=F32)


def spread_keys(keys, start, length):
    rows = keys.shape[0]
    pos = start + lax.broadcasted_iota(jnp.int32, (rows, HD), 0)
    lane = lax.broadcasted_iota(jnp.int32, (rows, HD), 1)
    bias = jnp.where((lane == 0) & (pos >= length), MASKED, 0.0)
    return jnp.concatenate([keys, bias], axis=1).astype(BF)


def spread_queries(queries):
    row = lax.broadcasted_iota(jnp.int32, queries.shape, 0)
    ones = jnp.where(row == 0, 1.0, 0.0)
    return jnp.concatenate([queries * HD**-0.5, ones], axis=0).astype(BF)


def attend_rows(tile, length, qkv, kx, qx, vx, emit):
    slabs, _, rows = qkv.shape
    per = rows // tile
    blocks = slabs * per
    for z in range(slabs):
        keys = qkv[z, HD : 2 * HD, :].astype(F32).T
        kx[z * rows : (z + 1) * rows, :] = spread_keys(keys, z * rows, length)
        queries = spread_queries(qkv[z, 0:HD, :].astype(F32))
        for b in range(per):
            cut = slice(b * tile, (b + 1) * tile)
            qx[z * per + b] = queries[:, cut]
            vx[z * per + b] = qkv[z, 2 * HD : 3 * HD, cut]
    later = lax.broadcasted_iota(jnp.int32, (tile, tile), 0) > lax.broadcasted_iota(
        jnp.int32, (tile, tile), 1
    )

    def query_block(i, _):
        queries = qx[i]

        def step(j, carry, masked):
            highest, total, mix = carry
            keys = kx[pl.ds(pl.multiple_of(j * tile, tile), tile), :]
            scores = mm(keys, queries, NN)
            if masked:
                scores = jnp.where(later, MASKED, scores)
            new = jnp.maximum(highest, jnp.max(scores, axis=0, keepdims=True))
            scale = jnp.exp(highest - new)
            probs = jnp.exp(scores - new)
            total = total * scale + jnp.sum(probs, axis=0, keepdims=True)
            mix = mix * scale + mm(vx[j], probs.astype(BF), NN)
            return new, total, mix

        first = (
            jnp.full((1, tile), -jnp.inf, F32),
            jnp.zeros((1, tile), F32),
            jnp.zeros((HD, tile), F32),
        )
        carry = lax.fori_loop(0, i, lambda j, c: step(j, c, False), first)
        highest, total, mix = step(i, carry, True)
        emit(i, mix / total, highest + jnp.log(total))
        return 0

    lax.fori_loop(0, blocks, query_block, 0)


def attend_kernel(tile, len_ref, qkv, o_ref, of_ref, lse_ref, kx, qx, vx):
    rows = qkv.shape[2]
    halves = o_ref.shape[1]
    half = rows // halves

    def emit(i, mix, lse):
        of_ref[i] = mix
        lse_ref[i] = lse
        for t in range(halves):
            o_ref[i, t] = mix[:, t * half : (t + 1) * half].astype(BF)

    attend_rows(tile, len_ref[0], qkv, kx, qx, vx, emit)


def front_kernel(
    len_ref, x, gains_own, wq, wk, wv,
    wt_hbm, normed_hbm, gains, qkv_a_hbm, qkv_b_hbm, mix_a, mix_b, of_a_hbm, of_b_hbm,
    lse_a_hbm, lse_b_hbm,
    wt, normed, qkv_a, qkv_b, of_a, of_b, lse_a, lse_b, out_sems, packed, parts, mixed, kx, qx, vx,
    gain_send, gain_recv, w_send, w_recv, part_send, part_recv, part_local,
    mix_send, mix_recv, mix_local,
):
    here, line, place = lax.axis_index("ctx"), lax.axis_index("tp"), lax.axis_index("fsdp")
    core, column = lax.rem(place, 2), place // 2
    pair = place + 1 - 2 * core
    other = lax.rem(place + 2, 4)
    mesh_id = pl.DeviceIdType.MESH
    slabs, halves = mix_a.shape[0], mix_a.shape[1]
    rows, width = x.shape
    half = rows // halves
    wide = slabs * 3 * HD
    depth = wq.shape[0]
    peers = [(dz, dt) for dz in range(slabs) for dt in range(halves) if dz or dt]

    def peer(dz, dt):
        return lax.rem(here + dz, slabs), lax.rem(line + dt, halves)

    barrier = pltpu.get_barrier_semaphore()
    for dz, dt in peers:
        z, t = peer(dz, dt)
        pl.semaphore_signal(barrier, inc=1, device_id={"ctx": z, "tp": t}, device_id_type=mesh_id)
    for device in (pair, other):
        pl.semaphore_signal(barrier, inc=1, device_id={"fsdp": device}, device_id_type=mesh_id)
    for q, w in enumerate((wq, wk, wv)):
        flat = w[...].astype(F32).T.astype(BF)
        for z in range(slabs):
            for h in range(2):
                at = (2 * z + h) * HD
                packed[h, (3 * z + q) * HD : (3 * z + q + 1) * HD, :] = flat[at : at + HD]

    def remote(source, target, send, recv, device):
        return pltpu.make_async_remote_copy(
            src_ref=source, dst_ref=target, send_sem=send, recv_sem=recv,
            device_id=device, device_id_type=mesh_id,
        )

    def lanes(index):
        return pl.ds(pl.multiple_of(index * depth, depth), depth)

    def weight(h, index):
        return wt.at[h * wide : (h + 1) * wide, lanes(index)]

    gains[:, lanes(place)] = gains_own[...]
    for h in range(2):
        wt[h * wide : (h + 1) * wide, lanes(place)] = packed[h]
    pl.semaphore_wait(barrier, len(peers) + 2)
    sent = []

    def launch(move):
        move.start()
        sent.append(move)
        return move

    for k, device in enumerate((pair, other)):
        launch(
            remote(
                gains_own, gains.at[:, lanes(place)], gain_send.at[k], gain_recv.at[k], {"fsdp": device}
            )
        )
    for h in range(2):
        for k, device in ((1, other), (0, pair)):
            launch(
                remote(
                    packed.at[h], weight(h, place), w_send.at[h, k], w_recv.at[h, k], {"fsdp": device}
                )
            )

    def arrived(ref, sem):
        remote(ref, ref, gain_send.at[0], sem, {"fsdp": pair}).wait_recv()

    arrived(gains.at[:, lanes(other)], gain_recv.at[1])
    launch(
        remote(
            gains.at[:, lanes(other)], gains.at[:, lanes(other)], gain_send.at[2], gain_recv.at[2],
            {"fsdp": pair},
        )
    )
    far = lax.rem(pair + 2, 4)
    arrived(gains.at[:, lanes(pair)], gain_recv.at[0])
    arrived(gains.at[:, lanes(far)], gain_recv.at[2])
    small = 64

    def norm(r, _):
        cut = pl.ds(pl.multiple_of(r * small, small), small)
        values = x[cut, :].astype(F32)
        inverse = lax.rsqrt(jnp.mean(values * values, axis=1, keepdims=True) + EPSILON)
        normed[cut, :] = (values * inverse * gains[0:1, :]).astype(BF)
        return 0

    lax.fori_loop(0, rows // small, norm, 0)
    kept = []

    def keep(source, target):
        move = pltpu.make_async_copy(source, target, out_sems.at[len(kept)])
        move.start()
        kept.append(move)

    keep(normed, normed_hbm)
    queues = (qkv_a, qkv_b)
    waits = []
    for h in range(2):
        arrived(weight(h, other), w_recv.at[h, 1])
        launch(
            remote(
                weight(h, other), weight(h, other), w_send.at[h, 2], w_recv.at[h, 2], {"fsdp": pair}
            )
        )
    for h in range(2):
        arrived(weight(h, pair), w_recv.at[h, 0])
        arrived(weight(h, far), w_recv.at[h, 2])

        def project(n, _):
            cut = pl.ds(pl.multiple_of(n * 256, 256), 256)
            value = mm(wt[h * wide : (h + 1) * wide, :], normed[cut, :], NT).astype(BF)
            for z in range(slabs):
                parts[h, z, :, cut] = value[z * 3 * HD : (z + 1) * 3 * HD]
            return 0

        lax.fori_loop(0, rows // 256, project, 0)
        for k in range(1, slabs):
            z = lax.rem(here + k, slabs)
            waits.append(
                launch(
                    remote(
                        parts.at[h, z], queues[h].at[here], part_send.at[h, k], part_recv.at[h, k],
                        {"ctx": z},
                    )
                )
            )
        stays = pltpu.make_async_copy(parts.at[h, here], queues[h].at[here], part_local.at[h])
        stays.start()
        waits.append(stays)

    keep(wt, wt_hbm)
    for h, (qkv, mix_ref, of_ref, lse_ref) in enumerate(
        ((qkv_a, mix_a, of_a, lse_a), (qkv_b, mix_b, of_b, lse_b))
    ):
        for move in waits[h * slabs : (h + 1) * slabs - 1]:
            move.wait_recv()
        waits[(h + 1) * slabs - 1].wait()
        keep(qkv, (qkv_a_hbm, qkv_b_hbm)[h])

        def emit(i, mix, lse):
            of_ref[i] = mix
            lse_ref[i] = lse
            for t in range(halves):
                mixed[h, i, t] = mix[:, t * half : (t + 1) * half].astype(BF)
                stay = (i == here) & (line == t)

                @pl.when(stay)
                def _():
                    pltpu.make_async_copy(
                        mixed.at[h, i, t], mix_ref.at[here, line], mix_local.at[h]
                    ).start()

                @pl.when(jnp.logical_not(stay))
                def _():
                    remote(
                        mixed.at[h, i, t], mix_ref.at[here, line], mix_send.at[h, i, t],
                        mix_recv.at[h, here, line], {"ctx": i, "tp": t},
                    ).start()

        attend_rows(rows, len_ref[0], qkv, kx, qx, vx, emit)
        keep(of_ref, (of_a_hbm, of_b_hbm)[h])
        keep(lse_ref, (lse_a_hbm, lse_b_hbm)[h])

    for move in sent:
        move.wait_send()
    for move in kept:
        move.wait()
    for h, mix_ref in enumerate((mix_a, mix_b)):
        pltpu.make_async_copy(mixed.at[h, here, line], mix_ref.at[here, line], mix_local.at[h]).wait()
        for dz, dt in peers:
            z, t = peer(dz, dt)
            remote(
                mixed.at[h, z, t], mix_ref.at[z, t], mix_send.at[h, z, t], mix_recv.at[h, z, t],
                {"ctx": z, "tp": t},
            ).wait()


def front_stage(length, x, gains, wq, wk, wv, slabs, halves):
    rows, width = x.shape
    half = rows // halves
    wide = slabs * 3 * HD
    total = slabs * rows
    work = total * (total + rows) // 2
    vmem = pl.BlockSpec(memory_space=pltpu.VMEM)
    outside = pl.BlockSpec(memory_space=pltpu.HBM)
    dma = pltpu.SemaphoreType.DMA
    shape = jax.ShapeDtypeStruct
    return pl.pallas_call(
        front_kernel,
        out_shape=(
            shape((2 * wide, width), BF),
            shape((rows, width), BF),
            shape((8, width), F32),
            *[shape((slabs, 3 * HD, rows), BF)] * 2,
            *[shape((slabs, halves, HD, half), BF)] * 2,
            *[shape((slabs, HD, rows), F32)] * 2,
            *[shape((slabs, 1, rows), F32)] * 2,
        ),
        in_specs=[pl.BlockSpec(memory_space=pltpu.SMEM)] + [vmem] * 5,
        out_specs=(outside, outside, vmem, *[outside] * 8),
        scratch_shapes=[
            pltpu.VMEM((2 * wide, width), BF),
            pltpu.VMEM((rows, width), BF),
            *[pltpu.VMEM((slabs, 3 * HD, rows), BF)] * 2,
            *[pltpu.VMEM((slabs, HD, rows), F32)] * 2,
            *[pltpu.VMEM((slabs, 1, rows), F32)] * 2,
            dma((8,)),
            pltpu.VMEM((2, wide, wq.shape[0]), BF),
            pltpu.VMEM((2, slabs, 3 * HD, rows), BF),
            pltpu.VMEM((2, slabs, halves, HD, half), BF),
            pltpu.VMEM((total, 2 * HD), BF),
            pltpu.VMEM((slabs, 2 * HD, rows), BF),
            pltpu.VMEM((slabs, HD, rows), BF),
            dma((3,)), dma((3,)), dma((2, 3)), dma((2, 3)),
            dma((2, slabs)), dma((2, slabs)), dma((2,)),
            dma((2, slabs, halves)), dma((2, slabs, halves)), dma((2,)),
        ],
        compiler_params=pltpu.CompilerParams(
            vmem_limit_bytes=60 << 20, collective_id=3, has_side_effects=True
        ),
        cost_estimate=pl.CostEstimate(
            flops=2 * work * 256 * 4, bytes_accessed=20 << 20, transcendentals=2 * work
        ),
    )(length, x, gains, wq, wk, wv)


def attend(length, qkv, halves, tile):
    slabs, _, rows = qkv.shape
    total = slabs * rows
    tile = min(tile, rows)
    work = total * (total + tile) // 2
    vmem = pl.BlockSpec(memory_space=pltpu.VMEM)
    return pl.pallas_call(
        functools.partial(attend_kernel, tile),
        out_shape=(
            jax.ShapeDtypeStruct((slabs, halves, HD, rows // halves), BF),
            jax.ShapeDtypeStruct((slabs, HD, rows), F32),
            jax.ShapeDtypeStruct((slabs, 1, rows), F32),
        ),
        in_specs=[pl.BlockSpec(memory_space=pltpu.SMEM), vmem],
        out_specs=(vmem, vmem, vmem),
        scratch_shapes=[
            pltpu.VMEM((total, 2 * HD), BF),
            pltpu.VMEM((total // tile, 2 * HD, tile), BF),
            pltpu.VMEM((total // tile, HD, tile), BF),
        ],
        compiler_params=pltpu.CompilerParams(vmem_limit_bytes=60 << 20),
        cost_estimate=pl.CostEstimate(
            flops=work * 256 * 4, bytes_accessed=qkv.size * 4, transcendentals=work
        ),
    )(length, qkv)


def attend_back_rows(tile, length, qkv, do_ref, of_ref, lse_ref, out, scratch, emit):
    kx, qx, vx, kt, dox, dq, st, dk, dv = scratch
    slabs, _, rows = qkv.shape
    halves, half = do_ref.shape[1], do_ref.shape[3]
    per = rows // tile
    blocks = slabs * per
    for z in range(slabs):
        keys = qkv[z, HD : 2 * HD, :]
        kx[z * rows : (z + 1) * rows, :] = spread_keys(keys.astype(F32).T, z * rows, length)
        queries = spread_queries(qkv[z, 0:HD, :].astype(F32))
        values = qkv[z, 2 * HD : 3 * HD, :].astype(F32).T
        vx[z * rows : (z + 1) * rows, :] = jnp.concatenate(
            [values, jnp.zeros((rows, HD), F32)], axis=1
        ).astype(BF)
        d_mix = jnp.concatenate([do_ref[z, t] for t in range(halves)], axis=1)
        delta = jnp.sum(d_mix.astype(F32) * of_ref[z], axis=0, keepdims=True)
        for b in range(per):
            cut = slice(b * tile, (b + 1) * tile)
            n = z * per + b
            qx[n] = queries[:, cut]
            kt[n] = keys[:, cut]
            dox[n, 0:HD] = d_mix[:, cut]
            dox[n, HD : 2 * HD] = jnp.zeros((HD, tile), BF)
            st[n, 0:1] = lse_ref[z, :, cut]
            st[n, 1:2] = delta[:, cut]
    for ref in (dq, dk, dv):
        ref[...] = jnp.zeros_like(ref)
    later = lax.broadcasted_iota(jnp.int32, (tile, tile), 0) > lax.broadcasted_iota(
        jnp.int32, (tile, tile), 1
    )

    def step(i, j, masked):
        here = pl.ds(pl.multiple_of(j * tile, tile), tile)
        scores = mm(kx[here, :], qx[i], NN)
        if masked:
            scores = jnp.where(later, MASKED, scores)
        probs = jnp.exp(scores - st[i, 0:1])
        d_probs = mm(vx[here, :], dox[i], NN)
        d_scores = (probs * (d_probs - st[i, 1:2])).astype(BF)
        dv[j] += mm(dox[i, 0:HD], probs.astype(BF), NT)
        dk[j] += mm(qx[i, 0:HD], d_scores, NT)
        dq[i] += mm(kt[j], d_scores, NN)

    def complete(n):
        z = n // per
        cut = pl.ds(pl.multiple_of(lax.rem(n, per) * tile, tile), tile)
        out[z, 0:HD, cut] = (dq[n] * HD**-0.5).astype(BF)
        out[z, HD : 2 * HD, cut] = dk[n].astype(BF)
        out[z, 2 * HD : 3 * HD, cut] = dv[n].astype(BF)
        if emit is not None:
            emit(n)

    def ring(k, _):
        last = blocks - 1 - k

        def down(i, _):
            step(i, k, False)
            return 0

        def across(j, _):
            step(last, j, False)
            return 0

        step(k, k, True)
        lax.fori_loop(k + 1, last + 1, down, 0)
        complete(k)
        lax.fori_loop(k + 1, last, across, 0)
        step(last, last, True)
        complete(last)
        return 0

    lax.fori_loop(0, blocks // 2, ring, 0)


def attend_back_scratch(slabs, rows, tile):
    total = slabs * rows
    blocks = total // tile
    return [
        pltpu.VMEM((total, 2 * HD), BF),
        pltpu.VMEM((blocks, 2 * HD, tile), BF),
        pltpu.VMEM((total, 2 * HD), BF),
        pltpu.VMEM((blocks, HD, tile), BF),
        pltpu.VMEM((blocks, 2 * HD, tile), BF),
        pltpu.VMEM((blocks, HD, tile), F32),
        pltpu.VMEM((blocks, 8, tile), F32),
        pltpu.VMEM((blocks, HD, tile), F32),
        pltpu.VMEM((blocks, HD, tile), F32),
    ]


def attend_back_kernel(tile, len_ref, qkv, do_ref, of_ref, lse_ref, out, *scratch):
    attend_back_rows(tile, len_ref[0], qkv, do_ref, of_ref, lse_ref, out, scratch, None)


def back_kernel(
    tile, len_ref, qkv_a, qkv_b, do_a, do_b, of_a, of_b, lse_a, lse_b, keep_hbm, got_hbm,
    out_a, out_b, rest,
    local, keep, got, low_got, high_got, swapped, *refs,
):
    scratch, sems = refs[:9], refs[9:]
    (load_sems, grad_send, grad_recv, grad_local, low_send, low_recv, high_send, high_recv,
     swap_send, swap_recv) = sems
    here, line, place = lax.axis_index("ctx"), lax.axis_index("tp"), lax.axis_index("fsdp")
    column = place // 2
    beside = {"fsdp": lax.rem(place + 2, 4)}
    across = {"tp": 1 - line}
    mesh_id = pl.DeviceIdType.MESH
    slabs, block = qkv_a.shape[0], qkv_a.shape[1]
    loads = [
        pltpu.make_async_copy(source, target, load_sems.at[k])
        for k, (source, target) in enumerate(((keep_hbm, keep), (got_hbm, got)))
    ]
    for load in loads:
        load.start()
    others = [lax.rem(here + k, slabs) for k in range(1, slabs)]
    barrier = pltpu.get_barrier_semaphore()
    for device in (*[{"ctx": z} for z in others], beside, across):
        pl.semaphore_signal(barrier, inc=1, device_id=device, device_id_type=mesh_id)
    pl.semaphore_wait(barrier, slabs + 1)

    def remote(source, target, send, recv, device):
        return pltpu.make_async_remote_copy(
            src_ref=source, dst_ref=target, send_sem=send, recv_sem=recv,
            device_id=device, device_id_type=mesh_id,
        )

    outs = (out_a, out_b)

    per = qkv_a.shape[2] // tile

    def lanes(b):
        return pl.ds(pl.multiple_of(b * tile, tile), tile)

    def window(h, at, b):
        return outs[h].at[pl.ds(pl.multiple_of(at * block, block), block), lanes(b)]

    def attend_head(h, qkv, do_ref, of_ref, lse_ref):
        def emit(n):
            z, b = n // per, lax.rem(n, per)

            @pl.when(z == here)
            def _():
                pltpu.make_async_copy(
                    local.at[h, z, :, lanes(b)], window(h, here, b), grad_local.at[h, b]
                ).start()

            @pl.when(z != here)
            def _():
                remote(
                    local.at[h, z, :, lanes(b)], window(h, here, b), grad_send.at[h, z, b],
                    grad_recv.at[h, here, b], {"ctx": z},
                ).start()

        attend_back_rows(
            tile, len_ref[0], qkv, do_ref, of_ref, lse_ref, local.at[h], scratch, emit
        )

    for load in loads:
        load.wait()
    cut = rest.shape[0] // 2
    for t in range(2):
        for x in range(2):
            keep[t, x] = (keep[t, x].astype(F32) + got[t, x].astype(F32)).astype(BF)
    moves = []
    for k in range(2):
        moves.append(
            remote(
                keep.at[1 - line, k, 0:cut], low_got.at[k], low_send.at[k], low_recv.at[k], across
            )
        )
        moves.append(
            remote(
                keep.at[k, 1 - column, cut : 2 * cut], high_got.at[k], high_send.at[k],
                high_recv.at[k], beside,
            )
        )
    for move in moves:
        move.start()
    attend_head(0, qkv_a, do_a, of_a, lse_a)
    attend_head(1, qkv_b, do_b, of_b, lse_b)
    for move in moves:
        move.wait_recv()
    low, high = slice(0, cut), slice(cut, 2 * cut)
    for k in range(2):
        keep[line, k, low] = (
            keep[line, k, low].astype(F32) + low_got[k].astype(F32)
        ).astype(BF)
        keep[k, column, high] = (
            keep[k, column, high].astype(F32) + high_got[k].astype(F32)
        ).astype(BF)
    swaps = [
        remote(
            keep.at[line, 1 - column, low], swapped.at[0], swap_send.at[0], swap_recv.at[0], beside
        ),
        remote(
            keep.at[1 - line, column, high], swapped.at[1], swap_send.at[1], swap_recv.at[1], across
        ),
    ]
    for move in swaps:
        move.start()
    for move in swaps:
        move.wait_recv()
    for k, part in enumerate((low, high)):
        rest[part] = (
            keep[line, column, part].astype(F32) + swapped[k].astype(F32)
        ).astype(BF)
    for h in range(2):
        for b in range(per):
            pltpu.make_async_copy(
                local.at[h, here, :, lanes(b)], window(h, here, b), grad_local.at[h, b]
            ).wait()
            for z in others:
                remote(
                    local.at[h, z, :, lanes(b)], window(h, z, b), grad_send.at[h, z, b],
                    grad_recv.at[h, z, b], {"ctx": z},
                ).wait()
    for move in (*moves, *swaps):
        move.wait_send()


def back_stage(length, qkv, d_mix, saved, keep, got):
    slabs, block, rows = qkv[0].shape
    tile = 512
    lanes = keep.shape[3]
    total = slabs * rows
    work = total * (total + tile) // 2
    vmem = pl.BlockSpec(memory_space=pltpu.VMEM)
    outside = pl.BlockSpec(memory_space=pl.ANY)
    dma = pltpu.SemaphoreType.DMA
    return pl.pallas_call(
        functools.partial(back_kernel, tile),
        out_shape=(
            jax.ShapeDtypeStruct((slabs * block, rows), BF),
            jax.ShapeDtypeStruct((slabs * block, rows), BF),
            jax.ShapeDtypeStruct((256, lanes), BF),
        ),
        in_specs=[pl.BlockSpec(memory_space=pltpu.SMEM)] + [vmem] * 8 + [outside] * 2,
        out_specs=(vmem,) * 3,
        scratch_shapes=[
            pltpu.VMEM((2, slabs, block, rows), BF),
            pltpu.VMEM(keep.shape, BF),
            pltpu.VMEM(keep.shape, BF),
            pltpu.VMEM((2, 128, lanes), BF),
            pltpu.VMEM((2, 128, lanes), BF),
            pltpu.VMEM((2, 128, lanes), BF),
            *attend_back_scratch(slabs, rows, tile),
            dma((2,)), dma((2, slabs, rows // tile)), dma((2, slabs, rows // tile)),
            dma((2, rows // tile)),
            dma((2,)), dma((2,)), dma((2,)), dma((2,)), dma((2,)), dma((2,)),
        ],
        compiler_params=pltpu.CompilerParams(
            vmem_limit_bytes=60 << 20, collective_id=4, has_side_effects=True
        ),
        cost_estimate=pl.CostEstimate(
            flops=2 * work * 256 * 10, bytes_accessed=24 << 20, transcendentals=2 * work
        ),
    )(length, *qkv, *d_mix, *[m for m, _ in saved], *[l for _, l in saved], keep, got)


def attend_back(length, qkv, d_mix, mix, lse, tile):
    slabs, _, rows = qkv.shape
    total = slabs * rows
    tile = min(tile, rows)
    work = total * (total + tile) // 2
    vmem = pl.BlockSpec(memory_space=pltpu.VMEM)
    return pl.pallas_call(
        functools.partial(attend_back_kernel, tile),
        out_shape=jax.ShapeDtypeStruct((slabs, 3 * HD, rows), BF),
        in_specs=[pl.BlockSpec(memory_space=pltpu.SMEM), vmem, vmem, vmem, vmem],
        out_specs=vmem,
        scratch_shapes=attend_back_scratch(slabs, rows, tile),
        compiler_params=pltpu.CompilerParams(vmem_limit_bytes=60 << 20),
        cost_estimate=pl.CostEstimate(
            flops=work * 256 * 10, bytes_accessed=qkv.size * 8, transcendentals=work
        ),
    )(length, qkv, d_mix, mix, lse)


def widths(total, step):
    return [(at, min(step, total - at)) for at in range(0, total, step)]


def middle_kernel(
    ff, split, scal, mix_a_hbm, mix_b_hbm, own_hbm, cot_hbm, gain, w_hbm,
    out_ref, dmid_ref, got_a, got_b, *refs,
):
    n_out = 3 if split < w_hbm.shape[2] else 1
    grads = refs[:n_out]
    (w, acts, att_t, mid, scale, dn, normed_ref, branch_ref, dattn_ref, turned, do_a, do_b,
     sems, out_sems, send_sems, recv_sems, local_sems, core_send, core_recv,
     own, cot, mix_a, mix_b, row_sems) = refs[n_out:]
    slabs, halves, _, half = mix_a.shape
    width = own.shape[1]
    side = pl.ds(pl.multiple_of(lax.axis_index("tp") * half, half), half)
    row_loads = [
        pltpu.make_async_copy(source.at[side, :], target, row_sems.at[k])
        for k, (source, target) in enumerate(((own_hbm, own), (cot_hbm, cot)))
    ]
    mix_loads = [
        pltpu.make_async_copy(source, target, row_sems.at[2 + k])
        for k, (source, target) in enumerate(((mix_a_hbm, mix_a), (mix_b_hbm, mix_b)))
    ]
    for load in (*mix_loads, *row_loads):
        load.start()
    inner = width // halves
    base = 3 * ff
    lanes = base + inner
    here, line = lax.axis_index("ctx"), lax.axis_index("tp")
    core = lax.rem(lax.axis_index("fsdp"), 2)
    sibling = {"fsdp": lax.axis_index("fsdp") + 1 - 2 * core}
    barrier = pltpu.get_barrier_semaphore()
    peers = [(dz, dt) for dz in range(slabs) for dt in range(halves) if dz or dt]

    def peer(dz, dt):
        return lax.rem(here + dz, slabs), lax.rem(line + dt, halves)

    for dz, dt in peers:
        z, t = peer(dz, dt)
        pl.semaphore_signal(
            barrier, inc=1, device_id={"ctx": z, "tp": t}, device_id_type=pl.DeviceIdType.MESH
        )
    if n_out == 3:
        pl.semaphore_signal(
            barrier, inc=1, device_id=sibling, device_id_type=pl.DeviceIdType.MESH
        )
    cuts = [(t, base, inner) for t in range(halves)]
    cuts += [(t, k * ff, ff) for t in range(halves) for k in range(3)]
    loads = [
        pltpu.make_async_copy(
            w_hbm.at[t, :, at : at + n], w.at[t, :, at : at + n], sems.at[k]
        )
        for k, (t, at, n) in enumerate(cuts)
    ]
    for load in loads:
        load.start()
    length, first = scal[0], scal[1]
    step = 256
    rows = 64

    for load in mix_loads:
        load.wait()
    for t in range(halves):
        for z in range(slabs):
            at = z * 2 * HD
            att_t[at : at + HD, :] = mix_a[z, t]
            att_t[at + HD : at + 2 * HD, :] = mix_b[z, t]
        acts[t, :, base:lanes] = att_t[...].astype(F32).T.astype(BF)
    for k in range(halves):
        loads[k].wait()
    for load in row_loads:
        load.wait()

    def project(n, _):
        cut = pl.ds(pl.multiple_of(n * step, step), step)
        total = own[:, cut].astype(F32)
        for t in range(halves):
            total = total + mm(acts[t, :, base:lanes], w[t, cut, base:lanes], NT)
        mid[:, cut] = total
        return 0

    lax.fori_loop(0, width // step, project, 0)

    def row_mask(r):
        pos = first + r * rows + lax.broadcasted_iota(jnp.int32, (rows, 1), 0)
        return jnp.where(pos < length, 1.0, 0.0)

    def norm(r, _):
        cut = pl.ds(pl.multiple_of(r * rows, rows), rows)
        values = mid[cut, :]
        inverse = lax.rsqrt(jnp.mean(values * values, axis=1, keepdims=True) + EPSILON)
        scale[cut, :] = jnp.broadcast_to(inverse, (rows, 128))
        normed_ref[cut, :] = (values * inverse * gain[...]).astype(BF)
        branch_ref[cut, :] = (cot[cut, :].astype(F32) * row_mask(r)).astype(BF)
        return 0

    lax.fori_loop(0, half // rows, norm, 0)

    for t in range(halves):
        for k in range(3):
            loads[halves + 3 * t + k].wait()

        def columns(at, n):
            def cut(k):
                return pl.ds(pl.multiple_of(k * ff + at, 128), n)

            gate = mm(normed_ref[...], w[t, :, cut(0)], NN)
            upward = mm(normed_ref[...], w[t, :, cut(1)], NN)
            d_hidden = mm(branch_ref[...], w[t, :, cut(2)], NN)
            sig = 1.0 / (1.0 + jnp.exp(-gate))
            active = gate * sig
            acts[t, :, cut(2)] = (active * upward).astype(BF)
            acts[t, :, cut(0)] = (
                d_hidden * upward * sig * (1.0 + gate * (1.0 - sig))
            ).astype(BF)
            acts[t, :, cut(1)] = (d_hidden * active).astype(BF)

        def chunk(c, _):
            columns(c * step, step)
            return 0

        lax.fori_loop(0, ff // step, chunk, 0)
        if ff % step:
            columns(ff - ff % step, ff % step)

    def back(n, _):
        cut = pl.ds(pl.multiple_of(n * step, step), step)
        total = mid[:, cut]
        grad = jnp.zeros((half, step), F32)
        for t in range(halves):
            total = total + mm(acts[t, :, 2 * ff : base], w[t, cut, 2 * ff : base], NT)
            grad = grad + mm(acts[t, :, 0:ff], w[t, cut, 0:ff], NT)
            grad = grad + mm(acts[t, :, ff : 2 * ff], w[t, cut, ff : 2 * ff], NT)
        dmid_ref[:, cut] = total
        dn[:, cut] = grad
        return 0

    lax.fori_loop(0, width // step, back, 0)

    def finish(r, _):
        cut = pl.ds(pl.multiple_of(r * rows, rows), rows)
        mask = row_mask(r)
        out_ref[cut, :] = (dmid_ref[cut, :] * mask).astype(BF)
        inverse = scale[cut, 0:1]
        scaled = mid[cut, :] * inverse
        d_scaled = dn[cut, :] * gain[...]
        mean = jnp.mean(d_scaled * scaled, axis=1, keepdims=True)
        total = cot[cut, :].astype(F32) * mask + inverse * (d_scaled - scaled * mean)
        dmid_ref[cut, :] = total
        dattn_ref[cut, :] = total.astype(BF)
        return 0

    lax.fori_loop(0, half // rows, finish, 0)
    for t in range(halves):
        for z in range(0, slabs, 2):
            at = base + z * 2 * HD
            grad = mm(dattn_ref[...], w[t, :, at : at + 4 * HD], NN).T.astype(BF)
            for k in range(2):
                do_a[z + k, t] = grad[2 * k * HD : (2 * k + 1) * HD]
                do_b[z + k, t] = grad[(2 * k + 1) * HD : (2 * k + 2) * HD]

    pl.semaphore_wait(barrier, len(peers) + (n_out == 3))
    moves = []
    for k, (dz, dt) in enumerate(peers):
        z, t = peer(dz, dt)
        for h, (source, target) in enumerate(((do_a, got_a), (do_b, got_b))):
            move = pltpu.make_async_remote_copy(
                src_ref=source.at[z, t],
                dst_ref=target.at[here, line],
                send_sem=send_sems.at[2 * k + h],
                recv_sem=recv_sems.at[2 * k + h],
                device_id={"ctx": z, "tp": t},
                device_id_type=pl.DeviceIdType.MESH,
            )
            move.start()
            moves.append(move)
    for h, (source, target) in enumerate(((do_a, got_a), (do_b, got_b))):
        move = pltpu.make_async_copy(
            source.at[here, line], target.at[here, line], local_sems.at[h]
        )
        move.start()
        moves.append(move)

    regions = ((0, 2 * ff), (2 * ff, base), (base, lanes))

    def own_copy(n, t):
        cut = pl.ds(pl.multiple_of(n * step, step), step)
        return pltpu.make_async_copy(
            w.at[t, cut, split:lanes], grads[1].at[t, n // 2], out_sems.at[n, t, 1]
        )

    def core_copy(n, t):
        cut = pl.ds(pl.multiple_of(n * step, step), step)
        return pltpu.make_async_remote_copy(
            src_ref=w.at[t, cut, split:lanes], dst_ref=grads[2].at[t, n // 2],
            send_sem=core_send.at[n, t], recv_sem=core_recv.at[n, t],
            device_id=sibling, device_id_type=pl.DeviceIdType.MESH,
        )

    def some_copy(t):
        return pltpu.make_async_copy(
            w.at[t, :, 0:split], grads[0].at[t], out_sems.at[0, t, 0]
        )

    def store(t):
        if n_out == 1:
            return

        def rows_of(n, _):
            @pl.when(lax.rem(n, 2) == core)
            def _():
                own_copy(n, t).start()

            @pl.when(lax.rem(n, 2) != core)
            def _():
                core_copy(n, t).start()

            return 0

        lax.fori_loop(0, width // step, rows_of, 0)

    for k, ref in enumerate((normed_ref, branch_ref, dattn_ref)):
        for b in range(0, width, step):
            turned[k, b : b + step] = ref[:, b : b + step].astype(F32).T.astype(BF)
    for t in range(halves):

        def fill(k, at, n):
            cut = pl.ds(at, n)
            w[t, :, cut] = mm(turned[k], acts[t, :, cut], NN).astype(BF)

        def span(k, start, stop):
            def chunk(c, _):
                fill(k, pl.multiple_of(start + c * step, 128), step)
                return 0

            count = (stop - start) // step
            lax.fori_loop(0, count, chunk, 0)
            if start + count * step < stop:
                fill(k, start + count * step, stop - start - count * step)

        for k, (at, end) in enumerate(regions):
            if at < split < end:
                span(k, at, split)
                at = split
                some_copy(t).start()
            span(k, at, end)
            if end == split:
                some_copy(t).start()
        store(t)

    for t in range(halves):
        some_copy(t).wait()

        def settle(n, _):
            @pl.when(lax.rem(n, 2) == core)
            def _():
                own_copy(n, t).wait()
                core_copy(n, t).wait_recv()

            @pl.when(lax.rem(n, 2) != core)
            def _():
                core_copy(n, t).wait_send()

            return 0

        if n_out == 3:
            lax.fori_loop(0, width // step, settle, 0)
    for move in moves:
        move.wait()


def middle_stage(scalars, mix_a, mix_b, own, cot, gain, w, split):
    halves, width, lanes = w.shape
    slabs, _, _, half = mix_a.shape
    ff = (lanes - width // halves) // 3
    blocks = width // 256
    peers = slabs * halves - 1
    vmem = pl.BlockSpec(memory_space=pltpu.VMEM)
    outside = pl.BlockSpec(memory_space=pl.ANY)
    out_shape = [
        jax.ShapeDtypeStruct((half, width), BF),
        jax.ShapeDtypeStruct((half, width), F32),
        jax.ShapeDtypeStruct(mix_a.shape, BF),
        jax.ShapeDtypeStruct(mix_a.shape, BF),
        jax.ShapeDtypeStruct((halves, width, split), BF),
    ]
    out_specs = [vmem] * 4 + [outside]
    if split < lanes:
        out_shape += [jax.ShapeDtypeStruct((halves, blocks // 2, 256, lanes - split), BF)] * 2
        out_specs += [outside] * 2
    flops = 2 * half * width * (9 * ff * halves + 3 * width)
    return pl.pallas_call(
        functools.partial(middle_kernel, ff, split),
        out_shape=out_shape,
        in_specs=[
            pl.BlockSpec(memory_space=pltpu.SMEM), *[pl.BlockSpec(memory_space=pltpu.HBM)] * 4,
            vmem, outside,
        ],
        out_specs=out_specs,
        scratch_shapes=[
            pltpu.VMEM((halves, width, lanes), BF),
            pltpu.VMEM((halves, half, lanes), BF),
            pltpu.VMEM((width // halves, half), BF),
            pltpu.VMEM((half, width), F32),
            pltpu.VMEM((half, 128), F32),
            pltpu.VMEM((half, width), F32),
            pltpu.VMEM((half, width), BF),
            pltpu.VMEM((half, width), BF),
            pltpu.VMEM((half, width), BF),
            pltpu.VMEM((3, width, half), BF),
            pltpu.VMEM(mix_a.shape, BF),
            pltpu.VMEM(mix_a.shape, BF),
            pltpu.SemaphoreType.DMA((4 * halves,)),
            pltpu.SemaphoreType.DMA((blocks, halves, 2)),
            pltpu.SemaphoreType.DMA((2 * peers,)),
            pltpu.SemaphoreType.DMA((2 * peers,)),
            pltpu.SemaphoreType.DMA((2,)),
            pltpu.SemaphoreType.DMA((blocks, halves)),
            pltpu.SemaphoreType.DMA((blocks, halves)),
            pltpu.VMEM((half, width), BF),
            pltpu.VMEM((half, width), BF),
            pltpu.VMEM(mix_a.shape, BF),
            pltpu.VMEM(mix_a.shape, BF),
            pltpu.SemaphoreType.DMA((4,)),
        ],
        compiler_params=pltpu.CompilerParams(
            vmem_limit_bytes=60 << 20, collective_id=1, has_side_effects=True
        ),
        cost_estimate=pl.CostEstimate(
            flops=flops, bytes_accessed=4 * w.size + 16 * half * width, transcendentals=half * lanes
        ),
    )(scalars, mix_a, mix_b, own, cot, gain, w)


class LineSum:
    def __init__(self, source, held, slots, out, sems):
        self.source, self.held, self.slots, self.out = source, held, slots, out
        self.sum_send, self.sum_recv, self.out_send, self.out_recv = sems
        here = lax.axis_index("ctx")
        self.low = here < 2
        self.place = jnp.where(self.low, here, 3 - here)
        self.inward = jnp.where(self.low, here + 1, here - 1)
        self.outward = jnp.where(self.low, here - 1, here + 1)
        self.size = out.shape[0] // 4

    def number(self, part):
        return jnp.where(self.low, part, 3 - part)

    def part(self, ref, part):
        at = pl.multiple_of(self.number(part) * self.size, self.size)
        return ref.at[pl.ds(at, self.size), :]

    def read(self, ref, part):
        at = pl.multiple_of(self.number(part) * self.size, self.size)
        return ref[pl.ds(at, self.size), :].astype(F32)

    def write(self, ref, part, value):
        at = pl.multiple_of(self.number(part) * self.size, self.size)
        ref[pl.ds(at, self.size), :] = value.astype(BF)

    def copy(self, source, target, send, recv, place):
        return pltpu.make_async_remote_copy(
            src_ref=source, dst_ref=target, send_sem=send, recv_sem=recv,
            device_id={"ctx": place}, device_id_type=pl.DeviceIdType.MESH,
        )

    def took(self, slot):
        ref = self.slots.at[slot]
        self.copy(ref, ref, self.sum_send.at[0], self.sum_recv.at[slot], self.inward).wait_recv()
        return self.slots[slot].astype(F32)

    def begin(self):
        @pl.when(self.place == 0)
        def _():
            for k in range(3):
                self.copy(
                    self.part(self.source, 3 - k), self.slots.at[k],
                    self.sum_send.at[k], self.sum_recv.at[k], self.inward,
                ).start()

    def left(self, k):
        self.copy(
            self.slots.at[0], self.slots.at[0],
            self.sum_send.at[k], self.sum_recv.at[0], self.inward,
        ).wait_send()

    def first(self, k):
        @pl.when(self.place == 1)
        def _():
            self.write(self.held, 3 - k, self.read(self.source, 3 - k) + self.took(k))
            self.copy(
                self.part(self.held, 3 - k), self.slots.at[3 + k],
                self.sum_send.at[k], self.sum_recv.at[3 + k], self.inward,
            ).start()

    def second(self):
        @pl.when(self.place == 1)
        def _():
            self.write(self.held, 0, self.read(self.source, 0) + self.took(3))
            self.copy(
                self.part(self.held, 0), self.slots.at[3],
                self.sum_send.at[2], self.sum_recv.at[3], self.outward,
            ).start()

    def give(self, part, send, place):
        ref = self.part(self.out, part)
        return self.copy(
            ref, ref, self.out_send.at[send], self.out_recv.at[self.number(part)], place
        )

    def final(self):
        @pl.when(self.place == 1)
        def _():
            self.write(self.out, 1, self.read(self.source, 1) + self.took(2) + self.took(4))
            self.give(1, 0, self.inward).start()
            self.give(1, 1, self.outward).start()

        @pl.when(self.place == 0)
        def _():
            self.write(self.out, 0, self.read(self.source, 0) + self.took(3))
            self.give(0, 0, self.inward).start()

    def forward(self):
        @pl.when(self.place == 1)
        def _():
            for k, (part, place) in enumerate(((0, self.inward), (2, self.outward), (3, self.outward))):
                self.give(part, 2 + k, place).wait_recv()
                self.give(part, 2 + k, place).start()

    def end(self):
        @pl.when(self.place == 0)
        def _():
            for k in range(3):
                self.left(k)
            self.give(0, 0, self.inward).wait_send()
            for part in (1, 2, 3):
                self.give(part, 0, self.inward).wait_recv()

        @pl.when(self.place == 1)
        def _():
            for k in range(3):
                self.left(k)
            for k in range(5):
                self.give(1, k, self.inward).wait_send()


def tail_kernel(
    back_a, back_b, some, rest, normed, weights, own_hbm, gain, dmid,
    grad_out, some_out, rest_out, qa_out, qb_out,
    turned, some_held, some_slots, rest_held, rest_slots,
    local, crossed, column_sum, columned, q_src, q_held, q_slots, theirs, got_theirs, mine,
    core_send, core_recv, col_send, col_recv,
    row_send, row_recv, out_send, out_recv, *line_sems,
):
    here, line, place = lax.axis_index("ctx"), lax.axis_index("tp"), lax.axis_index("fsdp")
    core, column = lax.rem(place, 2), place // 2
    sibling = {"fsdp": place + 1 - 2 * core}
    beside = {"fsdp": lax.rem(place + 2, 4)}
    across = {"tp": 1 - line}
    others = [{"ctx": lax.rem(here + k, 4)} for k in range(1, 4)]
    mesh_id = pl.DeviceIdType.MESH
    barrier = pltpu.get_barrier_semaphore()
    for device in (*others, sibling, beside, across):
        pl.semaphore_signal(barrier, inc=1, device_id=device, device_id_type=mesh_id)
    pl.semaphore_wait(barrier, 6)

    def remote(source, target, send, recv, device):
        return pltpu.make_async_remote_copy(
            src_ref=source, dst_ref=target, send_sem=send, recv_sem=recv,
            device_id=device, device_id_type=mesh_id,
        )

    rows = normed.shape[0]
    half = rows // 2
    depth = 256
    own, own_sem, *line_sems = line_sems
    load = pltpu.make_async_copy(
        own_hbm.at[pl.ds(pl.multiple_of(line * half, half), half), :], own, own_sem
    )
    load.start()
    a, b, qa, qb = (
        LineSum(src, held, slots, out, line_sems[4 * k : 4 * k + 4])
        for k, (src, held, slots, out) in enumerate(
            (
                (some, some_held, some_slots, some_out),
                (rest, rest_held, rest_slots, rest_out),
                (q_src.at[0], q_held.at[0], q_slots.at[0], qa_out),
                (q_src.at[1], q_held.at[1], q_slots.at[1], qb_out),
            )
        )
    )
    a.begin()

    def weight_gradient(h, grads):
        def step(n, _):
            cut = pl.ds(pl.multiple_of(n * depth, depth), depth)
            value = mm(grads[...], normed[:, cut], NN).astype(BF)
            local[h, lax.rem(n, 2), n // 2] = value
            return 0

        lax.fori_loop(0, 4, step, 0)
        move = remote(
            local.at[h, 1 - core], crossed.at[h], core_send.at[h], core_recv.at[h], sibling
        )
        move.start()
        return move

    def column_step(h, move):
        move.wait_recv()
        for x in range(2):
            column_sum[h, x] = (
                local[h, core, x].astype(F32) + crossed[h, x].astype(F32)
            ).astype(BF)
        move = remote(
            column_sum.at[h, 1 - column], columned.at[h], col_send.at[h], col_recv.at[h], beside
        )
        move.start()
        return move

    def column_end(h, move):
        move.wait_recv()
        q_src[h] = (column_sum[h, column].astype(F32) + columned[h].astype(F32)).astype(BF)

    def turn(h, grads):
        for k in range(0, grads.shape[0], 128):
            at = h * grads.shape[0] + k
            turned[:, at : at + 128] = grads[k : k + 128, :].astype(F32).T.astype(BF)

    pieces = 2
    piece = half // pieces
    sent_rows = []
    sent_out = []
    mine_start = pl.multiple_of(line * half, half)

    def make_theirs(k):
        cut = slice(k * piece, (k + 1) * piece)
        start = pl.multiple_of((1 - line) * half + k * piece, piece)

        def make(n, _):
            wide = pl.ds(pl.multiple_of(n * depth, depth), depth)
            value = mm(turned[pl.ds(start, piece), :], weights[:, wide], NN)
            theirs[cut, wide] = value.astype(BF)
            return 0

        lax.fori_loop(0, 4, make, 0)
        move = remote(theirs.at[cut], got_theirs.at[cut], row_send.at[k], row_recv.at[k], across)
        move.start()
        sent_rows.append(move)

    def make_mine(n, _):
        wide = pl.ds(pl.multiple_of(n * depth, depth), depth)
        mine[:, wide] = mm(turned[pl.ds(mine_start, half), :], weights[:, wide], NN)
        return 0

    def finish_rows(k):
        small = 64
        if k == 0:
            load.wait()
        sent_rows[k].wait_recv()

        def back(r, _):
            at = pl.multiple_of(k * piece + r * small, small)
            cut = pl.ds(at, small)
            values = own[cut, :].astype(F32)
            inverse = lax.rsqrt(jnp.mean(values * values, axis=1, keepdims=True) + EPSILON)
            scaled = values * inverse
            d_scaled = (mine[cut, :] + got_theirs[cut, :].astype(F32)) * gain[...]
            mean = jnp.mean(d_scaled * scaled, axis=1, keepdims=True)
            total = dmid[cut, :] + inverse * (d_scaled - scaled * mean)
            grad_out[pl.ds(pl.multiple_of(line * half + at, small), small), :] = total.astype(BF)
            return 0

        lax.fori_loop(0, piece // small, back, 0)
        ref = grad_out.at[pl.ds(pl.multiple_of(line * half + k * piece, piece), piece), :]
        move = remote(ref, ref, out_send.at[k], out_recv.at[k], across)
        move.start()
        sent_out.append(move)

    b.begin()
    turn(0, back_a)
    turn(1, back_b)
    make_theirs(0)
    core_a = weight_gradient(0, back_a)
    a.first(0)
    make_theirs(1)
    core_b = weight_gradient(1, back_b)
    a.first(1)
    col_a = column_step(0, core_a)
    lax.fori_loop(0, 4, make_mine, 0)
    a.second()
    col_b = column_step(1, core_b)
    b.first(0)
    a.final()
    b.first(1)
    finish_rows(0)
    b.second()
    a.forward()
    column_end(0, col_a)
    qa.begin()
    b.final()
    finish_rows(1)
    column_end(1, col_b)
    qb.begin()
    qa.first(0)
    qa.first(1)
    b.forward()
    qb.first(0)
    qb.first(1)
    qa.second()
    qa.final()
    qb.second()
    qb.final()
    qa.forward()
    qb.forward()
    for run in (a, b, qa, qb):
        run.end()
    for move in (core_a, core_b, col_a, col_b, *sent_rows):
        move.wait_send()
    for k, move in enumerate(sent_out):
        move.wait_send()
        ref = grad_out.at[pl.ds(pl.multiple_of((1 - line) * half + k * piece, piece), piece), :]
        remote(ref, ref, out_send.at[k], out_recv.at[k], across).wait_recv()


def tail_stage(back_a, back_b, some, rest, normed, weights, own, gain, dmid):
    rows, width = normed.shape
    half = rows // 2
    lanes_a, lanes_b = some.shape[1], rest.shape[1]
    wide = back_a.shape[0]
    vmem = pl.BlockSpec(memory_space=pltpu.VMEM)
    dma = pltpu.SemaphoreType.DMA
    return pl.pallas_call(
        tail_kernel,
        out_shape=(
            jax.ShapeDtypeStruct((rows, width), BF),
            jax.ShapeDtypeStruct((256, lanes_a), BF),
            jax.ShapeDtypeStruct((256, lanes_b), BF),
            jax.ShapeDtypeStruct((wide, 256), BF),
            jax.ShapeDtypeStruct((wide, 256), BF),
        ),
        in_specs=[vmem] * 6 + [pl.BlockSpec(memory_space=pl.ANY)] + [vmem] * 2,
        out_specs=(vmem,) * 5,
        scratch_shapes=[
            pltpu.VMEM((rows, 2 * wide), BF),
            pltpu.VMEM((256, lanes_a), BF),
            pltpu.VMEM((5, 64, lanes_a), BF),
            pltpu.VMEM((256, lanes_b), BF),
            pltpu.VMEM((5, 64, lanes_b), BF),
            pltpu.VMEM((2, 2, 2, wide, 256), BF),
            pltpu.VMEM((2, 2, wide, 256), BF),
            pltpu.VMEM((2, 2, wide, 256), BF),
            pltpu.VMEM((2, wide, 256), BF),
            pltpu.VMEM((2, wide, 256), BF),
            pltpu.VMEM((2, wide, 256), BF),
            pltpu.VMEM((2, 5, wide // 4, 256), BF),
            pltpu.VMEM((half, width), BF),
            pltpu.VMEM((half, width), BF),
            pltpu.VMEM((half, width), F32),
            dma((2,)), dma((2,)), dma((2,)), dma((2,)),
            dma((2,)), dma((2,)), dma((2,)), dma((2,)),
            pltpu.VMEM((half, width), BF), dma,
        ]
        + [dma((3,)), dma((5,)), dma((5,)), dma((4,))] * 4,
        compiler_params=pltpu.CompilerParams(
            vmem_limit_bytes=60 << 20, collective_id=2, has_side_effects=True
        ),
        cost_estimate=pl.CostEstimate(
            flops=8 * rows * width * wide, bytes_accessed=40 << 20, transcendentals=0
        ),
    )(back_a, back_b, some, rest, normed, weights, own, gain, dmid)


def pack_kernel(gate, up, down_hbm, out_hbm, packed_hbm, packed, down, out, sems):
    ff = gate.shape[1]
    first = packed.at[:, 0 : 2 * ff]
    last = packed.at[:, 2 * ff :]
    loads = [
        pltpu.make_async_copy(source, target, sems.at[k])
        for k, (source, target) in enumerate(
            (
                (gate, packed.at[:, 0:ff]),
                (up, packed.at[:, ff : 2 * ff]),
                (down_hbm, down),
                (out_hbm, out),
            )
        )
    ]
    for move in loads:
        move.start()
    loads[0].wait()
    loads[1].wait()
    stores = [
        pltpu.make_async_copy(first, packed_hbm.at[:, 0 : 2 * ff], sems.at[4]),
        pltpu.make_async_copy(last, packed_hbm.at[:, 2 * ff :], sems.at[5]),
    ]
    stores[0].start()
    loads[2].wait()
    loads[3].wait()
    packed[:, 2 * ff : 3 * ff] = down[...].astype(F32).T.astype(BF)
    packed[:, 3 * ff :] = out[...].astype(F32).T.astype(BF)
    stores[1].start()
    for move in stores:
        move.wait()


def pack_stage(gate, up, down, out):
    depth, ff = gate.shape
    outside = pl.BlockSpec(memory_space=pltpu.HBM)
    return pl.pallas_call(
        pack_kernel,
        out_shape=jax.ShapeDtypeStruct((depth, 3 * ff + out.shape[0]), BF),
        in_specs=[outside] * 4,
        out_specs=outside,
        scratch_shapes=[
            pltpu.VMEM((depth, 3 * ff + out.shape[0]), BF),
            pltpu.VMEM(down.shape, BF),
            pltpu.VMEM(out.shape, BF),
            pltpu.SemaphoreType.DMA((6,)),
        ],
        compiler_params=pltpu.CompilerParams(vmem_limit_bytes=60 << 20),
        cost_estimate=pl.CostEstimate(flops=0, bytes_accessed=14 * depth * ff, transcendentals=0),
    )(gate, up, down, out)


def finish_kernel(
    *refs,
):
    sources, gains, grad_in = refs[:9], refs[9], refs[10]
    gate, up, down, out, qg, kg, vg, part, grad_out = refs[11:20]
    held, grad_held, sems = refs[20:29], refs[29], refs[30]
    some, rest, qa, qb, wq, wk, wv, gate_w, up_w = held
    taken = pltpu.make_async_copy(grad_in, grad_held, sems.at[9])
    given = pltpu.make_async_copy(grad_held, grad_out, sems.at[10])
    loads = [
        pltpu.make_async_copy(source, target, sems.at[k])
        for k, (source, target) in enumerate(zip(sources, held))
    ]
    for load in loads:
        load.start()
    taken.start()
    for load in loads:
        load.wait()
    ff = gate.shape[1]
    split = some.shape[1]
    low = split - ff
    high = ff - low

    def fold(values):
        total = values[:, 0:128]
        for at in range(128, values.shape[1], 128):
            total = total + values[:, at : at + 128]
        return total

    value = some[:, 0:ff].astype(F32)
    gate[...] = value
    taken.wait()
    given.start()
    two = fold(value * gate_w[...].astype(F32))
    value = some[:, ff:split].astype(F32)
    up[:, 0:low] = value
    two = two + fold(value * up_w[:, 0:low].astype(F32))
    value = rest[:, 0:high].astype(F32)
    up[:, low:ff] = value
    two = two + fold(value * up_w[:, low:ff].astype(F32))
    down[...] = rest[:, high : high + ff].astype(F32).T
    out[...] = rest[:, high + ff :].astype(F32).T
    one = jnp.zeros((gate.shape[0], 128), F32)
    for k, (target, weight) in enumerate(((qg, wq), (kg, wk), (vg, wv))):
        for z in range(qa.shape[0] // (3 * HD)):
            at = (3 * z + k) * HD
            value = jnp.concatenate([qa[at : at + HD, :], qb[at : at + HD, :]], axis=0)
            value = value.astype(F32).T
            cut = slice(2 * HD * z, 2 * HD * (z + 1))
            target[:, cut] = value
            one = one + value * weight[:, cut].astype(F32)
    part[...] = jnp.zeros_like(part)
    part[0:1] = jnp.sum(one.T, axis=0, keepdims=True) / gains[0:1]
    part[1:2] = jnp.sum(two.T, axis=0, keepdims=True) / gains[1:2]
    given.wait()


def finish_stage(some, rest, qa, qb, weights, gate_w, up_w, gains, grad):
    depth, ff = gate_w.shape
    inner = weights[0].shape[1]
    vmem = pl.BlockSpec(memory_space=pltpu.VMEM)
    outside = pl.BlockSpec(memory_space=pltpu.HBM)
    shape = jax.ShapeDtypeStruct
    operands = (some, rest, qa, qb, *weights, gate_w, up_w)
    return pl.pallas_call(
        finish_kernel,
        out_shape=(
            shape((depth, ff), F32), shape((depth, ff), F32), shape((ff, depth), F32),
            shape((inner, depth), F32), *[shape((depth, inner), F32)] * 3,
            shape((8, depth), F32), shape(grad.shape, BF),
        ),
        in_specs=[outside] * 9 + [vmem, outside],
        out_specs=(vmem,) * 8 + (outside,),
        scratch_shapes=[
            *[pltpu.VMEM(a.shape, BF) for a in operands], pltpu.VMEM(grad.shape, BF),
            pltpu.SemaphoreType.DMA((11,)),
        ],
        compiler_params=pltpu.CompilerParams(vmem_limit_bytes=60 << 20),
        cost_estimate=pl.CostEstimate(flops=0, bytes_accessed=16 << 20, transcendentals=0),
    )(*operands, gains, grad)


def normalize(values, gain):
    inverse = lax.rsqrt(jnp.mean(values * values, axis=-1, keepdims=True) + EPSILON)
    scaled = values * inverse
    return scaled, inverse, (scaled * gain).astype(BF)


def norm_back(d_normed, scaled, inverse, gain):
    d_scaled = d_normed * gain
    d_values = inverse * (d_scaled - scaled * jnp.mean(d_scaled * scaled, axis=-1, keepdims=True))
    return d_values


def rows_first(values):
    return with_layout_constraint(values, Layout(major_to_minor=tuple(range(values.ndim))))


def swap(values, axis, bit):
    count = lax.axis_size(axis)
    return lax.ppermute(values, axis, [(k, k ^ bit) for k in range(count)])


def both_halves(values):
    other = swap(values, "tp", 1)
    first = lax.axis_index("tp") == 0
    return jnp.concatenate([jnp.where(first, values, other), jnp.where(first, other, values)])


def shards(
    inputs,
    lengths,
    first_gain,
    query_weight,
    key_weight,
    value_weight,
    out_weight,
    second_gain,
    gate_weight,
    up_weight,
    down_weight,
    cotangent,
):
    slabs, halves, parts = lax.axis_size("ctx"), lax.axis_size("tp"), lax.axis_size("fsdp")
    rows, width = inputs.shape[1], inputs.shape[2]
    depth = query_weight.shape[0]
    group = query_weight.shape[1] // HD // slabs
    half = rows // halves
    ff = gate_weight.shape[1]
    everywhere = ("tp", "fsdp")
    side = lax.axis_index("tp") * half

    paired = parts == 4 and halves == 2 and slabs == 4 and group == 2
    w_rest = pack_stage(gate_weight, up_weight, down_weight, out_weight)
    w_rest = rows_first(lax.all_gather(rows_first(w_rest), everywhere, axis=0, tiled=True))
    w_rest = w_rest.reshape(halves, width, -1)
    qkv_width = slabs * 3 * HD

    if paired:
        gains_own = jnp.stack([first_gain.astype(F32), second_gain.astype(F32)])
        gains_own = jnp.concatenate([gains_own, jnp.zeros((6, depth), F32)])
        w_turned, normed_one, gains, *rest = front_stage(
            lengths, inputs[0], gains_own, query_weight, key_weight, value_weight, slabs, halves
        )
        gain_one, gain_two = gains[0], gains[1]
        qkv, arrived = rest[0:2], rest[2:4]
        saved = [(rest[4], rest[6]), (rest[5], rest[7])]
    else:
        gains = lax.all_gather(jnp.stack([first_gain, second_gain]), "fsdp", axis=1, tiled=True)
        gain_one, gain_two = gains[0].astype(F32), gains[1].astype(F32)
        stacked = jnp.stack(
            [w.reshape(depth, slabs, group, HD) for w in (query_weight, key_weight, value_weight)]
        ).transpose(1, 3, 2, 0, 4)
        w_qkv = lax.all_gather(
            stacked.reshape(depth, group * qkv_width), "fsdp", axis=0, tiled=True
        )
        w_heads = [w_qkv[:, h * qkv_width : (h + 1) * qkv_width] for h in range(group)]
        _, _, normed_one = normalize(inputs[0].astype(F32), gain_one)
        qkv = []
        for h in range(group):
            part = mm(w_heads[h], normed_one, (((0,), (1,)), ((), ()))).astype(BF)
            part = part.reshape(slabs, 3 * HD, rows)
            qkv.append(lax.all_to_all(part, "ctx", 0, 0, tiled=True))
        arrived, saved = [], []
        for h in range(group):
            mix, mix_full, lse = attend(lengths, qkv[h], halves, rows)
            saved.append((mix_full, lse))
            mix = mix.reshape(slabs * halves, HD, half)
            mix = lax.all_to_all(mix, ("ctx", "tp"), 0, 0, tiled=True)
            arrived.append(mix.reshape(slabs, halves, HD, half))

    scalars = jnp.stack([lengths[0], lax.axis_index("ctx") * rows + side])
    split = 2304 if paired else w_rest.shape[2]
    output, d_middle, *d_mix, = middle_stage(
        scalars, *arrived, inputs[0], cotangent[0], gain_two[None], w_rest, split
    )
    d_mix, (g_some, *g_rest) = d_mix[:2], d_mix[2:]
    output = both_halves(output)
    s_some = lax.psum_scatter(
        rows_first(g_some.reshape(halves * width, -1)), everywhere, scatter_dimension=0, tiled=True
    )
    s_some = rows_first(s_some)

    if paired:
        back_a, back_b, g_rest = back_stage(lengths, qkv, d_mix, saved, *g_rest)
        input_gradient, s_some, s_rest, *q_grads = tail_stage(
            back_a, back_b, s_some, g_rest, normed_one, w_turned, inputs[0], gain_one[None], d_middle
        )
        s_gate, s_up, s_down, s_out, *s_qkv, d_gains, input_gradient = finish_stage(
            s_some, s_rest, *q_grads, (query_weight, key_weight, value_weight), gate_weight,
            up_weight, gains_own, input_gradient,
        )
        d_gains = d_gains[0:2]
        d_gains = d_gains + swap(d_gains, "tp", 1)
    else:
        d_local = [
            attend_back(lengths, qkv[h], d_mix[h], *saved[h], 512) for h in range(group)
        ]
        d_qkv = [
            lax.all_to_all(d, "ctx", 0, 0, tiled=True).reshape(qkv_width, rows) for d in d_local
        ]
        d_normed_one = jnp.zeros((rows, width), F32)
        s_qkv = []
        for h in range(group):
            d_normed_one = d_normed_one + mm(d_qkv[h], w_heads[h], (((0,), (1,)), ((), ())))
            grad = mm(normed_one, d_qkv[h], (((0,), (1,)), ((), ()))).astype(BF)
            grad = lax.psum_scatter(grad, "fsdp", scatter_dimension=0, tiled=True)
            s_qkv.append(lax.psum(grad, "ctx").reshape(depth, slabs, 3, HD))
        d_normed_one = lax.psum_scatter(d_normed_one, "tp", scatter_dimension=0, tiled=True)
        own = lax.dynamic_slice_in_dim(inputs[0], side, half, 0)
        scaled_one, inverse_one, _ = normalize(own.astype(F32), gain_one)
        d_from_one = norm_back(d_normed_one, scaled_one, inverse_one, gain_one)
        input_gradient = lax.all_gather(
            (d_middle + d_from_one).astype(BF), "tp", axis=0, tiled=True
        )
        s_qkv = jnp.stack(s_qkv, axis=2).transpose(3, 0, 1, 2, 4)
        s_qkv = s_qkv.reshape(3, depth, slabs * group * HD).astype(F32)
        s_all = lax.psum(s_some, "ctx").astype(F32)
        d_gain_one = sum(
            jnp.sum(w.astype(F32) * s, axis=1)
            for w, s in zip((query_weight, key_weight, value_weight), s_qkv)
        ) / first_gain.astype(F32)
        d_gain_two = (
            jnp.sum(gate_weight.astype(F32) * s_all[:, :ff], axis=1)
            + jnp.sum(up_weight.astype(F32) * s_all[:, ff : 2 * ff], axis=1)
        ) / second_gain.astype(F32)
        d_gains = jnp.stack([d_gain_one, d_gain_two])
        d_gains = lax.psum(d_gains, "tp")
        s_gate, s_up, s_down, s_out = (
            s_all[:, :ff], s_all[:, ff : 2 * ff], s_all[:, 2 * ff : 3 * ff].T, s_all[:, 3 * ff :].T
        )

    return (
        output[None],
        input_gradient[None],
        d_gains[0],
        s_qkv[0],
        s_qkv[1],
        s_qkv[2],
        s_out,
        d_gains[1],
        s_gate,
        s_up,
        s_down,
    )


def solution(mesh):
    rows = P("fsdp", "ctx", None)
    gain = P("fsdp")
    inward = P("fsdp", "tp")
    outward = P("tp", "fsdp")
    return jax.shard_map(
        shards,
        mesh=mesh,
        in_specs=(
            rows, gain, gain, inward, inward, inward, outward, gain, inward, inward, outward, rows,
        ),
        out_specs=(
            rows, rows, gain, inward, inward, inward, outward, gain, inward, inward, outward,
        ),
        check_vma=False,
    )
```
